32 devices in a mesh: ctx: 16 (over z, y, core), wt: 2 (over x).
Axes of the slice: x: 2, y: 2, z: 4, core: 2. Of those that a mesh axis runs over, the one named last changes fastest.
Arguments:
- tokens: bfloat16 [2, 2, 2048, 1024], P(None, 'wt', 'ctx'), may hold values from -6 to 6
- positions: int32 [2, 2, 2048], P(None, 'wt', 'ctx'), may hold values from 0 to 2047
- buckets: int32 [2, 2, 2048], P(None, 'wt', 'ctx'), may hold values from 0 to 63
- qkv_w: bfloat16 [1024, 3072], P('wt'), may hold values from -0.1875 to 0.1875
- out_w: bfloat16 [1024, 1024], P('wt'), may hold values from -6 to 6
- up_w: bfloat16 [1024, 4096], P('wt'), may hold values from -0.1875 to 0.1875
- down_w: bfloat16 [4096, 1024], P('wt'), may hold values from -0.09375 to 0.09375
- time_w: bfloat16 [256, 2048], P('wt'), may hold values from -0.1875 to 0.1875
- noise_table: bfloat16 [64, 256], P('wt'), may hold values from -6 to 6
- gain_one: bfloat16 [1024], P('wt'), may hold values from 0.099609375 to 1.8984375
- gain_two: bfloat16 [1024], P('wt'), may hold values from 0.099609375 to 1.8984375
- cotangent: bfloat16 [2, 2, 2048, 1024], P(None, 'wt', 'ctx'), may hold values from -6 to 6
Outputs:
- layer_out: bfloat16 [2, 2, 2048, 1024], P(None, 'wt', 'ctx')
- input_grad: bfloat16 [2, 2, 2048, 1024], P(None, 'wt', 'ctx')
- qkv_grad: float32 [1024, 3072], P('wt')
- out_grad: float32 [1024, 1024], P('wt')
- up_grad: float32 [1024, 4096], P('wt')
- down_grad: float32 [4096, 1024], P('wt')
- time_grad: float32 [256, 2048], P('wt')
- table_grad: float32 [64, 256], P('wt')
- gain_one_grad: float32 [1024], P('wt')
- gain_two_grad: float32 [1024], P('wt')
The draws below stay inside these ranges and needn't reach their ends.
All inputs are finite; a program needn't handle non-finite values.
Results may differ from the reference program's by a relative error of at most 0.024.
Values may be sent and summed in bfloat16 or wider, within the bound.
A program may use at most 320 MiB of HBM per device.

```python
import math
import jax
import jax.numpy as jnp
from jax import lax

D = 1024
HEADS = 16
HEAD = 64
FF = 4096
TEMB = 256
NB = 64
MICRO = 2
LENGTH = 2048
SEQS = 2


def plant(drawn, key, smallest, largest):
    index_at = [jax.random.randint(jax.random.fold_in(key, axis), (), 0, length) for axis, length in enumerate(drawn.shape)]
    widest = drawn.shape.index(max(drawn.shape))
    next_to = index_at[:widest] + [(index_at[widest] + 1) % drawn.shape[widest]] + index_at[widest + 1:]
    return drawn.at[tuple(index_at)].set(smallest).at[tuple(next_to)].set(largest)


def block_levels(key, shape, cuts, least, largest):
    def one(position, parts):
        steps = jax.random.uniform(jax.random.fold_in(jax.random.fold_in(key, 6), position), (parts,), jnp.float32, least / len(cuts), largest / len(cuts))
        return jnp.repeat(jnp.exp(steps), shape[position] // parts).reshape((-1,) + (1,) * (len(shape) - position - 1))

    loudness = one(*cuts[0])
    for cut in cuts[1:]:
        loudness = loudness * one(*cut)
    return loudness


def scatter_about(own_key, shape, spread, most, pieces=(), held_as=jnp.bfloat16):
    values = jax.random.normal(own_key, shape, jnp.float32) * spread
    if len(pieces) > 0:
        values = block_levels(own_key, shape, pieces, -0.22, 0.18) * values
    return jnp.clip(values, min=-most, max=most).astype(held_as)


def setup_inputs(seed: int = 0) -> dict:
    streams_of = jax.random.split(jax.random.key(seed), 13)
    return {
        "tokens": scatter_about(streams_of[0], (MICRO, SEQS, LENGTH, D), 1.0, 6.0, ((1, 2), (2, 16))),
        "positions": plant(jax.random.randint(streams_of[1], (MICRO, SEQS, LENGTH), 0, LENGTH), jax.random.fold_in(streams_of[1], 1), 0, LENGTH - 1).astype(jnp.int32),
        "buckets": plant(jax.random.randint(streams_of[2], (MICRO, SEQS, LENGTH), 0, NB), jax.random.fold_in(streams_of[2], 1), 0, NB - 1).astype(jnp.int32),
        "qkv_w": scatter_about(streams_of[3], (D, 3 * D), D ** -0.5, 0.1875, ((0, 2),)),
        "out_w": scatter_about(streams_of[4], (D, D), (((LENGTH // 3) // D + 1) ** 0.5), 6.0, ((0, 2),)),
        "up_w": scatter_about(streams_of[5], (D, FF), D ** -0.5, 0.1875, ((0, 2),)),
        "down_w": scatter_about(streams_of[6], (FF, D), FF ** -0.5, 0.09375, ((0, 2),)),
        "time_w": scatter_about(streams_of[7], (TEMB, 2 * D), (4 * TEMB) ** -0.5, 0.1875, ((0, 2),)),
        "noise_table": scatter_about(streams_of[8], (NB, TEMB), 1.0, 6.0, ((0, 2),)),
        "gain_one": jnp.clip(1.0 + 0.18 * jax.random.normal(streams_of[9], (D,), jnp.float32), 0.099609375, 1.8984375).astype(jnp.bfloat16),
        "gain_two": jnp.clip(1.0 + 0.18 * jax.random.normal(streams_of[10], (D,), jnp.float32), 0.099609375, 1.8984375).astype(jnp.bfloat16),
        "cotangent": scatter_about(streams_of[11], (MICRO, SEQS, LENGTH, D), 1.0, 6.0, ((1, 2), (2, 16))),
    }


@jax.custom_vjp
def low(v):
    return lax.optimization_barrier(v.astype(jnp.bfloat16)).astype(jnp.float32)

@jax.custom_vjp
def low_back(v):
    return v

def low_keep(v):
    return (low(v), None)

def low_pass(kept, grad):
    return (grad,)

def back_keep(v):
    return (v, None)

def back_low(kept, grad):
    return (low(grad),)
low.defvjp(low_keep, low_pass)
low_back.defvjp(back_keep, back_low)
epsilon = 1e-05

def matmul(left, right):
    return jnp.dot(left, right, precision=lax.Precision.HIGHEST, preferred_element_type=jnp.float32)

def rotate(head_rows, places):
    half_size = head_rows.shape[-1] // 2
    ladder = jnp.arange(half_size, dtype=jnp.float32)
    frequency = jnp.exp(ladder * (-math.log(10000.0) * 2.0 / head_rows.shape[-1]))
    angles = places[:, None, None] * frequency[None, None, :]
    cosine = jnp.cos(angles)
    sine_part = jnp.sin(angles)
    leading = head_rows[..., :half_size]
    second = head_rows[..., half_size:]
    return jnp.concatenate([leading * cosine - second * sine_part, second * cosine + leading * sine_part], axis=-1)

def layer_norm(sequence, gain_vec, scales):
    average = lax.optimization_barrier(jnp.mean(sequence, axis=-1, keepdims=True))
    centered = sequence - average
    variance = lax.optimization_barrier(jnp.mean(centered * centered, axis=-1, keepdims=True))
    return centered * lax.rsqrt(variance + epsilon) * gain_vec * scales

def forward(weights, sequence, places, onehot):
    qkv_w, out_w, up_w, down_w, time_w, noise_table, gain_one, gain_two = weights
    length = sequence.shape[0]
    embedding = matmul(onehot, noise_table)
    shifts = low_back(matmul(embedding, time_w))
    scale_one = 1.0 + shifts[:, :D]
    scale_two = 1.0 + shifts[:, D:]
    normed = low(layer_norm(sequence, gain_one, scale_one))
    qkv_out = low_back(matmul(normed, qkv_w))
    queries = low(rotate(qkv_out[:, :D].reshape(length, HEADS, HEAD), places))
    key_rows = low(rotate(qkv_out[:, D:2 * D].reshape(length, HEADS, HEAD), places))
    values = low(qkv_out[:, 2 * D:].reshape(length, HEADS, HEAD))

    def attend(query_block):
        raw_scores = jnp.einsum('qhd,khd->hqk', query_block, key_rows, precision=lax.Precision.HIGHEST)
        scores = low_back(raw_scores) * 0.125
        softmaxed = low(jax.nn.softmax(scores, axis=-1))
        return jnp.einsum('hqk,khd->qhd', softmaxed, values, precision=lax.Precision.HIGHEST)
    block_rows = min(512, length)
    blocks = queries.reshape(length // block_rows, block_rows, HEADS, HEAD)
    attended = lax.map(jax.checkpoint(attend), blocks).reshape(length, D)
    attended = low(low_back(attended))
    branch = low_back(matmul(attended, out_w))
    middle = sequence + branch
    normed_two = low(layer_norm(middle, gain_two, scale_two))
    pre_act = low_back(matmul(normed_two, up_w))
    hidden = low(jax.nn.gelu(pre_act, approximate=False))
    return middle + low_back(matmul(hidden, down_w))

def reference(tokens, positions, buckets, qkv_w, out_w, up_w, down_w, time_w, noise_table, gain_one, gain_two, cotangent):
    weights = tuple((w_item.astype(jnp.float32) for w_item in (qkv_w, out_w, up_w, down_w, time_w, noise_table, gain_one, gain_two)))
    sequences = tokens.reshape(-1, LENGTH, D).astype(jnp.float32)
    place_rows = positions.reshape(-1, LENGTH)
    bucket_rows = buckets.reshape(-1, LENGTH)
    cot_rows = cotangent.reshape(-1, LENGTH, D).astype(jnp.float32)

    def one_sequence(totals, sample):
        sequence, place_ids, bucket_ids, cot_seq = sample
        onehot = (bucket_ids[:, None] == jnp.arange(NB, dtype=jnp.int32)[None, :]).astype(jnp.float32)
        places = place_ids.astype(jnp.float32)

        def apply_layer(weight_set, seq_rows):
            return forward(weight_set, seq_rows, places, onehot)
        result, pullback = jax.vjp(apply_layer, weights, sequence)
        weight_grads, token_grads = pullback(cot_seq)
        totals = jax.tree.map(jnp.add, totals, weight_grads)
        return (totals, (result.astype(jnp.bfloat16), token_grads.astype(jnp.bfloat16)))
    initial = tuple((jnp.zeros(w_item.shape, jnp.float32) for w_item in weights))
    totals, (results, token_grads) = lax.scan(one_sequence, initial, (sequences, place_rows, bucket_rows, cot_rows))
    layer_out = results.reshape(tokens.shape)
    input_grad = token_grads.reshape(tokens.shape)
    return (layer_out, input_grad, totals[0], totals[1], totals[2], totals[3], totals[4], totals[5], totals[6], totals[7])
```

```python
import functools
import math

import jax
import jax.numpy as jnp
from jax import lax
from jax.experimental import pallas as pl
from jax.experimental.pallas import tpu as pltpu
from jax.sharding import PartitionSpec as P

HEADS = 16
HEAD = 64
EPSILON = 1e-05
SCALE = 0.125
LOG2E = math.log2(math.e)
BF = jnp.bfloat16
F32 = jnp.float32


def dot(a, b, ca=1, cb=0):
    return lax.dot_general(a, b, (((ca,), (cb,)), ((), ())), preferred_element_type=F32)


def gather_slots(own):
    n = lax.axis_size("wt")
    parts = [own]
    for k in range(1, n):
        parts.append(lax.ppermute(own, "wt", [((i + k) % n, i) for i in range(n)]))
    return jnp.stack(parts)


def sum_slots(partial):
    n = lax.axis_size("wt")
    total = partial[0]
    for k in range(1, n):
        sent = partial[k].astype(BF)
        total = total + lax.ppermute(sent, "wt", [(i, (i + k) % n) for i in range(n)]).astype(F32)
    return total


def spread(source, pieces, first, target):
    width = source.shape[-1]
    for c in range(pieces):
        target[:, c * width : (c + 1) * width] = source[c, 0, first : first + HEAD, :]


def attend_kernel(pieces, block, qkv_ref, low_ref, full_ref, lse_ref, q_t, k_t, v_t, keys):
    length = q_t.shape[1]
    width = length // pieces
    spread(qkv_ref, pieces, 0, q_t)
    spread(qkv_ref, pieces, HEAD, k_t)
    spread(qkv_ref, pieces, 2 * HEAD, v_t)
    keys[...] = k_t[...].T
    for j in range(length // block):
        cols = slice(j * block, (j + 1) * block)
        scores = dot(keys[...], q_t[:, cols]) * (SCALE * LOG2E)
        top = jnp.max(scores, axis=0, keepdims=True)
        exps = jnp.exp2(scores - top)
        total = jnp.sum(exps, axis=0, keepdims=True)
        out = dot(v_t[...], exps.astype(BF)) / total
        full_ref[0, :, cols] = out
        lse_ref[0, :, cols] = top + jnp.log2(total)
        for c in range(block // width):
            low_ref[j * (block // width) + c, 0] = out[:, c * width : (c + 1) * width].astype(BF)


def attend(qkv, block):
    pieces, pairs, _, width = qkv.shape
    length = pieces * width
    return pl.pallas_call(
        functools.partial(attend_kernel, pieces, block),
        grid=(pairs,),
        in_specs=[pl.BlockSpec((pieces, 1, 3 * HEAD, width), lambda p: (0, p, 0, 0))],
        out_specs=[
            pl.BlockSpec((pieces, 1, HEAD, width), lambda p: (0, p, 0, 0)),
            pl.BlockSpec((1, HEAD, length), lambda p: (p, 0, 0)),
            pl.BlockSpec((1, 1, length), lambda p: (p, 0, 0)),
        ],
        out_shape=[
            jax.ShapeDtypeStruct((pieces, pairs, HEAD, width), BF),
            jax.ShapeDtypeStruct((pairs, HEAD, length), F32),
            jax.ShapeDtypeStruct((pairs, 1, length), F32),
        ],
        scratch_shapes=[pltpu.VMEM((HEAD, length), BF)] * 3 + [pltpu.VMEM((length, HEAD), BF)],
        compiler_params=pltpu.CompilerParams(vmem_limit_bytes=48 << 20),
        name="attend",
    )(qkv)


def attend_back_kernel(
    pieces, block, qkv_ref, grad_ref, full_ref, lse_ref, out_ref,
    q_t, k_t, v_t, g_t, keys, values, dq_t, dk, dv,
):
    length = q_t.shape[1]
    width = length // pieces
    spread(qkv_ref, pieces, 0, q_t)
    spread(qkv_ref, pieces, HEAD, k_t)
    spread(qkv_ref, pieces, 2 * HEAD, v_t)
    spread(grad_ref, pieces, 0, g_t)
    keys[...] = k_t[...].T
    values[...] = v_t[...].T
    for j in range(length // block):
        cols = slice(j * block, (j + 1) * block)
        query = q_t[:, cols]
        grad = g_t[:, cols]
        delta = jnp.sum(grad.astype(F32) * full_ref[0, :, cols], axis=0, keepdims=True)
        scores = dot(keys[...], query) * (SCALE * LOG2E)
        soft = jnp.exp2(scores - lse_ref[0, :, cols])
        term_v = dot(soft.astype(BF), grad, 1, 1)
        grad_soft = dot(values[...], grad)
        raw = (soft * (grad_soft - delta) * SCALE).astype(BF)
        term_k = dot(raw, query, 1, 1)
        dq_t[:, cols] = dot(k_t[...], raw)
        if j == 0:
            dv[...] = term_v
            dk[...] = term_k
        else:
            dv[...] += term_v
            dk[...] += term_k
    dk_t = dk[...].T.astype(BF)
    dv_t = dv[...].T.astype(BF)
    for c in range(pieces):
        piece = slice(c * width, (c + 1) * width)
        out_ref[c, 0, 0:HEAD, :] = dq_t[:, piece].astype(BF)
        out_ref[c, 0, HEAD : 2 * HEAD, :] = dk_t[:, piece]
        out_ref[c, 0, 2 * HEAD :, :] = dv_t[:, piece]


def attend_back(qkv, grad, full, lse, block):
    pieces, pairs, _, width = qkv.shape
    length = pieces * width
    return pl.pallas_call(
        functools.partial(attend_back_kernel, pieces, block),
        grid=(pairs,),
        in_specs=[
            pl.BlockSpec((pieces, 1, 3 * HEAD, width), lambda p: (0, p, 0, 0)),
            pl.BlockSpec((pieces, 1, HEAD, width), lambda p: (0, p, 0, 0)),
            pl.BlockSpec((1, HEAD, length), lambda p: (p, 0, 0)),
            pl.BlockSpec((1, 1, length), lambda p: (p, 0, 0)),
        ],
        out_specs=pl.BlockSpec((pieces, 1, 3 * HEAD, width), lambda p: (0, p, 0, 0)),
        out_shape=jax.ShapeDtypeStruct(qkv.shape, BF),
        scratch_shapes=[pltpu.VMEM((HEAD, length), BF)] * 4
        + [pltpu.VMEM((length, HEAD), BF)] * 2
        + [pltpu.VMEM((HEAD, length), F32)]
        + [pltpu.VMEM((length, HEAD), F32)] * 2,
        compiler_params=pltpu.CompilerParams(vmem_limit_bytes=56 << 20),
        name="attend_back",
    )(qkv, grad, full, lse)


def normed(rows):
    centered = rows - jnp.mean(rows, axis=-1, keepdims=True)
    scale = lax.rsqrt(jnp.mean(centered * centered, axis=-1, keepdims=True) + EPSILON)
    return centered * scale, scale


def norm_back(grad, hat, scale, weight):
    c = grad * weight
    return (
        c - jnp.mean(c, axis=-1, keepdims=True) - hat * jnp.mean(c * hat, axis=-1, keepdims=True)
    ) * scale


def turn(first, second, cosine, sine):
    return first * cosine - second * sine, second * cosine + first * sine


def shards(
    tokens, positions, buckets, qkv_w, out_w, up_w, down_w, time_w, noise_table,
    gain_one, gain_two, cotangent,
):
    n, ring = lax.axis_size("wt"), lax.axis_size("ctx")
    me = lax.axis_index("wt")
    micro, _, width, model = tokens.shape
    local = HEADS // n
    rows = micro * width
    total = n * rows
    pairs = HEADS * micro // ring
    length = ring * width
    block = 256

    token_slots = gather_slots(tokens.reshape(rows, model))
    cot_slots = gather_slots(cotangent.reshape(rows, model))
    index_slots = gather_slots(
        jnp.stack([positions.reshape(rows), buckets.reshape(rows)])
    )
    x = token_slots.reshape(total, model).astype(F32)
    cot = cot_slots.reshape(total, model)
    places = index_slots[:, 0].reshape(total)
    levels = index_slots[:, 1].reshape(total)

    w_qkv = lax.all_to_all(
        qkv_w.reshape(model // n, 3, n, local * HEAD), "wt", 2, 0, tiled=True
    ).reshape(model, 3 * local * HEAD)
    hidden_size = up_w.shape[1] // n
    w_up = lax.all_to_all(up_w, "wt", 1, 0, tiled=True)
    w_time = lax.all_gather(time_w, "wt", axis=0, tiled=True)
    table = lax.all_gather(noise_table, "wt", axis=0, tiled=True)
    gains = lax.all_gather(jnp.stack([gain_one, gain_two]), "wt", axis=1, tiled=True).astype(F32)
    g_one, g_two = gains[0], gains[1]

    onehot = levels[:, None] == jnp.arange(table.shape[0], dtype=jnp.int32)[None, :]
    embed = dot(onehot.astype(BF), table).astype(BF)
    shifts = dot(embed, w_time)
    scale_one = 1.0 + shifts[:, :model]
    scale_two = 1.0 + shifts[:, model:]

    hat_one, rs_one = normed(x)
    norm_one = (hat_one * g_one * scale_one).astype(BF)

    qkv_t = dot(w_qkv, norm_one, 0, 1).reshape(3, local, 2, HEAD // 2, total)
    frequency = jnp.exp(
        jnp.arange(HEAD // 2, dtype=F32) * (-math.log(10000.0) * 2.0 / HEAD)
    )
    angles = frequency[:, None] * places.astype(F32)[None, :]
    cosine, sine = jnp.cos(angles), jnp.sin(angles)
    turned = turn(qkv_t[:2, :, 0], qkv_t[:2, :, 1], cosine, sine)
    queries_keys = jnp.stack(turned, axis=2)
    qkv_low = jnp.concatenate([queries_keys.astype(BF), qkv_t[2:].astype(BF)])

    def to_heads(columns):
        parts = columns.shape[0]
        split = columns.reshape(parts, local, HEAD, n, micro, width)
        split = jnp.transpose(split, (3, 1, 4, 0, 2, 5))
        split = split.reshape(ring, pairs, parts * HEAD, width)
        return lax.all_to_all(split, "ctx", 0, 0, tiled=True)

    def to_tokens(pieces):
        parts = pieces.shape[2] // HEAD
        back = lax.all_to_all(pieces, "ctx", 0, 0, tiled=True)
        back = back.reshape(n, local, micro, parts, HEAD, width)
        return jnp.transpose(back, (3, 1, 4, 0, 2, 5)).reshape(parts, local * HEAD, total)

    qkv_heads = to_heads(qkv_low.reshape(3, local, HEAD, total))
    low, full, lse = attend(qkv_heads, block)
    attended = to_tokens(low)[0]

    branch = dot(attended, out_w, 0, 0).reshape(n, rows, model)
    summed = branch + exchange_sum(branch)
    middle = x + summed.reshape(total, model)
    hat_two, rs_two = normed(middle)
    weight_two = g_two * scale_two
    norm_two = (hat_two * weight_two).astype(BF)
    pre = dot(norm_two, w_up)
    phi_cdf = 0.5 * (1.0 + lax.erf(pre * (2.0**-0.5)))
    hidden = (pre * phi_cdf).astype(BF)
    out_part = dot(hidden, down_w).reshape(n, rows, model)
    layer_out = middle[:rows] + sum_slots(out_part)

    grad_hidden = dot(cot, down_w, 1, 1)
    density = jnp.exp(-0.5 * pre * pre) * (1.0 / math.sqrt(2.0 * math.pi))
    grad_pre = (grad_hidden * (phi_cdf + pre * density)).astype(BF)
    down_term = dot(hidden, cot, 0, 0)
    up_term = dot(norm_two, grad_pre, 0, 0)
    part = dot(grad_pre, w_up, 1, 1).reshape(n, rows, model)
    grad_norm_two = (part + exchange_sum(part)).reshape(total, model)
    grad_mid = cot.astype(F32) + norm_back(grad_norm_two, hat_two, rs_two, weight_two)
    grad_branch = grad_mid.astype(BF)
    own = slice(0, rows)
    eh_two = grad_norm_two[own] * hat_two[own]
    grad_scale_two = eh_two * g_two
    gain_two_term = jnp.sum(eh_two * scale_two[own], axis=0)
    out_term = dot(attended, grad_branch, 1, 0)

    grad_attn = dot(out_w, grad_branch, 1, 1).astype(BF)
    grad_heads = to_heads(grad_attn.reshape(1, local, HEAD, total))
    grad_pieces = attend_back(qkv_heads, grad_heads, full, lse, block)
    back = to_tokens(grad_pieces).reshape(3, local, 2, HEAD // 2, total)
    unturned = turn(back[:2, :, 0].astype(F32), back[:2, :, 1].astype(F32), cosine, -sine)
    grad_qkv = jnp.concatenate([jnp.stack(unturned, axis=2).astype(BF), back[2:]])
    grad_qkv = grad_qkv.reshape(3 * local * HEAD, total)
    qkv_term = dot(norm_one, grad_qkv, 0, 1)
    grad_norm_one = sum_slots(dot(grad_qkv, w_qkv, 0, 1).reshape(n, rows, model))

    scale_own = scale_one[own]
    input_grad = grad_mid[own] + norm_back(
        grad_norm_one, hat_one[own], rs_one[own], g_one * scale_own
    )
    eh_one = grad_norm_one * hat_one[own]
    grad_scale_one = eh_one * g_one
    gain_one_term = jnp.sum(eh_one * scale_own, axis=0)

    grad_shifts = jnp.concatenate([grad_scale_one, grad_scale_two], axis=1).astype(BF)
    level_term = dot(onehot[own].astype(BF), grad_shifts, 0, 0)
    small = jnp.concatenate([level_term, jnp.concatenate([gain_one_term, gain_two_term])[None]])
    small = lax.psum(small, ("ctx", "wt"))
    by_level = small[:-1]
    levels_here, time_here = noise_table.shape[0], time_w.shape[0]
    high = lax.Precision.HIGHEST
    time_rows = lax.dynamic_slice_in_dim(table, me * time_here, time_here, 1).astype(F32)
    time_grad = lax.dot_general(
        time_rows, by_level, (((0,), (0,)), ((), ())), precision=high, preferred_element_type=F32
    )
    level_rows = lax.dynamic_slice_in_dim(by_level, me * levels_here, levels_here, 0)
    table_grad = lax.dot_general(
        level_rows, w_time.astype(F32), (((1,), (1,)), ((), ())), precision=high,
        preferred_element_type=F32,
    )
    gain_here = gain_one.shape[0]
    gain_one_grad = lax.dynamic_slice_in_dim(small[-1], me * gain_here, gain_here, 0)
    gain_two_grad = lax.dynamic_slice_in_dim(small[-1], model + me * gain_here, gain_here, 0)

    def reduce_columns(term, groups):
        columns = term.shape[1]
        share = lax.psum_scatter(
            term.astype(BF).reshape(n, model // n, columns), "ctx", scatter_dimension=1, tiled=True
        )
        share = lax.all_to_all(share, "wt", 0, 0, tiled=True)
        whole = lax.all_gather(share, "ctx", axis=1, tiled=True)
        whole = whole.reshape(n, model // n, groups, columns // groups)
        return jnp.transpose(whole, (1, 2, 0, 3)).reshape(model // n, n * columns).astype(F32)

    up_grad = reduce_columns(up_term, 1)
    qkv_grad = reduce_columns(qkv_term, 3)
    down_grad = lax.psum(down_term.astype(BF), "ctx").astype(F32)
    out_grad = lax.psum(out_term.astype(BF), "ctx").astype(F32)
    return (
        layer_out.astype(BF).reshape(tokens.shape),
        input_grad.astype(BF).reshape(tokens.shape),
        qkv_grad,
        out_grad,
        up_grad,
        down_grad,
        time_grad,
        table_grad,
        gain_one_grad,
        gain_two_grad,
    )


def exchange_sum(partial):
    n = lax.axis_size("wt")
    low = partial.astype(BF)
    added = None
    for k in range(1, n):
        came = lax.ppermute(low, "wt", [((i + k) % n, i) for i in range(n)])
        came = jnp.roll(came, k, axis=0).astype(F32)
        added = came if added is None else added + came
    return added


def solution(mesh):
    rows = P(None, "wt", "ctx", None)
    marks = P(None, "wt", "ctx")
    weight = P("wt", None)
    gain = P("wt")
    return jax.shard_map(
        shards,
        mesh=mesh,
        in_specs=(rows, marks, marks) + (weight,) * 6 + (gain, gain, rows),
        out_specs=(rows, rows) + (weight,) * 6 + (gain, gain),
        check_vma=False,
    )
```

```python
import functools
import math

import jax
import jax.numpy as jnp
from jax import lax
from jax.experimental import pallas as pl
from jax.experimental.pallas import tpu as pltpu
from jax.sharding import PartitionSpec as P

HEADS = 16
HEAD = 64
EPSILON = 1e-05
SCALE = 0.125
LOG2E = math.log2(math.e)
BF = jnp.bfloat16
F32 = jnp.float32


def dot(a, b, ca=1, cb=0):
    return lax.dot_general(a, b, (((ca,), (cb,)), ((), ())), preferred_element_type=F32)


def swap_ring(value, places):
    n = lax.axis_size("wt")
    return lax.ppermute(value, "wt", [((i + places) % n, i) for i in range(n)])


def gather_slots(own):
    n = lax.axis_size("wt")
    return jnp.stack([own] + [swap_ring(own, k) for k in range(1, n)])


def sum_slots(partial):
    n = lax.axis_size("wt")
    total = partial[0]
    for k in range(1, n):
        total = total + swap_ring(partial[k].astype(BF), n - k).astype(F32)
    return total


MESH = pl.DeviceIdType.MESH
DEPTH = 4


class Place:
    def __init__(self):
        self.ctx = lax.axis_index("ctx")
        self.wt = lax.axis_index("wt")
        self.z = lax.div(self.ctx, 4)
        self.y = lax.rem(lax.div(self.ctx, 2), 2)
        self.core = lax.rem(self.ctx, 2)
        self.right = {"ctx": self.index(lax.min(self.z + 1, DEPTH - 1), self.y, self.core)}
        self.left = {"ctx": self.index(lax.max(self.z - 1, 0), self.y, self.core)}
        self.across = {"ctx": self.index(self.z, 1 - self.y, self.core)}
        self.twin = {"ctx": self.index(self.z, self.y, 1 - self.core)}
        self.pair = {"wt": 1 - self.wt}

    @staticmethod
    def index(z, y, core):
        return (z * 2 + y) * 2 + core

    def greet(self, everyone=False, pair=True):
        barrier = pltpu.get_barrier_semaphore()

        def signal(device):
            pl.semaphore_signal(barrier, inc=1, device_id=device, device_id_type=MESH)

        if everyone:
            for d in range(1, 16):
                signal({"ctx": lax.rem(self.ctx + d, 16)})
            count = 15
        else:
            signal(self.across)
            signal(self.twin)
            pl.when(self.z > 0)(lambda: signal(self.left))
            pl.when(self.z < DEPTH - 1)(lambda: signal(self.right))
            inner = jnp.logical_and(self.z > 0, self.z < DEPTH - 1).astype(jnp.int32)
            count = 3 + inner
        if pair:
            signal(self.pair)
            count = count + 1
        pl.semaphore_wait(barrier, count)


def push(source, target, send, receive, device):
    return pltpu.make_async_remote_copy(
        src_ref=source, dst_ref=target, send_sem=send, recv_sem=receive,
        device_id=device, device_id_type=MESH,
    )


class Gather:
    def __init__(self, place, items, sems):
        self.p, self.items = place, items
        (self.sl, self.sr, self.sy, self.sc, self.rl, self.rr, self.ry, self.rc) = sems

    @staticmethod
    def semaphores(count):
        dma = pltpu.SemaphoreType.DMA
        line, square = dma((count, DEPTH)), dma((count, DEPTH, 2))
        return [line, line, line, square, line, line, line, square]

    def rightward(self, t, d, source=None):
        here = self.items[t](self.p.index(self.p.z - d, self.p.y, self.p.core))
        return push(here if source is None else source, here, self.sr.at[t, d], self.rl.at[t, d + 1], self.p.right)

    def leftward(self, t, d, source=None):
        here = self.items[t](self.p.index(self.p.z + d, self.p.y, self.p.core))
        return push(here if source is None else source, here, self.sl.at[t, d], self.rr.at[t, d + 1], self.p.left)

    def crossing(self, t, z, source=None):
        here = self.items[t](self.p.index(z, self.p.y, self.p.core))
        return push(here if source is None else source, here, self.sy.at[t, z], self.ry.at[t, z], self.p.across)

    def twinning(self, t, z, y, source=None):
        here = self.items[t](self.p.index(z, y, self.p.core))
        return push(here if source is None else source, here, self.sc.at[t, z, y], self.rc.at[t, z, y], self.p.twin)

    def own(self, t, source=None):
        p = self.p
        pl.when(p.z < DEPTH - 1)(lambda: self.rightward(t, 0, source).start())
        pl.when(p.z > 0)(lambda: self.leftward(t, 0, source).start())
        self.crossing(t, p.z, source).start()
        self.twinning(t, p.z, p.y, source).start()

    def arrived(self, t, z, y, core, semaphore):
        piece = self.items[t](self.p.index(z, y, core))
        push(piece, piece, semaphore, semaphore, self.p.twin).wait_recv()

    def along(self, t, d):
        p = self.p

        @pl.when(p.z - d >= 0)
        def _():
            self.arrived(t, p.z - d, p.y, p.core, self.rl.at[t, d])
            pl.when(p.z < DEPTH - 1)(lambda: self.rightward(t, d).start())
            self.crossing(t, p.z - d).start()
            self.twinning(t, p.z - d, p.y).start()

        @pl.when(p.z + d < DEPTH)
        def _():
            self.arrived(t, p.z + d, p.y, p.core, self.rr.at[t, d])
            pl.when(p.z > 0)(lambda: self.leftward(t, d).start())
            self.crossing(t, p.z + d).start()
            self.twinning(t, p.z + d, p.y).start()

    def crossed(self, t, d):
        p = self.p

        def one(z):
            self.arrived(t, z, 1 - p.y, p.core, self.ry.at[t, z])
            self.twinning(t, z, 1 - p.y).start()

        if d == 0:
            one(p.z)
        else:
            pl.when(p.z - d >= 0)(lambda: one(p.z - d))
            pl.when(p.z + d < DEPTH)(lambda: one(p.z + d))

    def finish(self, t):
        p = self.p
        for z in range(DEPTH):
            self.crossing(t, z).wait_send()
            for y in range(2):
                self.twinning(t, z, y).wait_send()
                self.arrived(t, z, y, 1 - p.core, self.rc.at[t, z, y])
        for d in range(DEPTH):
            pl.when(jnp.logical_and(p.z - d >= 0, p.z < DEPTH - 1))(lambda d=d: self.rightward(t, d).wait_send())
            pl.when(jnp.logical_and(p.z + d < DEPTH, p.z > 0))(lambda d=d: self.leftward(t, d).wait_send())


FIXED = 5


def sum_kernel(
    up_own, down_own, out_own, term, small,
    up_all, down_all, out_all, qkv_all, small_all,
    from_twin, to_pair, from_pair, kept, to_across, from_across, line, to_right, from_left, to_left, from_right,
    small_in, small_mine, small_pair,
    local_sem, twin_s, twin_r, pair_s, pair_r, across_s, across_r, right_s, left_r, left_s, right_r,
    small_s, small_r, small_x, spread_s, spread_r, *gather_sems,
):
    p = Place()
    half = down_own.shape[0] // 2
    split = term.shape[2] // 2
    items = [
        lambda c: up_all.at[0, c],
        lambda c: up_all.at[1, c],
        lambda c: down_all.at[c, 0:half],
        lambda c: down_all.at[c, half:],
        lambda c: out_all.at[c],
        lambda c: qkv_all.at[c, 0:split],
        lambda c: qkv_all.at[c, split:],
    ]
    owned = [up_own.at[0], up_own.at[1], down_own.at[0:half], down_own.at[half:], out_own]
    g = Gather(p, items, gather_sems)
    fixed, late = range(FIXED), range(FIXED, len(items))
    p.greet(everyone=True)

    def to_twin(w, z, y):
        return push(
            term.at[w, p.index(z, y, 1 - p.core)], from_twin.at[w, z, y], twin_s.at[w, z, y], twin_r.at[w, z, y], p.twin
        )

    for z in range(DEPTH):
        for y in range(2):
            to_twin(1 - p.wt, z, y).start()
    for z in range(DEPTH):
        for y in range(2):
            to_twin(p.wt, z, y).start()
    for t in fixed:
        g.own(t, owned[t])
    copies = [pltpu.make_async_copy(owned[t], items[t](p.ctx), local_sem.at[t]) for t in fixed]
    for copy in copies:
        copy.start()

    def small_to(d):
        peer = lax.rem(p.ctx + d, 16)
        return push(small.at[peer], small_in.at[p.ctx], small_s.at[d], small_r.at[d], {"ctx": peer})

    for d in range(1, 16):
        small_to(d).start()
    small_in[p.ctx] = small[p.ctx]

    def with_twin(w, z, y):
        mine = term[w, p.index(z, y, p.core)].astype(F32)
        return mine + from_twin[w, z, y].astype(F32)

    def to_other(z, y):
        return push(to_pair.at[z, y], from_pair.at[z, y], pair_s.at[z, y], pair_r.at[z, y], p.pair)

    for z in range(DEPTH):
        for y in range(2):
            to_twin(1 - p.wt, z, y).wait_recv()
            to_pair[z, y] = with_twin(1 - p.wt, z, y).astype(BF)
            to_other(z, y).start()
    for z in range(DEPTH):
        for y in range(2):
            to_twin(p.wt, z, y).wait_recv()
            kept[z, y] = with_twin(p.wt, z, y).astype(BF)

    for t in fixed:
        g.along(t, 1)

    for d in range(1, 16):
        small_to(d).wait_recv()
    small_mine[...] = jnp.sum(small_in[...].astype(F32), axis=0)
    small_pair[0] = small_mine[...].astype(BF)
    small_cross = push(small_pair.at[0], small_pair.at[1], small_x.at[0], small_x.at[1], p.pair)
    small_cross.start()

    def to_y(z):
        return push(to_across.at[z], from_across.at[z], across_s.at[z], across_r.at[z], p.across)

    for z in range(DEPTH):
        for y in range(2):
            to_other(z, y).wait_recv()
        to_across[z] = (kept[z, 1 - p.y].astype(F32) + from_pair[z, 1 - p.y].astype(F32)).astype(BF)
        to_y(z).start()
        if z == 1:
            for t in fixed:
                g.along(t, 2)

    small_cross.wait()
    both = small_pair[0].astype(F32) + small_pair[1].astype(F32)
    small_all[p.ctx] = both.astype(BF)

    def small_spread(d):
        peer = lax.rem(p.ctx + d, 16)
        return push(small_all.at[p.ctx], small_all.at[p.ctx], spread_s.at[d], spread_r.at[d], {"ctx": peer})

    for d in range(1, 16):
        small_spread(d).start()

    for z in range(DEPTH):
        to_y(z).wait_recv()
        line[z] = (
            kept[z, p.y].astype(F32) + from_pair[z, p.y].astype(F32) + from_across[z].astype(F32)
        )

    def go_right(j):
        return push(to_right.at[j], from_left.at[j], right_s.at[j], left_r.at[j], p.right)

    def go_left(j):
        return push(to_left.at[j], from_right.at[j], left_s.at[j], right_r.at[j], p.left)

    def add_left(j):
        go_right(j).wait_recv()
        line[j] = line[j] + from_left[j].astype(F32)

    def add_right(j):
        go_left(j).wait_recv()
        line[j] = line[j] + from_right[j].astype(F32)

    for step in range(DEPTH - 1):
        j, i = DEPTH - 1 - step, step

        @pl.when(p.z < j)
        def _(j=j):
            pl.when(p.z > 0)(lambda: add_left(j))
            to_right[j] = line[j].astype(BF)
            go_right(j).start()

        @pl.when(p.z > i)
        def _(i=i):
            pl.when(p.z < DEPTH - 1)(lambda: add_right(i))
            to_left[i] = line[i].astype(BF)
            go_left(i).start()

    pl.when(p.z > 0)(lambda: add_left(p.z))
    pl.when(p.z < DEPTH - 1)(lambda: add_right(p.z))
    kept[0, 0] = line[p.z].astype(BF)
    final = kept.at[0, 0]
    parts = [final.at[0:split], final.at[split:]]
    for t in late:
        g.own(t, parts[t - FIXED])
    copies += [
        pltpu.make_async_copy(parts[t - FIXED], items[t](p.ctx), local_sem.at[t]) for t in late
    ]
    for t in late:
        copies[t].start()
    for t in fixed:
        g.along(t, 3)
    for t in fixed:
        g.crossed(t, 0)
    for d in (1, 2, 3):
        for t in late:
            g.along(t, d)
        for t in fixed:
            g.crossed(t, d)
    for d in range(DEPTH):
        for t in late:
            g.crossed(t, d)

    for t in range(len(items)):
        copies[t].wait()
        g.finish(t)
    for d in range(1, 16):
        small_to(d).wait_send()
        small_spread(d).wait()
    for z in range(DEPTH):
        to_y(z).wait_send()
        for y in range(2):
            to_other(z, y).wait_send()
            for w in range(2):
                to_twin(w, z, y).wait_send()
    for step in range(DEPTH - 1):
        j, i = DEPTH - 1 - step, step
        pl.when(p.z < j)(lambda j=j: go_right(j).wait_send())
        pl.when(p.z > i)(lambda i=i: go_left(i).wait_send())


def sum_and_spread(up_own, down_own, out_own, term, small):
    dma = pltpu.SemaphoreType.DMA
    rows, columns = term.shape[2:]
    piece = (rows, columns)
    vmem = pl.BlockSpec(memory_space=pltpu.VMEM)
    anywhere = pl.BlockSpec(memory_space=pl.ANY)
    outs = [
        jax.ShapeDtypeStruct((2, 16) + up_own.shape[1:], BF),
        jax.ShapeDtypeStruct((16,) + down_own.shape, BF),
        jax.ShapeDtypeStruct((16,) + out_own.shape, BF),
        jax.ShapeDtypeStruct((16,) + piece, BF),
        jax.ShapeDtypeStruct(small.shape, BF),
    ]
    return pl.pallas_call(
        sum_kernel,
        out_shape=outs,
        in_specs=[anywhere, anywhere, anywhere, vmem, vmem],
        out_specs=[anywhere, anywhere, anywhere, anywhere, vmem],
        scratch_shapes=[
            pltpu.VMEM((2, DEPTH, 2) + piece, BF),
            pltpu.VMEM((DEPTH, 2) + piece, BF),
            pltpu.VMEM((DEPTH, 2) + piece, BF),
            pltpu.VMEM((DEPTH, 2) + piece, BF),
            pltpu.VMEM((DEPTH,) + piece, BF),
            pltpu.VMEM((DEPTH,) + piece, BF),
            pltpu.VMEM((DEPTH,) + piece, F32),
            pltpu.VMEM((DEPTH,) + piece, BF),
            pltpu.VMEM((DEPTH,) + piece, BF),
            pltpu.VMEM((DEPTH,) + piece, BF),
            pltpu.VMEM((DEPTH,) + piece, BF),
            pltpu.VMEM(small.shape, BF),
            pltpu.VMEM(small.shape[1:], F32),
            pltpu.VMEM((2,) + small.shape[1:], BF),
            dma((FIXED + 2,)),
            dma((2, DEPTH, 2)),
            dma((2, DEPTH, 2)),
            dma((DEPTH, 2)),
            dma((DEPTH, 2)),
            dma((DEPTH,)),
            dma((DEPTH,)),
            dma((DEPTH,)),
            dma((DEPTH,)),
            dma((DEPTH,)),
            dma((DEPTH,)),
            dma((16,)),
            dma((16,)),
            dma((2,)),
            dma((16,)),
            dma((16,)),
        ]
        + Gather.semaphores(FIXED + 2),
        compiler_params=pltpu.CompilerParams(
            collective_id=3, has_side_effects=True, vmem_limit_bytes=56 << 20
        ),
        name="sum_and_spread",
    )(up_own, down_own, out_own, term, small)


def widen_kernel(up_ref, down_ref, out_ref, qkv_ref, up_to, down_to, out_to, qkv_to):
    columns = up_ref.shape[-1]
    up_to[:, :columns] = up_ref[0, 0].astype(F32)
    up_to[:, columns:] = up_ref[1, 0].astype(F32)
    down_to[...] = down_ref[0].astype(F32)
    out_to[...] = out_ref[0].astype(F32)
    qkv_to[...] = qkv_ref[0].astype(F32)


def widen(up, down, out, qkv):
    _, ring, up_rows, up_columns = up.shape

    def piece(a):
        return pl.BlockSpec((1,) + a.shape[1:], lambda i: (i, 0, 0))

    def row_block(a):
        return pl.BlockSpec(a.shape[1:], lambda i: (i, 0))

    def whole(a):
        return jax.ShapeDtypeStruct((ring * a.shape[1], a.shape[2]), F32)

    return pl.pallas_call(
        widen_kernel,
        grid=(ring,),
        in_specs=[
            pl.BlockSpec((2, 1, up_rows, up_columns), lambda i: (0, i, 0, 0)),
            piece(down), piece(out), piece(qkv),
        ],
        out_specs=[
            pl.BlockSpec((up_rows, 2 * up_columns), lambda i: (i, 0)),
            row_block(down), row_block(out), row_block(qkv),
        ],
        out_shape=[
            jax.ShapeDtypeStruct((ring * up_rows, 2 * up_columns), F32),
            whole(down), whole(out), whole(qkv),
        ],
        name="widen",
    )(up, down, out, qkv)


def spread(source, pieces, first, target):
    width = source.shape[-1]
    for c in range(pieces):
        target[:, c * width : (c + 1) * width] = source[c, 0, first : first + HEAD, :]


def attend_kernel(pieces, block, qkv_ref, low_ref, full_ref, lse_ref, q_t, k_t, v_t, keys):
    length = q_t.shape[1]
    width = length // pieces
    spread(qkv_ref, pieces, 0, q_t)
    spread(qkv_ref, pieces, HEAD, k_t)
    spread(qkv_ref, pieces, 2 * HEAD, v_t)
    keys[...] = k_t[...].T
    for j in range(length // block):
        cols = slice(j * block, (j + 1) * block)
        scores = dot(keys[...], q_t[:, cols]) * (SCALE * LOG2E)
        top = jnp.max(scores, axis=0, keepdims=True)
        exps = jnp.exp2(scores - top)
        total = jnp.sum(exps, axis=0, keepdims=True)
        out = dot(v_t[...], exps.astype(BF)) / total
        full_ref[0, :, cols] = out
        lse_ref[0, :, cols] = top + jnp.log2(total)
        for c in range(block // width):
            low_ref[j * (block // width) + c, 0] = out[:, c * width : (c + 1) * width].astype(BF)


def attend(qkv, block):
    pieces, pairs, _, width = qkv.shape
    length = pieces * width
    return pl.pallas_call(
        functools.partial(attend_kernel, pieces, block),
        grid=(pairs,),
        in_specs=[pl.BlockSpec((pieces, 1, 3 * HEAD, width), lambda p: (0, p, 0, 0))],
        out_specs=[
            pl.BlockSpec((pieces, 1, HEAD, width), lambda p: (0, p, 0, 0)),
            pl.BlockSpec((1, HEAD, length), lambda p: (p, 0, 0)),
            pl.BlockSpec((1, 1, length), lambda p: (p, 0, 0)),
        ],
        out_shape=[
            jax.ShapeDtypeStruct((pieces, pairs, HEAD, width), BF),
            jax.ShapeDtypeStruct((pairs, HEAD, length), F32),
            jax.ShapeDtypeStruct((pairs, 1, length), F32),
        ],
        scratch_shapes=[pltpu.VMEM((HEAD, length), BF)] * 3 + [pltpu.VMEM((length, HEAD), BF)],
        compiler_params=pltpu.CompilerParams(vmem_limit_bytes=48 << 20),
        name="attend",
    )(qkv)


def attend_back_kernel(
    pieces, block, qkv_ref, grad_ref, full_ref, lse_ref, out_ref,
    q_t, k_t, v_t, g_t, keys, values, dq_t, dk, dv,
):
    length = q_t.shape[1]
    width = length // pieces
    spread(qkv_ref, pieces, 0, q_t)
    spread(qkv_ref, pieces, HEAD, k_t)
    spread(qkv_ref, pieces, 2 * HEAD, v_t)
    spread(grad_ref, pieces, 0, g_t)
    keys[...] = k_t[...].T
    values[...] = v_t[...].T
    for j in range(length // block):
        cols = slice(j * block, (j + 1) * block)
        query = q_t[:, cols]
        grad = g_t[:, cols]
        delta = jnp.sum(grad.astype(F32) * full_ref[0, :, cols], axis=0, keepdims=True)
        scores = dot(keys[...], query) * (SCALE * LOG2E)
        soft = jnp.exp2(scores - lse_ref[0, :, cols])
        term_v = dot(soft.astype(BF), grad, 1, 1)
        grad_soft = dot(values[...], grad)
        raw = (soft * (grad_soft - delta) * SCALE).astype(BF)
        term_k = dot(raw, query, 1, 1)
        dq_t[:, cols] = dot(k_t[...], raw)
        if j == 0:
            dv[...] = term_v
            dk[...] = term_k
        else:
            dv[...] += term_v
            dk[...] += term_k
    dk_t = dk[...].T.astype(BF)
    dv_t = dv[...].T.astype(BF)
    for c in range(pieces):
        piece = slice(c * width, (c + 1) * width)
        out_ref[c, 0, 0:HEAD, :] = dq_t[:, piece].astype(BF)
        out_ref[c, 0, HEAD : 2 * HEAD, :] = dk_t[:, piece]
        out_ref[c, 0, 2 * HEAD :, :] = dv_t[:, piece]


def attend_back(qkv, grad, full, lse, block):
    pieces, pairs, _, width = qkv.shape
    length = pieces * width
    return pl.pallas_call(
        functools.partial(attend_back_kernel, pieces, block),
        grid=(pairs,),
        in_specs=[
            pl.BlockSpec((pieces, 1, 3 * HEAD, width), lambda p: (0, p, 0, 0)),
            pl.BlockSpec((pieces, 1, HEAD, width), lambda p: (0, p, 0, 0)),
            pl.BlockSpec((1, HEAD, length), lambda p: (p, 0, 0)),
            pl.BlockSpec((1, 1, length), lambda p: (p, 0, 0)),
        ],
        out_specs=pl.BlockSpec((pieces, 1, 3 * HEAD, width), lambda p: (0, p, 0, 0)),
        out_shape=jax.ShapeDtypeStruct(qkv.shape, BF),
        scratch_shapes=[pltpu.VMEM((HEAD, length), BF)] * 4
        + [pltpu.VMEM((length, HEAD), BF)] * 2
        + [pltpu.VMEM((HEAD, length), F32)]
        + [pltpu.VMEM((length, HEAD), F32)] * 2,
        compiler_params=pltpu.CompilerParams(vmem_limit_bytes=56 << 20),
        name="attend_back",
    )(qkv, grad, full, lse)


def normed(rows):
    centered = rows - jnp.mean(rows, axis=-1, keepdims=True)
    scale = lax.rsqrt(jnp.mean(centered * centered, axis=-1, keepdims=True) + EPSILON)
    return centered * scale, scale


def norm_back(grad, hat, scale, weight):
    c = grad * weight
    return (
        c - jnp.mean(c, axis=-1, keepdims=True) - hat * jnp.mean(c * hat, axis=-1, keepdims=True)
    ) * scale


def turn(first, second, cosine, sine):
    return first * cosine - second * sine, second * cosine + first * sine


def shards(
    tokens, positions, buckets, qkv_w, out_w, up_w, down_w, time_w, noise_table,
    gain_one, gain_two, cotangent,
):
    n, ring = lax.axis_size("wt"), lax.axis_size("ctx")
    me = lax.axis_index("wt")
    micro, _, width, model = tokens.shape
    rows = micro * width
    pairs = HEADS * micro // ring
    block = 256
    planar = n == 2 and ring == 16

    x = tokens.reshape(rows, model).astype(F32)
    cot_low = cotangent.reshape(rows, model)
    places = positions.reshape(rows)
    levels = buckets.reshape(rows)

    def whole_rows(weight):
        return lax.all_gather(weight, "wt", axis=0, tiled=True)

    w_qkv = whole_rows(qkv_w)
    w_out = whole_rows(out_w)
    w_time = whole_rows(time_w)
    table = whole_rows(noise_table)
    gains = lax.all_gather(jnp.stack([gain_one, gain_two]), "wt", axis=1, tiled=True).astype(F32)
    g_one, g_two = gains[0], gains[1]
    w_up = lax.all_to_all(up_w, "wt", 1, 0, tiled=True)

    onehot = levels[:, None] == jnp.arange(table.shape[0], dtype=jnp.int32)[None, :]
    embed = dot(onehot.astype(BF), table).astype(BF)
    shifts = dot(embed, w_time)
    scale_one = 1.0 + shifts[:, :model]
    scale_two = 1.0 + shifts[:, model:]

    hat_one, rs_one = normed(x)
    weight_one = g_one * scale_one
    norm_one = (hat_one * weight_one).astype(BF)

    qkv_t = dot(w_qkv, norm_one, 0, 1).reshape(3, HEADS, 2, HEAD // 2, rows)
    frequency = jnp.exp(
        jnp.arange(HEAD // 2, dtype=F32) * (-math.log(10000.0) * 2.0 / HEAD)
    )
    angles = frequency[:, None] * places.astype(F32)[None, :]
    cosine, sine = jnp.cos(angles), jnp.sin(angles)
    turned = turn(qkv_t[:2, :, 0], qkv_t[:2, :, 1], cosine, sine)
    queries_keys = jnp.stack(turned, axis=2)
    qkv_low = jnp.concatenate([queries_keys.astype(BF), qkv_t[2:].astype(BF)])

    def to_heads(columns):
        parts = columns.shape[0]
        split = columns.reshape(parts, HEADS, HEAD, micro, width)
        split = jnp.transpose(split, (1, 3, 0, 2, 4))
        split = split.reshape(ring, pairs, parts * HEAD, width)
        return lax.all_to_all(split, "ctx", 0, 0, tiled=True)

    def to_tokens(pieces):
        parts = pieces.shape[2] // HEAD
        back = lax.all_to_all(pieces, "ctx", 0, 0, tiled=True)
        back = back.reshape(HEADS, micro, parts, HEAD, width)
        return jnp.transpose(back, (2, 0, 3, 1, 4)).reshape(parts, HEADS * HEAD, rows)

    qkv_heads = to_heads(qkv_low.reshape(3, HEADS, HEAD, rows))
    low, full, lse = attend(qkv_heads, block)
    attended = to_tokens(low)[0]

    middle = x + dot(attended, w_out, 0, 0)
    hat_two, rs_two = normed(middle)
    weight_two = g_two * scale_two
    norm_two_own = (hat_two * weight_two).astype(BF)

    norm_two = gather_slots(norm_two_own).reshape(n * rows, model)
    cot = gather_slots(cot_low).reshape(n * rows, model)
    pre = dot(norm_two, w_up)
    phi_cdf = 0.5 * (1.0 + lax.erf(pre * (2.0**-0.5)))
    hidden = (pre * phi_cdf).astype(BF)
    layer_out = middle + sum_slots(dot(hidden, down_w).reshape(n, rows, model))

    grad_hidden = dot(cot, down_w, 1, 1)
    density = jnp.exp(-0.5 * pre * pre) * (1.0 / math.sqrt(2.0 * math.pi))
    grad_pre = (grad_hidden * (phi_cdf + pre * density)).astype(BF)
    grad_norm_two = sum_slots(dot(grad_pre, w_up, 1, 1).reshape(n, rows, model))
    down_term = dot(hidden, cot, 0, 0).astype(BF)
    up_term = dot(norm_two, grad_pre, 0, 0).astype(BF)
    up_share = lax.psum_scatter(
        up_term.reshape(n, model // n, -1), "ctx", scatter_dimension=1, tiled=True
    )
    down_share = lax.psum_scatter(down_term, "ctx", scatter_dimension=0, tiled=True)

    grad_mid = cot_low.astype(F32) + norm_back(grad_norm_two, hat_two, rs_two, weight_two)
    grad_branch = grad_mid.astype(BF)
    eh_two = grad_norm_two * hat_two
    grad_scale_two = eh_two * g_two
    gain_two_term = jnp.sum(eh_two * scale_two, axis=0)
    out_term = dot(attended, grad_branch, 1, 0).astype(BF)
    out_share = lax.psum_scatter(
        out_term.reshape(n, model // n, model), "ctx", scatter_dimension=1, tiled=True
    )

    grad_attn = dot(w_out, grad_branch, 1, 1).astype(BF)
    grad_heads = to_heads(grad_attn.reshape(1, HEADS, HEAD, rows))
    grad_pieces = attend_back(qkv_heads, grad_heads, full, lse, block)
    back = to_tokens(grad_pieces).reshape(3, HEADS, 2, HEAD // 2, rows)
    unturned = turn(back[:2, :, 0].astype(F32), back[:2, :, 1].astype(F32), cosine, -sine)
    grad_qkv = jnp.concatenate([jnp.stack(unturned, axis=2).astype(BF), back[2:]])
    grad_qkv = grad_qkv.reshape(3 * model, rows)
    qkv_term = dot(norm_one, grad_qkv, 0, 1).astype(BF)
    grad_norm_one = dot(grad_qkv, w_qkv, 0, 1)

    input_grad = grad_mid + norm_back(grad_norm_one, hat_one, rs_one, weight_one)
    eh_one = grad_norm_one * hat_one
    grad_scale_one = eh_one * g_one
    gain_one_term = jnp.sum(eh_one * scale_one, axis=0)

    grad_shifts = jnp.concatenate([grad_scale_one, grad_scale_two], axis=1).astype(BF)
    level_term = dot(onehot.astype(BF), grad_shifts, 0, 0)
    small = jnp.concatenate([level_term, jnp.concatenate([gain_one_term, gain_two_term])[None]])

    up_share = lax.all_to_all(up_share, "wt", 0, 0, tiled=True)
    out_share = sum_owned(out_share)
    if planar:
        wide = small.shape[1] // ring
        padded = jnp.pad(small, ((0, -small.shape[0] % 16), (0, 0)))
        pieces = jnp.transpose(padded.reshape(-1, ring, wide), (1, 0, 2)).astype(BF)
        term = qkv_term.reshape(n, ring, model // n // ring, 3 * model)
        up_all, down_all, out_all, qkv_all, small_all = sum_and_spread(
            up_share, down_share, out_share, term, pieces
        )
        up_grad, down_grad, out_grad, qkv_grad = widen(up_all, down_all, out_all, qkv_all)
        small = jnp.transpose(small_all, (1, 0, 2)).reshape(padded.shape)[: small.shape[0]]
        small = small.astype(F32)
    else:
        small = lax.psum(small, ("ctx", "wt"))
        share = lax.psum_scatter(
            qkv_term.reshape(n, model // n, -1), "ctx", scatter_dimension=1, tiled=True
        )

        def spread_rows(share):
            return lax.all_gather(share, "ctx", axis=0, tiled=True).astype(F32)

        up_grad = lax.all_gather(up_share, "ctx", axis=1, tiled=True).astype(F32)
        up_grad = jnp.transpose(up_grad, (1, 0, 2)).reshape(model // n, -1)
        down_grad = spread_rows(down_share)
        out_grad = spread_rows(out_share)
        qkv_grad = spread_rows(sum_owned(share))

    by_level = small[: table.shape[0]]
    gain_sums = small[table.shape[0]]
    levels_here, time_here = noise_table.shape[0], time_w.shape[0]
    high = lax.Precision.HIGHEST
    time_rows = lax.dynamic_slice_in_dim(table, me * time_here, time_here, 1).astype(F32)
    time_grad = lax.dot_general(
        time_rows, by_level, (((0,), (0,)), ((), ())), precision=high, preferred_element_type=F32
    )
    level_rows = lax.dynamic_slice_in_dim(by_level, me * levels_here, levels_here, 0)
    table_grad = lax.dot_general(
        level_rows, w_time.astype(F32), (((1,), (1,)), ((), ())), precision=high,
        preferred_element_type=F32,
    )
    gain_here = gain_one.shape[0]
    gain_one_grad = lax.dynamic_slice_in_dim(gain_sums, me * gain_here, gain_here, 0)
    gain_two_grad = lax.dynamic_slice_in_dim(gain_sums, model + me * gain_here, gain_here, 0)

    return (
        layer_out.astype(BF).reshape(tokens.shape),
        input_grad.astype(BF).reshape(tokens.shape),
        qkv_grad,
        out_grad,
        up_grad,
        down_grad,
        time_grad,
        table_grad,
        gain_one_grad,
        gain_two_grad,
    )


def sum_owned(share):
    n, me = lax.axis_size("wt"), lax.axis_index("wt")
    slots = jnp.stack(
        [lax.dynamic_index_in_dim(share, lax.rem(me + k, n), 0, keepdims=False) for k in range(n)]
    )
    return sum_slots(slots.astype(F32)).astype(BF)


def solution(mesh):
    rows = P(None, "wt", "ctx", None)
    marks = P(None, "wt", "ctx")
    weight = P("wt", None)
    gain = P("wt")
    return jax.shard_map(
        shards,
        mesh=mesh,
        in_specs=(rows, marks, marks) + (weight,) * 6 + (gain, gain, rows),
        out_specs=(rows, rows) + (weight,) * 6 + (gain, gain),
        check_vma=False,
    )
```

```python
import functools
import math

import jax
import jax.numpy as jnp
from jax import lax
from jax.experimental import pallas as pl
from jax.experimental.pallas import tpu as pltpu
from jax.sharding import PartitionSpec as P

HEADS = 16
HEAD = 64
EPSILON = 1e-05
SCALE = 0.125
LOG2E = math.log2(math.e)
BF = jnp.bfloat16
F32 = jnp.float32


def dot(a, b, ca=1, cb=0):
    return lax.dot_general(a, b, (((ca,), (cb,)), ((), ())), preferred_element_type=F32)


def swap_ring(value, places):
    n = lax.axis_size("wt")
    return lax.ppermute(value, "wt", [((i + places) % n, i) for i in range(n)])


def gather_slots(own):
    n = lax.axis_size("wt")
    return jnp.stack([own] + [swap_ring(own, k) for k in range(1, n)])


def sum_slots(partial):
    n = lax.axis_size("wt")
    total = partial[0]
    for k in range(1, n):
        total = total + swap_ring(partial[k].astype(BF), n - k).astype(F32)
    return total


MESH = pl.DeviceIdType.MESH
DEPTH = 4


class Place:
    def __init__(self):
        self.ctx = lax.axis_index("ctx")
        self.wt = lax.axis_index("wt")
        self.z = lax.div(self.ctx, 4)
        self.y = lax.rem(lax.div(self.ctx, 2), 2)
        self.core = lax.rem(self.ctx, 2)
        self.right = {"ctx": self.index(lax.min(self.z + 1, DEPTH - 1), self.y, self.core)}
        self.left = {"ctx": self.index(lax.max(self.z - 1, 0), self.y, self.core)}
        self.across = {"ctx": self.index(self.z, 1 - self.y, self.core)}
        self.twin = {"ctx": self.index(self.z, self.y, 1 - self.core)}
        self.pair = {"wt": 1 - self.wt}

    @staticmethod
    def index(z, y, core):
        return (z * 2 + y) * 2 + core

    def greet(self, everyone=False, pair=True):
        barrier = pltpu.get_barrier_semaphore()

        def signal(device):
            pl.semaphore_signal(barrier, inc=1, device_id=device, device_id_type=MESH)

        if everyone:
            for d in range(1, 16):
                signal({"ctx": lax.rem(self.ctx + d, 16)})
            count = 15
        else:
            signal(self.across)
            signal(self.twin)
            pl.when(self.z > 0)(lambda: signal(self.left))
            pl.when(self.z < DEPTH - 1)(lambda: signal(self.right))
            inner = jnp.logical_and(self.z > 0, self.z < DEPTH - 1).astype(jnp.int32)
            count = 3 + inner
        if pair:
            signal(self.pair)
            count = count + 1
        pl.semaphore_wait(barrier, count)


def push(source, target, send, receive, device):
    return pltpu.make_async_remote_copy(
        src_ref=source, dst_ref=target, send_sem=send, recv_sem=receive,
        device_id=device, device_id_type=MESH,
    )


class Gather:
    def __init__(self, place, items, sems):
        self.p, self.items = place, items
        (self.sl, self.sr, self.sy, self.sc, self.rl, self.rr, self.ry, self.rc) = sems

    @staticmethod
    def semaphores(count):
        dma = pltpu.SemaphoreType.DMA
        line, square = dma((count, DEPTH)), dma((count, DEPTH, 2))
        return [line, line, line, square, line, line, line, square]

    def rightward(self, t, d, source=None):
        here = self.items[t](self.p.index(self.p.z - d, self.p.y, self.p.core))
        return push(here if source is None else source, here, self.sr.at[t, d], self.rl.at[t, d + 1], self.p.right)

    def leftward(self, t, d, source=None):
        here = self.items[t](self.p.index(self.p.z + d, self.p.y, self.p.core))
        return push(here if source is None else source, here, self.sl.at[t, d], self.rr.at[t, d + 1], self.p.left)

    def crossing(self, t, z, source=None):
        here = self.items[t](self.p.index(z, self.p.y, self.p.core))
        return push(here if source is None else source, here, self.sy.at[t, z], self.ry.at[t, z], self.p.across)

    def twinning(self, t, z, y, source=None):
        here = self.items[t](self.p.index(z, y, self.p.core))
        return push(here if source is None else source, here, self.sc.at[t, z, y], self.rc.at[t, z, y], self.p.twin)

    def own(self, t, source=None):
        p = self.p
        pl.when(p.z < DEPTH - 1)(lambda: self.rightward(t, 0, source).start())
        pl.when(p.z > 0)(lambda: self.leftward(t, 0, source).start())
        self.crossing(t, p.z, source).start()
        self.twinning(t, p.z, p.y, source).start()

    def arrived(self, t, z, y, core, semaphore):
        piece = self.items[t](self.p.index(z, y, core))
        push(piece, piece, semaphore, semaphore, self.p.twin).wait_recv()

    def along(self, t, d):
        p = self.p

        @pl.when(p.z - d >= 0)
        def _():
            self.arrived(t, p.z - d, p.y, p.core, self.rl.at[t, d])
            pl.when(p.z < DEPTH - 1)(lambda: self.rightward(t, d).start())
            self.crossing(t, p.z - d).start()
            self.twinning(t, p.z - d, p.y).start()

        @pl.when(p.z + d < DEPTH)
        def _():
            self.arrived(t, p.z + d, p.y, p.core, self.rr.at[t, d])
            pl.when(p.z > 0)(lambda: self.leftward(t, d).start())
            self.crossing(t, p.z + d).start()
            self.twinning(t, p.z + d, p.y).start()

    def crossed(self, t, d):
        p = self.p

        def one(z):
            self.arrived(t, z, 1 - p.y, p.core, self.ry.at[t, z])
            self.twinning(t, z, 1 - p.y).start()

        if d == 0:
            one(p.z)
        else:
            pl.when(p.z - d >= 0)(lambda: one(p.z - d))
            pl.when(p.z + d < DEPTH)(lambda: one(p.z + d))

    def finish(self, t):
        p = self.p
        for z in range(DEPTH):
            self.crossing(t, z).wait_send()
            for y in range(2):
                self.twinning(t, z, y).wait_send()
                self.arrived(t, z, y, 1 - p.core, self.rc.at[t, z, y])
        for d in range(DEPTH):
            pl.when(jnp.logical_and(p.z - d >= 0, p.z < DEPTH - 1))(lambda d=d: self.rightward(t, d).wait_send())
            pl.when(jnp.logical_and(p.z + d < DEPTH, p.z > 0))(lambda d=d: self.leftward(t, d).wait_send())


class Reduce:
    ORDER = (3, 0, 2, 1)

    def __init__(self, place, sources, refs):
        self.p, self.sources, count = place, sources, len(sources)
        groups = [refs[i * count : (i + 1) * count] for i in range(5)]
        self.mine, self.from_twin, self.from_across, self.from_left, self.from_right = groups
        (self.ls, self.ts, self.tr, self.ys, self.yr, self.rs, self.rr, self.vs, self.vr) = refs[5 * count :]

    @staticmethod
    def scratch(shapes):
        dma = pltpu.SemaphoreType.DMA
        count = len(shapes)
        buffers = []
        for lead in ((DEPTH, 2), (DEPTH, 2), (DEPTH,), (DEPTH,), (DEPTH,)):
            buffers += [pltpu.VMEM(lead + shape, BF) for shape in shapes]
        square, line = dma((count, DEPTH, 2)), dma((count, DEPTH))
        return buffers + [square] * 3 + [line] * 6

    def terms(self):
        return range(len(self.sources))

    def load(self, t, z, y):
        return pltpu.make_async_copy(
            self.sources[t](self.p.index(z, y, self.p.core)), self.mine[t].at[z, y], self.ls.at[t, z, y]
        )

    def twin(self, t, z, y):
        return push(
            self.sources[t](self.p.index(z, y, 1 - self.p.core)), self.from_twin[t].at[z, y],
            self.ts.at[t, z, y], self.tr.at[t, z, y], self.p.twin,
        )

    def across(self, t, z):
        return push(
            self.mine[t].at[z, 1 - self.p.y], self.from_across[t].at[z],
            self.ys.at[t, z], self.yr.at[t, z], self.p.across,
        )

    def rightward(self, t, j, first):
        source = self.from_across if first else self.from_left
        return push(source[t].at[j], self.from_left[t].at[j], self.rs.at[t, j], self.rr.at[t, j], self.p.right)

    def leftward(self, t, j, first):
        source = self.from_across if first else self.from_right
        return push(source[t].at[j], self.from_right[t].at[j], self.vs.at[t, j], self.vr.at[t, j], self.p.left)

    def begin(self):
        for z in self.ORDER:
            for y in (1 - self.p.y, self.p.y):
                for t in self.terms():
                    self.load(t, z, y).start()
                    self.twin(t, z, y).start()

    def halve(self, z):
        for y in (1 - self.p.y, self.p.y):
            for t in self.terms():
                self.load(t, z, y).wait()
                self.twin(t, z, y).wait_recv()
                both = self.mine[t][z, y].astype(F32) + self.from_twin[t][z, y].astype(F32)
                self.mine[t][z, y] = both.astype(BF)

    def cross(self, z):
        for t in self.terms():
            self.across(t, z).start()

    def quarter(self, z):
        for t in self.terms():
            self.across(t, z).wait_recv()
            both = self.mine[t][z, self.p.y].astype(F32) + self.from_across[t][z].astype(F32)
            self.from_across[t][z] = both.astype(BF)

    def add_left(self, t, j):
        self.rightward(t, j, False).wait_recv()
        return self.from_across[t][j].astype(F32) + self.from_left[t][j].astype(F32)

    def add_right(self, t, j):
        self.leftward(t, j, False).wait_recv()
        return self.from_across[t][j].astype(F32) + self.from_right[t][j].astype(F32)

    def go_right(self, j):
        p = self.p
        for t in self.terms():
            @pl.when(p.z == 0)
            def _(t=t):
                self.rightward(t, j, True).start()

            @pl.when(jnp.logical_and(p.z > 0, p.z < j))
            def _(t=t):
                self.from_left[t][j] = self.add_left(t, j).astype(BF)
                self.rightward(t, j, False).start()

    def go_left(self, j):
        p = self.p
        for t in self.terms():
            @pl.when(p.z == DEPTH - 1)
            def _(t=t):
                self.leftward(t, j, True).start()

            @pl.when(jnp.logical_and(p.z < DEPTH - 1, p.z > j))
            def _(t=t):
                self.from_right[t][j] = self.add_right(t, j).astype(BF)
                self.leftward(t, j, False).start()

    def end(self, results):
        p = self.p
        for t in self.terms():
            @pl.when(p.z == 0)
            def _(t=t):
                results[t][...] = self.add_right(t, 0).astype(BF)

            @pl.when(p.z == DEPTH - 1)
            def _(t=t):
                results[t][...] = self.add_left(t, DEPTH - 1).astype(BF)

            @pl.when(jnp.logical_and(p.z > 0, p.z < DEPTH - 1))
            def _(t=t):
                total = self.add_left(t, p.z)
                self.leftward(t, p.z, False).wait_recv()
                results[t][...] = (total + self.from_right[t][p.z].astype(F32)).astype(BF)

    def finish(self):
        p = self.p
        for t in self.terms():
            for z in range(DEPTH):
                for y in range(2):
                    self.twin(t, z, y).wait_send()
                self.across(t, z).wait_send()
            for step in range(DEPTH - 1):
                j, i = DEPTH - 1 - step, step
                pl.when(p.z < j)(lambda t=t, j=j: self.rightward(t, j, False).wait_send())
                pl.when(p.z > i)(lambda t=t, i=i: self.leftward(t, i, False).wait_send())


FIXED = 5


def sum_kernel(
    up_own, down_own, out_low, term, small,
    up_all, down_all, out_all, qkv_all, small_all,
    from_twin, to_pair, from_pair, kept, to_across, from_across, line, to_right, from_left, to_left, from_right,
    small_in, small_mine, small_pair, out_pair, out_own,
    cross_s, cross_r, local_sem, twin_s, twin_r, pair_s, pair_r, across_s, across_r, right_s, left_r, left_s, right_r,
    small_s, small_r, small_x, spread_s, spread_r, *gather_sems,
):
    p = Place()
    half = down_own.shape[0] // 2
    split = term.shape[2] // 2
    items = [
        lambda c: up_all.at[p.wt, c],
        lambda c: up_all.at[1 - p.wt, c],
        lambda c: down_all.at[c, 0:half],
        lambda c: down_all.at[c, half:],
        lambda c: out_all.at[c],
        lambda c: qkv_all.at[c, 0:split],
        lambda c: qkv_all.at[c, split:],
    ]
    owned = [up_own.at[p.wt], None, down_own.at[0:half], down_own.at[half:], out_own]
    g = Gather(p, items, gather_sems)
    fixed, late = range(FIXED), range(FIXED, len(items))
    p.greet(everyone=True)
    out_cross = push(out_low.at[1 - p.wt], out_pair, cross_s.at[0], cross_r.at[0], p.pair)
    up_cross = push(up_own.at[1 - p.wt], up_all.at[p.wt, p.ctx], cross_s.at[1], cross_r.at[1], p.pair)
    out_cross.start()
    up_cross.start()

    def to_twin(w, z, y):
        return push(
            term.at[w, p.index(z, y, 1 - p.core)], from_twin.at[w, z, y], twin_s.at[w, z, y], twin_r.at[w, z, y], p.twin
        )

    for z in range(DEPTH):
        for y in range(2):
            to_twin(1 - p.wt, z, y).start()
    for z in range(DEPTH):
        for y in range(2):
            to_twin(p.wt, z, y).start()
    for t in (0, 2, 3):
        g.own(t, owned[t])
    out_cross.wait_recv()
    out_own[...] = (out_low[p.wt].astype(F32) + out_pair[...].astype(F32)).astype(BF)
    g.own(4, owned[4])
    push(up_own.at[p.wt], up_all.at[1 - p.wt, p.ctx], cross_s.at[1], cross_r.at[1], p.pair).wait_recv()
    g.own(1)
    copies = [pltpu.make_async_copy(owned[t], items[t](p.ctx), local_sem.at[t]) for t in fixed if t != 1]
    for copy in copies:
        copy.start()

    def small_to(d):
        peer = lax.rem(p.ctx + d, 16)
        return push(small.at[peer], small_in.at[p.ctx], small_s.at[d], small_r.at[d], {"ctx": peer})

    for d in range(1, 16):
        small_to(d).start()
    small_in[p.ctx] = small[p.ctx]

    def with_twin(w, z, y):
        mine = term[w, p.index(z, y, p.core)].astype(F32)
        return mine + from_twin[w, z, y].astype(F32)

    def to_other(z, y):
        return push(to_pair.at[z, y], from_pair.at[z, y], pair_s.at[z, y], pair_r.at[z, y], p.pair)

    for z in range(DEPTH):
        for y in range(2):
            to_twin(1 - p.wt, z, y).wait_recv()
            to_pair[z, y] = with_twin(1 - p.wt, z, y).astype(BF)
            to_other(z, y).start()
    for z in range(DEPTH):
        for y in range(2):
            to_twin(p.wt, z, y).wait_recv()
            kept[z, y] = with_twin(p.wt, z, y).astype(BF)

    for t in fixed:
        g.along(t, 1)

    for d in range(1, 16):
        small_to(d).wait_recv()
    small_mine[...] = jnp.sum(small_in[...].astype(F32), axis=0)
    small_pair[0] = small_mine[...].astype(BF)
    small_cross = push(small_pair.at[0], small_pair.at[1], small_x.at[0], small_x.at[1], p.pair)
    small_cross.start()

    def to_y(z):
        return push(to_across.at[z], from_across.at[z], across_s.at[z], across_r.at[z], p.across)

    for z in range(DEPTH):
        for y in range(2):
            to_other(z, y).wait_recv()
        to_across[z] = (kept[z, 1 - p.y].astype(F32) + from_pair[z, 1 - p.y].astype(F32)).astype(BF)
        to_y(z).start()
        if z == 1:
            for t in fixed:
                g.along(t, 2)

    small_cross.wait()
    both = small_pair[0].astype(F32) + small_pair[1].astype(F32)
    small_all[p.ctx] = both.astype(BF)

    def small_spread(d):
        peer = lax.rem(p.ctx + d, 16)
        return push(small_all.at[p.ctx], small_all.at[p.ctx], spread_s.at[d], spread_r.at[d], {"ctx": peer})

    for d in range(1, 16):
        small_spread(d).start()

    for z in range(DEPTH):
        to_y(z).wait_recv()
        line[z] = (
            kept[z, p.y].astype(F32) + from_pair[z, p.y].astype(F32) + from_across[z].astype(F32)
        )

    def go_right(j):
        return push(to_right.at[j], from_left.at[j], right_s.at[j], left_r.at[j], p.right)

    def go_left(j):
        return push(to_left.at[j], from_right.at[j], left_s.at[j], right_r.at[j], p.left)

    def add_left(j):
        go_right(j).wait_recv()
        line[j] = line[j] + from_left[j].astype(F32)

    def add_right(j):
        go_left(j).wait_recv()
        line[j] = line[j] + from_right[j].astype(F32)

    for step in range(DEPTH - 1):
        j, i = DEPTH - 1 - step, step

        @pl.when(p.z < j)
        def _(j=j):
            pl.when(p.z > 0)(lambda: add_left(j))
            to_right[j] = line[j].astype(BF)
            go_right(j).start()

        @pl.when(p.z > i)
        def _(i=i):
            pl.when(p.z < DEPTH - 1)(lambda: add_right(i))
            to_left[i] = line[i].astype(BF)
            go_left(i).start()

    pl.when(p.z > 0)(lambda: add_left(p.z))
    pl.when(p.z < DEPTH - 1)(lambda: add_right(p.z))
    kept[0, 0] = line[p.z].astype(BF)
    final = kept.at[0, 0]
    parts = [final.at[0:split], final.at[split:]]
    for t in late:
        g.own(t, parts[t - FIXED])
    copies += [
        pltpu.make_async_copy(parts[t - FIXED], items[t](p.ctx), local_sem.at[t]) for t in late
    ]
    for copy in copies[FIXED - 1 :]:
        copy.start()
    for t in fixed:
        g.along(t, 3)
    for t in fixed:
        g.crossed(t, 0)
    for d in (1, 2, 3):
        for t in late:
            g.along(t, d)
        for t in fixed:
            g.crossed(t, d)
    for d in range(DEPTH):
        for t in late:
            g.crossed(t, d)

    for copy in copies:
        copy.wait()
    out_cross.wait_send()
    up_cross.wait_send()
    for t in range(len(items)):
        g.finish(t)
    for d in range(1, 16):
        small_to(d).wait_send()
        small_spread(d).wait()
    for z in range(DEPTH):
        to_y(z).wait_send()
        for y in range(2):
            to_other(z, y).wait_send()
            for w in range(2):
                to_twin(w, z, y).wait_send()
    for step in range(DEPTH - 1):
        j, i = DEPTH - 1 - step, step
        pl.when(p.z < j)(lambda j=j: go_right(j).wait_send())
        pl.when(p.z > i)(lambda i=i: go_left(i).wait_send())


def sum_and_spread(up_own, down_own, out_own, term, small):
    dma = pltpu.SemaphoreType.DMA
    rows, columns = term.shape[2:]
    piece = (rows, columns)
    vmem = pl.BlockSpec(memory_space=pltpu.VMEM)
    anywhere = pl.BlockSpec(memory_space=pl.ANY)
    outs = [
        jax.ShapeDtypeStruct((2, 16) + up_own.shape[1:], BF),
        jax.ShapeDtypeStruct((16,) + down_own.shape, BF),
        jax.ShapeDtypeStruct((16,) + out_own.shape[1:], BF),
        jax.ShapeDtypeStruct((16,) + piece, BF),
        jax.ShapeDtypeStruct(small.shape, BF),
    ]
    return pl.pallas_call(
        sum_kernel,
        out_shape=outs,
        in_specs=[anywhere, anywhere, vmem, vmem, vmem],
        out_specs=[anywhere, anywhere, anywhere, anywhere, vmem],
        scratch_shapes=[
            pltpu.VMEM((2, DEPTH, 2) + piece, BF),
            pltpu.VMEM((DEPTH, 2) + piece, BF),
            pltpu.VMEM((DEPTH, 2) + piece, BF),
            pltpu.VMEM((DEPTH, 2) + piece, BF),
            pltpu.VMEM((DEPTH,) + piece, BF),
            pltpu.VMEM((DEPTH,) + piece, BF),
            pltpu.VMEM((DEPTH,) + piece, F32),
            pltpu.VMEM((DEPTH,) + piece, BF),
            pltpu.VMEM((DEPTH,) + piece, BF),
            pltpu.VMEM((DEPTH,) + piece, BF),
            pltpu.VMEM((DEPTH,) + piece, BF),
            pltpu.VMEM(small.shape, BF),
            pltpu.VMEM(small.shape[1:], F32),
            pltpu.VMEM((2,) + small.shape[1:], BF),
            pltpu.VMEM(out_own.shape[1:], BF),
            pltpu.VMEM(out_own.shape[1:], BF),
            dma((2,)),
            dma((2,)),
            dma((FIXED + 2,)),
            dma((2, DEPTH, 2)),
            dma((2, DEPTH, 2)),
            dma((DEPTH, 2)),
            dma((DEPTH, 2)),
            dma((DEPTH,)),
            dma((DEPTH,)),
            dma((DEPTH,)),
            dma((DEPTH,)),
            dma((DEPTH,)),
            dma((DEPTH,)),
            dma((16,)),
            dma((16,)),
            dma((2,)),
            dma((16,)),
            dma((16,)),
        ]
        + Gather.semaphores(FIXED + 2),
        compiler_params=pltpu.CompilerParams(
            collective_id=3, has_side_effects=True, vmem_limit_bytes=56 << 20
        ),
        name="sum_and_spread",
    )(up_own, down_own, out_own, term, small)


def widen_kernel(up_ref, down_ref, out_ref, qkv_ref, up_to, down_to, out_to, qkv_to):
    columns = up_ref.shape[-1]
    up_to[:, :columns] = up_ref[0, 0].astype(F32)
    up_to[:, columns:] = up_ref[1, 0].astype(F32)
    down_to[...] = down_ref[0].astype(F32)
    out_to[...] = out_ref[0].astype(F32)
    qkv_to[...] = qkv_ref[0].astype(F32)


def widen(up, down, out, qkv):
    _, ring, up_rows, up_columns = up.shape

    def piece(a):
        return pl.BlockSpec((1,) + a.shape[1:], lambda i: (i, 0, 0))

    def row_block(a):
        return pl.BlockSpec(a.shape[1:], lambda i: (i, 0))

    def whole(a):
        return jax.ShapeDtypeStruct((ring * a.shape[1], a.shape[2]), F32)

    return pl.pallas_call(
        widen_kernel,
        grid=(ring,),
        in_specs=[
            pl.BlockSpec((2, 1, up_rows, up_columns), lambda i: (0, i, 0, 0)),
            piece(down), piece(out), piece(qkv),
        ],
        out_specs=[
            pl.BlockSpec((up_rows, 2 * up_columns), lambda i: (i, 0)),
            row_block(down), row_block(out), row_block(qkv),
        ],
        out_shape=[
            jax.ShapeDtypeStruct((ring * up_rows, 2 * up_columns), F32),
            whole(down), whole(out), whole(qkv),
        ],
        name="widen",
    )(up, down, out, qkv)


def start_kernel(
    qkv_own, time_own, table_own, gain_own, qkv_all, time_all, table_all, gain_all,
    hold_qkv, hold_time, local_in, local_out, cross_s, cross_r, *gather_sems,
):
    p = Place()
    other = 1 - p.wt
    split = qkv_all.shape[2] // 2
    deep = time_all.shape[2]
    items = [
        lambda c: qkv_all.at[other, c, 0:split],
        lambda c: qkv_all.at[other, c, split:],
        lambda c: time_all.at[other, c],
    ]
    g = Gather(p, items, gather_sems)
    into = [pltpu.make_async_copy(qkv_own, hold_qkv, local_in.at[0]),
            pltpu.make_async_copy(time_own, hold_time, local_in.at[1])]
    for copy in into:
        copy.start()
    p.greet()
    c = p.ctx
    sent = [
        push(qkv_own.at[pl.ds(2 * split * c, split)], qkv_all.at[p.wt, c, 0:split], cross_s.at[0], cross_r.at[0], p.pair),
        push(qkv_own.at[pl.ds(2 * split * c + split, split)], qkv_all.at[p.wt, c, split:], cross_s.at[1], cross_r.at[1], p.pair),
        push(time_own.at[pl.ds(deep * c, deep)], time_all.at[p.wt, c], cross_s.at[2], cross_r.at[2], p.pair),
        push(table_own, table_all.at[p.wt], cross_s.at[3], cross_r.at[3], p.pair),
        push(gain_own, gain_all.at[p.wt], cross_s.at[4], cross_r.at[4], p.pair),
    ]
    for copy in sent:
        copy.start()
    table_all[p.wt] = table_own[...]
    gain_all[p.wt] = gain_own[...]
    for t in range(len(items)):
        sent[t].wait_recv()
        g.own(t)
    for copy in into:
        copy.wait()
    out = []
    for k in range(16):
        out.append(pltpu.make_async_copy(
            hold_qkv.at[2 * split * k : 2 * split * (k + 1)], qkv_all.at[p.wt, k], local_out.at[0, k]))
        out.append(pltpu.make_async_copy(
            hold_time.at[deep * k : deep * (k + 1)], time_all.at[p.wt, k], local_out.at[1, k]))
    for copy in out:
        copy.start()
    every = range(len(items))
    for t in every:
        g.along(t, 1)
    for t in every:
        g.along(t, 2)
    for t in every:
        g.crossed(t, 0)
    for t in every:
        g.along(t, 3)
    for d in (1, 2, 3):
        for t in every:
            g.crossed(t, d)
    for copy in out:
        copy.wait()
    for t in every:
        g.finish(t)
        sent[t].wait_send()
    sent[3].wait()
    sent[4].wait()


def start(qkv_w, time_w, table, gains):
    dma = pltpu.SemaphoreType.DMA
    vmem = pl.BlockSpec(memory_space=pltpu.VMEM)
    anywhere = pl.BlockSpec(memory_space=pl.ANY)
    qkv_rows, time_rows = qkv_w.shape[0] // 16, time_w.shape[0] // 16
    qkv_all, time_all, table_all, gain_all = pl.pallas_call(
        start_kernel,
        out_shape=[
            jax.ShapeDtypeStruct((2, 16, qkv_rows, qkv_w.shape[1]), BF),
            jax.ShapeDtypeStruct((2, 16, time_rows, time_w.shape[1]), BF),
            jax.ShapeDtypeStruct((2,) + table.shape, BF),
            jax.ShapeDtypeStruct((2,) + gains.shape, BF),
        ],
        in_specs=[anywhere, anywhere, vmem, vmem],
        out_specs=[anywhere, anywhere, vmem, vmem],
        scratch_shapes=[
            pltpu.VMEM(qkv_w.shape, BF), pltpu.VMEM(time_w.shape, BF),
            dma((2,)), dma((2, 16)), dma((5,)), dma((5,)),
        ] + Gather.semaphores(3),
        compiler_params=pltpu.CompilerParams(
            collective_id=1, has_side_effects=True, vmem_limit_bytes=32 << 20
        ),
        name="start",
    )(qkv_w, time_w, table, gains)
    return (
        qkv_all.reshape(-1, qkv_w.shape[1]),
        time_all.reshape(-1, time_w.shape[1]),
        table_all.reshape(-1, table.shape[1]),
        jnp.transpose(gain_all, (1, 0, 2)).reshape(gains.shape[0], -1),
    )


def ring_peer(p, d):
    return lax.rem(p.ctx + d, 16)


def heads_kernel(
    block, qkv_t, up_w, out_w, cot,
    qkv_in, att, full_ref, lse_ref, up_all, out_all, cot_all,
    keys, low, hold_up, hold_out, hold_cot, own_s, in_s, in_r, back_s, back_r, hold_in, hold_to,
    cross_s, cross_r, twin_s, twin_r,
):
    p = Place()
    micro, _, length = qkv_in.shape
    width = length // 16
    model = att.shape[0]
    half_up, half_out = up_w.shape[0] // 2, out_w.shape[0] // 2
    columns = up_all.shape[2]
    other = 1 - p.wt
    mine = pl.ds(pl.multiple_of(p.wt * columns, columns), columns)
    theirs = pl.ds(pl.multiple_of(other * columns, columns), columns)
    holds = [
        pltpu.make_async_copy(up_w.at[:, mine], hold_up, hold_in.at[0]),
        pltpu.make_async_copy(out_w, hold_out, hold_in.at[1]),
        pltpu.make_async_copy(cot, hold_cot, hold_in.at[2]),
    ]
    for copy in holds:
        copy.start()
    p.greet(everyone=True)

    def piece(part, c):
        return pl.ds(pl.multiple_of(part * model + c * HEAD, HEAD), HEAD)

    def lanes(c):
        return pl.ds(pl.multiple_of(c * width, width), width)

    def to_head(m, d, part):
        c = ring_peer(p, d)
        return push(
            qkv_t.at[piece(part, c), m * width : (m + 1) * width],
            qkv_in.at[m, part * HEAD : (part + 1) * HEAD, lanes(p.ctx)],
            in_s.at[m, d, part], in_r.at[m, d, part], {"ctx": c},
        )

    stay = [
        pltpu.make_async_copy(
            qkv_t.at[piece(part, p.ctx), m * width : (m + 1) * width],
            qkv_in.at[m, part * HEAD : (part + 1) * HEAD, lanes(p.ctx)],
            own_s.at[m, part],
        )
        for m in range(micro) for part in range(3)
    ]
    rows_up = pl.ds(pl.multiple_of(p.core * half_up, half_up), half_up)
    rows_out = pl.ds(pl.multiple_of(p.core * half_out, half_out), half_out)
    crossing = [
        push(out_w.at[rows_out], out_all.at[p.wt, rows_out], cross_s.at[0], cross_r.at[0], p.pair),
        push(up_w.at[rows_up, theirs], up_all.at[p.wt, rows_up], cross_s.at[1], cross_r.at[1], p.pair),
        push(cot, cot_all.at[1], cross_s.at[2], cross_r.at[2], p.pair),
    ]
    twins = [
        push(out_all.at[other, rows_out], out_all.at[other, rows_out], twin_s.at[0], twin_r.at[0], p.twin),
        push(up_all.at[other, rows_up], up_all.at[other, rows_up], twin_s.at[1], twin_r.at[1], p.twin),
    ]
    for copy in stay:
        copy.start()
    for m in range(micro):
        for d in range(1, 16):
            for part in range(3):
                to_head(m, d, part).start()
        if m == 0:
            for copy in crossing:
                copy.start()
    for copy in holds:
        copy.wait()
    placing = [
        pltpu.make_async_copy(hold_up, up_all.at[p.wt], hold_to.at[0]),
        pltpu.make_async_copy(hold_out, out_all.at[p.wt], hold_to.at[1]),
        pltpu.make_async_copy(hold_cot, cot_all.at[0], hold_to.at[2]),
    ]
    for copy in placing:
        copy.start()

    def to_owner(m, c):
        return push(
            low.at[m, :, c * width : (c + 1) * width],
            att.at[pl.ds(pl.multiple_of(p.ctx * HEAD, HEAD), HEAD), m * width : (m + 1) * width],
            back_s.at[m, c], back_r.at[m, p.ctx], {"ctx": c},
        )

    for m in range(micro):
        for part in range(3):
            stay[3 * m + part].wait()
            for d in range(1, 16):
                to_head(m, d, part).wait_recv()
        keys[...] = qkv_in[m, HEAD : 2 * HEAD, :].T
        for j in range(length // block):
            cols = slice(j * block, (j + 1) * block)
            scores = dot(keys[...], qkv_in[m, 0:HEAD, cols]) * (SCALE * LOG2E)
            top = jnp.max(scores, axis=0, keepdims=True)
            exps = jnp.exp2(scores - top)
            total = jnp.sum(exps, axis=0, keepdims=True)
            out = dot(qkv_in[m, 2 * HEAD :, :], exps.astype(BF)) / total
            full_ref[m, :, cols] = out
            lse_ref[m, :, cols] = top + jnp.log2(total)
            low[m, :, cols] = out.astype(BF)
            for c in range(j * block // width, (j + 1) * block // width):
                pl.when(p.ctx != c)(lambda m=m, c=c: to_owner(m, c).start())
        att[pl.ds(pl.multiple_of(p.ctx * HEAD, HEAD), HEAD), m * width : (m + 1) * width] = low[
            m, :, pl.ds(pl.multiple_of(p.ctx * width, width), width)
        ]
        if m == 0:
            for t in range(2):
                crossing[t].wait_recv()
                twins[t].start()

    for m in range(micro):
        for d in range(1, 16):
            c = ring_peer(p, d)
            push(
                low.at[m, :, 0:width],
                att.at[pl.ds(pl.multiple_of(c * HEAD, HEAD), HEAD), m * width : (m + 1) * width],
                back_s.at[m, 0], back_r.at[m, c], {"ctx": c},
            ).wait_recv()
            for part in range(3):
                to_head(m, d, part).wait_send()
        for c in range(16):
            pl.when(p.ctx != c)(lambda m=m, c=c: to_owner(m, c).wait_send())
    crossing[2].wait_recv()
    for copy in crossing:
        copy.wait_send()
    for copy in twins + placing:
        copy.wait()


def heads(qkv_t, up_w, out_w, cot, micro, block):
    dma = pltpu.SemaphoreType.DMA
    vmem = pl.BlockSpec(memory_space=pltpu.VMEM)
    anywhere = pl.BlockSpec(memory_space=pl.ANY)
    rows = qkv_t.shape[1]
    length = rows // micro * 16
    model = out_w.shape[1]
    columns = up_w.shape[1] // 2
    qkv_in, att, full, lse, up_all, out_all, cot_all = pl.pallas_call(
        functools.partial(heads_kernel, block),
        out_shape=[
            jax.ShapeDtypeStruct((micro, 3 * HEAD, length), BF),
            jax.ShapeDtypeStruct((model, rows), BF),
            jax.ShapeDtypeStruct((micro, HEAD, length), F32),
            jax.ShapeDtypeStruct((micro, 1, length), F32),
            jax.ShapeDtypeStruct((2, up_w.shape[0], columns), BF),
            jax.ShapeDtypeStruct((2,) + out_w.shape, BF),
            jax.ShapeDtypeStruct((2,) + cot.shape, BF),
        ],
        in_specs=[vmem, anywhere, anywhere, anywhere],
        out_specs=[vmem, vmem, vmem, vmem, anywhere, anywhere, anywhere],
        scratch_shapes=[
            pltpu.VMEM((length, HEAD), BF),
            pltpu.VMEM((micro, HEAD, length), BF),
            pltpu.VMEM((up_w.shape[0], columns), BF),
            pltpu.VMEM(out_w.shape, BF),
            pltpu.VMEM(cot.shape, BF),
            dma((micro, 3)),
            dma((micro, 16, 3)),
            dma((micro, 16, 3)),
            dma((micro, 16)),
            dma((micro, 16)),
            dma((3,)),
            dma((3,)),
            dma((3,)),
            dma((3,)),
            dma((2,)),
            dma((2,)),
        ],
        compiler_params=pltpu.CompilerParams(
            collective_id=2, has_side_effects=True, vmem_limit_bytes=48 << 20
        ),
        name="heads",
    )(qkv_t, up_w, out_w, cot)
    return (
        qkv_in, att, full, lse,
        up_all.reshape(-1, columns), out_all.reshape(-1, model), cot_all.reshape(-1, model),
    )


def heads_back_kernel(
    block, grad_t, qkv_in, full_ref, lse_ref, up_term, down_term, out_term,
    out_ref, up_sum, down_sum, out_sum,
    keys, values, g_in, dq, dq_low, dkv_low, delta, own_s, in_s, in_r, back_s, back_r, *sum_refs,
):
    p = Place()
    micro, _, length = qkv_in.shape
    width = length // 16
    model = grad_t.shape[0]
    p.greet(everyone=True, pair=False)

    def rows_of(part, c):
        return pl.ds(pl.multiple_of(part * model + c * HEAD, HEAD), HEAD)

    def lanes(c):
        return pl.ds(pl.multiple_of(c * width, width), width)

    def to_head(m, d):
        c = ring_peer(p, d)
        return push(
            grad_t.at[rows_of(0, c), m * width : (m + 1) * width],
            g_in.at[m, :, lanes(p.ctx)], in_s.at[m, d], in_r.at[m, d], {"ctx": c},
        )

    stay = [
        pltpu.make_async_copy(
            grad_t.at[rows_of(0, p.ctx), m * width : (m + 1) * width],
            g_in.at[m, :, lanes(p.ctx)], own_s.at[m],
        )
        for m in range(micro)
    ]
    sums = Reduce(
        p, [lambda c: up_term.at[:, c], lambda c: down_term.at[c], lambda c: out_term.at[:, c]], sum_refs
    )
    for m in range(micro):
        stay[m].start()
        for d in range(1, 16):
            to_head(m, d).start()
    sums.begin()
    sums.halve(3)
    sums.cross(3)
    sums.halve(0)
    sums.cross(0)

    def to_owner(m, c, part):
        source = dq_low.at[m] if part == 0 else dkv_low.at[m, part - 1]
        return push(
            source.at[:, c * width : (c + 1) * width],
            out_ref.at[rows_of(part, p.ctx), m * width : (m + 1) * width],
            back_s.at[m, c, part], back_r.at[m, p.ctx, part], {"ctx": c},
        )

    def send(m, c, part):
        pl.when(p.ctx != c)(lambda: to_owner(m, c, part).start())

    for m in range(micro):
        keys[...] = qkv_in[m, HEAD : 2 * HEAD, :].T
        values[...] = qkv_in[m, 2 * HEAD :, :].T
        stay[m].wait()
        for d in range(1, 16):
            to_head(m, d).wait_recv()
        delta[...] = jnp.sum(g_in[m].astype(F32) * full_ref[m], axis=0, keepdims=True)
        for j in range(length // block):
            cols = slice(j * block, (j + 1) * block)
            scores = dot(keys[cols, :], qkv_in[m, 0:HEAD, :]) * (SCALE * LOG2E)
            soft = jnp.exp2(scores - lse_ref[m])
            grad_soft = dot(values[cols, :], g_in[m])
            raw = (soft * (grad_soft - delta[...]) * SCALE).astype(BF)
            dkv_low[m, 0, :, cols] = dot(qkv_in[m, 0:HEAD, :], raw, 1, 1).astype(BF)
            dkv_low[m, 1, :, cols] = dot(g_in[m], soft.astype(BF), 1, 1).astype(BF)
            term = dot(qkv_in[m, HEAD : 2 * HEAD, cols], raw)
            if j == 0:
                dq[...] = term
            else:
                dq[...] += term
            for c in range(j * block // width, (j + 1) * block // width):
                send(m, c, 1)
                send(m, c, 2)
        dq_low[m] = dq[...].astype(BF)
        for c in range(16):
            send(m, c, 0)
        if m == 0:
            sums.halve(2)
            sums.halve(1)
        here = lanes(p.ctx)
        to = slice(m * width, (m + 1) * width)
        out_ref[rows_of(0, p.ctx), to] = dq_low[m, :, here]
        out_ref[rows_of(1, p.ctx), to] = dkv_low[m, 0, :, here]
        out_ref[rows_of(2, p.ctx), to] = dkv_low[m, 1, :, here]

    sums.cross(2)
    sums.cross(1)
    sums.quarter(3)
    sums.go_right(3)
    sums.quarter(0)
    sums.go_left(0)
    sums.quarter(2)
    sums.go_right(2)
    sums.quarter(1)
    sums.go_left(1)
    sums.go_right(1)
    sums.go_left(2)
    sums.end([up_sum, down_sum, out_sum])
    sums.finish()

    for m in range(micro):
        for d in range(1, 16):
            c = ring_peer(p, d)
            for part in range(3):
                push(
                    dq_low.at[m, :, 0:width],
                    out_ref.at[rows_of(part, c), m * width : (m + 1) * width],
                    back_s.at[m, 0, part], back_r.at[m, c, part], {"ctx": c},
                ).wait_recv()
            to_head(m, d).wait_send()
        for c in range(16):
            for part in range(3):
                pl.when(p.ctx != c)(lambda m=m, c=c, part=part: to_owner(m, c, part).wait_send())


def heads_back(grad_t, qkv_in, full, lse, up, down, out, block):
    dma = pltpu.SemaphoreType.DMA
    vmem = pl.BlockSpec(memory_space=pltpu.VMEM)
    micro, _, length = qkv_in.shape
    model, rows = grad_t.shape
    anywhere = pl.BlockSpec(memory_space=pl.ANY)
    pieces = [up.shape[:1] + up.shape[2:], down.shape[1:], out.shape[:1] + out.shape[2:]]
    return pl.pallas_call(
        functools.partial(heads_back_kernel, block),
        out_shape=[jax.ShapeDtypeStruct((3 * model, rows), BF)]
        + [jax.ShapeDtypeStruct(shape, BF) for shape in pieces],
        in_specs=[vmem] * 4 + [anywhere] * 3,
        out_specs=[vmem] * 4,
        scratch_shapes=[
            pltpu.VMEM((length, HEAD), BF),
            pltpu.VMEM((length, HEAD), BF),
            pltpu.VMEM((micro, HEAD, length), BF),
            pltpu.VMEM((HEAD, length), F32),
            pltpu.VMEM((micro, HEAD, length), BF),
            pltpu.VMEM((micro, 2, HEAD, length), BF),
            pltpu.VMEM((1, length), F32),
            dma((micro,)),
            dma((micro, 16)),
            dma((micro, 16)),
            dma((micro, 16, 3)),
            dma((micro, 16, 3)),
        ] + Reduce.scratch(pieces),
        compiler_params=pltpu.CompilerParams(
            collective_id=4, has_side_effects=True, vmem_limit_bytes=60 << 20
        ),
        name="heads_back",
    )(grad_t, qkv_in, full, lse, up, down, out)


def spread(source, pieces, first, target):
    width = source.shape[-1]
    for c in range(pieces):
        target[:, c * width : (c + 1) * width] = source[c, 0, first : first + HEAD, :]


def attend_kernel(pieces, block, qkv_ref, low_ref, full_ref, lse_ref, q_t, k_t, v_t, keys):
    length = q_t.shape[1]
    width = length // pieces
    spread(qkv_ref, pieces, 0, q_t)
    spread(qkv_ref, pieces, HEAD, k_t)
    spread(qkv_ref, pieces, 2 * HEAD, v_t)
    keys[...] = k_t[...].T
    for j in range(length // block):
        cols = slice(j * block, (j + 1) * block)
        scores = dot(keys[...], q_t[:, cols]) * (SCALE * LOG2E)
        top = jnp.max(scores, axis=0, keepdims=True)
        exps = jnp.exp2(scores - top)
        total = jnp.sum(exps, axis=0, keepdims=True)
        out = dot(v_t[...], exps.astype(BF)) / total
        full_ref[0, :, cols] = out
        lse_ref[0, :, cols] = top + jnp.log2(total)
        for c in range(block // width):
            low_ref[j * (block // width) + c, 0] = out[:, c * width : (c + 1) * width].astype(BF)


def attend(qkv, block):
    pieces, pairs, _, width = qkv.shape
    length = pieces * width
    return pl.pallas_call(
        functools.partial(attend_kernel, pieces, block),
        grid=(pairs,),
        in_specs=[pl.BlockSpec((pieces, 1, 3 * HEAD, width), lambda p: (0, p, 0, 0))],
        out_specs=[
            pl.BlockSpec((pieces, 1, HEAD, width), lambda p: (0, p, 0, 0)),
            pl.BlockSpec((1, HEAD, length), lambda p: (p, 0, 0)),
            pl.BlockSpec((1, 1, length), lambda p: (p, 0, 0)),
        ],
        out_shape=[
            jax.ShapeDtypeStruct((pieces, pairs, HEAD, width), BF),
            jax.ShapeDtypeStruct((pairs, HEAD, length), F32),
            jax.ShapeDtypeStruct((pairs, 1, length), F32),
        ],
        scratch_shapes=[pltpu.VMEM((HEAD, length), BF)] * 3 + [pltpu.VMEM((length, HEAD), BF)],
        compiler_params=pltpu.CompilerParams(vmem_limit_bytes=48 << 20),
        name="attend",
    )(qkv)


def attend_back_kernel(
    pieces, block, qkv_ref, grad_ref, full_ref, lse_ref, out_ref,
    q_t, k_t, v_t, g_t, keys, values, dq_t, dk, dv,
):
    length = q_t.shape[1]
    width = length // pieces
    spread(qkv_ref, pieces, 0, q_t)
    spread(qkv_ref, pieces, HEAD, k_t)
    spread(qkv_ref, pieces, 2 * HEAD, v_t)
    spread(grad_ref, pieces, 0, g_t)
    keys[...] = k_t[...].T
    values[...] = v_t[...].T
    for j in range(length // block):
        cols = slice(j * block, (j + 1) * block)
        query = q_t[:, cols]
        grad = g_t[:, cols]
        delta = jnp.sum(grad.astype(F32) * full_ref[0, :, cols], axis=0, keepdims=True)
        scores = dot(keys[...], query) * (SCALE * LOG2E)
        soft = jnp.exp2(scores - lse_ref[0, :, cols])
        term_v = dot(soft.astype(BF), grad, 1, 1)
        grad_soft = dot(values[...], grad)
        raw = (soft * (grad_soft - delta) * SCALE).astype(BF)
        term_k = dot(raw, query, 1, 1)
        dq_t[:, cols] = dot(k_t[...], raw)
        if j == 0:
            dv[...] = term_v
            dk[...] = term_k
        else:
            dv[...] += term_v
            dk[...] += term_k
    dk_t = dk[...].T.astype(BF)
    dv_t = dv[...].T.astype(BF)
    for c in range(pieces):
        piece = slice(c * width, (c + 1) * width)
        out_ref[c, 0, 0:HEAD, :] = dq_t[:, piece].astype(BF)
        out_ref[c, 0, HEAD : 2 * HEAD, :] = dk_t[:, piece]
        out_ref[c, 0, 2 * HEAD :, :] = dv_t[:, piece]


def attend_back(qkv, grad, full, lse, block):
    pieces, pairs, _, width = qkv.shape
    length = pieces * width
    return pl.pallas_call(
        functools.partial(attend_back_kernel, pieces, block),
        grid=(pairs,),
        in_specs=[
            pl.BlockSpec((pieces, 1, 3 * HEAD, width), lambda p: (0, p, 0, 0)),
            pl.BlockSpec((pieces, 1, HEAD, width), lambda p: (0, p, 0, 0)),
            pl.BlockSpec((1, HEAD, length), lambda p: (p, 0, 0)),
            pl.BlockSpec((1, 1, length), lambda p: (p, 0, 0)),
        ],
        out_specs=pl.BlockSpec((pieces, 1, 3 * HEAD, width), lambda p: (0, p, 0, 0)),
        out_shape=jax.ShapeDtypeStruct(qkv.shape, BF),
        scratch_shapes=[pltpu.VMEM((HEAD, length), BF)] * 4
        + [pltpu.VMEM((length, HEAD), BF)] * 2
        + [pltpu.VMEM((HEAD, length), F32)]
        + [pltpu.VMEM((length, HEAD), F32)] * 2,
        compiler_params=pltpu.CompilerParams(vmem_limit_bytes=56 << 20),
        name="attend_back",
    )(qkv, grad, full, lse)


def normed(rows):
    centered = rows - jnp.mean(rows, axis=-1, keepdims=True)
    scale = lax.rsqrt(jnp.mean(centered * centered, axis=-1, keepdims=True) + EPSILON)
    return centered * scale, scale


def norm_back(grad, hat, scale, weight):
    c = grad * weight
    return (
        c - jnp.mean(c, axis=-1, keepdims=True) - hat * jnp.mean(c * hat, axis=-1, keepdims=True)
    ) * scale


def turn(first, second, cosine, sine):
    return first * cosine - second * sine, second * cosine + first * sine


def shards(
    tokens, positions, buckets, qkv_w, out_w, up_w, down_w, time_w, noise_table,
    gain_one, gain_two, cotangent,
):
    n, ring = lax.axis_size("wt"), lax.axis_size("ctx")
    me = lax.axis_index("wt")
    micro, _, width, model = tokens.shape
    rows = micro * width
    pairs = HEADS * micro // ring
    block = 256
    planar = n == 2 and ring == 16

    x = tokens.reshape(rows, model).astype(F32)
    cot_low = cotangent.reshape(rows, model)
    places = positions.reshape(rows)
    levels = buckets.reshape(rows)

    def whole_rows(weight):
        return lax.all_gather(weight, "wt", axis=0, tiled=True)

    stacked = jnp.stack([gain_one, gain_two])
    if planar:
        w_qkv, w_time, table, gains = start(qkv_w, time_w, noise_table, stacked)
    else:
        w_qkv = whole_rows(qkv_w)
        w_out = whole_rows(out_w)
        w_time = whole_rows(time_w)
        table = whole_rows(noise_table)
        gains = lax.all_gather(stacked, "wt", axis=1, tiled=True)
        w_up = lax.all_to_all(up_w, "wt", 1, 0, tiled=True)
    g_one, g_two = gains[0].astype(F32), gains[1].astype(F32)

    onehot = levels[:, None] == jnp.arange(table.shape[0], dtype=jnp.int32)[None, :]
    embed = dot(onehot.astype(BF), table).astype(BF)
    shifts = dot(embed, w_time)
    scale_one = 1.0 + shifts[:, :model]
    scale_two = 1.0 + shifts[:, model:]

    hat_one, rs_one = normed(x)
    weight_one = g_one * scale_one
    norm_one = (hat_one * weight_one).astype(BF)

    qkv_t = dot(w_qkv, norm_one, 0, 1).reshape(3, HEADS, 2, HEAD // 2, rows)
    frequency = jnp.exp(
        jnp.arange(HEAD // 2, dtype=F32) * (-math.log(10000.0) * 2.0 / HEAD)
    )
    angles = frequency[:, None] * places.astype(F32)[None, :]
    cosine, sine = jnp.cos(angles), jnp.sin(angles)
    turned = turn(qkv_t[:2, :, 0], qkv_t[:2, :, 1], cosine, sine)
    queries_keys = jnp.stack(turned, axis=2)
    qkv_low = jnp.concatenate([queries_keys.astype(BF), qkv_t[2:].astype(BF)])

    def to_heads(columns):
        parts = columns.shape[0]
        split = columns.reshape(parts, HEADS, HEAD, micro, width)
        split = jnp.transpose(split, (1, 3, 0, 2, 4))
        split = split.reshape(ring, pairs, parts * HEAD, width)
        return lax.all_to_all(split, "ctx", 0, 0, tiled=True)

    def to_tokens(pieces):
        parts = pieces.shape[2] // HEAD
        back = lax.all_to_all(pieces, "ctx", 0, 0, tiled=True)
        back = back.reshape(HEADS, micro, parts, HEAD, width)
        return jnp.transpose(back, (2, 0, 3, 1, 4)).reshape(parts, HEADS * HEAD, rows)

    if planar:
        qkv_heads, attended, full, lse, w_up, w_out, cot = heads(
            qkv_low.reshape(3 * model, rows), up_w, out_w, cot_low, micro, block
        )
    else:
        qkv_heads = to_heads(qkv_low.reshape(3, HEADS, HEAD, rows))
        low, full, lse = attend(qkv_heads, block)
        attended = to_tokens(low)[0]
        cot = gather_slots(cot_low).reshape(n * rows, model)

    middle = x + dot(attended, w_out, 0, 0)
    hat_two, rs_two = normed(middle)
    weight_two = g_two * scale_two
    norm_two_own = (hat_two * weight_two).astype(BF)

    norm_two = gather_slots(norm_two_own).reshape(n * rows, model)
    pre = dot(norm_two, w_up)
    phi_cdf = 0.5 * (1.0 + lax.erf(pre * (2.0**-0.5)))
    hidden = (pre * phi_cdf).astype(BF)
    layer_out = middle + sum_slots(dot(hidden, down_w).reshape(n, rows, model))

    grad_hidden = dot(cot, down_w, 1, 1)
    density = jnp.exp(-0.5 * pre * pre) * (1.0 / math.sqrt(2.0 * math.pi))
    grad_pre = (grad_hidden * (phi_cdf + pre * density)).astype(BF)
    grad_norm_two = sum_slots(dot(grad_pre, w_up, 1, 1).reshape(n, rows, model))
    down_term = dot(hidden, cot, 0, 0).astype(BF)
    up_term = dot(norm_two, grad_pre, 0, 0).astype(BF)
    grad_norm_two, down_term, up_term = lax.optimization_barrier((grad_norm_two, down_term, up_term))
    grad_mid = cot_low.astype(F32) + norm_back(grad_norm_two, hat_two, rs_two, weight_two)
    grad_branch = grad_mid.astype(BF)
    eh_two = grad_norm_two * hat_two
    grad_scale_two = eh_two * g_two
    gain_two_term = jnp.sum(eh_two * scale_two, axis=0)
    out_term = dot(attended, grad_branch, 1, 0).astype(BF)
    grad_attn = dot(w_out, grad_branch, 1, 1).astype(BF)
    if planar:
        def pieces_of(array, *lead):
            return array.reshape(lead + (-1, array.shape[-1]))

        back, up_share, down_share, out_share = heads_back(
            grad_attn, qkv_heads, full, lse, pieces_of(up_term, n, ring), pieces_of(down_term, ring),
            pieces_of(out_term, n, ring), block,
        )
    else:
        up_share = lax.psum_scatter(
            up_term.reshape(n, model // n, -1), "ctx", scatter_dimension=1, tiled=True
        )
        down_share = lax.psum_scatter(down_term, "ctx", scatter_dimension=0, tiled=True)
        out_share = lax.psum_scatter(
            out_term.reshape(n, model // n, model), "ctx", scatter_dimension=1, tiled=True
        )
        grad_heads = to_heads(grad_attn.reshape(1, HEADS, HEAD, rows))
        back = to_tokens(attend_back(qkv_heads, grad_heads, full, lse, block))
    back = back.reshape(3, HEADS, 2, HEAD // 2, rows)
    unturned = turn(back[:2, :, 0].astype(F32), back[:2, :, 1].astype(F32), cosine, -sine)
    grad_qkv = jnp.concatenate([jnp.stack(unturned, axis=2).astype(BF), back[2:]])
    grad_qkv = grad_qkv.reshape(3 * model, rows)
    qkv_term = dot(norm_one, grad_qkv, 0, 1).astype(BF)
    grad_norm_one = dot(grad_qkv, w_qkv, 0, 1)

    input_grad = grad_mid + norm_back(grad_norm_one, hat_one, rs_one, weight_one)
    eh_one = grad_norm_one * hat_one
    grad_scale_one = eh_one * g_one
    gain_one_term = jnp.sum(eh_one * scale_one, axis=0)

    grad_shifts = jnp.concatenate([grad_scale_one, grad_scale_two], axis=1).astype(BF)
    level_term = dot(onehot.astype(BF), grad_shifts, 0, 0)
    small = jnp.concatenate([level_term, jnp.concatenate([gain_one_term, gain_two_term])[None]])

    if planar:
        wide = small.shape[1] // ring
        padded = jnp.pad(small, ((0, -small.shape[0] % 16), (0, 0)))
        pieces = jnp.transpose(padded.reshape(-1, ring, wide), (1, 0, 2)).astype(BF)
        term = qkv_term.reshape(n, ring, model // n // ring, 3 * model)
        up_all, down_all, out_all, qkv_all, small_all = sum_and_spread(
            up_share, down_share, out_share, term, pieces
        )
        up_grad, down_grad, out_grad, qkv_grad = widen(up_all, down_all, out_all, qkv_all)
        small = jnp.transpose(small_all, (1, 0, 2)).reshape(padded.shape)[: small.shape[0]]
        small = small.astype(F32)
    else:
        small = lax.psum(small, ("ctx", "wt"))
        share = lax.psum_scatter(
            qkv_term.reshape(n, model // n, -1), "ctx", scatter_dimension=1, tiled=True
        )

        def spread_rows(share):
            return lax.all_gather(share, "ctx", axis=0, tiled=True).astype(F32)

        up_share = lax.all_to_all(up_share, "wt", 0, 0, tiled=True)
        up_grad = lax.all_gather(up_share, "ctx", axis=1, tiled=True).astype(F32)
        up_grad = jnp.transpose(up_grad, (1, 0, 2)).reshape(model // n, -1)
        down_grad = spread_rows(down_share)
        out_grad = spread_rows(sum_owned(out_share))
        qkv_grad = spread_rows(sum_owned(share))

    by_level = small[: table.shape[0]]
    gain_sums = small[table.shape[0]]
    levels_here, time_here = noise_table.shape[0], time_w.shape[0]
    high = lax.Precision.HIGHEST
    time_rows = lax.dynamic_slice_in_dim(table, me * time_here, time_here, 1).astype(F32)
    time_grad = lax.dot_general(
        time_rows, by_level, (((0,), (0,)), ((), ())), precision=high, preferred_element_type=F32
    )
    level_rows = lax.dynamic_slice_in_dim(by_level, me * levels_here, levels_here, 0)
    table_grad = lax.dot_general(
        level_rows, w_time.astype(F32), (((1,), (1,)), ((), ())), precision=high,
        preferred_element_type=F32,
    )
    gain_here = gain_one.shape[0]
    gain_one_grad = lax.dynamic_slice_in_dim(gain_sums, me * gain_here, gain_here, 0)
    gain_two_grad = lax.dynamic_slice_in_dim(gain_sums, model + me * gain_here, gain_here, 0)

    return (
        layer_out.astype(BF).reshape(tokens.shape),
        input_grad.astype(BF).reshape(tokens.shape),
        qkv_grad,
        out_grad,
        up_grad,
        down_grad,
        time_grad,
        table_grad,
        gain_one_grad,
        gain_two_grad,
    )


def sum_owned(share):
    n, me = lax.axis_size("wt"), lax.axis_index("wt")
    slots = jnp.stack(
        [lax.dynamic_index_in_dim(share, lax.rem(me + k, n), 0, keepdims=False) for k in range(n)]
    )
    return sum_slots(slots.astype(F32)).astype(BF)


def solution(mesh):
    rows = P(None, "wt", "ctx", None)
    marks = P(None, "wt", "ctx")
    weight = P("wt", None)
    gain = P("wt")
    return jax.shard_map(
        shards,
        mesh=mesh,
        in_specs=(rows, marks, marks) + (weight,) * 6 + (gain, gain, rows),
        out_specs=(rows, rows) + (weight,) * 6 + (gain, gain),
        check_vma=False,
    )
```

```python
import functools
import math

import jax
import jax.numpy as jnp
from jax import lax
from jax.experimental import pallas as pl
from jax.experimental.pallas import tpu as pltpu
from jax.sharding import PartitionSpec as P

HEADS = 16
HEAD = 64
EPSILON = 1e-05
SCALE = 0.125
LOG2E = math.log2(math.e)
BF = jnp.bfloat16
F32 = jnp.float32


def dot(a, b, ca=1, cb=0):
    return lax.dot_general(a, b, (((ca,), (cb,)), ((), ())), preferred_element_type=F32)


def swap_ring(value, places):
    n = lax.axis_size("wt")
    return lax.ppermute(value, "wt", [((i + places) % n, i) for i in range(n)])


def gather_slots(own):
    n = lax.axis_size("wt")
    return jnp.stack([own] + [swap_ring(own, k) for k in range(1, n)])


def sum_slots(partial):
    n = lax.axis_size("wt")
    total = partial[0]
    for k in range(1, n):
        total = total + swap_ring(partial[k].astype(BF), n - k).astype(F32)
    return total


MESH = pl.DeviceIdType.MESH
DEPTH = 4


class Place:
    def __init__(self):
        self.ctx = lax.axis_index("ctx")
        self.wt = lax.axis_index("wt")
        self.z = lax.div(self.ctx, 4)
        self.y = lax.rem(lax.div(self.ctx, 2), 2)
        self.core = lax.rem(self.ctx, 2)
        self.right = {"ctx": self.index(lax.min(self.z + 1, DEPTH - 1), self.y, self.core)}
        self.left = {"ctx": self.index(lax.max(self.z - 1, 0), self.y, self.core)}
        self.across = {"ctx": self.index(self.z, 1 - self.y, self.core)}
        self.twin = {"ctx": self.index(self.z, self.y, 1 - self.core)}
        self.pair = {"wt": 1 - self.wt}

    @staticmethod
    def index(z, y, core):
        return (z * 2 + y) * 2 + core

    def greet(self, everyone=False, pair=True):
        barrier = pltpu.get_barrier_semaphore()

        def signal(device):
            pl.semaphore_signal(barrier, inc=1, device_id=device, device_id_type=MESH)

        if everyone:
            for d in range(1, 16):
                signal({"ctx": lax.rem(self.ctx + d, 16)})
            count = 15
        else:
            signal(self.across)
            signal(self.twin)
            pl.when(self.z > 0)(lambda: signal(self.left))
            pl.when(self.z < DEPTH - 1)(lambda: signal(self.right))
            inner = jnp.logical_and(self.z > 0, self.z < DEPTH - 1).astype(jnp.int32)
            count = 3 + inner
        if pair:
            signal(self.pair)
            count = count + 1
        pl.semaphore_wait(barrier, count)


def push(source, target, send, receive, device):
    return pltpu.make_async_remote_copy(
        src_ref=source, dst_ref=target, send_sem=send, recv_sem=receive,
        device_id=device, device_id_type=MESH,
    )


class Gather:
    def __init__(self, place, items, sems):
        self.p, self.items = place, items
        (self.sl, self.sr, self.sy, self.sc, self.rz, self.ry, self.rc) = sems

    @staticmethod
    def semaphores(count):
        dma = pltpu.SemaphoreType.DMA
        line, square = dma((count, DEPTH)), dma((count, DEPTH, 2))
        return [line, line, line, square, line, line, square]

    def piece(self, t, z, y, core):
        return self.items[t](self.p.index(z, y, core))

    def copy(self, t, z, y, source, send, receive, device):
        here = self.piece(t, z, y, self.p.core)
        return push(here if source is None else source, here, send, receive, device)

    def rightward(self, t, z, source=None):
        return self.copy(t, z, self.p.y, source, self.sr.at[t, z], self.rz.at[t, z], self.p.right)

    def leftward(self, t, z, source=None):
        return self.copy(t, z, self.p.y, source, self.sl.at[t, z], self.rz.at[t, z], self.p.left)

    def crossing(self, t, z, source=None):
        return self.copy(t, z, self.p.y, source, self.sy.at[t, z], self.ry.at[t, z], self.p.across)

    def twinning(self, t, z, y, source=None):
        return self.copy(t, z, y, source, self.sc.at[t, z, y], self.rc.at[t, z, y], self.p.twin)

    def own(self, t, source=None):
        p = self.p
        pl.when(p.z < DEPTH - 1)(lambda: self.rightward(t, p.z, source).start())
        pl.when(p.z > 0)(lambda: self.leftward(t, p.z, source).start())
        self.crossing(t, p.z, source).start()
        self.twinning(t, p.z, p.y, source).start()

    def arrived(self, t, z, y, core, semaphore):
        piece = self.piece(t, z, y, core)
        push(piece, piece, semaphore, semaphore, self.p.twin).wait_recv()

    def arrive(self, t, z):
        p = self.p
        self.arrived(t, z, p.y, p.core, self.rz.at[t, z])
        pl.when(jnp.logical_and(p.z > z, p.z < DEPTH - 1))(lambda: self.rightward(t, z).start())
        pl.when(jnp.logical_and(p.z < z, p.z > 0))(lambda: self.leftward(t, z).start())
        self.crossing(t, z).start()
        self.twinning(t, z, p.y).start()

    def along(self, t, d):
        p = self.p
        pl.when(p.z - d >= 0)(lambda: self.arrive(t, p.z - d))
        pl.when(p.z + d < DEPTH)(lambda: self.arrive(t, p.z + d))

    def crossed(self, t, z):
        self.arrived(t, z, 1 - self.p.y, self.p.core, self.ry.at[t, z])
        self.twinning(t, z, 1 - self.p.y).start()

    def crossed_at(self, t, d):
        p = self.p
        if d == 0:
            self.crossed(t, p.z)
        else:
            pl.when(p.z - d >= 0)(lambda: self.crossed(t, p.z - d))
            pl.when(p.z + d < DEPTH)(lambda: self.crossed(t, p.z + d))

    def finish(self, t):
        p = self.p
        for z in range(DEPTH):
            self.crossing(t, z).wait_send()
            for y in range(2):
                self.twinning(t, z, y).wait_send()
                self.arrived(t, z, y, 1 - p.core, self.rc.at[t, z, y])
            pl.when(jnp.logical_and(p.z >= z, p.z < DEPTH - 1))(lambda z=z: self.rightward(t, z).wait_send())
            pl.when(jnp.logical_and(p.z <= z, p.z > 0))(lambda z=z: self.leftward(t, z).wait_send())


class Line:
    def __init__(self, place, count, mine, refs):
        self.p, self.mine, self.terms = place, mine, range(count)
        self.from_across, self.slots = refs[:count], refs[count : 2 * count]
        self.ys, self.yr, self.rs, self.rr, self.vs, self.vr = refs[2 * count :]

    @staticmethod
    def scratch(shapes):
        line = pltpu.SemaphoreType.DMA((len(shapes), DEPTH))
        return (
            [pltpu.VMEM((DEPTH,) + shape, BF) for shape in shapes]
            + [pltpu.VMEM((DEPTH + 1,) + shape, BF) for shape in shapes]
            + [line] * 6
        )

    def across(self, t, z):
        return push(
            self.mine(t, z, 1 - self.p.y), self.from_across[t].at[z], self.ys.at[t, z], self.yr.at[t, z], self.p.across
        )

    def rightward(self, t, j, first):
        target = self.slots[t].at[j + 1]
        return push(self.from_across[t].at[j] if first else target, target, self.rs.at[t, j], self.rr.at[t, j], self.p.right)

    def leftward(self, t, j, first):
        target = self.slots[t].at[j]
        return push(self.from_across[t].at[j] if first else target, target, self.vs.at[t, j], self.vr.at[t, j], self.p.left)

    def cross(self, z):
        for t in self.terms:
            self.across(t, z).start()

    def quarter(self, z):
        for t in self.terms:
            self.across(t, z).wait_recv()
            both = self.mine(t, z, self.p.y)[...].astype(F32) + self.from_across[t][z].astype(F32)
            self.from_across[t][z] = both.astype(BF)

    def with_left(self, t, j):
        self.rightward(t, j, False).wait_recv()
        return self.from_across[t][j].astype(F32) + self.slots[t][j + 1].astype(F32)

    def with_right(self, t, j):
        self.leftward(t, j, False).wait_recv()
        return self.from_across[t][j].astype(F32) + self.slots[t][j].astype(F32)

    def right(self, j, z):
        @pl.when(self.p.z == z)
        def _():
            for t in self.terms:
                if z > 0:
                    self.slots[t][j + 1] = self.with_left(t, j).astype(BF)
                self.rightward(t, j, z == 0).start()

    def left(self, j, z):
        @pl.when(self.p.z == z)
        def _():
            for t in self.terms:
                if z < DEPTH - 1:
                    self.slots[t][j] = self.with_right(t, j).astype(BF)
                self.leftward(t, j, z == DEPTH - 1).start()

    def end(self, z, results):
        for t in self.terms:
            if z == 0:
                total = self.with_right(t, z)
            else:
                total = self.with_left(t, z)
                if z < DEPTH - 1:
                    self.leftward(t, z, False).wait_recv()
                    total = total + self.slots[t][z].astype(F32)
            results[t][...] = total.astype(BF)

    def finish(self):
        p = self.p
        for t in self.terms:
            for z in range(DEPTH):
                self.across(t, z).wait_send()
                pl.when(p.z < z)(lambda t=t, z=z: self.rightward(t, z, False).wait_send())
                pl.when(p.z > z)(lambda t=t, z=z: self.leftward(t, z, False).wait_send())


class Halves:
    def __init__(self, place, sources, refs):
        count = len(sources)
        self.p, self.sources, self.terms = place, sources, range(count)
        self.kept, self.from_twin = refs[:count], refs[count : 2 * count]
        self.ls, self.ts, self.tr = refs[2 * count :]

    @staticmethod
    def scratch(shapes):
        square = pltpu.SemaphoreType.DMA((len(shapes), DEPTH, 2))
        return [pltpu.VMEM((DEPTH, 2) + shape, BF) for shape in shapes] * 2 + [square] * 3

    def mine(self, t, z, y):
        return self.kept[t].at[z, y]

    def load(self, t, z, y):
        source = self.sources[t](self.p.index(z, y, self.p.core))
        return pltpu.make_async_copy(source, self.kept[t].at[z, y], self.ls.at[t, z, y])

    def twin(self, t, z, y):
        source = self.sources[t](self.p.index(z, y, 1 - self.p.core))
        return push(source, self.from_twin[t].at[z, y], self.ts.at[t, z, y], self.tr.at[t, z, y], self.p.twin)

    def begin(self, z):
        for y in (1 - self.p.y, self.p.y):
            for t in self.terms:
                self.load(t, z, y).start()
                self.twin(t, z, y).start()

    def halve(self, z):
        for y in (1 - self.p.y, self.p.y):
            for t in self.terms:
                self.load(t, z, y).wait()
                self.twin(t, z, y).wait_recv()
                both = self.kept[t][z, y].astype(F32) + self.from_twin[t][z, y].astype(F32)
                self.kept[t][z, y] = both.astype(BF)

    def finish(self):
        for t in self.terms:
            for z in range(DEPTH):
                for y in range(2):
                    self.twin(t, z, y).wait_send()


def widen_kernel(up_ref, down_ref, out_ref, qkv_ref, up_to, down_to, out_to, qkv_to):
    columns = up_ref.shape[-1]
    up_to[:, :columns] = up_ref[0, 0].astype(F32)
    up_to[:, columns:] = up_ref[1, 0].astype(F32)
    down_to[...] = down_ref[0].astype(F32)
    out_to[...] = out_ref[0].astype(F32)
    qkv_to[...] = qkv_ref[0].astype(F32)


def widen(up, down, out, qkv):
    _, ring, up_rows, up_columns = up.shape

    def piece(a):
        return pl.BlockSpec((1,) + a.shape[1:], lambda i: (i, 0, 0))

    def row_block(a):
        return pl.BlockSpec(a.shape[1:], lambda i: (i, 0))

    def whole(a):
        return jax.ShapeDtypeStruct((ring * a.shape[1], a.shape[2]), F32)

    return pl.pallas_call(
        widen_kernel,
        grid=(ring,),
        in_specs=[
            pl.BlockSpec((2, 1, up_rows, up_columns), lambda i: (0, i, 0, 0)),
            piece(down), piece(out), piece(qkv),
        ],
        out_specs=[
            pl.BlockSpec((up_rows, 2 * up_columns), lambda i: (i, 0)),
            row_block(down), row_block(out), row_block(qkv),
        ],
        out_shape=[
            jax.ShapeDtypeStruct((ring * up_rows, 2 * up_columns), F32),
            whole(down), whole(out), whole(qkv),
        ],
        name="widen",
    )(up, down, out, qkv)


def start_kernel(
    qkv_own, time_own, table_own, gain_own, qkv_all, time_all, table_all, gain_all,
    hold_qkv, hold_time, local_in, local_out, cross_s, cross_r, *gather_sems,
):
    p = Place()
    other = 1 - p.wt
    split = qkv_all.shape[2] // 2
    deep = time_all.shape[2]
    items = [
        lambda c: qkv_all.at[other, c, 0:split],
        lambda c: qkv_all.at[other, c, split:],
        lambda c: time_all.at[other, c],
    ]
    g = Gather(p, items, gather_sems)
    into = [pltpu.make_async_copy(qkv_own, hold_qkv, local_in.at[0]),
            pltpu.make_async_copy(time_own, hold_time, local_in.at[1])]
    for copy in into:
        copy.start()
    p.greet()
    c = p.ctx
    sent = [
        push(qkv_own.at[pl.ds(2 * split * c, split)], qkv_all.at[p.wt, c, 0:split], cross_s.at[0], cross_r.at[0], p.pair),
        push(qkv_own.at[pl.ds(2 * split * c + split, split)], qkv_all.at[p.wt, c, split:], cross_s.at[1], cross_r.at[1], p.pair),
        push(time_own.at[pl.ds(deep * c, deep)], time_all.at[p.wt, c], cross_s.at[2], cross_r.at[2], p.pair),
        push(table_own, table_all.at[p.wt], cross_s.at[3], cross_r.at[3], p.pair),
        push(gain_own, gain_all.at[p.wt], cross_s.at[4], cross_r.at[4], p.pair),
    ]
    for copy in sent:
        copy.start()
    table_all[p.wt] = table_own[...]
    gain_all[p.wt] = gain_own[...]
    for t in range(len(items)):
        sent[t].wait_recv()
        g.own(t)
    for copy in into:
        copy.wait()
    out = []
    for k in range(16):
        out.append(pltpu.make_async_copy(
            hold_qkv.at[2 * split * k : 2 * split * (k + 1)], qkv_all.at[p.wt, k], local_out.at[0, k]))
        out.append(pltpu.make_async_copy(
            hold_time.at[deep * k : deep * (k + 1)], time_all.at[p.wt, k], local_out.at[1, k]))
    for copy in out:
        copy.start()
    every = range(len(items))
    for t in every:
        g.along(t, 1)
    for t in every:
        g.along(t, 2)
    for t in every:
        g.crossed_at(t, 0)
    for t in every:
        g.along(t, 3)
    for d in (1, 2, 3):
        for t in every:
            g.crossed_at(t, d)
    for copy in out:
        copy.wait()
    for t in every:
        g.finish(t)
        sent[t].wait_send()
    sent[3].wait()
    sent[4].wait()


def start(qkv_w, time_w, table, gains):
    dma = pltpu.SemaphoreType.DMA
    vmem = pl.BlockSpec(memory_space=pltpu.VMEM)
    anywhere = pl.BlockSpec(memory_space=pl.ANY)
    qkv_rows, time_rows = qkv_w.shape[0] // 16, time_w.shape[0] // 16
    qkv_all, time_all, table_all, gain_all = pl.pallas_call(
        start_kernel,
        out_shape=[
            jax.ShapeDtypeStruct((2, 16, qkv_rows, qkv_w.shape[1]), BF),
            jax.ShapeDtypeStruct((2, 16, time_rows, time_w.shape[1]), BF),
            jax.ShapeDtypeStruct((2,) + table.shape, BF),
            jax.ShapeDtypeStruct((2,) + gains.shape, BF),
        ],
        in_specs=[anywhere, anywhere, vmem, vmem],
        out_specs=[anywhere, anywhere, vmem, vmem],
        scratch_shapes=[
            pltpu.VMEM(qkv_w.shape, BF), pltpu.VMEM(time_w.shape, BF),
            dma((2,)), dma((2, 16)), dma((5,)), dma((5,)),
        ] + Gather.semaphores(3),
        compiler_params=pltpu.CompilerParams(
            collective_id=1, has_side_effects=True, vmem_limit_bytes=32 << 20
        ),
        name="start",
    )(qkv_w, time_w, table, gains)
    return (
        qkv_all.reshape(-1, qkv_w.shape[1]),
        time_all.reshape(-1, time_w.shape[1]),
        table_all.reshape(-1, table.shape[1]),
        jnp.transpose(gain_all, (1, 0, 2)).reshape(gains.shape[0], -1),
    )


def ring_peer(p, d):
    return lax.rem(p.ctx + d, 16)


def heads_kernel(
    block, qkv_t, up_w, out_w, cot,
    qkv_in, att, full_ref, lse_ref, up_all, out_all, cot_all,
    keys, low, hold_up, hold_out, hold_cot, own_s, in_s, in_r, back_s, back_r, hold_in, hold_to,
    cross_s, cross_r, twin_s, twin_r,
):
    p = Place()
    micro, _, length = qkv_in.shape
    width = length // 16
    model = att.shape[0]
    half_up, half_out = up_w.shape[0] // 2, out_w.shape[0] // 2
    columns = up_all.shape[2]
    other = 1 - p.wt
    mine = pl.ds(pl.multiple_of(p.wt * columns, columns), columns)
    theirs = pl.ds(pl.multiple_of(other * columns, columns), columns)
    holds = [
        pltpu.make_async_copy(up_w.at[:, mine], hold_up, hold_in.at[0]),
        pltpu.make_async_copy(out_w, hold_out, hold_in.at[1]),
        pltpu.make_async_copy(cot, hold_cot, hold_in.at[2]),
    ]
    for copy in holds:
        copy.start()
    p.greet(everyone=True)

    def piece(part, c):
        return pl.ds(pl.multiple_of(part * model + c * HEAD, HEAD), HEAD)

    def lanes(c):
        return pl.ds(pl.multiple_of(c * width, width), width)

    def to_head(m, d, part):
        c = ring_peer(p, d)
        return push(
            qkv_t.at[piece(part, c), m * width : (m + 1) * width],
            qkv_in.at[m, part * HEAD : (part + 1) * HEAD, lanes(p.ctx)],
            in_s.at[m, d, part], in_r.at[m, d, part], {"ctx": c},
        )

    stay = [
        pltpu.make_async_copy(
            qkv_t.at[piece(part, p.ctx), m * width : (m + 1) * width],
            qkv_in.at[m, part * HEAD : (part + 1) * HEAD, lanes(p.ctx)],
            own_s.at[m, part],
        )
        for m in range(micro) for part in range(3)
    ]
    rows_up = pl.ds(pl.multiple_of(p.core * half_up, half_up), half_up)
    rows_out = pl.ds(pl.multiple_of(p.core * half_out, half_out), half_out)
    crossing = [
        push(out_w.at[rows_out], out_all.at[p.wt, rows_out], cross_s.at[0], cross_r.at[0], p.pair),
        push(up_w.at[rows_up, theirs], up_all.at[p.wt, rows_up], cross_s.at[1], cross_r.at[1], p.pair),
        push(cot, cot_all.at[1], cross_s.at[2], cross_r.at[2], p.pair),
    ]
    twins = [
        push(out_all.at[other, rows_out], out_all.at[other, rows_out], twin_s.at[0], twin_r.at[0], p.twin),
        push(up_all.at[other, rows_up], up_all.at[other, rows_up], twin_s.at[1], twin_r.at[1], p.twin),
    ]
    for copy in stay:
        copy.start()
    for m in range(micro):
        for d in range(1, 16):
            for part in range(3):
                to_head(m, d, part).start()
        if m == 0:
            for copy in crossing:
                copy.start()
    for copy in holds:
        copy.wait()
    placing = [
        pltpu.make_async_copy(hold_up, up_all.at[p.wt], hold_to.at[0]),
        pltpu.make_async_copy(hold_out, out_all.at[p.wt], hold_to.at[1]),
        pltpu.make_async_copy(hold_cot, cot_all.at[0], hold_to.at[2]),
    ]
    for copy in placing:
        copy.start()

    def to_owner(m, c):
        return push(
            low.at[m, :, c * width : (c + 1) * width],
            att.at[pl.ds(pl.multiple_of(p.ctx * HEAD, HEAD), HEAD), m * width : (m + 1) * width],
            back_s.at[m, c], back_r.at[m, p.ctx], {"ctx": c},
        )

    for m in range(micro):
        for part in range(3):
            stay[3 * m + part].wait()
            for d in range(1, 16):
                to_head(m, d, part).wait_recv()
        keys[...] = qkv_in[m, HEAD : 2 * HEAD, :].T
        for j in range(length // block):
            cols = slice(j * block, (j + 1) * block)
            scores = dot(keys[...], qkv_in[m, 0:HEAD, cols]) * (SCALE * LOG2E)
            top = jnp.max(scores, axis=0, keepdims=True)
            exps = jnp.exp2(scores - top)
            total = jnp.sum(exps, axis=0, keepdims=True)
            out = dot(qkv_in[m, 2 * HEAD :, :], exps.astype(BF)) / total
            full_ref[m, :, cols] = out
            lse_ref[m, :, cols] = top + jnp.log2(total)
            low[m, :, cols] = out.astype(BF)
            for c in range(j * block // width, (j + 1) * block // width):
                pl.when(p.ctx != c)(lambda m=m, c=c: to_owner(m, c).start())
        att[pl.ds(pl.multiple_of(p.ctx * HEAD, HEAD), HEAD), m * width : (m + 1) * width] = low[
            m, :, pl.ds(pl.multiple_of(p.ctx * width, width), width)
        ]
        if m == 0:
            for t in range(2):
                crossing[t].wait_recv()
                twins[t].start()

    for m in range(micro):
        for d in range(1, 16):
            c = ring_peer(p, d)
            push(
                low.at[m, :, 0:width],
                att.at[pl.ds(pl.multiple_of(c * HEAD, HEAD), HEAD), m * width : (m + 1) * width],
                back_s.at[m, 0], back_r.at[m, c], {"ctx": c},
            ).wait_recv()
            for part in range(3):
                to_head(m, d, part).wait_send()
        for c in range(16):
            pl.when(p.ctx != c)(lambda m=m, c=c: to_owner(m, c).wait_send())
    crossing[2].wait_recv()
    for copy in crossing:
        copy.wait_send()
    for copy in twins + placing:
        copy.wait()


def heads(qkv_t, up_w, out_w, cot, micro, block):
    dma = pltpu.SemaphoreType.DMA
    vmem = pl.BlockSpec(memory_space=pltpu.VMEM)
    anywhere = pl.BlockSpec(memory_space=pl.ANY)
    rows = qkv_t.shape[1]
    length = rows // micro * 16
    model = out_w.shape[1]
    columns = up_w.shape[1] // 2
    qkv_in, att, full, lse, up_all, out_all, cot_all = pl.pallas_call(
        functools.partial(heads_kernel, block),
        out_shape=[
            jax.ShapeDtypeStruct((micro, 3 * HEAD, length), BF),
            jax.ShapeDtypeStruct((model, rows), BF),
            jax.ShapeDtypeStruct((micro, HEAD, length), F32),
            jax.ShapeDtypeStruct((micro, 1, length), F32),
            jax.ShapeDtypeStruct((2, up_w.shape[0], columns), BF),
            jax.ShapeDtypeStruct((2,) + out_w.shape, BF),
            jax.ShapeDtypeStruct((2,) + cot.shape, BF),
        ],
        in_specs=[vmem, anywhere, anywhere, anywhere],
        out_specs=[vmem, vmem, vmem, vmem, anywhere, anywhere, anywhere],
        scratch_shapes=[
            pltpu.VMEM((length, HEAD), BF),
            pltpu.VMEM((micro, HEAD, length), BF),
            pltpu.VMEM((up_w.shape[0], columns), BF),
            pltpu.VMEM(out_w.shape, BF),
            pltpu.VMEM(cot.shape, BF),
            dma((micro, 3)),
            dma((micro, 16, 3)),
            dma((micro, 16, 3)),
            dma((micro, 16)),
            dma((micro, 16)),
            dma((3,)),
            dma((3,)),
            dma((3,)),
            dma((3,)),
            dma((2,)),
            dma((2,)),
        ],
        compiler_params=pltpu.CompilerParams(
            collective_id=2, has_side_effects=True, vmem_limit_bytes=48 << 20
        ),
        name="heads",
    )(qkv_t, up_w, out_w, cot)
    return (
        qkv_in, att, full, lse,
        up_all.reshape(-1, columns), out_all.reshape(-1, model), cot_all.reshape(-1, model),
    )


ORDER = (3, 0, 2, 1)


def back_kernel(
    block, grad_t, qkv_in, full_ref, lse_ref, up_term, down_term, out_term, w_qkv,
    cosine, sine, norm_t, hat, rs_one, g_one, scale_one, grad_mid, grad_scale_two, gain_two, onehot_t,
    input_grad, up_all, down_all, out_all, qkv_all, small_all,
    keys, values, g_in, dq, dq_low, dkv_low, delta, grad_qkv, w_hold, grad_norm_t,
    term, q_twin, q_pair, up_sum, down_sum, out_sum, out_pair, out_own, qkv_sum, small, small_in, small_pair,
    own_s, in_s, in_r, back_s, back_r, w_s, q_ts, q_tr, q_ps, q_pr, cross_s, cross_r, local_s,
    small_s, small_r, small_x, spread_s, spread_r, *more,
):
    p = Place()
    micro, _, length = qkv_in.shape
    width = length // 16
    model = grad_t.shape[0]
    count = 3
    cut = 2 * count + 3
    halves = Halves(
        p, [lambda c: up_term.at[:, c], lambda c: down_term.at[c], lambda c: out_term.at[:, c]], more[:cut]
    )
    more = more[cut:]
    cut = 2 * count + 6
    f_line = Line(p, count, halves.mine, more[:cut])
    more = more[cut:]
    q_line = Line(p, 1, lambda t, z, y: term.at[p.wt, p.index(z, y, p.core)], more[:8])
    half = down_term.shape[1] // 2
    depth = term.shape[2]
    split = depth // 2
    g = Gather(
        p,
        [
            lambda c: up_all.at[p.wt, c],
            lambda c: up_all.at[1 - p.wt, c],
            lambda c: down_all.at[c, 0:half],
            lambda c: down_all.at[c, half:],
            lambda c: out_all.at[c],
            lambda c: qkv_all.at[c, 0:split],
            lambda c: qkv_all.at[c, split:],
        ],
        more[8:],
    )
    fixed, late = (2, 3, 0, 4, 1), (5, 6)
    p.greet(everyone=True)

    def rows_of(part, c):
        return pl.ds(pl.multiple_of(part * model + c * HEAD, HEAD), HEAD)

    def lanes(c):
        return pl.ds(pl.multiple_of(c * width, width), width)

    def to_head(m, d):
        c = ring_peer(p, d)
        return push(
            grad_t.at[rows_of(0, c), m * width : (m + 1) * width],
            g_in.at[m, :, lanes(p.ctx)], in_s.at[m, d], in_r.at[m, d], {"ctx": c},
        )

    stay = [
        pltpu.make_async_copy(
            grad_t.at[rows_of(0, p.ctx), m * width : (m + 1) * width],
            g_in.at[m, :, lanes(p.ctx)], own_s.at[m],
        )
        for m in range(micro)
    ]
    for m in range(micro):
        stay[m].start()
        for d in range(1, 16):
            to_head(m, d).start()
        halves.begin(ORDER[m])
    for z in ORDER[micro:]:
        halves.begin(z)
    chunk = w_hold.shape[1]
    chunks = model // chunk

    def w_chunk(k):
        return pltpu.make_async_copy(w_qkv.at[k * chunk : (k + 1) * chunk], w_hold.at[k % 2], w_s.at[k % 2])

    w_chunk(0).start()
    w_chunk(1).start()
    for z in (3, 0):
        halves.halve(z)
        f_line.cross(z)

    def to_owner(m, c, part):
        source = dq_low.at[m] if part == 0 else dkv_low.at[m, part - 1]
        return push(
            source.at[:, c * width : (c + 1) * width],
            grad_qkv.at[rows_of(part, p.ctx), m * width : (m + 1) * width],
            back_s.at[m, c, part], back_r.at[m, p.ctx, part], {"ctx": c},
        )

    def send(m, c, part):
        pl.when(p.ctx != c)(lambda: to_owner(m, c, part).start())

    for m in range(micro):
        keys[...] = qkv_in[m, HEAD : 2 * HEAD, :].T
        values[...] = qkv_in[m, 2 * HEAD :, :].T
        stay[m].wait()
        for d in range(1, 16):
            to_head(m, d).wait_recv()
        delta[...] = jnp.sum(g_in[m].astype(F32) * full_ref[m], axis=0, keepdims=True)
        for j in range(length // block):
            cols = slice(j * block, (j + 1) * block)
            scores = dot(keys[cols, :], qkv_in[m, 0:HEAD, :]) * (SCALE * LOG2E)
            soft = jnp.exp2(scores - lse_ref[m])
            grad_soft = dot(values[cols, :], g_in[m])
            raw = (soft * (grad_soft - delta[...]) * SCALE).astype(BF)
            dkv_low[m, 0, :, cols] = dot(qkv_in[m, 0:HEAD, :], raw, 1, 1).astype(BF)
            dkv_low[m, 1, :, cols] = dot(g_in[m], soft.astype(BF), 1, 1).astype(BF)
            part = dot(qkv_in[m, HEAD : 2 * HEAD, cols], raw)
            if j == 0:
                dq[...] = part
            else:
                dq[...] += part
            for c in range(j * block // width, (j + 1) * block // width):
                send(m, c, 1)
                send(m, c, 2)
            if m == micro - 1 and (j + 1) * block * 2 == length:
                f_line.quarter(3)
                f_line.right(3, 0)
        dq_low[m] = dq[...].astype(BF)
        for c in range(16):
            send(m, c, 0)
        if m == 0:
            halves.halve(2)
            halves.halve(1)
        here = lanes(p.ctx)
        to = slice(m * width, (m + 1) * width)
        grad_qkv[rows_of(0, p.ctx), to] = dq_low[m, :, here]
        grad_qkv[rows_of(1, p.ctx), to] = dkv_low[m, 0, :, here]
        grad_qkv[rows_of(2, p.ctx), to] = dkv_low[m, 1, :, here]

    f_line.cross(2)
    f_line.cross(1)
    f_line.quarter(0)
    f_line.left(0, 3)
    f_line.right(3, 1)
    f_line.left(0, 2)

    for m in range(micro):
        for d in range(1, 16):
            c = ring_peer(p, d)
            for part in range(3):
                push(
                    dq_low.at[m, :, 0:width],
                    grad_qkv.at[rows_of(part, c), m * width : (m + 1) * width],
                    back_s.at[m, 0, part], back_r.at[m, c, part], {"ctx": c},
                ).wait_recv()

    low_half = HEAD // 2
    for r in range(0, 2 * model, HEAD):
        first = grad_qkv[r : r + low_half, :].astype(F32)
        second = grad_qkv[r + low_half : r + HEAD, :].astype(F32)
        grad_qkv[r : r + low_half, :] = (first * cosine[...] + second * sine[...]).astype(BF)
        grad_qkv[r + low_half : r + HEAD, :] = (second * cosine[...] - first * sine[...]).astype(BF)

    group = 4 * depth

    def q_to_twin(w, z, y):
        return push(
            term.at[w, p.index(z, y, 1 - p.core)], q_twin.at[w, z, y], q_ts.at[w, z, y], q_tr.at[w, z, y], p.twin
        )

    def q_to_pair(z, y):
        return push(
            term.at[1 - p.wt, p.index(z, y, p.core)], q_pair.at[z, y], q_ps.at[z, y], q_pr.at[z, y], p.pair
        )

    def with_twin(w, z, y):
        q_to_twin(w, z, y).wait_recv()
        here = p.index(z, y, p.core)
        term[w, here] = (term[w, here].astype(F32) + q_twin[w, z, y].astype(F32)).astype(BF)

    def product(w, z):
        start_row = pl.multiple_of(w * (model // 2) + z * group, group)
        rows = dot(norm_t[pl.ds(start_row, group), :], grad_qkv[...], 1, 1).astype(BF)
        for i in range(4):
            term[w, 4 * z + i] = rows[i * depth : (i + 1) * depth]
        for y in range(2):
            q_to_twin(w, z, y).start()

    for z in ORDER:
        product(1 - p.wt, z)
    f_line.right(3, 2)
    f_line.left(0, 1)
    for z in ORDER:
        for y in range(2):
            with_twin(1 - p.wt, z, y)
            q_to_pair(z, y).start()
    for z in ORDER:
        product(p.wt, z)

    for k in range(chunks):
        w_chunk(k).wait()
        grad_norm_t[k * chunk : (k + 1) * chunk, :] = dot(w_hold[k % 2], grad_qkv[...])
        if k + 2 < chunks:
            w_chunk(k + 2).start()
    grad_norm = grad_norm_t[...].T
    c_rows = grad_norm * (g_one[...] * scale_one[...])
    input_grad[...] = (
        grad_mid[...]
        + (
            c_rows
            - jnp.mean(c_rows, axis=-1, keepdims=True)
            - hat[...] * jnp.mean(c_rows * hat[...], axis=-1, keepdims=True)
        )
        * rs_one[...]
    ).astype(BF)
    eh = grad_norm * hat[...]
    grad_scale_one = (eh * g_one[...]).astype(BF)
    gain_one = jnp.sum(eh * scale_one[...], axis=0, keepdims=True)

    levels = onehot_t.shape[0]
    fill = jnp.zeros((small.shape[1] - levels - 1, 128), BF)
    for side, shifts, gain in ((0, grad_scale_one, gain_one), (1, grad_scale_two[...], gain_two[...])):
        level = dot(onehot_t[...], shifts).astype(BF)
        for k in range(8):
            cols = slice(k * 128, (k + 1) * 128)
            small[8 * side + k, 0:levels, :] = level[:, cols]
            small[8 * side + k, levels:, :] = jnp.concatenate([gain[:, cols].astype(BF), fill])

    def small_to(d):
        peer = ring_peer(p, d)
        return push(small.at[peer], small_in.at[p.ctx], small_s.at[d], small_r.at[d], {"ctx": peer})

    for d in range(1, 16):
        small_to(d).start()
    small_in[p.ctx] = small[p.ctx]
    for z in ORDER:
        for y in range(2):
            with_twin(p.wt, z, y)

    out_cross = push(out_sum.at[1 - p.wt], out_pair, cross_s.at[0], cross_r.at[0], p.pair)
    up_cross = push(up_sum.at[1 - p.wt], up_all.at[p.wt, p.ctx], cross_s.at[1], cross_r.at[1], p.pair)
    up_came = push(up_sum.at[p.wt], up_all.at[1 - p.wt, p.ctx], cross_s.at[1], cross_r.at[1], p.pair)
    sources = {0: up_sum.at[p.wt], 2: down_sum.at[0:half], 3: down_sum.at[half:], 4: out_own,
               5: qkv_sum.at[0:split], 6: qkv_sum.at[split:]}

    def f_end(z):
        @pl.when(p.z == z)
        def _():
            f_line.end(z, [up_sum, down_sum, out_sum])
            out_cross.start()
            up_cross.start()

    def q_cross(z):
        for y in (1 - p.y, p.y):
            q_to_pair(z, y).wait_recv()
            here = p.index(z, y, p.core)
            term[p.wt, here] = (term[p.wt, here].astype(F32) + q_pair[z, y].astype(F32)).astype(BF)
        q_line.cross(z)

    f_line.quarter(2)
    f_line.right(2, 0)
    q_cross(3)
    f_line.right(2, 1)
    f_line.quarter(1)
    f_line.left(1, 3)
    f_line.right(1, 0)
    f_line.left(2, 3)
    q_cross(0)
    q_line.quarter(3)
    q_line.right(3, 0)
    f_line.left(1, 2)
    q_cross(2)
    q_line.quarter(0)
    q_line.left(0, 3)
    q_line.right(3, 1)
    q_line.left(0, 2)
    q_cross(1)
    q_line.right(3, 2)
    q_line.left(0, 1)
    q_line.quarter(2)
    q_line.right(2, 0)
    q_line.quarter(1)
    q_line.left(1, 3)
    q_line.right(1, 0)
    q_line.left(2, 3)
    for z in range(DEPTH):
        f_end(z)
    for d in range(1, 16):
        small_to(d).wait_recv()
    small_pair[0] = jnp.sum(small_in[...].astype(F32), axis=0).astype(BF)
    small_cross = push(small_pair.at[0], small_pair.at[1], small_x.at[0], small_x.at[1], p.pair)
    small_cross.start()
    q_line.right(2, 1)
    q_line.left(1, 2)

    for t in (2, 3, 0):
        g.own(t, sources[t])
    out_cross.wait_recv()
    out_own[...] = (out_sum[p.wt].astype(F32) + out_pair[...].astype(F32)).astype(BF)
    g.own(4, sources[4])
    up_came.wait_recv()
    g.own(1)
    for z in range(DEPTH):
        pl.when(p.z == z)(lambda z=z: q_line.end(z, [qkv_sum]))
    for t in late:
        g.own(t, sources[t])

    small_cross.wait()
    small_all[p.ctx] = (small_pair[0].astype(F32) + small_pair[1].astype(F32)).astype(BF)

    def small_spread(d):
        peer = ring_peer(p, d)
        return push(small_all.at[p.ctx], small_all.at[p.ctx], spread_s.at[d], spread_r.at[d], {"ctx": peer})

    for d in range(1, 16):
        small_spread(d).start()
    copies = [pltpu.make_async_copy(sources[t], g.items[t](p.ctx), local_s.at[t]) for t in sources]
    for copy in copies:
        copy.start()
    every = fixed + late
    for t in every:
        g.along(t, 1)
    for t in every:
        g.along(t, 2)
    for t in every:
        g.crossed_at(t, 0)
    for t in every:
        g.along(t, 3)
    for d in (1, 2, 3):
        for t in every:
            g.crossed_at(t, d)

    for copy in copies:
        copy.wait()
    for t in range(len(g.items)):
        g.finish(t)
    halves.finish()
    f_line.finish()
    q_line.finish()
    out_cross.wait_send()
    up_cross.wait_send()
    for d in range(1, 16):
        small_to(d).wait_send()
        small_spread(d).wait()
    for z in range(DEPTH):
        for y in range(2):
            q_to_pair(z, y).wait_send()
            for w in range(2):
                q_to_twin(w, z, y).wait_send()
    for m in range(micro):
        for d in range(1, 16):
            to_head(m, d).wait_send()
        for c in range(16):
            for part in range(3):
                pl.when(p.ctx != c)(lambda m=m, c=c, part=part: to_owner(m, c, part).wait_send())


def back_pass(grad_t, qkv_in, full, lse, up, down, out, w_qkv, rest, block):
    dma = pltpu.SemaphoreType.DMA
    vmem = pl.BlockSpec(memory_space=pltpu.VMEM)
    anywhere = pl.BlockSpec(memory_space=pl.ANY)
    micro, _, length = qkv_in.shape
    model, rows = grad_t.shape
    pieces = [up.shape[:1] + up.shape[2:], down.shape[1:], out.shape[:1] + out.shape[2:]]
    piece = (model // 32, 3 * model)
    small = (16, 80, 128)
    return pl.pallas_call(
        functools.partial(back_kernel, block),
        out_shape=[
            jax.ShapeDtypeStruct((rows, model), BF),
            jax.ShapeDtypeStruct((2, 16) + up.shape[2:], BF),
            jax.ShapeDtypeStruct(down.shape, BF),
            jax.ShapeDtypeStruct(out.shape[1:], BF),
            jax.ShapeDtypeStruct((16,) + piece, BF),
            jax.ShapeDtypeStruct(small, BF),
        ],
        in_specs=[vmem] * 4 + [anywhere] * 4 + [vmem] * len(rest),
        out_specs=[vmem] + [anywhere] * 4 + [vmem],
        scratch_shapes=[
            pltpu.VMEM((length, HEAD), BF),
            pltpu.VMEM((length, HEAD), BF),
            pltpu.VMEM((micro, HEAD, length), BF),
            pltpu.VMEM((HEAD, length), F32),
            pltpu.VMEM((micro, HEAD, length), BF),
            pltpu.VMEM((micro, 2, HEAD, length), BF),
            pltpu.VMEM((1, length), F32),
            pltpu.VMEM((3 * model, rows), BF),
            pltpu.VMEM((2, 128, 3 * model), BF),
            pltpu.VMEM((model, rows), F32),
            pltpu.VMEM((2, 16) + piece, BF),
            pltpu.VMEM((2, DEPTH, 2) + piece, BF),
            pltpu.VMEM((DEPTH, 2) + piece, BF),
            pltpu.VMEM(pieces[0], BF),
            pltpu.VMEM(pieces[1], BF),
            pltpu.VMEM(pieces[2], BF),
            pltpu.VMEM(pieces[2][1:], BF),
            pltpu.VMEM(pieces[2][1:], BF),
            pltpu.VMEM(piece, BF),
            pltpu.VMEM(small, BF),
            pltpu.VMEM(small, BF),
            pltpu.VMEM((2,) + small[1:], BF),
            dma((micro,)),
            dma((micro, 16)),
            dma((micro, 16)),
            dma((micro, 16, 3)),
            dma((micro, 16, 3)),
            dma((2,)),
            dma((2, DEPTH, 2)),
            dma((2, DEPTH, 2)),
            dma((DEPTH, 2)),
            dma((DEPTH, 2)),
            dma((2,)),
            dma((2,)),
            dma((7,)),
            dma((16,)),
            dma((16,)),
            dma((2,)),
            dma((16,)),
            dma((16,)),
        ]
        + Halves.scratch(pieces)
        + Line.scratch(pieces)
        + Line.scratch([piece])
        + Gather.semaphores(7),
        compiler_params=pltpu.CompilerParams(
            collective_id=4, has_side_effects=True, vmem_limit_bytes=63 << 20
        ),
        name="back_pass",
    )(grad_t, qkv_in, full, lse, up, down, out, w_qkv, *rest)


def spread(source, pieces, first, target):
    width = source.shape[-1]
    for c in range(pieces):
        target[:, c * width : (c + 1) * width] = source[c, 0, first : first + HEAD, :]


def attend_kernel(pieces, block, qkv_ref, low_ref, full_ref, lse_ref, q_t, k_t, v_t, keys):
    length = q_t.shape[1]
    width = length // pieces
    spread(qkv_ref, pieces, 0, q_t)
    spread(qkv_ref, pieces, HEAD, k_t)
    spread(qkv_ref, pieces, 2 * HEAD, v_t)
    keys[...] = k_t[...].T
    for j in range(length // block):
        cols = slice(j * block, (j + 1) * block)
        scores = dot(keys[...], q_t[:, cols]) * (SCALE * LOG2E)
        top = jnp.max(scores, axis=0, keepdims=True)
        exps = jnp.exp2(scores - top)
        total = jnp.sum(exps, axis=0, keepdims=True)
        out = dot(v_t[...], exps.astype(BF)) / total
        full_ref[0, :, cols] = out
        lse_ref[0, :, cols] = top + jnp.log2(total)
        for c in range(block // width):
            low_ref[j * (block // width) + c, 0] = out[:, c * width : (c + 1) * width].astype(BF)


def attend(qkv, block):
    pieces, pairs, _, width = qkv.shape
    length = pieces * width
    return pl.pallas_call(
        functools.partial(attend_kernel, pieces, block),
        grid=(pairs,),
        in_specs=[pl.BlockSpec((pieces, 1, 3 * HEAD, width), lambda p: (0, p, 0, 0))],
        out_specs=[
            pl.BlockSpec((pieces, 1, HEAD, width), lambda p: (0, p, 0, 0)),
            pl.BlockSpec((1, HEAD, length), lambda p: (p, 0, 0)),
            pl.BlockSpec((1, 1, length), lambda p: (p, 0, 0)),
        ],
        out_shape=[
            jax.ShapeDtypeStruct((pieces, pairs, HEAD, width), BF),
            jax.ShapeDtypeStruct((pairs, HEAD, length), F32),
            jax.ShapeDtypeStruct((pairs, 1, length), F32),
        ],
        scratch_shapes=[pltpu.VMEM((HEAD, length), BF)] * 3 + [pltpu.VMEM((length, HEAD), BF)],
        compiler_params=pltpu.CompilerParams(vmem_limit_bytes=48 << 20),
        name="attend",
    )(qkv)


def attend_back_kernel(
    pieces, block, qkv_ref, grad_ref, full_ref, lse_ref, out_ref,
    q_t, k_t, v_t, g_t, keys, values, dq_t, dk, dv,
):
    length = q_t.shape[1]
    width = length // pieces
    spread(qkv_ref, pieces, 0, q_t)
    spread(qkv_ref, pieces, HEAD, k_t)
    spread(qkv_ref, pieces, 2 * HEAD, v_t)
    spread(grad_ref, pieces, 0, g_t)
    keys[...] = k_t[...].T
    values[...] = v_t[...].T
    for j in range(length // block):
        cols = slice(j * block, (j + 1) * block)
        query = q_t[:, cols]
        grad = g_t[:, cols]
        delta = jnp.sum(grad.astype(F32) * full_ref[0, :, cols], axis=0, keepdims=True)
        scores = dot(keys[...], query) * (SCALE * LOG2E)
        soft = jnp.exp2(scores - lse_ref[0, :, cols])
        term_v = dot(soft.astype(BF), grad, 1, 1)
        grad_soft = dot(values[...], grad)
        raw = (soft * (grad_soft - delta) * SCALE).astype(BF)
        term_k = dot(raw, query, 1, 1)
        dq_t[:, cols] = dot(k_t[...], raw)
        if j == 0:
            dv[...] = term_v
            dk[...] = term_k
        else:
            dv[...] += term_v
            dk[...] += term_k
    dk_t = dk[...].T.astype(BF)
    dv_t = dv[...].T.astype(BF)
    for c in range(pieces):
        piece = slice(c * width, (c + 1) * width)
        out_ref[c, 0, 0:HEAD, :] = dq_t[:, piece].astype(BF)
        out_ref[c, 0, HEAD : 2 * HEAD, :] = dk_t[:, piece]
        out_ref[c, 0, 2 * HEAD :, :] = dv_t[:, piece]


def attend_back(qkv, grad, full, lse, block):
    pieces, pairs, _, width = qkv.shape
    length = pieces * width
    return pl.pallas_call(
        functools.partial(attend_back_kernel, pieces, block),
        grid=(pairs,),
        in_specs=[
            pl.BlockSpec((pieces, 1, 3 * HEAD, width), lambda p: (0, p, 0, 0)),
            pl.BlockSpec((pieces, 1, HEAD, width), lambda p: (0, p, 0, 0)),
            pl.BlockSpec((1, HEAD, length), lambda p: (p, 0, 0)),
            pl.BlockSpec((1, 1, length), lambda p: (p, 0, 0)),
        ],
        out_specs=pl.BlockSpec((pieces, 1, 3 * HEAD, width), lambda p: (0, p, 0, 0)),
        out_shape=jax.ShapeDtypeStruct(qkv.shape, BF),
        scratch_shapes=[pltpu.VMEM((HEAD, length), BF)] * 4
        + [pltpu.VMEM((length, HEAD), BF)] * 2
        + [pltpu.VMEM((HEAD, length), F32)]
        + [pltpu.VMEM((length, HEAD), F32)] * 2,
        compiler_params=pltpu.CompilerParams(vmem_limit_bytes=56 << 20),
        name="attend_back",
    )(qkv, grad, full, lse)


def normed(rows):
    centered = rows - jnp.mean(rows, axis=-1, keepdims=True)
    scale = lax.rsqrt(jnp.mean(centered * centered, axis=-1, keepdims=True) + EPSILON)
    return centered * scale, scale


def norm_back(grad, hat, scale, weight):
    c = grad * weight
    return (
        c - jnp.mean(c, axis=-1, keepdims=True) - hat * jnp.mean(c * hat, axis=-1, keepdims=True)
    ) * scale


def turn(first, second, cosine, sine):
    return first * cosine - second * sine, second * cosine + first * sine


def shards(
    tokens, positions, buckets, qkv_w, out_w, up_w, down_w, time_w, noise_table,
    gain_one, gain_two, cotangent,
):
    n, ring = lax.axis_size("wt"), lax.axis_size("ctx")
    me = lax.axis_index("wt")
    micro, _, width, model = tokens.shape
    rows = micro * width
    pairs = HEADS * micro // ring
    block = 256
    planar = n == 2 and ring == 16

    x = tokens.reshape(rows, model).astype(F32)
    cot_low = cotangent.reshape(rows, model)
    places = positions.reshape(rows)
    levels = buckets.reshape(rows)

    def whole_rows(weight):
        return lax.all_gather(weight, "wt", axis=0, tiled=True)

    stacked = jnp.stack([gain_one, gain_two])
    if planar:
        w_qkv, w_time, table, gains = start(qkv_w, time_w, noise_table, stacked)
    else:
        w_qkv = whole_rows(qkv_w)
        w_out = whole_rows(out_w)
        w_time = whole_rows(time_w)
        table = whole_rows(noise_table)
        gains = lax.all_gather(stacked, "wt", axis=1, tiled=True)
        w_up = lax.all_to_all(up_w, "wt", 1, 0, tiled=True)
    g_one, g_two = gains[0].astype(F32), gains[1].astype(F32)

    onehot = levels[:, None] == jnp.arange(table.shape[0], dtype=jnp.int32)[None, :]
    embed = dot(onehot.astype(BF), table).astype(BF)
    shifts = dot(embed, w_time)
    scale_one = 1.0 + shifts[:, :model]
    scale_two = 1.0 + shifts[:, model:]

    hat_one, rs_one = normed(x)
    weight_one = g_one * scale_one
    norm_one = (hat_one * weight_one).astype(BF)

    qkv_t = dot(w_qkv, norm_one, 0, 1).reshape(3, HEADS, 2, HEAD // 2, rows)
    frequency = jnp.exp(
        jnp.arange(HEAD // 2, dtype=F32) * (-math.log(10000.0) * 2.0 / HEAD)
    )
    angles = frequency[:, None] * places.astype(F32)[None, :]
    cosine, sine = jnp.cos(angles), jnp.sin(angles)
    turned = turn(qkv_t[:2, :, 0], qkv_t[:2, :, 1], cosine, sine)
    queries_keys = jnp.stack(turned, axis=2)
    qkv_low = jnp.concatenate([queries_keys.astype(BF), qkv_t[2:].astype(BF)])

    def to_heads(columns):
        parts = columns.shape[0]
        split = columns.reshape(parts, HEADS, HEAD, micro, width)
        split = jnp.transpose(split, (1, 3, 0, 2, 4))
        split = split.reshape(ring, pairs, parts * HEAD, width)
        return lax.all_to_all(split, "ctx", 0, 0, tiled=True)

    def to_tokens(pieces):
        parts = pieces.shape[2] // HEAD
        back = lax.all_to_all(pieces, "ctx", 0, 0, tiled=True)
        back = back.reshape(HEADS, micro, parts, HEAD, width)
        return jnp.transpose(back, (2, 0, 3, 1, 4)).reshape(parts, HEADS * HEAD, rows)

    if planar:
        qkv_heads, attended, full, lse, w_up, w_out, cot = heads(
            qkv_low.reshape(3 * model, rows), up_w, out_w, cot_low, micro, block
        )
    else:
        qkv_heads = to_heads(qkv_low.reshape(3, HEADS, HEAD, rows))
        low, full, lse = attend(qkv_heads, block)
        attended = to_tokens(low)[0]
        cot = gather_slots(cot_low).reshape(n * rows, model)

    middle = x + dot(attended, w_out, 0, 0)
    hat_two, rs_two = normed(middle)
    weight_two = g_two * scale_two
    norm_two_own = (hat_two * weight_two).astype(BF)

    norm_two = gather_slots(norm_two_own).reshape(n * rows, model)
    pre = dot(norm_two, w_up)
    phi_cdf = 0.5 * (1.0 + lax.erf(pre * (2.0**-0.5)))
    hidden = (pre * phi_cdf).astype(BF)
    layer_out = middle + sum_slots(dot(hidden, down_w).reshape(n, rows, model))

    grad_hidden = dot(cot, down_w, 1, 1)
    density = jnp.exp(-0.5 * pre * pre) * (1.0 / math.sqrt(2.0 * math.pi))
    grad_pre = (grad_hidden * (phi_cdf + pre * density)).astype(BF)
    grad_norm_two = sum_slots(dot(grad_pre, w_up, 1, 1).reshape(n, rows, model))
    down_term = dot(hidden, cot, 0, 0).astype(BF)
    up_term = dot(norm_two, grad_pre, 0, 0).astype(BF)
    grad_norm_two, down_term, up_term = lax.optimization_barrier((grad_norm_two, down_term, up_term))
    grad_mid = cot_low.astype(F32) + norm_back(grad_norm_two, hat_two, rs_two, weight_two)
    grad_branch = grad_mid.astype(BF)
    eh_two = grad_norm_two * hat_two
    grad_scale_two = eh_two * g_two
    gain_two_term = jnp.sum(eh_two * scale_two, axis=0)
    out_term = dot(attended, grad_branch, 1, 0).astype(BF)
    grad_attn = dot(w_out, grad_branch, 1, 1).astype(BF)
    if planar:

        def pieces_of(array, *lead):
            return array.reshape(lead + (-1, array.shape[-1]))

        rest = (
            cosine, sine, norm_one.T, hat_one, rs_one, g_one[None], scale_one, grad_mid,
            grad_scale_two.astype(BF), gain_two_term[None], onehot.astype(BF).T,
        )
        input_grad, up_all, down_all, out_all, qkv_all, small_all = back_pass(
            grad_attn, qkv_heads, full, lse, pieces_of(up_term, n, ring), pieces_of(down_term, ring),
            pieces_of(out_term, n, ring), w_qkv, rest, block,
        )
        up_grad, down_grad, out_grad, qkv_grad = widen(up_all, down_all, out_all, qkv_all)
        small = jnp.transpose(small_all, (1, 0, 2)).reshape(small_all.shape[1], -1).astype(F32)
    else:
        up_share = lax.psum_scatter(
            up_term.reshape(n, model // n, -1), "ctx", scatter_dimension=1, tiled=True
        )
        down_share = lax.psum_scatter(down_term, "ctx", scatter_dimension=0, tiled=True)
        out_share = lax.psum_scatter(
            out_term.reshape(n, model // n, model), "ctx", scatter_dimension=1, tiled=True
        )
        grad_heads = to_heads(grad_attn.reshape(1, HEADS, HEAD, rows))
        back = to_tokens(attend_back(qkv_heads, grad_heads, full, lse, block))
        back = back.reshape(3, HEADS, 2, HEAD // 2, rows)
        unturned = turn(back[:2, :, 0].astype(F32), back[:2, :, 1].astype(F32), cosine, -sine)
        grad_qkv = jnp.concatenate([jnp.stack(unturned, axis=2).astype(BF), back[2:]])
        grad_qkv = grad_qkv.reshape(3 * model, rows)
        qkv_term = dot(norm_one, grad_qkv, 0, 1).astype(BF)
        grad_norm_one = dot(grad_qkv, w_qkv, 0, 1)

        input_grad = grad_mid + norm_back(grad_norm_one, hat_one, rs_one, weight_one)
        eh_one = grad_norm_one * hat_one
        grad_scale_one = eh_one * g_one
        gain_one_term = jnp.sum(eh_one * scale_one, axis=0)

        grad_shifts = jnp.concatenate([grad_scale_one, grad_scale_two], axis=1).astype(BF)
        level_term = dot(onehot.astype(BF), grad_shifts, 0, 0)
        gain_terms = jnp.concatenate([gain_one_term, gain_two_term])
        small = lax.psum(jnp.concatenate([level_term, gain_terms[None]]), ("ctx", "wt"))
        share = lax.psum_scatter(
            qkv_term.reshape(n, model // n, -1), "ctx", scatter_dimension=1, tiled=True
        )

        def spread_rows(share):
            return lax.all_gather(share, "ctx", axis=0, tiled=True).astype(F32)

        up_share = lax.all_to_all(up_share, "wt", 0, 0, tiled=True)
        up_grad = lax.all_gather(up_share, "ctx", axis=1, tiled=True).astype(F32)
        up_grad = jnp.transpose(up_grad, (1, 0, 2)).reshape(model // n, -1)
        down_grad = spread_rows(down_share)
        out_grad = spread_rows(sum_owned(out_share))
        qkv_grad = spread_rows(sum_owned(share))

    by_level = small[: table.shape[0]]
    gain_sums = small[table.shape[0]]
    levels_here, time_here = noise_table.shape[0], time_w.shape[0]
    high = lax.Precision.HIGHEST
    time_rows = lax.dynamic_slice_in_dim(table, me * time_here, time_here, 1).astype(F32)
    time_grad = lax.dot_general(
        time_rows, by_level, (((0,), (0,)), ((), ())), precision=high, preferred_element_type=F32
    )
    level_rows = lax.dynamic_slice_in_dim(by_level, me * levels_here, levels_here, 0)
    table_grad = lax.dot_general(
        level_rows, w_time.astype(F32), (((1,), (1,)), ((), ())), precision=high,
        preferred_element_type=F32,
    )
    gain_here = gain_one.shape[0]
    gain_one_grad = lax.dynamic_slice_in_dim(gain_sums, me * gain_here, gain_here, 0)
    gain_two_grad = lax.dynamic_slice_in_dim(gain_sums, model + me * gain_here, gain_here, 0)

    return (
        layer_out.astype(BF).reshape(tokens.shape),
        input_grad.astype(BF).reshape(tokens.shape),
        qkv_grad,
        out_grad,
        up_grad,
        down_grad,
        time_grad,
        table_grad,
        gain_one_grad,
        gain_two_grad,
    )


def sum_owned(share):
    n, me = lax.axis_size("wt"), lax.axis_index("wt")
    slots = jnp.stack(
        [lax.dynamic_index_in_dim(share, lax.rem(me + k, n), 0, keepdims=False) for k in range(n)]
    )
    return sum_slots(slots.astype(F32)).astype(BF)


def solution(mesh):
    rows = P(None, "wt", "ctx", None)
    marks = P(None, "wt", "ctx")
    weight = P("wt", None)
    gain = P("wt")
    return jax.shard_map(
        shards,
        mesh=mesh,
        in_specs=(rows, marks, marks) + (weight,) * 6 + (gain, gain, rows),
        out_specs=(rows, rows) + (weight,) * 6 + (gain, gain),
        check_vma=False,
    )
```

```python
import functools
import math

import jax
import jax.numpy as jnp
from jax import lax
from jax.experimental import pallas as pl
from jax.experimental.pallas import tpu as pltpu
from jax.sharding import PartitionSpec as P

HEADS = 16
HEAD = 64
LEVELS = 64
EPSILON = 1e-05
SCALE = 0.125
LOG2E = math.log2(math.e)
BF = jnp.bfloat16
F32 = jnp.float32


def dot(a, b, ca=1, cb=0):
    return lax.dot_general(a, b, (((ca,), (cb,)), ((), ())), preferred_element_type=F32)


def swap_ring(value, places):
    n = lax.axis_size("wt")
    return lax.ppermute(value, "wt", [((i + places) % n, i) for i in range(n)])


def gather_slots(own):
    n = lax.axis_size("wt")
    return jnp.stack([own] + [swap_ring(own, k) for k in range(1, n)])


def sum_slots(partial):
    n = lax.axis_size("wt")
    total = partial[0]
    for k in range(1, n):
        total = total + swap_ring(partial[k].astype(BF), n - k).astype(F32)
    return total


MESH = pl.DeviceIdType.MESH
DEPTH = 4


class Place:
    def __init__(self):
        self.ctx = lax.axis_index("ctx")
        self.wt = lax.axis_index("wt")
        self.z = lax.div(self.ctx, 4)
        self.y = lax.rem(lax.div(self.ctx, 2), 2)
        self.core = lax.rem(self.ctx, 2)
        self.right = {"ctx": self.index(lax.min(self.z + 1, DEPTH - 1), self.y, self.core)}
        self.left = {"ctx": self.index(lax.max(self.z - 1, 0), self.y, self.core)}
        self.across = {"ctx": self.index(self.z, 1 - self.y, self.core)}
        self.twin = {"ctx": self.index(self.z, self.y, 1 - self.core)}
        self.pair = {"wt": 1 - self.wt}

    @staticmethod
    def index(z, y, core):
        return (z * 2 + y) * 2 + core

    def greet(self, everyone=False, pair=True):
        barrier = pltpu.get_barrier_semaphore()

        def signal(device):
            pl.semaphore_signal(barrier, inc=1, device_id=device, device_id_type=MESH)

        if everyone:
            for d in range(1, 16):
                signal({"ctx": lax.rem(self.ctx + d, 16)})
            count = 15
        else:
            signal(self.across)
            signal(self.twin)
            pl.when(self.z > 0)(lambda: signal(self.left))
            pl.when(self.z < DEPTH - 1)(lambda: signal(self.right))
            inner = jnp.logical_and(self.z > 0, self.z < DEPTH - 1).astype(jnp.int32)
            count = 3 + inner
        if pair:
            signal(self.pair)
            count = count + 1
        pl.semaphore_wait(barrier, count)


def push(source, target, send, receive, device):
    return pltpu.make_async_remote_copy(
        src_ref=source, dst_ref=target, send_sem=send, recv_sem=receive,
        device_id=device, device_id_type=MESH,
    )


class Gather:
    def __init__(self, place, items, sems):
        self.p, self.items = place, items
        (self.sl, self.sr, self.sy, self.sc, self.rz, self.ry, self.rc) = sems

    @staticmethod
    def semaphores(count):
        dma = pltpu.SemaphoreType.DMA
        line, square = dma((count, DEPTH)), dma((count, DEPTH, 2))
        return [line, line, line, square, line, line, square]

    def piece(self, t, z, y, core):
        return self.items[t](self.p.index(z, y, core))

    def copy(self, t, z, y, source, send, receive, device):
        here = self.piece(t, z, y, self.p.core)
        return push(here if source is None else source, here, send, receive, device)

    def rightward(self, t, z, source=None):
        return self.copy(t, z, self.p.y, source, self.sr.at[t, z], self.rz.at[t, z], self.p.right)

    def leftward(self, t, z, source=None):
        return self.copy(t, z, self.p.y, source, self.sl.at[t, z], self.rz.at[t, z], self.p.left)

    def crossing(self, t, z, source=None):
        return self.copy(t, z, self.p.y, source, self.sy.at[t, z], self.ry.at[t, z], self.p.across)

    def twinning(self, t, z, y, source=None):
        return self.copy(t, z, y, source, self.sc.at[t, z, y], self.rc.at[t, z, y], self.p.twin)

    def own(self, t, source=None):
        p = self.p
        pl.when(p.z < DEPTH - 1)(lambda: self.rightward(t, p.z, source).start())
        pl.when(p.z > 0)(lambda: self.leftward(t, p.z, source).start())
        self.crossing(t, p.z, source).start()
        self.twinning(t, p.z, p.y, source).start()

    def arrived(self, t, z, y, core, semaphore):
        piece = self.piece(t, z, y, core)
        push(piece, piece, semaphore, semaphore, self.p.twin).wait_recv()

    def arrive(self, t, z):
        p = self.p
        self.arrived(t, z, p.y, p.core, self.rz.at[t, z])
        pl.when(jnp.logical_and(p.z > z, p.z < DEPTH - 1))(lambda: self.rightward(t, z).start())
        pl.when(jnp.logical_and(p.z < z, p.z > 0))(lambda: self.leftward(t, z).start())
        self.crossing(t, z).start()
        self.twinning(t, z, p.y).start()

    def along(self, t, d):
        p = self.p
        pl.when(p.z - d >= 0)(lambda: self.arrive(t, p.z - d))
        pl.when(p.z + d < DEPTH)(lambda: self.arrive(t, p.z + d))

    def crossed(self, t, z):
        self.arrived(t, z, 1 - self.p.y, self.p.core, self.ry.at[t, z])
        self.twinning(t, z, 1 - self.p.y).start()

    def crossed_at(self, t, d):
        p = self.p
        if d == 0:
            self.crossed(t, p.z)
        else:
            pl.when(p.z - d >= 0)(lambda: self.crossed(t, p.z - d))
            pl.when(p.z + d < DEPTH)(lambda: self.crossed(t, p.z + d))

    def finish(self, t):
        p = self.p
        for z in range(DEPTH):
            self.crossing(t, z).wait_send()
            for y in range(2):
                self.twinning(t, z, y).wait_send()
                self.arrived(t, z, y, 1 - p.core, self.rc.at[t, z, y])
            pl.when(jnp.logical_and(p.z >= z, p.z < DEPTH - 1))(lambda z=z: self.rightward(t, z).wait_send())
            pl.when(jnp.logical_and(p.z <= z, p.z > 0))(lambda z=z: self.leftward(t, z).wait_send())


class Line:
    def __init__(self, place, count, mine, refs):
        self.p, self.mine, self.terms = place, mine, range(count)
        self.from_across, self.slots = refs[:count], refs[count : 2 * count]
        self.ys, self.yr, self.rs, self.rr, self.vs, self.vr = refs[2 * count :]

    @staticmethod
    def scratch(shapes):
        line = pltpu.SemaphoreType.DMA((len(shapes), DEPTH))
        return (
            [pltpu.VMEM((DEPTH,) + shape, BF) for shape in shapes]
            + [pltpu.VMEM((DEPTH + 1,) + shape, BF) for shape in shapes]
            + [line] * 6
        )

    def across(self, t, z):
        return push(
            self.mine(t, z, 1 - self.p.y), self.from_across[t].at[z], self.ys.at[t, z], self.yr.at[t, z], self.p.across
        )

    def rightward(self, t, j, first):
        target = self.slots[t].at[j + 1]
        return push(self.from_across[t].at[j] if first else target, target, self.rs.at[t, j], self.rr.at[t, j], self.p.right)

    def leftward(self, t, j, first):
        target = self.slots[t].at[j]
        return push(self.from_across[t].at[j] if first else target, target, self.vs.at[t, j], self.vr.at[t, j], self.p.left)

    def cross(self, z):
        for t in self.terms:
            self.across(t, z).start()

    def quarter(self, z):
        for t in self.terms:
            self.across(t, z).wait_recv()
            both = self.mine(t, z, self.p.y)[...].astype(F32) + self.from_across[t][z].astype(F32)
            self.from_across[t][z] = both.astype(BF)

    def with_left(self, t, j):
        self.rightward(t, j, False).wait_recv()
        return self.from_across[t][j].astype(F32) + self.slots[t][j + 1].astype(F32)

    def with_right(self, t, j):
        self.leftward(t, j, False).wait_recv()
        return self.from_across[t][j].astype(F32) + self.slots[t][j].astype(F32)

    def right(self, j, z):
        @pl.when(self.p.z == z)
        def _():
            for t in self.terms:
                if z > 0:
                    self.slots[t][j + 1] = self.with_left(t, j).astype(BF)
                self.rightward(t, j, z == 0).start()

    def left(self, j, z):
        @pl.when(self.p.z == z)
        def _():
            for t in self.terms:
                if z < DEPTH - 1:
                    self.slots[t][j] = self.with_right(t, j).astype(BF)
                self.leftward(t, j, z == DEPTH - 1).start()

    def end(self, z, results):
        for t in self.terms:
            if z == 0:
                total = self.with_right(t, z)
            else:
                total = self.with_left(t, z)
                if z < DEPTH - 1:
                    self.leftward(t, z, False).wait_recv()
                    total = total + self.slots[t][z].astype(F32)
            results[t][...] = total.astype(BF)

    def finish(self):
        p = self.p
        for t in self.terms:
            for z in range(DEPTH):
                self.across(t, z).wait_send()
                pl.when(p.z < z)(lambda t=t, z=z: self.rightward(t, z, False).wait_send())
                pl.when(p.z > z)(lambda t=t, z=z: self.leftward(t, z, False).wait_send())


class Halves:
    def __init__(self, place, sources, refs):
        count = len(sources)
        self.p, self.sources, self.terms = place, sources, range(count)
        self.kept, self.from_twin = refs[:count], refs[count : 2 * count]
        self.ls, self.ts, self.tr = refs[2 * count :]

    @staticmethod
    def scratch(shapes):
        square = pltpu.SemaphoreType.DMA((len(shapes), DEPTH, 2))
        return [pltpu.VMEM((DEPTH, 2) + shape, BF) for shape in shapes] * 2 + [square] * 3

    def mine(self, t, z, y):
        return self.kept[t].at[z, y]

    def load(self, t, z, y):
        source = self.sources[t](self.p.index(z, y, self.p.core))
        return pltpu.make_async_copy(source, self.kept[t].at[z, y], self.ls.at[t, z, y])

    def twin(self, t, z, y):
        source = self.sources[t](self.p.index(z, y, 1 - self.p.core))
        return push(source, self.from_twin[t].at[z, y], self.ts.at[t, z, y], self.tr.at[t, z, y], self.p.twin)

    def begin(self, z):
        for y in (1 - self.p.y, self.p.y):
            for t in self.terms:
                self.load(t, z, y).start()
                self.twin(t, z, y).start()

    def halve(self, z):
        for y in (1 - self.p.y, self.p.y):
            for t in self.terms:
                self.load(t, z, y).wait()
                self.twin(t, z, y).wait_recv()
                both = self.kept[t][z, y].astype(F32) + self.from_twin[t][z, y].astype(F32)
                self.kept[t][z, y] = both.astype(BF)

    def finish(self):
        for t in self.terms:
            for z in range(DEPTH):
                for y in range(2):
                    self.twin(t, z, y).wait_send()


def widen_kernel(
    up_ref, down_ref, out_ref, qkv_ref, small_ref, rows_ref, time_ref,
    up_to, down_to, out_to, qkv_to, time_to, table_to, gain_to,
):
    columns = up_ref.shape[-1]
    levels, here = rows_ref.shape[0], table_to.shape[0]
    mine = pl.ds(pl.multiple_of(lax.axis_index("wt") * here, here), here)
    table = None
    for i in range(up_ref.shape[1]):
        rows = slice(i * up_ref.shape[2], (i + 1) * up_ref.shape[2])
        up_to[rows, :columns] = up_ref[0, i].astype(F32)
        up_to[rows, columns:] = up_ref[1, i].astype(F32)
        for source, target in ((down_ref, down_to), (out_ref, out_to), (qkv_ref, qkv_to)):
            depth = source.shape[1]
            target[i * depth : (i + 1) * depth, :] = source[i].astype(F32)
        cols = slice(i * 128, (i + 1) * 128)
        time_to[:, cols] = dot(rows_ref[...], small_ref[i, 0:levels, :], 0, 0)
        gain_to[:, cols] = small_ref[i, levels : levels + 1, :].astype(F32)
        part = dot(small_ref[i, mine, :], time_ref[:, cols], 1, 1)
        table = part if table is None else table + part
    first = pl.program_id(0) == 0

    @pl.when(first)
    def _():
        table_to[...] = table

    @pl.when(jnp.logical_not(first))
    def _():
        table_to[...] += table


def widen(up, down, out, qkv, small, table_rows, w_time, step=2):
    _, ring, up_rows, up_columns = up.shape
    wide = small.shape[2]

    def piece(a):
        return pl.BlockSpec((step,) + a.shape[1:], lambda i: (i, 0, 0))

    def row_block(a):
        return pl.BlockSpec((step * a.shape[1], a.shape[2]), lambda i: (i, 0))

    def whole(a):
        return jax.ShapeDtypeStruct((ring * a.shape[1], a.shape[2]), F32)

    def columns(rows):
        return pl.BlockSpec((rows, step * wide), lambda i: (0, i))

    time_rows, depth = table_rows.shape[1], w_time.shape[0]
    return pl.pallas_call(
        widen_kernel,
        grid=(ring // step,),
        in_specs=[
            pl.BlockSpec((2, step, up_rows, up_columns), lambda i: (0, i, 0, 0)),
            piece(down), piece(out), piece(qkv), piece(small),
            pl.BlockSpec(table_rows.shape, lambda i: (0, 0)), columns(depth),
        ],
        out_specs=[
            pl.BlockSpec((step * up_rows, 2 * up_columns), lambda i: (i, 0)),
            row_block(down), row_block(out), row_block(qkv),
            columns(time_rows), pl.BlockSpec((table_rows.shape[0] // 2, depth), lambda i: (0, 0)), columns(1),
        ],
        out_shape=[
            jax.ShapeDtypeStruct((ring * up_rows, 2 * up_columns), F32),
            whole(down), whole(out), whole(qkv),
            jax.ShapeDtypeStruct((time_rows, ring * wide), F32),
            jax.ShapeDtypeStruct((table_rows.shape[0] // 2, depth), F32),
            jax.ShapeDtypeStruct((1, ring * wide), F32),
        ],
        compiler_params=pltpu.CompilerParams(vmem_limit_bytes=62 << 20),
        name="widen",
    )(up, down, out, qkv, small, table_rows, w_time)


def start_kernel(
    qkv_own, time_own, table_own, gain_own, qkv_all, time_all, table_all, gain_all,
    hold_qkv, hold_time, local_in, local_out, cross_s, cross_r, *gather_sems,
):
    p = Place()
    other = 1 - p.wt
    split = qkv_all.shape[2] // 2
    deep = time_all.shape[2]
    items = [
        lambda c: qkv_all.at[other, c, 0:split],
        lambda c: qkv_all.at[other, c, split:],
        lambda c: time_all.at[other, c],
    ]
    g = Gather(p, items, gather_sems)
    into = [pltpu.make_async_copy(qkv_own, hold_qkv, local_in.at[0]),
            pltpu.make_async_copy(time_own, hold_time, local_in.at[1])]
    for copy in into:
        copy.start()
    p.greet()
    c = p.ctx
    sent = [
        push(qkv_own.at[pl.ds(2 * split * c, split)], qkv_all.at[p.wt, c, 0:split], cross_s.at[0], cross_r.at[0], p.pair),
        push(qkv_own.at[pl.ds(2 * split * c + split, split)], qkv_all.at[p.wt, c, split:], cross_s.at[1], cross_r.at[1], p.pair),
        push(time_own.at[pl.ds(deep * c, deep)], time_all.at[p.wt, c], cross_s.at[2], cross_r.at[2], p.pair),
        push(table_own, table_all.at[p.wt], cross_s.at[3], cross_r.at[3], p.pair),
        push(gain_own, gain_all.at[p.wt], cross_s.at[4], cross_r.at[4], p.pair),
    ]
    for copy in sent:
        copy.start()
    table_all[p.wt] = table_own[...]
    gain_all[p.wt] = gain_own[...]
    for t in range(len(items)):
        sent[t].wait_recv()
        g.own(t)
    for copy in into:
        copy.wait()
    out = []
    for k in range(16):
        out.append(pltpu.make_async_copy(
            hold_qkv.at[2 * split * k : 2 * split * (k + 1)], qkv_all.at[p.wt, k], local_out.at[0, k]))
        out.append(pltpu.make_async_copy(
            hold_time.at[deep * k : deep * (k + 1)], time_all.at[p.wt, k], local_out.at[1, k]))
    for copy in out:
        copy.start()
    every = range(len(items))
    for t in every:
        g.along(t, 1)
    for t in every:
        g.along(t, 2)
    for t in every:
        g.crossed_at(t, 0)
    for t in every:
        g.along(t, 3)
    for d in (1, 2, 3):
        for t in every:
            g.crossed_at(t, d)
    for copy in out:
        copy.wait()
    for t in every:
        g.finish(t)
        sent[t].wait_send()
    sent[3].wait()
    sent[4].wait()


def start(qkv_w, time_w, table, gains):
    dma = pltpu.SemaphoreType.DMA
    vmem = pl.BlockSpec(memory_space=pltpu.VMEM)
    anywhere = pl.BlockSpec(memory_space=pltpu.HBM)
    qkv_rows, time_rows = qkv_w.shape[0] // 16, time_w.shape[0] // 16
    qkv_all, time_all, table_all, gain_all = pl.pallas_call(
        start_kernel,
        out_shape=[
            jax.ShapeDtypeStruct((2, 16, qkv_rows, qkv_w.shape[1]), BF),
            jax.ShapeDtypeStruct((2, 16, time_rows, time_w.shape[1]), BF),
            jax.ShapeDtypeStruct((2,) + table.shape, BF),
            jax.ShapeDtypeStruct((2,) + gains.shape, BF),
        ],
        in_specs=[anywhere, anywhere, vmem, vmem],
        out_specs=[anywhere, anywhere, vmem, vmem],
        scratch_shapes=[
            pltpu.VMEM(qkv_w.shape, BF), pltpu.VMEM(time_w.shape, BF),
            dma((2,)), dma((2, 16)), dma((5,)), dma((5,)),
        ] + Gather.semaphores(3),
        compiler_params=pltpu.CompilerParams(
            collective_id=1, has_side_effects=True, vmem_limit_bytes=63 << 20
        ),
        name="start",
    )(qkv_w, time_w, table, gains)
    return (
        qkv_all.reshape(-1, qkv_w.shape[1]),
        time_all.reshape(-1, time_w.shape[1]),
        table_all.reshape(-1, table.shape[1]),
        jnp.transpose(gain_all, (1, 0, 2)).reshape(gains.shape[0], -1),
    )


def ring_peer(p, d):
    return lax.rem(p.ctx + d, 16)


def heads_kernel(
    block, qkv_t, up_w, out_w, cot,
    qkv_keep, att, full_keep, lse_ref, up_all, out_all, cot_all,
    qkv_in, full_ref, keep_s, keys, low, hold_up, hold_out, hold_cot, own_s, in_s, in_r, back_s, back_r, hold_in, hold_to,
    cross_s, cross_r, twin_s, twin_r,
):
    p = Place()
    micro, _, length = qkv_in.shape
    width = length // 16
    model = att.shape[0]
    half_up, half_out = up_w.shape[0] // 2, out_w.shape[0] // 2
    columns = up_all.shape[2]
    other = 1 - p.wt
    mine = pl.ds(pl.multiple_of(p.wt * columns, columns), columns)
    theirs = pl.ds(pl.multiple_of(other * columns, columns), columns)
    holds = [
        pltpu.make_async_copy(up_w.at[:, mine], hold_up, hold_in.at[0]),
        pltpu.make_async_copy(out_w, hold_out, hold_in.at[1]),
        pltpu.make_async_copy(cot, hold_cot, hold_in.at[2]),
    ]
    for copy in holds:
        copy.start()
    p.greet(everyone=True)

    def piece(part, c):
        return pl.ds(pl.multiple_of(part * model + c * HEAD, HEAD), HEAD)

    def lanes(c):
        return pl.ds(pl.multiple_of(c * width, width), width)

    def to_head(m, d, part):
        c = ring_peer(p, d)
        return push(
            qkv_t.at[piece(part, c), m * width : (m + 1) * width],
            qkv_in.at[m, part * HEAD : (part + 1) * HEAD, lanes(p.ctx)],
            in_s.at[m, d, part], in_r.at[m, d, part], {"ctx": c},
        )

    stay = [
        pltpu.make_async_copy(
            qkv_t.at[piece(part, p.ctx), m * width : (m + 1) * width],
            qkv_in.at[m, part * HEAD : (part + 1) * HEAD, lanes(p.ctx)],
            own_s.at[m, part],
        )
        for m in range(micro) for part in range(3)
    ]
    rows_up = pl.ds(pl.multiple_of(p.core * half_up, half_up), half_up)
    rows_out = pl.ds(pl.multiple_of(p.core * half_out, half_out), half_out)
    crossing = [
        push(out_w.at[rows_out], out_all.at[p.wt, rows_out], cross_s.at[0], cross_r.at[0], p.pair),
        push(up_w.at[rows_up, theirs], up_all.at[p.wt, rows_up], cross_s.at[1], cross_r.at[1], p.pair),
        push(cot, cot_all.at[1], cross_s.at[2], cross_r.at[2], p.pair),
    ]
    twins = [
        push(out_all.at[other, rows_out], out_all.at[other, rows_out], twin_s.at[0], twin_r.at[0], p.twin),
        push(up_all.at[other, rows_up], up_all.at[other, rows_up], twin_s.at[1], twin_r.at[1], p.twin),
    ]
    for copy in stay:
        copy.start()
    for m in range(micro):
        for d in range(1, 16):
            for part in range(3):
                to_head(m, d, part).start()
        if m == 0:
            for copy in crossing:
                copy.start()
    for copy in holds:
        copy.wait()
    placing = [
        pltpu.make_async_copy(hold_up, up_all.at[p.wt], hold_to.at[0]),
        pltpu.make_async_copy(hold_out, out_all.at[p.wt], hold_to.at[1]),
        pltpu.make_async_copy(hold_cot, cot_all.at[0], hold_to.at[2]),
    ]
    for copy in placing:
        copy.start()

    def to_owner(m, c):
        return push(
            low.at[m, :, lanes(c)],
            att.at[pl.ds(pl.multiple_of(p.ctx * HEAD, HEAD), HEAD), m * width : (m + 1) * width],
            back_s.at[m, c], back_r.at[m, p.ctx], {"ctx": c},
        )

    keep_qkv = [pltpu.make_async_copy(qkv_in.at[m], qkv_keep.at[m], keep_s.at[0, m]) for m in range(micro)]
    keep_full = [pltpu.make_async_copy(full_ref.at[m], full_keep.at[m], keep_s.at[1, m]) for m in range(micro)]
    for m in range(micro):
        for part in range(3):
            stay[3 * m + part].wait()
            for d in range(1, 16):
                to_head(m, d, part).wait_recv()
        keep_qkv[m].start()
        keys[...] = qkv_in[m, HEAD : 2 * HEAD, :].T
        for step in range(length // block):
            j = lax.rem(step + lax.div(p.ctx * width, block), length // block)
            cols = pl.ds(pl.multiple_of(j * block, block), block)
            scores = dot(keys[...], qkv_in[m, 0:HEAD, cols]) * (SCALE * LOG2E)
            top = jnp.max(scores, axis=0, keepdims=True)
            exps = jnp.exp2(scores - top)
            total = jnp.sum(exps, axis=0, keepdims=True)
            out = dot(qkv_in[m, 2 * HEAD :, :], exps.astype(BF)) / total
            full_ref[m, :, cols] = out
            lse_ref[m, :, cols] = top + jnp.log2(total)
            low[m, :, cols] = out.astype(BF)
            for i in range(block // width):
                c = j * (block // width) + i
                pl.when(p.ctx != c)(lambda m=m, c=c: to_owner(m, c).start())
        keep_full[m].start()
        att[pl.ds(pl.multiple_of(p.ctx * HEAD, HEAD), HEAD), m * width : (m + 1) * width] = low[
            m, :, pl.ds(pl.multiple_of(p.ctx * width, width), width)
        ]
        if m == 0:
            for t in range(2):
                crossing[t].wait_recv()
                twins[t].start()

    for m in range(micro):
        for d in range(1, 16):
            c = ring_peer(p, d)
            push(
                low.at[m, :, 0:width],
                att.at[pl.ds(pl.multiple_of(c * HEAD, HEAD), HEAD), m * width : (m + 1) * width],
                back_s.at[m, 0], back_r.at[m, c], {"ctx": c},
            ).wait_recv()
            for part in range(3):
                to_head(m, d, part).wait_send()
        for c in range(16):
            pl.when(p.ctx != c)(lambda m=m, c=c: to_owner(m, c).wait_send())
    crossing[2].wait_recv()
    for copy in crossing:
        copy.wait_send()
    for copy in twins + placing + keep_qkv + keep_full:
        copy.wait()


def heads(qkv_t, up_w, out_w, cot, micro, block):
    dma = pltpu.SemaphoreType.DMA
    vmem = pl.BlockSpec(memory_space=pltpu.VMEM)
    anywhere = pl.BlockSpec(memory_space=pltpu.HBM)
    rows = qkv_t.shape[1]
    length = rows // micro * 16
    model = out_w.shape[1]
    columns = up_w.shape[1] // 2
    qkv_in, att, full, lse, up_all, out_all, cot_all = pl.pallas_call(
        functools.partial(heads_kernel, block),
        out_shape=[
            jax.ShapeDtypeStruct((micro, 3 * HEAD, length), BF),
            jax.ShapeDtypeStruct((model, rows), BF),
            jax.ShapeDtypeStruct((micro, HEAD, length), F32),
            jax.ShapeDtypeStruct((micro, 1, length), F32),
            jax.ShapeDtypeStruct((2, up_w.shape[0], columns), BF),
            jax.ShapeDtypeStruct((2,) + out_w.shape, BF),
            jax.ShapeDtypeStruct((2,) + cot.shape, BF),
        ],
        in_specs=[vmem, anywhere, anywhere, anywhere],
        out_specs=[anywhere, vmem, anywhere, vmem, anywhere, anywhere, anywhere],
        scratch_shapes=[
            pltpu.VMEM((micro, 3 * HEAD, length), BF),
            pltpu.VMEM((micro, HEAD, length), F32),
            dma((2, micro)),
            pltpu.VMEM((length, HEAD), BF),
            pltpu.VMEM((micro, HEAD, length), BF),
            pltpu.VMEM((up_w.shape[0], columns), BF),
            pltpu.VMEM(out_w.shape, BF),
            pltpu.VMEM(cot.shape, BF),
            dma((micro, 3)),
            dma((micro, 16, 3)),
            dma((micro, 16, 3)),
            dma((micro, 16)),
            dma((micro, 16)),
            dma((3,)),
            dma((3,)),
            dma((3,)),
            dma((3,)),
            dma((2,)),
            dma((2,)),
        ],
        compiler_params=pltpu.CompilerParams(
            collective_id=2, has_side_effects=True, vmem_limit_bytes=48 << 20
        ),
        name="heads",
    )(qkv_t, up_w, out_w, cot)
    return (
        qkv_in, att, full, lse,
        up_all.reshape(-1, columns), out_all.reshape(-1, model), cot_all.reshape(-1, model),
    )


def mid_kernel(
    att, tokens, scale_two, g_two, w_out, w_up, w_down, cot,
    out_part, out_other, grad_t, grad_mid, grad_scale, gain_two, up_term, down_term, out_term,
    middle, hat, scales, rows_two, hidden, grad_pre, far, far_grad, near_grad,
    go_s, go_r, back_s, back_r,
):
    p = Place()
    rows, model = tokens.shape
    half = rows // 2
    barrier = pltpu.get_barrier_semaphore()
    pl.semaphore_signal(barrier, inc=1, device_id=p.pair, device_id_type=MESH)

    def to_pair(m):
        part = slice(m * half, (m + 1) * half)
        there = slice(rows + m * half, rows + (m + 1) * half)
        return push(rows_two.at[part], rows_two.at[there], go_s.at[m], go_r.at[m], p.pair)

    def to_owner(m):
        part = slice(m * half, (m + 1) * half)
        return push(far.at[part], far_grad.at[part], back_s.at[m], back_r.at[m], p.pair)

    weight = g_two[...] * scale_two[...]
    for m in range(2):
        part = slice(m * half, (m + 1) * half)
        middle[part] = tokens[part].astype(F32) + dot(att[:, part], w_out[...], 0, 0)
        normal, scale = normed(middle[part])
        hat[part] = normal
        scales[part] = scale
        rows_two[part] = (normal * weight[part]).astype(BF)
        if m == 0:
            pl.semaphore_wait(barrier, 1)
        to_pair(m).start()

    def feed(part):
        pre = dot(rows_two[part], w_up[...])
        cdf = 0.5 * (1.0 + lax.erf(pre * (2.0**-0.5)))
        hidden[part] = (pre * cdf).astype(BF)
        density = jnp.exp(-0.5 * pre * pre) * (1.0 / math.sqrt(2.0 * math.pi))
        grad_pre[part] = (dot(cot[part], w_down[...], 1, 1) * (cdf + pre * density)).astype(BF)

    feed(slice(0, rows))
    for m in range(2):
        to_pair(m).wait_recv()
        there = slice(rows + m * half, rows + (m + 1) * half)
        feed(there)
        far[m * half : (m + 1) * half] = dot(grad_pre[there], w_up[...], 1, 1).astype(BF)
        to_owner(m).start()
    near_grad[...] = dot(grad_pre[0:rows], w_up[...], 1, 1)
    wide = 512
    for k in range(up_term.shape[1] // wide):
        part = slice(k * wide, (k + 1) * wide)
        up_term[:, part] = dot(rows_two[...], grad_pre[:, part], 0, 0).astype(BF)
    for k in range(down_term.shape[0] // wide):
        part = slice(k * wide, (k + 1) * wide)
        down_term[part, :] = dot(hidden[:, part], cot[...], 0, 0).astype(BF)
    out_part[...] = middle[...] + dot(hidden[0:rows], w_down[...])
    out_other[...] = dot(hidden[rows:], w_down[...]).astype(BF)

    for m in range(2):
        to_owner(m).wait_recv()
    grad = near_grad[...] + far_grad[...].astype(F32)
    mid = cot[0:rows].astype(F32) + norm_back(grad, hat[...], scales[...], weight)
    grad_mid[...] = mid
    low = mid.astype(BF)
    grad_t[...] = dot(w_out[...], low, 1, 1).astype(BF)
    eh = grad * hat[...]
    grad_scale[...] = (eh * g_two[...]).astype(BF)
    gain_two[...] = jnp.sum(eh * scale_two[...], axis=0, keepdims=True)
    out_term[...] = dot(att[...], low).astype(BF)
    for m in range(2):
        to_pair(m).wait_send()
        to_owner(m).wait_send()


def mid_pass(att, tokens, scale_two, g_two, w_out, w_up, w_down, cot):
    dma = pltpu.SemaphoreType.DMA
    vmem = pl.BlockSpec(memory_space=pltpu.VMEM)
    rows, model = tokens.shape
    hidden = w_up.shape[1]
    shape = jax.ShapeDtypeStruct
    return pl.pallas_call(
        mid_kernel,
        out_shape=[
            shape((rows, model), F32), shape((rows, model), BF), shape((model, rows), BF),
            shape((rows, model), F32), shape((rows, model), BF), shape((1, model), F32),
            shape((model, hidden), BF), shape((hidden, model), BF), shape((model, model), BF),
        ],
        in_specs=[vmem] * 8,
        out_specs=[vmem] * 9,
        scratch_shapes=[
            pltpu.VMEM((rows, model), F32),
            pltpu.VMEM((rows, model), F32),
            pltpu.VMEM((rows, 1), F32),
            pltpu.VMEM((2 * rows, model), BF),
            pltpu.VMEM((2 * rows, hidden), BF),
            pltpu.VMEM((2 * rows, hidden), BF),
            pltpu.VMEM((rows, model), BF),
            pltpu.VMEM((rows, model), BF),
            pltpu.VMEM((rows, model), F32),
            dma((2,)), dma((2,)), dma((2,)), dma((2,)),
        ],
        compiler_params=pltpu.CompilerParams(
            collective_id=5, has_side_effects=True, vmem_limit_bytes=60 << 20
        ),
        name="mid_pass",
    )(att, tokens, scale_two, g_two, w_out, w_up, w_down, cot)


ORDER = (3, 0, 2, 1)


def back_kernel(
    block, grad_t, qkv_in, full_ref, lse_ref, up_term, down_term, out_term, w_qkv,
    cosine, sine, tokens, levels_row, g_one, scale_one, grad_mid, grad_scale_two, gain_two,
    out_part, out_other, input_grad, layer_out, up_all, down_all, out_all, qkv_all, small_all,
    keys, values, g_in, dq, dq_low, dkv_low, delta, grad_qkv, w_hold, grad_norm_t,
    term, q_twin, q_pair, up_sum, down_sum, out_sum, out_pair, out_own, qkv_sum, small, small_in, small_pair, out_came, norm_t, hat, rs_one,
    own_s, in_s, in_r, back_s, back_r, w_s, q_ts, q_tr, q_ps, q_pr, cross_s, cross_r, local_s,
    small_s, small_r, small_x, spread_s, spread_r, *more,
):
    p = Place()
    micro, _, length = qkv_in.shape
    width = length // 16
    model = grad_t.shape[0]
    count = 3
    cut = 2 * count + 3
    halves = Halves(
        p, [lambda c: up_term.at[:, c], lambda c: down_term.at[c], lambda c: out_term.at[:, c]], more[:cut]
    )
    more = more[cut:]
    cut = 2 * count + 6
    f_line = Line(p, count, halves.mine, more[:cut])
    more = more[cut:]
    q_line = Line(p, 1, lambda t, z, y: term.at[p.wt, p.index(z, y, p.core)], more[:8])
    half = down_term.shape[1] // 2
    depth = term.shape[2]
    split = depth // 2
    g = Gather(
        p,
        [
            lambda c: up_all.at[p.wt, c],
            lambda c: up_all.at[1 - p.wt, c],
            lambda c: down_all.at[c, 0:half],
            lambda c: down_all.at[c, half:],
            lambda c: out_all.at[c],
            lambda c: qkv_all.at[c, 0:split],
            lambda c: qkv_all.at[c, split:],
        ],
        more[8:],
    )
    fixed, late = (2, 3, 0, 4, 1), (5, 6)
    p.greet(everyone=True)

    def rows_of(part, c):
        return pl.ds(pl.multiple_of(part * model + c * HEAD, HEAD), HEAD)

    def lanes(c):
        return pl.ds(pl.multiple_of(c * width, width), width)

    def to_head(m, d):
        c = ring_peer(p, d)
        return push(
            grad_t.at[rows_of(0, c), m * width : (m + 1) * width],
            g_in.at[m, :, lanes(p.ctx)], in_s.at[m, d], in_r.at[m, d], {"ctx": c},
        )

    stay = [
        pltpu.make_async_copy(
            grad_t.at[rows_of(0, p.ctx), m * width : (m + 1) * width],
            g_in.at[m, :, lanes(p.ctx)], own_s.at[m],
        )
        for m in range(micro)
    ]
    layer_cross = push(out_other, out_came, cross_s.at[2], cross_r.at[2], p.pair)
    layer_cross.start()
    for m in range(micro):
        stay[m].start()
        for d in range(1, 16):
            to_head(m, d).start()
        halves.begin(ORDER[m])
    for z in ORDER[micro:]:
        halves.begin(z)
    chunk = w_hold.shape[1]
    chunks = model // chunk

    normal, rs_one[...] = normed(tokens[...].astype(F32))
    hat[...] = normal
    norm_t[...] = (normal * (g_one[...] * scale_one[...])).T.astype(BF)

    def w_chunk(k):
        return pltpu.make_async_copy(w_qkv.at[k * chunk : (k + 1) * chunk], w_hold.at[k % 2], w_s.at[k % 2])

    w_chunk(0).start()
    w_chunk(1).start()
    for z in (3, 0):
        halves.halve(z)
        f_line.cross(z)

    def to_owner(m, c, part):
        source = dq_low.at[m] if part == 0 else dkv_low.at[m, part - 1]
        return push(
            source.at[:, lanes(c)],
            grad_qkv.at[rows_of(part, p.ctx), m * width : (m + 1) * width],
            back_s.at[m, c, part], back_r.at[m, p.ctx, part], {"ctx": c},
        )

    def send(m, c, part):
        pl.when(p.ctx != c)(lambda: to_owner(m, c, part).start())

    for m in range(micro):
        keys[...] = qkv_in[m, HEAD : 2 * HEAD, :].T
        values[...] = qkv_in[m, 2 * HEAD :, :].T
        stay[m].wait()
        for d in range(1, 16):
            to_head(m, d).wait_recv()
        delta[...] = jnp.sum(g_in[m].astype(F32) * full_ref[m], axis=0, keepdims=True)
        for step in range(length // block):
            j = lax.rem(step + lax.div(p.ctx * width, block), length // block)
            cols = pl.ds(pl.multiple_of(j * block, block), block)
            scores = dot(keys[cols, :], qkv_in[m, 0:HEAD, :]) * (SCALE * LOG2E)
            soft = jnp.exp2(scores - lse_ref[m])
            grad_soft = dot(values[cols, :], g_in[m])
            raw = (soft * (grad_soft - delta[...]) * SCALE).astype(BF)
            dkv_low[m, 0, :, cols] = dot(qkv_in[m, 0:HEAD, :], raw, 1, 1).astype(BF)
            dkv_low[m, 1, :, cols] = dot(g_in[m], soft.astype(BF), 1, 1).astype(BF)
            part = dot(qkv_in[m, HEAD : 2 * HEAD, cols], raw)
            if step == 0:
                dq[...] = part
            else:
                dq[...] += part
            for i in range(block // width):
                send(m, j * (block // width) + i, 1)
                send(m, j * (block // width) + i, 2)
            if m == micro - 1 and (step + 1) * block * 2 == length:
                f_line.quarter(3)
                f_line.right(3, 0)
        dq_low[m] = dq[...].astype(BF)
        for d in range(1, 16):
            to_owner(m, ring_peer(p, d), 0).start()
        if m == 0:
            halves.halve(2)
            halves.halve(1)
        here = lanes(p.ctx)
        to = slice(m * width, (m + 1) * width)
        grad_qkv[rows_of(0, p.ctx), to] = dq_low[m, :, here]
        grad_qkv[rows_of(1, p.ctx), to] = dkv_low[m, 0, :, here]
        grad_qkv[rows_of(2, p.ctx), to] = dkv_low[m, 1, :, here]

    f_line.cross(2)
    f_line.cross(1)
    layer_cross.wait()
    layer_out[...] = (out_part[...] + out_came[...].astype(F32)).astype(BF)
    f_line.quarter(0)
    f_line.left(0, 3)
    f_line.right(3, 1)
    f_line.left(0, 2)

    for m in range(micro):
        for d in range(1, 16):
            c = ring_peer(p, d)
            for part in range(3):
                push(
                    dq_low.at[m, :, 0:width],
                    grad_qkv.at[rows_of(part, c), m * width : (m + 1) * width],
                    back_s.at[m, 0, part], back_r.at[m, c, part], {"ctx": c},
                ).wait_recv()

    low_half = HEAD // 2
    for r in range(0, 2 * model, HEAD):
        first = grad_qkv[r : r + low_half, :].astype(F32)
        second = grad_qkv[r + low_half : r + HEAD, :].astype(F32)
        grad_qkv[r : r + low_half, :] = (first * cosine[...] + second * sine[...]).astype(BF)
        grad_qkv[r + low_half : r + HEAD, :] = (second * cosine[...] - first * sine[...]).astype(BF)

    group = 4 * depth

    def q_to_twin(w, z, y):
        return push(
            term.at[w, p.index(z, y, 1 - p.core)], q_twin.at[w, z, y], q_ts.at[w, z, y], q_tr.at[w, z, y], p.twin
        )

    def q_to_pair(z, y):
        return push(
            term.at[1 - p.wt, p.index(z, y, p.core)], q_pair.at[z, y], q_ps.at[z, y], q_pr.at[z, y], p.pair
        )

    def with_twin(w, z, y):
        q_to_twin(w, z, y).wait_recv()
        here = p.index(z, y, p.core)
        term[w, here] = (term[w, here].astype(F32) + q_twin[w, z, y].astype(F32)).astype(BF)

    def product(w, z):
        start_row = pl.multiple_of(w * (model // 2) + z * group, group)
        rows = dot(norm_t[pl.ds(start_row, group), :], grad_qkv[...], 1, 1).astype(BF)
        for i in range(4):
            term[w, 4 * z + i] = rows[i * depth : (i + 1) * depth]
        for y in range(2):
            q_to_twin(w, z, y).start()

    for z in ORDER:
        product(1 - p.wt, z)
    f_line.right(3, 2)
    f_line.left(0, 1)
    for z in ORDER:
        for y in range(2):
            with_twin(1 - p.wt, z, y)
            q_to_pair(z, y).start()
    for z in ORDER:
        product(p.wt, z)

    for k in range(chunks):
        w_chunk(k).wait()
        grad_norm_t[k * chunk : (k + 1) * chunk, :] = dot(w_hold[k % 2], grad_qkv[...])
        if k + 2 < chunks:
            w_chunk(k + 2).start()
    grad_norm = grad_norm_t[...].T
    c_rows = grad_norm * (g_one[...] * scale_one[...])
    input_grad[...] = (
        grad_mid[...]
        + (
            c_rows
            - jnp.mean(c_rows, axis=-1, keepdims=True)
            - hat[...] * jnp.mean(c_rows * hat[...], axis=-1, keepdims=True)
        )
        * rs_one[...]
    ).astype(BF)
    eh = grad_norm * hat[...]
    grad_scale_one = (eh * g_one[...]).astype(BF)
    gain_one = jnp.sum(eh * scale_one[...], axis=0, keepdims=True)

    levels = LEVELS
    marks = lax.broadcasted_iota(jnp.int32, (levels, levels_row.shape[1]), 0)
    onehot_t = (marks == levels_row[...]).astype(F32).astype(BF)
    fill = jnp.zeros((small.shape[1] - levels - 1, 128), BF)
    for side, shifts, gain in ((0, grad_scale_one, gain_one), (1, grad_scale_two[...], gain_two[...])):
        level = dot(onehot_t, shifts).astype(BF)
        for k in range(8):
            cols = slice(k * 128, (k + 1) * 128)
            small[8 * side + k, 0:levels, :] = level[:, cols]
            small[8 * side + k, levels:, :] = jnp.concatenate([gain[:, cols].astype(BF), fill])

    def small_to(d):
        peer = ring_peer(p, d)
        return push(small.at[peer], small_in.at[p.ctx], small_s.at[d], small_r.at[d], {"ctx": peer})

    for d in range(1, 16):
        small_to(d).start()
    small_in[p.ctx] = small[p.ctx]
    for z in ORDER:
        for y in range(2):
            with_twin(p.wt, z, y)

    out_cross = push(out_sum.at[1 - p.wt], out_pair, cross_s.at[0], cross_r.at[0], p.pair)
    up_cross = push(up_sum.at[1 - p.wt], up_all.at[p.wt, p.ctx], cross_s.at[1], cross_r.at[1], p.pair)
    up_came = push(up_sum.at[p.wt], up_all.at[1 - p.wt, p.ctx], cross_s.at[1], cross_r.at[1], p.pair)
    sources = {0: up_sum.at[p.wt], 2: down_sum.at[0:half], 3: down_sum.at[half:], 4: out_own,
               5: qkv_sum.at[0:split], 6: qkv_sum.at[split:]}

    def f_end(z):
        @pl.when(p.z == z)
        def _():
            f_line.end(z, [up_sum, down_sum, out_sum])
            out_cross.start()
            up_cross.start()

    def q_cross(z):
        for y in (1 - p.y, p.y):
            q_to_pair(z, y).wait_recv()
            here = p.index(z, y, p.core)
            term[p.wt, here] = (term[p.wt, here].astype(F32) + q_pair[z, y].astype(F32)).astype(BF)
        q_line.cross(z)

    f_line.quarter(2)
    f_line.right(2, 0)
    q_cross(3)
    f_line.right(2, 1)
    f_line.quarter(1)
    f_line.left(1, 3)
    f_line.right(1, 0)
    f_line.left(2, 3)
    q_cross(0)
    q_line.quarter(3)
    q_line.right(3, 0)
    f_line.left(1, 2)
    q_cross(2)
    q_line.quarter(0)
    q_line.left(0, 3)
    q_line.right(3, 1)
    q_line.left(0, 2)
    q_cross(1)
    q_line.right(3, 2)
    q_line.left(0, 1)
    q_line.quarter(2)
    q_line.right(2, 0)
    q_line.quarter(1)
    q_line.left(1, 3)
    q_line.right(1, 0)
    q_line.left(2, 3)
    for z in range(DEPTH):
        f_end(z)
    for d in range(1, 16):
        small_to(d).wait_recv()
    small_pair[0] = jnp.sum(small_in[...].astype(F32), axis=0).astype(BF)
    small_cross = push(small_pair.at[0], small_pair.at[1], small_x.at[0], small_x.at[1], p.pair)
    small_cross.start()
    q_line.right(2, 1)
    q_line.left(1, 2)

    for t in (2, 3, 0):
        g.own(t, sources[t])
    out_cross.wait_recv()
    out_own[...] = (out_sum[p.wt].astype(F32) + out_pair[...].astype(F32)).astype(BF)
    g.own(4, sources[4])
    up_came.wait_recv()
    g.own(1)
    for z in range(DEPTH):
        pl.when(p.z == z)(lambda z=z: q_line.end(z, [qkv_sum]))
    for t in late:
        g.own(t, sources[t])

    small_cross.wait()
    small_all[p.ctx] = (small_pair[0].astype(F32) + small_pair[1].astype(F32)).astype(BF)

    def small_spread(d):
        peer = ring_peer(p, d)
        return push(small_all.at[p.ctx], small_all.at[p.ctx], spread_s.at[d], spread_r.at[d], {"ctx": peer})

    for d in range(1, 16):
        small_spread(d).start()
    copies = [pltpu.make_async_copy(sources[t], g.items[t](p.ctx), local_s.at[t]) for t in sources]
    for copy in copies:
        copy.start()
    every = fixed + late
    for t in every:
        g.along(t, 1)
    for t in every:
        g.along(t, 2)
    for t in every:
        g.crossed_at(t, 0)
    for t in every:
        g.along(t, 3)
    for d in (1, 2, 3):
        for t in every:
            g.crossed_at(t, d)

    for copy in copies:
        copy.wait()
    for t in range(len(g.items)):
        g.finish(t)
    halves.finish()
    f_line.finish()
    q_line.finish()
    out_cross.wait_send()
    up_cross.wait_send()
    for d in range(1, 16):
        small_to(d).wait_send()
        small_spread(d).wait()
    for z in range(DEPTH):
        for y in range(2):
            q_to_pair(z, y).wait_send()
            for w in range(2):
                q_to_twin(w, z, y).wait_send()
    for m in range(micro):
        for d in range(1, 16):
            to_head(m, d).wait_send()
        for c in range(16):
            for part in range(3):
                pl.when(p.ctx != c)(lambda m=m, c=c, part=part: to_owner(m, c, part).wait_send())


def back_pass(grad_t, qkv_in, full, lse, up, down, out, w_qkv, rest, block):
    dma = pltpu.SemaphoreType.DMA
    vmem = pl.BlockSpec(memory_space=pltpu.VMEM)
    anywhere = pl.BlockSpec(memory_space=pltpu.HBM)
    micro, _, length = qkv_in.shape
    model, rows = grad_t.shape
    pieces = [up.shape[:1] + up.shape[2:], down.shape[1:], out.shape[:1] + out.shape[2:]]
    piece = (model // 32, 3 * model)
    small = (16, 80, 128)
    return pl.pallas_call(
        functools.partial(back_kernel, block),
        out_shape=[
            jax.ShapeDtypeStruct((rows, model), BF),
            jax.ShapeDtypeStruct((rows, model), BF),
            jax.ShapeDtypeStruct((2, 16) + up.shape[2:], BF),
            jax.ShapeDtypeStruct(down.shape, BF),
            jax.ShapeDtypeStruct(out.shape[1:], BF),
            jax.ShapeDtypeStruct((16,) + piece, BF),
            jax.ShapeDtypeStruct(small, BF),
        ],
        in_specs=[vmem] * 4 + [anywhere] * 4 + [vmem] * len(rest),
        out_specs=[vmem] * 2 + [anywhere] * 4 + [vmem],
        scratch_shapes=[
            pltpu.VMEM((length, HEAD), BF),
            pltpu.VMEM((length, HEAD), BF),
            pltpu.VMEM((micro, HEAD, length), BF),
            pltpu.VMEM((HEAD, length), F32),
            pltpu.VMEM((micro, HEAD, length), BF),
            pltpu.VMEM((micro, 2, HEAD, length), BF),
            pltpu.VMEM((1, length), F32),
            pltpu.VMEM((3 * model, rows), BF),
            pltpu.VMEM((2, 128, 3 * model), BF),
            pltpu.VMEM((model, rows), F32),
            pltpu.VMEM((2, 16) + piece, BF),
            pltpu.VMEM((2, DEPTH, 2) + piece, BF),
            pltpu.VMEM((DEPTH, 2) + piece, BF),
            pltpu.VMEM(pieces[0], BF),
            pltpu.VMEM(pieces[1], BF),
            pltpu.VMEM(pieces[2], BF),
            pltpu.VMEM(pieces[2][1:], BF),
            pltpu.VMEM(pieces[2][1:], BF),
            pltpu.VMEM(piece, BF),
            pltpu.VMEM(small, BF),
            pltpu.VMEM(small, BF),
            pltpu.VMEM((2,) + small[1:], BF),
            pltpu.VMEM((rows, model), BF),
            pltpu.VMEM((model, rows), BF),
            pltpu.VMEM((rows, model), F32),
            pltpu.VMEM((rows, 1), F32),
            dma((micro,)),
            dma((micro, 16)),
            dma((micro, 16)),
            dma((micro, 16, 3)),
            dma((micro, 16, 3)),
            dma((2,)),
            dma((2, DEPTH, 2)),
            dma((2, DEPTH, 2)),
            dma((DEPTH, 2)),
            dma((DEPTH, 2)),
            dma((3,)),
            dma((3,)),
            dma((7,)),
            dma((16,)),
            dma((16,)),
            dma((2,)),
            dma((16,)),
            dma((16,)),
        ]
        + Halves.scratch(pieces)
        + Line.scratch(pieces)
        + Line.scratch([piece])
        + Gather.semaphores(7),
        compiler_params=pltpu.CompilerParams(
            collective_id=4, has_side_effects=True, vmem_limit_bytes=63 << 20
        ),
        name="back_pass",
    )(grad_t, qkv_in, full, lse, up, down, out, w_qkv, *rest)


def spread(source, pieces, first, target):
    width = source.shape[-1]
    for c in range(pieces):
        target[:, c * width : (c + 1) * width] = source[c, 0, first : first + HEAD, :]


def attend_kernel(pieces, block, qkv_ref, low_ref, full_ref, lse_ref, q_t, k_t, v_t, keys):
    length = q_t.shape[1]
    width = length // pieces
    spread(qkv_ref, pieces, 0, q_t)
    spread(qkv_ref, pieces, HEAD, k_t)
    spread(qkv_ref, pieces, 2 * HEAD, v_t)
    keys[...] = k_t[...].T
    for j in range(length // block):
        cols = slice(j * block, (j + 1) * block)
        scores = dot(keys[...], q_t[:, cols]) * (SCALE * LOG2E)
        top = jnp.max(scores, axis=0, keepdims=True)
        exps = jnp.exp2(scores - top)
        total = jnp.sum(exps, axis=0, keepdims=True)
        out = dot(v_t[...], exps.astype(BF)) / total
        full_ref[0, :, cols] = out
        lse_ref[0, :, cols] = top + jnp.log2(total)
        for c in range(block // width):
            low_ref[j * (block // width) + c, 0] = out[:, c * width : (c + 1) * width].astype(BF)


def attend(qkv, block):
    pieces, pairs, _, width = qkv.shape
    length = pieces * width
    return pl.pallas_call(
        functools.partial(attend_kernel, pieces, block),
        grid=(pairs,),
        in_specs=[pl.BlockSpec((pieces, 1, 3 * HEAD, width), lambda p: (0, p, 0, 0))],
        out_specs=[
            pl.BlockSpec((pieces, 1, HEAD, width), lambda p: (0, p, 0, 0)),
            pl.BlockSpec((1, HEAD, length), lambda p: (p, 0, 0)),
            pl.BlockSpec((1, 1, length), lambda p: (p, 0, 0)),
        ],
        out_shape=[
            jax.ShapeDtypeStruct((pieces, pairs, HEAD, width), BF),
            jax.ShapeDtypeStruct((pairs, HEAD, length), F32),
            jax.ShapeDtypeStruct((pairs, 1, length), F32),
        ],
        scratch_shapes=[pltpu.VMEM((HEAD, length), BF)] * 3 + [pltpu.VMEM((length, HEAD), BF)],
        compiler_params=pltpu.CompilerParams(vmem_limit_bytes=48 << 20),
        name="attend",
    )(qkv)


def attend_back_kernel(
    pieces, block, qkv_ref, grad_ref, full_ref, lse_ref, out_ref,
    q_t, k_t, v_t, g_t, keys, values, dq_t, dk, dv,
):
    length = q_t.shape[1]
    width = length // pieces
    spread(qkv_ref, pieces, 0, q_t)
    spread(qkv_ref, pieces, HEAD, k_t)
    spread(qkv_ref, pieces, 2 * HEAD, v_t)
    spread(grad_ref, pieces, 0, g_t)
    keys[...] = k_t[...].T
    values[...] = v_t[...].T
    for j in range(length // block):
        cols = slice(j * block, (j + 1) * block)
        query = q_t[:, cols]
        grad = g_t[:, cols]
        delta = jnp.sum(grad.astype(F32) * full_ref[0, :, cols], axis=0, keepdims=True)
        scores = dot(keys[...], query) * (SCALE * LOG2E)
        soft = jnp.exp2(scores - lse_ref[0, :, cols])
        term_v = dot(soft.astype(BF), grad, 1, 1)
        grad_soft = dot(values[...], grad)
        raw = (soft * (grad_soft - delta) * SCALE).astype(BF)
        term_k = dot(raw, query, 1, 1)
        dq_t[:, cols] = dot(k_t[...], raw)
        if j == 0:
            dv[...] = term_v
            dk[...] = term_k
        else:
            dv[...] += term_v
            dk[...] += term_k
    dk_t = dk[...].T.astype(BF)
    dv_t = dv[...].T.astype(BF)
    for c in range(pieces):
        piece = slice(c * width, (c + 1) * width)
        out_ref[c, 0, 0:HEAD, :] = dq_t[:, piece].astype(BF)
        out_ref[c, 0, HEAD : 2 * HEAD, :] = dk_t[:, piece]
        out_ref[c, 0, 2 * HEAD :, :] = dv_t[:, piece]


def attend_back(qkv, grad, full, lse, block):
    pieces, pairs, _, width = qkv.shape
    length = pieces * width
    return pl.pallas_call(
        functools.partial(attend_back_kernel, pieces, block),
        grid=(pairs,),
        in_specs=[
            pl.BlockSpec((pieces, 1, 3 * HEAD, width), lambda p: (0, p, 0, 0)),
            pl.BlockSpec((pieces, 1, HEAD, width), lambda p: (0, p, 0, 0)),
            pl.BlockSpec((1, HEAD, length), lambda p: (p, 0, 0)),
            pl.BlockSpec((1, 1, length), lambda p: (p, 0, 0)),
        ],
        out_specs=pl.BlockSpec((pieces, 1, 3 * HEAD, width), lambda p: (0, p, 0, 0)),
        out_shape=jax.ShapeDtypeStruct(qkv.shape, BF),
        scratch_shapes=[pltpu.VMEM((HEAD, length), BF)] * 4
        + [pltpu.VMEM((length, HEAD), BF)] * 2
        + [pltpu.VMEM((HEAD, length), F32)]
        + [pltpu.VMEM((length, HEAD), F32)] * 2,
        compiler_params=pltpu.CompilerParams(vmem_limit_bytes=56 << 20),
        name="attend_back",
    )(qkv, grad, full, lse)


def normed(rows):
    centered = rows - jnp.mean(rows, axis=-1, keepdims=True)
    scale = lax.rsqrt(jnp.mean(centered * centered, axis=-1, keepdims=True) + EPSILON)
    return centered * scale, scale


def norm_back(grad, hat, scale, weight):
    c = grad * weight
    return (
        c - jnp.mean(c, axis=-1, keepdims=True) - hat * jnp.mean(c * hat, axis=-1, keepdims=True)
    ) * scale


def turn(first, second, cosine, sine):
    return first * cosine - second * sine, second * cosine + first * sine


def shards(
    tokens, positions, buckets, qkv_w, out_w, up_w, down_w, time_w, noise_table,
    gain_one, gain_two, cotangent,
):
    n, ring = lax.axis_size("wt"), lax.axis_size("ctx")
    me = lax.axis_index("wt")
    micro, _, width, model = tokens.shape
    rows = micro * width
    pairs = HEADS * micro // ring
    block = 256
    planar = n == 2 and ring == 16

    x = tokens.reshape(rows, model).astype(F32)
    cot_low = cotangent.reshape(rows, model)
    places = positions.reshape(rows)
    levels = buckets.reshape(rows)

    def whole_rows(weight):
        return lax.all_gather(weight, "wt", axis=0, tiled=True)

    stacked = jnp.stack([gain_one, gain_two])
    if planar:
        w_qkv, w_time, table, gains = start(qkv_w, time_w, noise_table, stacked)
    else:
        w_qkv = whole_rows(qkv_w)
        w_out = whole_rows(out_w)
        w_time = whole_rows(time_w)
        table = whole_rows(noise_table)
        gains = lax.all_gather(stacked, "wt", axis=1, tiled=True)
        w_up = lax.all_to_all(up_w, "wt", 1, 0, tiled=True)
    g_one, g_two = gains[0].astype(F32), gains[1].astype(F32)

    onehot = levels[:, None] == jnp.arange(table.shape[0], dtype=jnp.int32)[None, :]
    embed = dot(onehot.astype(BF), table).astype(BF)
    shifts = dot(embed, w_time)
    scale_one = 1.0 + shifts[:, :model]
    scale_two = 1.0 + shifts[:, model:]

    hat_one, rs_one = normed(x)
    weight_one = g_one * scale_one
    norm_one = (hat_one * weight_one).astype(BF)

    qkv_t = dot(w_qkv, norm_one, 0, 1).reshape(3, HEADS, 2, HEAD // 2, rows)
    frequency = jnp.exp(
        jnp.arange(HEAD // 2, dtype=F32) * (-math.log(10000.0) * 2.0 / HEAD)
    )
    angles = frequency[:, None] * places.astype(F32)[None, :]
    cosine, sine = jnp.cos(angles), jnp.sin(angles)
    turned = turn(qkv_t[:2, :, 0], qkv_t[:2, :, 1], cosine, sine)
    queries_keys = jnp.stack(turned, axis=2)
    qkv_low = jnp.concatenate([queries_keys.astype(BF), qkv_t[2:].astype(BF)])

    def to_heads(columns):
        parts = columns.shape[0]
        split = columns.reshape(parts, HEADS, HEAD, micro, width)
        split = jnp.transpose(split, (1, 3, 0, 2, 4))
        split = split.reshape(ring, pairs, parts * HEAD, width)
        return lax.all_to_all(split, "ctx", 0, 0, tiled=True)

    def to_tokens(pieces):
        parts = pieces.shape[2] // HEAD
        back = lax.all_to_all(pieces, "ctx", 0, 0, tiled=True)
        back = back.reshape(HEADS, micro, parts, HEAD, width)
        return jnp.transpose(back, (2, 0, 3, 1, 4)).reshape(parts, HEADS * HEAD, rows)

    if planar:
        qkv_heads, attended, full, lse, w_up, w_out, cot = heads(
            qkv_low.reshape(3 * model, rows), up_w, out_w, cot_low, micro, block
        )
    else:
        qkv_heads = to_heads(qkv_low.reshape(3, HEADS, HEAD, rows))
        low, full, lse = attend(qkv_heads, block)
        attended = to_tokens(low)[0]
        cot = gather_slots(cot_low).reshape(n * rows, model)

    if not planar:
        middle = x + dot(attended, w_out, 0, 0)
        hat_two, rs_two = normed(middle)
        weight_two = g_two * scale_two
        norm_two_own = (hat_two * weight_two).astype(BF)

        norm_two = gather_slots(norm_two_own).reshape(n * rows, model)
        pre = dot(norm_two, w_up)
        phi_cdf = 0.5 * (1.0 + lax.erf(pre * (2.0**-0.5)))
        hidden = (pre * phi_cdf).astype(BF)
        out_parts = dot(hidden, down_w).reshape(n, rows, model)

        grad_hidden = dot(cot, down_w, 1, 1)
        density = jnp.exp(-0.5 * pre * pre) * (1.0 / math.sqrt(2.0 * math.pi))
        grad_pre = (grad_hidden * (phi_cdf + pre * density)).astype(BF)
        grad_norm_two = sum_slots(dot(grad_pre, w_up, 1, 1).reshape(n, rows, model))
        down_term = dot(hidden, cot, 0, 0).astype(BF)
        up_term = dot(norm_two, grad_pre, 0, 0).astype(BF)
        grad_mid = cot_low.astype(F32) + norm_back(grad_norm_two, hat_two, rs_two, weight_two)
        grad_branch = grad_mid.astype(BF)
        eh_two = grad_norm_two * hat_two
        grad_scale_two = eh_two * g_two
        gain_two_term = jnp.sum(eh_two * scale_two, axis=0)
        out_term = dot(attended, grad_branch, 1, 0).astype(BF)
        grad_attn = dot(w_out, grad_branch, 1, 1).astype(BF)

    if planar:

        def pieces_of(array, *lead):
            return array.reshape(lead + (-1, array.shape[-1]))

        (
            out_part, out_other, grad_attn, grad_mid, grad_scale_two, gain_two_term, up_term, down_term, out_term,
        ) = mid_pass(attended, tokens.reshape(rows, model), scale_two, g_two[None], w_out, w_up, down_w, cot)
        rest = (
            cosine, sine, tokens.reshape(rows, model), levels[None], g_one[None], scale_one, grad_mid,
            grad_scale_two, gain_two_term, out_part, out_other,
        )
        input_grad, layer_out, up_all, down_all, out_all, qkv_all, small_all = back_pass(
            grad_attn, qkv_heads, full, lse, pieces_of(up_term, n, ring), pieces_of(down_term, ring),
            pieces_of(out_term, n, ring), w_qkv, rest, block,
        )
        time_here = time_w.shape[0]
        table_rows = lax.dynamic_slice_in_dim(table, me * time_here, time_here, 1)
        up_grad, down_grad, out_grad, qkv_grad, time_grad, table_grad, gain_sums = widen(
            up_all, down_all, out_all, qkv_all, small_all, table_rows, w_time
        )
        gain_sums = gain_sums[0]
    else:
        layer_out = middle + sum_slots(out_parts)
        up_share = lax.psum_scatter(
            up_term.reshape(n, model // n, -1), "ctx", scatter_dimension=1, tiled=True
        )
        down_share = lax.psum_scatter(down_term, "ctx", scatter_dimension=0, tiled=True)
        out_share = lax.psum_scatter(
            out_term.reshape(n, model // n, model), "ctx", scatter_dimension=1, tiled=True
        )
        grad_heads = to_heads(grad_attn.reshape(1, HEADS, HEAD, rows))
        back = to_tokens(attend_back(qkv_heads, grad_heads, full, lse, block))
        back = back.reshape(3, HEADS, 2, HEAD // 2, rows)
        unturned = turn(back[:2, :, 0].astype(F32), back[:2, :, 1].astype(F32), cosine, -sine)
        grad_qkv = jnp.concatenate([jnp.stack(unturned, axis=2).astype(BF), back[2:]])
        grad_qkv = grad_qkv.reshape(3 * model, rows)
        qkv_term = dot(norm_one, grad_qkv, 0, 1).astype(BF)
        grad_norm_one = dot(grad_qkv, w_qkv, 0, 1)

        input_grad = grad_mid + norm_back(grad_norm_one, hat_one, rs_one, weight_one)
        eh_one = grad_norm_one * hat_one
        grad_scale_one = eh_one * g_one
        gain_one_term = jnp.sum(eh_one * scale_one, axis=0)

        grad_shifts = jnp.concatenate([grad_scale_one, grad_scale_two], axis=1).astype(BF)
        level_term = dot(onehot.astype(BF), grad_shifts, 0, 0)
        gain_terms = jnp.concatenate([gain_one_term, gain_two_term])
        small = lax.psum(jnp.concatenate([level_term, gain_terms[None]]), ("ctx", "wt"))
        share = lax.psum_scatter(
            qkv_term.reshape(n, model // n, -1), "ctx", scatter_dimension=1, tiled=True
        )

        def spread_rows(share):
            return lax.all_gather(share, "ctx", axis=0, tiled=True).astype(F32)

        up_share = lax.all_to_all(up_share, "wt", 0, 0, tiled=True)
        up_grad = lax.all_gather(up_share, "ctx", axis=1, tiled=True).astype(F32)
        up_grad = jnp.transpose(up_grad, (1, 0, 2)).reshape(model // n, -1)
        down_grad = spread_rows(down_share)
        out_grad = spread_rows(sum_owned(out_share))
        qkv_grad = spread_rows(sum_owned(share))

        by_level = small[: table.shape[0]]
        gain_sums = small[table.shape[0]]
        levels_here, time_here = noise_table.shape[0], time_w.shape[0]
        high = lax.Precision.HIGHEST
        time_rows = lax.dynamic_slice_in_dim(table, me * time_here, time_here, 1).astype(F32)
        time_grad = lax.dot_general(
            time_rows, by_level, (((0,), (0,)), ((), ())), precision=high, preferred_element_type=F32
        )
        level_rows = lax.dynamic_slice_in_dim(by_level, me * levels_here, levels_here, 0)
        table_grad = lax.dot_general(
            level_rows, w_time.astype(F32), (((1,), (1,)), ((), ())), precision=high,
            preferred_element_type=F32,
        )

    gain_here = gain_one.shape[0]
    gain_one_grad = lax.dynamic_slice_in_dim(gain_sums, me * gain_here, gain_here, 0)
    gain_two_grad = lax.dynamic_slice_in_dim(gain_sums, model + me * gain_here, gain_here, 0)

    return (
        layer_out.astype(BF).reshape(tokens.shape),
        input_grad.astype(BF).reshape(tokens.shape),
        qkv_grad,
        out_grad,
        up_grad,
        down_grad,
        time_grad,
        table_grad,
        gain_one_grad,
        gain_two_grad,
    )


def sum_owned(share):
    n, me = lax.axis_size("wt"), lax.axis_index("wt")
    slots = jnp.stack(
        [lax.dynamic_index_in_dim(share, lax.rem(me + k, n), 0, keepdims=False) for k in range(n)]
    )
    return sum_slots(slots.astype(F32)).astype(BF)


def solution(mesh):
    rows = P(None, "wt", "ctx", None)
    marks = P(None, "wt", "ctx")
    weight = P("wt", None)
    gain = P("wt")
    return jax.shard_map(
        shards,
        mesh=mesh,
        in_specs=(rows, marks, marks) + (weight,) * 6 + (gain, gain, rows),
        out_specs=(rows, rows) + (weight,) * 6 + (gain, gain),
        check_vma=False,
    )
```

```python
import functools
import math

import jax
import jax.numpy as jnp
from jax import lax
from jax.experimental import pallas as pl
from jax.experimental.pallas import tpu as pltpu
from jax.sharding import PartitionSpec as P

HEADS = 16
HEAD = 64
LEVELS = 64
EPSILON = 1e-05
SCALE = 0.125
LOG2E = math.log2(math.e)
BF = jnp.bfloat16
F32 = jnp.float32


def dot(a, b, ca=1, cb=0):
    return lax.dot_general(a, b, (((ca,), (cb,)), ((), ())), preferred_element_type=F32)


def swap_ring(value, places):
    n = lax.axis_size("wt")
    return lax.ppermute(value, "wt", [((i + places) % n, i) for i in range(n)])


def gather_slots(own):
    n = lax.axis_size("wt")
    return jnp.stack([own] + [swap_ring(own, k) for k in range(1, n)])


def sum_slots(partial):
    n = lax.axis_size("wt")
    total = partial[0]
    for k in range(1, n):
        total = total + swap_ring(partial[k].astype(BF), n - k).astype(F32)
    return total


MESH = pl.DeviceIdType.MESH
DEPTH = 4


class Place:
    def __init__(self):
        self.ctx = lax.axis_index("ctx")
        self.wt = lax.axis_index("wt")
        self.z = lax.div(self.ctx, 4)
        self.y = lax.rem(lax.div(self.ctx, 2), 2)
        self.core = lax.rem(self.ctx, 2)
        self.right = {"ctx": self.index(lax.min(self.z + 1, DEPTH - 1), self.y, self.core)}
        self.left = {"ctx": self.index(lax.max(self.z - 1, 0), self.y, self.core)}
        self.across = {"ctx": self.index(self.z, 1 - self.y, self.core)}
        self.twin = {"ctx": self.index(self.z, self.y, 1 - self.core)}
        self.pair = {"wt": 1 - self.wt}

    @staticmethod
    def index(z, y, core):
        return (z * 2 + y) * 2 + core

    def greet(self, everyone=False, pair=True):
        barrier = pltpu.get_barrier_semaphore()

        def signal(device):
            pl.semaphore_signal(barrier, inc=1, device_id=device, device_id_type=MESH)

        if everyone:

            @pl.loop(1, 16)
            def _(d):
                signal({"ctx": lax.rem(self.ctx + d, 16)})

            count = 15
        else:
            signal(self.across)
            signal(self.twin)
            pl.when(self.z > 0)(lambda: signal(self.left))
            pl.when(self.z < DEPTH - 1)(lambda: signal(self.right))
            inner = jnp.logical_and(self.z > 0, self.z < DEPTH - 1).astype(jnp.int32)
            count = 3 + inner
        if pair:
            signal(self.pair)
            count = count + 1
        pl.semaphore_wait(barrier, count)


def push(source, target, send, receive, device):
    return pltpu.make_async_remote_copy(
        src_ref=source, dst_ref=target, send_sem=send, recv_sem=receive,
        device_id=device, device_id_type=MESH,
    )


class Gather:
    def __init__(self, place, items, sems, wide=()):
        self.p, self.items, self.wide = place, items, wide
        (self.sl, self.sr, self.sy, self.sc, self.rz, self.ry, self.rc) = sems

    @staticmethod
    def semaphores(count):
        dma = pltpu.SemaphoreType.DMA
        line, square = dma((count, DEPTH)), dma((count, DEPTH, 2))
        return [square, square, line, square, square, line, square]

    def piece(self, t, z, y, core):
        return self.items[t](self.p.index(z, y, core))

    def copy(self, t, z, y, source, send, receive, device):
        here = self.piece(t, z, y, self.p.core)
        return push(here if source is None else source, here, send, receive, device)

    def rightward(self, t, z, source=None, far=0):
        y = 1 - self.p.y if far else self.p.y
        return self.copy(t, z, y, source, self.sr.at[t, z, far], self.rz.at[t, z, far], self.p.right)

    def leftward(self, t, z, source=None, far=0):
        y = 1 - self.p.y if far else self.p.y
        return self.copy(t, z, y, source, self.sl.at[t, z, far], self.rz.at[t, z, far], self.p.left)

    def crossing(self, t, z, source=None):
        return self.copy(t, z, self.p.y, source, self.sy.at[t, z], self.ry.at[t, z], self.p.across)

    def twinning(self, t, z, y, source=None):
        return self.copy(t, z, y, source, self.sc.at[t, z, y], self.rc.at[t, z, y], self.p.twin)

    def own(self, t, source=None):
        p = self.p
        pl.when(p.z < DEPTH - 1)(lambda: self.rightward(t, p.z, source).start())
        pl.when(p.z > 0)(lambda: self.leftward(t, p.z, source).start())
        self.crossing(t, p.z, source).start()
        self.twinning(t, p.z, p.y, source).start()

    def arrived(self, t, z, y, core, semaphore):
        piece = self.piece(t, z, y, core)
        push(piece, piece, semaphore, semaphore, self.p.twin).wait_recv()

    def arrive(self, t, z, far=0):
        p = self.p
        y = 1 - p.y if far else p.y
        self.arrived(t, z, y, p.core, self.rz.at[t, z, far])
        pl.when(jnp.logical_and(p.z > z, p.z < DEPTH - 1))(lambda: self.rightward(t, z, far=far).start())
        pl.when(jnp.logical_and(p.z < z, p.z > 0))(lambda: self.leftward(t, z, far=far).start())
        if t not in self.wide:
            self.crossing(t, z).start()
        self.twinning(t, z, y).start()

    def along(self, t, d):
        p = self.p
        for far in (0, 1) if t in self.wide else (0,):
            pl.when(p.z - d >= 0)(lambda far=far: self.arrive(t, p.z - d, far))
            pl.when(p.z + d < DEPTH)(lambda far=far: self.arrive(t, p.z + d, far))

    def crossed(self, t, z):
        self.arrived(t, z, 1 - self.p.y, self.p.core, self.ry.at[t, z])
        self.twinning(t, z, 1 - self.p.y).start()

    def crossed_at(self, t, d):
        p = self.p
        if t in self.wide:
            if d == 0:
                self.arrived(t, p.z, 1 - p.y, p.core, self.ry.at[t, p.z])
                pl.when(p.z < DEPTH - 1)(lambda: self.rightward(t, p.z, far=1).start())
                pl.when(p.z > 0)(lambda: self.leftward(t, p.z, far=1).start())
                self.twinning(t, p.z, 1 - p.y).start()
        elif d == 0:
            self.crossed(t, p.z)
        else:
            pl.when(p.z - d >= 0)(lambda: self.crossed(t, p.z - d))
            pl.when(p.z + d < DEPTH)(lambda: self.crossed(t, p.z + d))

    def finish(self, t):
        p = self.p
        wide = t in self.wide
        if wide:
            self.crossing(t, p.z).wait_send()
        for z in range(DEPTH):
            if not wide:
                self.crossing(t, z).wait_send()
            for y in range(2):
                self.twinning(t, z, y).wait_send()
                self.arrived(t, z, y, 1 - p.core, self.rc.at[t, z, y])
            for far in (0, 1) if wide else (0,):
                pl.when(jnp.logical_and(p.z >= z, p.z < DEPTH - 1))(
                    lambda z=z, far=far: self.rightward(t, z, far=far).wait_send()
                )
                pl.when(jnp.logical_and(p.z <= z, p.z > 0))(
                    lambda z=z, far=far: self.leftward(t, z, far=far).wait_send()
                )


class Line:
    def __init__(self, place, count, mine, refs):
        self.p, self.mine, self.terms = place, mine, range(count)
        self.from_across, self.slots = refs[:count], refs[count : 2 * count]
        self.ys, self.yr, self.rs, self.rr, self.vs, self.vr = refs[2 * count :]

    @staticmethod
    def scratch(shapes):
        line = pltpu.SemaphoreType.DMA((len(shapes), DEPTH))
        return (
            [pltpu.VMEM((DEPTH,) + shape, BF) for shape in shapes]
            + [pltpu.VMEM((DEPTH + 1,) + shape, BF) for shape in shapes]
            + [line] * 6
        )

    def across(self, t, z):
        return push(
            self.mine(t, z, 1 - self.p.y), self.from_across[t].at[z], self.ys.at[t, z], self.yr.at[t, z], self.p.across
        )

    def rightward(self, t, j, first):
        target = self.slots[t].at[j + 1]
        return push(self.from_across[t].at[j] if first else target, target, self.rs.at[t, j], self.rr.at[t, j], self.p.right)

    def leftward(self, t, j, first):
        target = self.slots[t].at[j]
        return push(self.from_across[t].at[j] if first else target, target, self.vs.at[t, j], self.vr.at[t, j], self.p.left)

    def cross(self, z):
        for t in self.terms:
            self.across(t, z).start()

    def quarter(self, z):
        for t in self.terms:
            self.across(t, z).wait_recv()
            both = self.mine(t, z, self.p.y)[...].astype(F32) + self.from_across[t][z].astype(F32)
            self.from_across[t][z] = both.astype(BF)

    def with_left(self, t, j):
        self.rightward(t, j, False).wait_recv()
        return self.from_across[t][j].astype(F32) + self.slots[t][j + 1].astype(F32)

    def with_right(self, t, j):
        self.leftward(t, j, False).wait_recv()
        return self.from_across[t][j].astype(F32) + self.slots[t][j].astype(F32)

    def right(self, j, z):
        @pl.when(self.p.z == z)
        def _():
            for t in self.terms:
                if z > 0:
                    self.slots[t][j + 1] = self.with_left(t, j).astype(BF)
                self.rightward(t, j, z == 0).start()

    def left(self, j, z):
        @pl.when(self.p.z == z)
        def _():
            for t in self.terms:
                if z < DEPTH - 1:
                    self.slots[t][j] = self.with_right(t, j).astype(BF)
                self.leftward(t, j, z == DEPTH - 1).start()

    def end(self, z, results):
        for t in self.terms:
            if z == 0:
                total = self.with_right(t, z)
            else:
                total = self.with_left(t, z)
                if z < DEPTH - 1:
                    self.leftward(t, z, False).wait_recv()
                    total = total + self.slots[t][z].astype(F32)
            results[t][...] = total.astype(BF)

    def finish(self):
        p = self.p
        for t in self.terms:
            for z in range(DEPTH):
                self.across(t, z).wait_send()
                pl.when(p.z < z)(lambda t=t, z=z: self.rightward(t, z, False).wait_send())
                pl.when(p.z > z)(lambda t=t, z=z: self.leftward(t, z, False).wait_send())


class Halves:
    def __init__(self, place, sources, refs):
        count = len(sources)
        self.p, self.sources, self.terms = place, sources, range(count)
        self.kept, self.from_twin = refs[:count], refs[count : 2 * count]
        self.ls, self.ts, self.tr = refs[2 * count :]

    @staticmethod
    def scratch(shapes):
        square = pltpu.SemaphoreType.DMA((len(shapes), DEPTH, 2))
        return [pltpu.VMEM((DEPTH, 2) + shape, BF) for shape in shapes] * 2 + [square] * 3

    def mine(self, t, z, y):
        return self.kept[t].at[z, y]

    def load(self, t, z, y):
        source = self.sources[t](self.p.index(z, y, self.p.core))
        return pltpu.make_async_copy(source, self.kept[t].at[z, y], self.ls.at[t, z, y])

    def twin(self, t, z, y):
        source = self.sources[t](self.p.index(z, y, 1 - self.p.core))
        return push(source, self.from_twin[t].at[z, y], self.ts.at[t, z, y], self.tr.at[t, z, y], self.p.twin)

    def begin(self, z):
        for y in (1 - self.p.y, self.p.y):
            for t in self.terms:
                self.load(t, z, y).start()
                self.twin(t, z, y).start()

    def halve(self, z):
        for y in (1 - self.p.y, self.p.y):
            for t in self.terms:
                self.load(t, z, y).wait()
                self.twin(t, z, y).wait_recv()
                both = self.kept[t][z, y].astype(F32) + self.from_twin[t][z, y].astype(F32)
                self.kept[t][z, y] = both.astype(BF)

    def finish(self):
        for t in self.terms:
            for z in range(DEPTH):
                for y in range(2):
                    self.twin(t, z, y).wait_send()


def widen_kernel(
    up_ref, down_ref, out_ref, qkv_ref, small_ref, rows_ref, time_ref, grad_ref, layer_ref,
    up_to, down_to, out_to, qkv_to, time_to, table_to, gain_one_to, gain_two_to, grad_to, layer_to,
):
    grad_to[...] = grad_ref[...]
    layer_to[...] = layer_ref[...]
    columns = up_ref.shape[-1]
    levels, here = rows_ref.shape[0], table_to.shape[0]
    me, step = lax.axis_index("wt"), pl.program_id(0)
    mine = pl.ds(pl.multiple_of(me * here, here), here)
    table = None
    gains = []
    for i in range(up_ref.shape[1]):
        rows = slice(i * up_ref.shape[2], (i + 1) * up_ref.shape[2])
        up_to[rows, :columns] = up_ref[0, i].astype(F32)
        up_to[rows, columns:] = up_ref[1, i].astype(F32)
        for source, target in ((down_ref, down_to), (out_ref, out_to), (qkv_ref, qkv_to)):
            depth = source.shape[1]
            target[i * depth : (i + 1) * depth, :] = source[i].astype(F32)
        cols = slice(i * 128, (i + 1) * 128)
        time_to[:, cols] = dot(rows_ref[...], small_ref[i, 0:levels, :], 0, 0)
        gains.append(small_ref[i, levels : levels + 1, :].astype(F32))
        part = dot(small_ref[i, mine, :], time_ref[:, cols], 1, 1)
        table = part if table is None else table + part
    gain = jnp.concatenate(gains, axis=1)
    wide = gain.shape[1]
    count = gain_one_to.shape[1] // wide
    place = pl.ds(pl.multiple_of(lax.rem(step, count) * wide, wide), wide)

    @pl.when(lax.div(step, count) == me)
    def _():
        gain_one_to[:, place] = gain

    @pl.when(lax.div(step, count) == me + 2)
    def _():
        gain_two_to[:, place] = gain

    first = step == 0

    @pl.when(first)
    def _():
        table_to[...] = table

    @pl.when(jnp.logical_not(first))
    def _():
        table_to[...] += table


def widen(up, down, out, qkv, small, table_rows, w_time, grad, layer, step=2):
    _, ring, up_rows, up_columns = up.shape
    wide = small.shape[2]

    def piece(a):
        return pl.BlockSpec((step,) + a.shape[1:], lambda i: (i, 0, 0))

    def row_block(a):
        return pl.BlockSpec((step * a.shape[1], a.shape[2]), lambda i: (i, 0))

    def whole(a):
        return jax.ShapeDtypeStruct((ring * a.shape[1], a.shape[2]), F32)

    def columns(rows):
        return pl.BlockSpec((rows, step * wide), lambda i: (0, i))

    def share(a):
        return pl.BlockSpec((a.shape[0] * step // ring, a.shape[1]), lambda i: (i, 0))

    time_rows, depth = table_rows.shape[1], w_time.shape[0]
    gain = pl.BlockSpec((1, ring * wide // 4), lambda i: (0, 0))
    return pl.pallas_call(
        widen_kernel,
        grid=(ring // step,),
        in_specs=[
            pl.BlockSpec((2, step, up_rows, up_columns), lambda i: (0, i, 0, 0)),
            piece(down), piece(out), piece(qkv), piece(small),
            pl.BlockSpec(table_rows.shape, lambda i: (0, 0)), columns(depth), share(grad), share(layer),
        ],
        out_specs=[
            pl.BlockSpec((step * up_rows, 2 * up_columns), lambda i: (i, 0)),
            row_block(down), row_block(out), row_block(qkv),
            columns(time_rows), pl.BlockSpec((table_rows.shape[0] // 2, depth), lambda i: (0, 0)),
            gain, gain, share(grad), share(layer),
        ],
        out_shape=[
            jax.ShapeDtypeStruct((ring * up_rows, 2 * up_columns), F32),
            whole(down), whole(out), whole(qkv),
            jax.ShapeDtypeStruct((time_rows, ring * wide), F32),
            jax.ShapeDtypeStruct((table_rows.shape[0] // 2, depth), F32),
            jax.ShapeDtypeStruct((1, ring * wide // 4), F32),
            jax.ShapeDtypeStruct((1, ring * wide // 4), F32),
            jax.ShapeDtypeStruct(grad.shape, BF),
            jax.ShapeDtypeStruct(layer.shape, BF),
        ],
        compiler_params=pltpu.CompilerParams(vmem_limit_bytes=62 << 20),
        name="widen",
    )(up, down, out, qkv, small, table_rows, w_time, grad, layer)


def start_kernel(
    qkv_own, time_own, table_own, gain_own, tokens, levels, cosine, sine,
    qkv_all, time_all, table_all, gain_all, qkv_t, scale_one, scale_two,
    hold_qkv, hold_time, far_qkv, far_time, normal, embed, low, total,
    local_in, local_out, cross_s, cross_r, *gather_sems,
):
    p = Place()
    other = 1 - p.wt
    split = far_qkv.shape[1] // 2
    deep = far_time.shape[1]
    model = tokens.shape[1]
    items = [
        lambda c: far_time.at[c],
        lambda c: far_qkv.at[c, 0:split],
        lambda c: far_qkv.at[c, split:],
    ]
    g = Gather(p, items, gather_sems)
    into = [pltpu.make_async_copy(qkv_own, hold_qkv, local_in.at[0]),
            pltpu.make_async_copy(time_own, hold_time, local_in.at[1])]
    for copy in into:
        copy.start()
    p.greet()
    c = p.ctx
    sent = [
        push(time_own.at[pl.ds(deep * c, deep)], far_time.at[c], cross_s.at[0], cross_r.at[0], p.pair),
        push(qkv_own.at[pl.ds(2 * split * c, split)], far_qkv.at[c, 0:split], cross_s.at[1], cross_r.at[1], p.pair),
        push(qkv_own.at[pl.ds(2 * split * c + split, split)], far_qkv.at[c, split:], cross_s.at[2], cross_r.at[2], p.pair),
        push(table_own, table_all.at[p.wt], cross_s.at[3], cross_r.at[3], p.pair),
        push(gain_own, gain_all.at[p.wt], cross_s.at[4], cross_r.at[4], p.pair),
    ]
    for copy in sent[3:] + sent[:3]:
        copy.start()
    table_all[p.wt] = table_own[...]
    gain_all[p.wt] = gain_own[...]
    normal[...] = normed(tokens[...].astype(F32))[0]
    every = range(len(items))
    for t in every:
        sent[t].wait_recv()
        g.own(t)
    for copy in into:
        copy.wait()
    out = [pltpu.make_async_copy(hold_time, time_all.at[p.wt], local_out.at[0]),
           pltpu.make_async_copy(hold_qkv, qkv_all.at[p.wt], local_out.at[1])]
    for copy in out:
        copy.start()
    for copy in sent[3:]:
        copy.wait_recv()
    kinds = 2 * table_own.shape[0]
    onehot = (lax.broadcasted_iota(jnp.int32, (tokens.shape[0], kinds), 1) == levels[...]).astype(F32).astype(BF)
    embed[...] = dot(onehot, jnp.concatenate([table_all[0], table_all[1]])).astype(BF)
    for t in every:
        g.along(t, 1)
    for t in every:
        g.along(t, 2)
    for t in every:
        g.crossed_at(t, 0)
    for t in every:
        g.along(t, 3)
    for d in (1, 2, 3):
        g.crossed_at(0, d)
    g.finish(0)
    more = [pltpu.make_async_copy(far_time, time_all.at[other].reshape(far_time.shape), local_out.at[2])]
    more[0].start()

    depth = hold_time.shape[0]

    def columns(w, size):
        return pl.ds(pl.multiple_of(w * size, size), size)

    far_rows = jnp.concatenate([far_time[k] for k in range(16)])
    shifts = dot(embed[:, columns(p.wt, depth)], hold_time[...]) + dot(embed[:, columns(other, depth)], far_rows)
    scale_one[...] = 1.0 + shifts[:, :model]
    scale_two[...] = 1.0 + shifts[:, model:]
    gain_one = jnp.concatenate([gain_all[0, 0:1], gain_all[1, 0:1]], axis=1).astype(F32)
    low[...] = (normal[...] * (gain_one * scale_one[...])).astype(BF)
    half = hold_qkv.shape[0]
    total[...] = dot(low[:, columns(p.wt, half)], hold_qkv[...])
    for d in (1, 2, 3):
        for t in (1, 2):
            g.crossed_at(t, d)
    for t in (1, 2):
        g.finish(t)
    more.append(pltpu.make_async_copy(far_qkv, qkv_all.at[other].reshape(far_qkv.shape), local_out.at[3]))
    more[1].start()
    far = low[:, columns(other, half)]
    quarter = HEAD // 2
    wide = 4 * HEAD

    @pl.loop(0, 3 * model // wide)
    def _(k):
        cols = pl.ds(pl.multiple_of(k * wide, wide), wide)
        weights = far_qkv[:, :, cols].reshape(half, wide)
        part = (total[:, cols] + dot(far, weights)).T

        @pl.when(k < 2 * model // wide)
        def _():
            for h in range(4):
                first = part[h * HEAD : h * HEAD + quarter]
                second = part[h * HEAD + quarter : (h + 1) * HEAD]
                row = pl.multiple_of(k * wide + h * HEAD, HEAD)
                qkv_t[pl.ds(row, quarter), :] = (first * cosine[...] - second * sine[...]).astype(BF)
                row = pl.multiple_of(k * wide + h * HEAD + quarter, quarter)
                qkv_t[pl.ds(row, quarter), :] = (second * cosine[...] + first * sine[...]).astype(BF)

        @pl.when(k >= 2 * model // wide)
        def _():
            qkv_t[cols, :] = part.astype(BF)

    for copy in out + more:
        copy.wait()
    for copy in sent:
        copy.wait_send()


def start(qkv_w, time_w, table, gains, tokens, levels, cosine, sine):
    dma = pltpu.SemaphoreType.DMA
    vmem = pl.BlockSpec(memory_space=pltpu.VMEM)
    anywhere = pl.BlockSpec(memory_space=pltpu.HBM)
    shape = jax.ShapeDtypeStruct
    rows, model = tokens.shape
    far_qkv = (16, qkv_w.shape[0] // 16, qkv_w.shape[1])
    far_time = (16, time_w.shape[0] // 16, time_w.shape[1])
    qkv_all, time_all, table_all, gain_all, qkv_t, scale_one, scale_two = pl.pallas_call(
        start_kernel,
        out_shape=[
            shape((2,) + qkv_w.shape, BF),
            shape((2,) + time_w.shape, BF),
            shape((2,) + table.shape, BF),
            shape((2,) + gains.shape, BF),
            shape((qkv_w.shape[1], rows), BF),
            shape((rows, model), F32),
            shape((rows, model), F32),
        ],
        in_specs=[anywhere, anywhere] + [vmem] * 6,
        out_specs=[anywhere, anywhere] + [vmem] * 5,
        scratch_shapes=[
            pltpu.VMEM(qkv_w.shape, BF), pltpu.VMEM(time_w.shape, BF),
            pltpu.VMEM(far_qkv, BF), pltpu.VMEM(far_time, BF),
            pltpu.VMEM((rows, model), F32), pltpu.VMEM((rows, table.shape[1]), BF),
            pltpu.VMEM((rows, model), BF), pltpu.VMEM((rows, qkv_w.shape[1]), F32),
            dma((2,)), dma((4,)), dma((5,)), dma((5,)),
        ] + Gather.semaphores(3),
        compiler_params=pltpu.CompilerParams(
            collective_id=1, has_side_effects=True, vmem_limit_bytes=63 << 20
        ),
        name="start",
    )(qkv_w, time_w, table, gains, tokens, levels, cosine, sine)
    return (
        qkv_all.reshape(-1, qkv_w.shape[1]),
        time_all.reshape(-1, time_w.shape[1]),
        table_all.reshape(-1, table.shape[1]),
        jnp.transpose(gain_all, (1, 0, 2)).reshape(gains.shape[0], -1),
        qkv_t, scale_one, scale_two,
    )


def ring_peer(p, d):
    return lax.rem(p.ctx + d, 16)


def heads_kernel(
    block, qkv_t, up_w, out_w, cot,
    qkv_keep, att, full_keep, lse_ref, up_all, out_all, cot_all,
    qkv_in, full_ref, keep_s, keys, low, hold_up, hold_out, hold_cot, own_s, in_s, in_r, back_s, back_r, hold_in, hold_to,
    cross_s, cross_r, twin_s, twin_r,
):
    p = Place()
    micro, _, length = qkv_in.shape
    width = length // 16
    model = att.shape[0]
    half_up, half_out = up_w.shape[0] // 2, out_w.shape[0] // 2
    columns = up_all.shape[2]
    other = 1 - p.wt
    mine = pl.ds(pl.multiple_of(p.wt * columns, columns), columns)
    theirs = pl.ds(pl.multiple_of(other * columns, columns), columns)
    holds = [
        pltpu.make_async_copy(up_w.at[:, mine], hold_up, hold_in.at[0]),
        pltpu.make_async_copy(out_w, hold_out, hold_in.at[1]),
        pltpu.make_async_copy(cot, hold_cot, hold_in.at[2]),
    ]
    for copy in holds:
        copy.start()
    p.greet(everyone=True)

    def piece(part, c):
        return pl.ds(pl.multiple_of(part * model + c * HEAD, HEAD), HEAD)

    def lanes(c):
        return pl.ds(pl.multiple_of(c * width, width), width)

    def to_head(m, d, part):
        c = ring_peer(p, d)
        return push(
            qkv_t.at[piece(part, c), m * width : (m + 1) * width],
            qkv_in.at[m, part * HEAD : (part + 1) * HEAD, lanes(p.ctx)],
            in_s.at[m, d, part], in_r.at[m, d, part], {"ctx": c},
        )

    stay = [
        pltpu.make_async_copy(
            qkv_t.at[piece(part, p.ctx), m * width : (m + 1) * width],
            qkv_in.at[m, part * HEAD : (part + 1) * HEAD, lanes(p.ctx)],
            own_s.at[m, part],
        )
        for m in range(micro) for part in range(3)
    ]
    rows_up = pl.ds(pl.multiple_of(p.core * half_up, half_up), half_up)
    rows_out = pl.ds(pl.multiple_of(p.core * half_out, half_out), half_out)
    crossing = [
        push(out_w.at[rows_out], out_all.at[p.wt, rows_out], cross_s.at[0], cross_r.at[0], p.pair),
        push(up_w.at[rows_up, theirs], up_all.at[p.wt, rows_up], cross_s.at[1], cross_r.at[1], p.pair),
        push(cot, cot_all.at[1], cross_s.at[2], cross_r.at[2], p.pair),
    ]
    twins = [
        push(out_all.at[other, rows_out], out_all.at[other, rows_out], twin_s.at[0], twin_r.at[0], p.twin),
        push(up_all.at[other, rows_up], up_all.at[other, rows_up], twin_s.at[1], twin_r.at[1], p.twin),
    ]
    for copy in stay:
        copy.start()
    for m in range(micro):

        @pl.loop(1, 16)
        def _(d, m=m):
            for part in range(3):
                to_head(m, d, part).start()

        if m == 0:
            for copy in crossing:
                copy.start()
    for copy in holds:
        copy.wait()
    placing = [
        pltpu.make_async_copy(hold_up, up_all.at[p.wt], hold_to.at[0]),
        pltpu.make_async_copy(hold_out, out_all.at[p.wt], hold_to.at[1]),
        pltpu.make_async_copy(hold_cot, cot_all.at[0], hold_to.at[2]),
    ]
    for copy in placing:
        copy.start()

    def to_owner(m, c):
        return push(
            low.at[m, :, lanes(c)],
            att.at[pl.ds(pl.multiple_of(p.ctx * HEAD, HEAD), HEAD), m * width : (m + 1) * width],
            back_s.at[m, c], back_r.at[m, p.ctx], {"ctx": c},
        )

    keep_qkv = [pltpu.make_async_copy(qkv_in.at[m], qkv_keep.at[m], keep_s.at[0, m]) for m in range(micro)]
    keep_full = [pltpu.make_async_copy(full_ref.at[m], full_keep.at[m], keep_s.at[1, m]) for m in range(micro)]
    for m in range(micro):
        for part in range(3):
            stay[3 * m + part].wait()

        @pl.loop(1, 16)
        def _(d, m=m):
            for part in range(3):
                to_head(m, d, part).wait_recv()

        keep_qkv[m].start()
        keys[...] = qkv_in[m, HEAD : 2 * HEAD, :].T
        @pl.loop(0, length // block)
        def _(step, m=m):
            j = lax.rem(step + lax.div(p.ctx * width, block), length // block)
            cols = pl.ds(pl.multiple_of(j * block, block), block)
            scores = dot(keys[...], qkv_in[m, 0:HEAD, cols]) * (SCALE * LOG2E)
            top = jnp.max(scores, axis=0, keepdims=True)
            exps = jnp.exp2(scores - top)
            total = jnp.sum(exps, axis=0, keepdims=True)
            out = dot(qkv_in[m, 2 * HEAD :, :], exps.astype(BF)) / total
            full_ref[m, :, cols] = out
            lse_ref[m, :, cols] = top + jnp.log2(total)
            low[m, :, cols] = out.astype(BF)
            for i in range(block // width):
                c = j * (block // width) + i
                pl.when(p.ctx != c)(lambda c=c: to_owner(m, c).start())

        keep_full[m].start()
        att[pl.ds(pl.multiple_of(p.ctx * HEAD, HEAD), HEAD), m * width : (m + 1) * width] = low[
            m, :, pl.ds(pl.multiple_of(p.ctx * width, width), width)
        ]
        if m == 0:
            for t in range(2):
                crossing[t].wait_recv()
                twins[t].start()

    for m in range(micro):

        @pl.loop(1, 16)
        def _(d, m=m):
            c = ring_peer(p, d)
            push(
                low.at[m, :, 0:width],
                att.at[pl.ds(pl.multiple_of(c * HEAD, HEAD), HEAD), m * width : (m + 1) * width],
                back_s.at[m, 0], back_r.at[m, c], {"ctx": c},
            ).wait_recv()
            for part in range(3):
                to_head(m, d, part).wait_send()
            to_owner(m, c).wait_send()

    crossing[2].wait_recv()
    for copy in crossing:
        copy.wait_send()
    for copy in twins + placing + keep_qkv + keep_full:
        copy.wait()


def heads(qkv_t, up_w, out_w, cot, micro, block):
    dma = pltpu.SemaphoreType.DMA
    vmem = pl.BlockSpec(memory_space=pltpu.VMEM)
    anywhere = pl.BlockSpec(memory_space=pltpu.HBM)
    rows = qkv_t.shape[1]
    length = rows // micro * 16
    model = out_w.shape[1]
    columns = up_w.shape[1] // 2
    qkv_in, att, full, lse, up_all, out_all, cot_all = pl.pallas_call(
        functools.partial(heads_kernel, block),
        out_shape=[
            jax.ShapeDtypeStruct((micro, 3 * HEAD, length), BF),
            jax.ShapeDtypeStruct((model, rows), BF),
            jax.ShapeDtypeStruct((micro, HEAD, length), F32),
            jax.ShapeDtypeStruct((micro, 1, length), F32),
            jax.ShapeDtypeStruct((2, up_w.shape[0], columns), BF),
            jax.ShapeDtypeStruct((2,) + out_w.shape, BF),
            jax.ShapeDtypeStruct((2,) + cot.shape, BF),
        ],
        in_specs=[vmem, anywhere, anywhere, anywhere],
        out_specs=[anywhere, vmem, anywhere, vmem, anywhere, anywhere, anywhere],
        scratch_shapes=[
            pltpu.VMEM((micro, 3 * HEAD, length), BF),
            pltpu.VMEM((micro, HEAD, length), F32),
            dma((2, micro)),
            pltpu.VMEM((length, HEAD), BF),
            pltpu.VMEM((micro, HEAD, length), BF),
            pltpu.VMEM((up_w.shape[0], columns), BF),
            pltpu.VMEM(out_w.shape, BF),
            pltpu.VMEM(cot.shape, BF),
            dma((micro, 3)),
            dma((micro, 16, 3)),
            dma((micro, 16, 3)),
            dma((micro, 16)),
            dma((micro, 16)),
            dma((3,)),
            dma((3,)),
            dma((3,)),
            dma((3,)),
            dma((2,)),
            dma((2,)),
        ],
        compiler_params=pltpu.CompilerParams(
            collective_id=2, has_side_effects=True, vmem_limit_bytes=48 << 20
        ),
        name="heads",
    )(qkv_t, up_w, out_w, cot)
    return (
        qkv_in, att, full, lse,
        up_all.reshape(-1, columns), out_all.reshape(-1, model), cot_all.reshape(-1, model),
    )


def mid_kernel(
    att, tokens, scale_two, g_two, w_out, w_up, w_down, cot,
    out_part, out_other, grad_t, grad_mid, grad_scale, gain_two, up_term, down_term, out_term,
    middle, hat, scales, rows_two, hidden, grad_pre, far, far_grad, near_grad,
    go_s, go_r, back_s, back_r,
):
    p = Place()
    rows, model = tokens.shape
    half = rows // 2
    barrier = pltpu.get_barrier_semaphore()
    pl.semaphore_signal(barrier, inc=1, device_id=p.pair, device_id_type=MESH)

    def to_pair(m):
        part = pl.ds(pl.multiple_of(m * half, half), half)
        there = pl.ds(pl.multiple_of(rows + m * half, half), half)
        return push(rows_two.at[part], rows_two.at[there], go_s.at[m], go_r.at[m], p.pair)

    def to_owner(m):
        part = pl.ds(pl.multiple_of(m * half, half), half)
        return push(far.at[part], far_grad.at[part], back_s.at[m], back_r.at[m], p.pair)

    weight = g_two[...] * scale_two[...]
    for m in range(2):
        part = slice(m * half, (m + 1) * half)
        middle[part] = tokens[part].astype(F32) + dot(att[:, part], w_out[...], 0, 0)
        normal, scale = normed(middle[part])
        hat[part] = normal
        scales[part] = scale
        rows_two[part] = (normal * weight[part]).astype(BF)
        if m == 0:
            pl.semaphore_wait(barrier, 1)
        to_pair(m).start()

    wide = 512

    def chunk(k):
        return pl.ds(pl.multiple_of(k * wide, wide), wide)

    def feed(part):
        @pl.loop(0, w_up.shape[1] // wide)
        def _(k):
            cols = chunk(k)
            pre = dot(rows_two[part], w_up[:, cols])
            cdf = 0.5 * (1.0 + lax.erf(pre * (2.0**-0.5)))
            hidden[part, cols] = (pre * cdf).astype(BF)
            density = jnp.exp(-0.5 * pre * pre) * (1.0 / math.sqrt(2.0 * math.pi))
            grad_pre[part, cols] = (dot(cot[part], w_down[cols, :], 1, 1) * (cdf + pre * density)).astype(BF)

    feed(slice(0, rows))

    @pl.loop(0, 2)
    def _(m):
        to_pair(m).wait_recv()
        there = pl.ds(pl.multiple_of(rows + m * half, half), half)
        feed(there)
        far[pl.ds(pl.multiple_of(m * half, half), half)] = dot(grad_pre[there], w_up[...], 1, 1).astype(BF)
        to_owner(m).start()

    @pl.loop(0, model // wide)
    def _(k):
        cols = chunk(k)
        near_grad[:, cols] = dot(grad_pre[0:rows], w_up[cols, :], 1, 1)

    @pl.loop(0, up_term.shape[1] // wide)
    def _(k):
        cols = chunk(k)
        up_term[:, cols] = dot(rows_two[...], grad_pre[:, cols], 0, 0).astype(BF)
        down_term[cols, :] = dot(hidden[:, cols], cot[...], 0, 0).astype(BF)

    @pl.loop(0, model // wide)
    def _(k):
        cols = chunk(k)
        both = dot(hidden[...], w_down[:, cols])
        out_part[:, cols] = middle[:, cols] + both[:rows]
        out_other[:, cols] = both[rows:].astype(BF)


    for m in range(2):
        to_owner(m).wait_recv()
    grad = near_grad[...] + far_grad[...].astype(F32)
    mid = cot[0:rows].astype(F32) + norm_back(grad, hat[...], scales[...], weight)
    grad_mid[...] = mid
    low = mid.astype(BF)
    grad_t[...] = dot(w_out[...], low, 1, 1).astype(BF)
    eh = grad * hat[...]
    grad_scale[...] = (eh * g_two[...]).astype(BF)
    gain_two[...] = jnp.sum(eh * scale_two[...], axis=0, keepdims=True)
    out_term[...] = dot(att[...], low).astype(BF)
    for m in range(2):
        to_pair(m).wait_send()
        to_owner(m).wait_send()


def mid_pass(att, tokens, scale_two, g_two, w_out, w_up, w_down, cot):
    dma = pltpu.SemaphoreType.DMA
    vmem = pl.BlockSpec(memory_space=pltpu.VMEM)
    rows, model = tokens.shape
    hidden = w_up.shape[1]
    shape = jax.ShapeDtypeStruct
    return pl.pallas_call(
        mid_kernel,
        out_shape=[
            shape((rows, model), F32), shape((rows, model), BF), shape((model, rows), BF),
            shape((rows, model), F32), shape((rows, model), BF), shape((1, model), F32),
            shape((model, hidden), BF), shape((hidden, model), BF), shape((model, model), BF),
        ],
        in_specs=[vmem] * 8,
        out_specs=[vmem] * 9,
        scratch_shapes=[
            pltpu.VMEM((rows, model), F32),
            pltpu.VMEM((rows, model), F32),
            pltpu.VMEM((rows, 1), F32),
            pltpu.VMEM((2 * rows, model), BF),
            pltpu.VMEM((2 * rows, hidden), BF),
            pltpu.VMEM((2 * rows, hidden), BF),
            pltpu.VMEM((rows, model), BF),
            pltpu.VMEM((rows, model), BF),
            pltpu.VMEM((rows, model), F32),
            dma((2,)), dma((2,)), dma((2,)), dma((2,)),
        ],
        compiler_params=pltpu.CompilerParams(
            collective_id=5, has_side_effects=True, vmem_limit_bytes=60 << 20
        ),
        name="mid_pass",
    )(att, tokens, scale_two, g_two, w_out, w_up, w_down, cot)


ORDER = (3, 0, 2, 1)


def back_kernel(
    block, grad_t, qkv_in, full_ref, lse_ref, up_term, down_term, out_term, w_qkv,
    cosine, sine, tokens, levels_row, g_one, scale_one, grad_mid, grad_scale_two, gain_two,
    out_part, out_other, input_grad, layer_out, up_all, down_all, out_all, qkv_all, small_all,
    keys, values, g_in, dq, dq_low, dkv_low, delta, grad_qkv, w_hold, grad_norm_t,
    term, q_twin, q_pair, up_sum, down_sum, out_sum, out_pair, out_own, qkv_sum, small, small_in, small_pair, out_came, norm_t, hat, rs_one,
    own_s, in_s, in_r, back_s, back_r, w_s, q_ts, q_tr, q_ps, q_pr, cross_s, cross_r, local_s,
    small_s, small_r, small_x, spread_s, spread_r, *more,
):
    p = Place()
    micro, _, length = qkv_in.shape
    width = length // 16
    model = grad_t.shape[0]
    count = 3
    cut = 2 * count + 3
    halves = Halves(
        p, [lambda c: up_term.at[:, c], lambda c: down_term.at[c], lambda c: out_term.at[:, c]], more[:cut]
    )
    more = more[cut:]
    cut = 2 * count + 6
    f_line = Line(p, count, halves.mine, more[:cut])
    more = more[cut:]
    q_line = Line(p, 1, lambda t, z, y: term.at[p.wt, p.index(z, y, p.core)], more[:8])
    half = down_term.shape[1] // 2
    depth = term.shape[2]
    split = depth // 2
    g = Gather(
        p,
        [
            lambda c: up_all.at[p.wt, c],
            lambda c: up_all.at[1 - p.wt, c],
            lambda c: down_all.at[c, 0:half],
            lambda c: down_all.at[c, half:],
            lambda c: out_all.at[c],
            lambda c: qkv_all.at[c, 0:split],
            lambda c: qkv_all.at[c, split:],
        ],
        more[8:],
        wide=(),
    )
    fixed, late = (3, 2, 0, 4, 1), (5, 6)
    p.greet(everyone=True)

    def rows_of(part, c):
        return pl.ds(pl.multiple_of(part * model + c * HEAD, HEAD), HEAD)

    def lanes(c):
        return pl.ds(pl.multiple_of(c * width, width), width)

    def to_head(m, d):
        c = ring_peer(p, d)
        return push(
            grad_t.at[rows_of(0, c), m * width : (m + 1) * width],
            g_in.at[m, :, lanes(p.ctx)], in_s.at[m, d], in_r.at[m, d], {"ctx": c},
        )

    stay = [
        pltpu.make_async_copy(
            grad_t.at[rows_of(0, p.ctx), m * width : (m + 1) * width],
            g_in.at[m, :, lanes(p.ctx)], own_s.at[m],
        )
        for m in range(micro)
    ]
    layer_cross = push(out_other, out_came, cross_s.at[2], cross_r.at[2], p.pair)
    layer_cross.start()
    for m in range(micro):
        stay[m].start()

        @pl.loop(1, 16)
        def _(d, m=m):
            to_head(m, d).start()

        halves.begin(ORDER[m])
    for z in ORDER[micro:]:
        halves.begin(z)
    chunk = w_hold.shape[1]
    chunks = model // chunk

    normal, rs_one[...] = normed(tokens[...].astype(F32))
    hat[...] = normal
    norm_t[...] = (normal * (g_one[...] * scale_one[...])).T.astype(BF)

    def w_chunk(k):
        slot = lax.rem(k, 2)
        return pltpu.make_async_copy(
            w_qkv.at[pl.ds(pl.multiple_of(k * chunk, chunk), chunk)], w_hold.at[slot], w_s.at[slot]
        )

    w_chunk(jnp.int32(0)).start()
    w_chunk(jnp.int32(1)).start()
    for z in (3, 0):
        halves.halve(z)
        f_line.cross(z)

    def to_owner(m, c, part):
        source = dq_low.at[m] if part == 0 else dkv_low.at[m, part - 1]
        return push(
            source.at[:, lanes(c)],
            grad_qkv.at[rows_of(part, p.ctx), m * width : (m + 1) * width],
            back_s.at[m, c, part], back_r.at[m, p.ctx, part], {"ctx": c},
        )

    def send(m, c, part):
        pl.when(p.ctx != c)(lambda: to_owner(m, c, part).start())

    for m in range(micro):
        keys[...] = qkv_in[m, HEAD : 2 * HEAD, :].T
        values[...] = qkv_in[m, 2 * HEAD :, :].T
        stay[m].wait()

        @pl.loop(1, 16)
        def _(d, m=m):
            to_head(m, d).wait_recv()

        delta[...] = jnp.sum(g_in[m].astype(F32) * full_ref[m], axis=0, keepdims=True)
        dq[...] = jnp.zeros_like(dq)

        @pl.loop(0, length // block)
        def _(step, m=m):
            j = lax.rem(step + lax.div(p.ctx * width, block), length // block)
            cols = pl.ds(pl.multiple_of(j * block, block), block)
            scores = dot(keys[cols, :], qkv_in[m, 0:HEAD, :]) * (SCALE * LOG2E)
            soft = jnp.exp2(scores - lse_ref[m])
            grad_soft = dot(values[cols, :], g_in[m])
            raw = (soft * (grad_soft - delta[...]) * SCALE).astype(BF)
            dkv_low[m, 0, :, cols] = dot(qkv_in[m, 0:HEAD, :], raw, 1, 1).astype(BF)
            dkv_low[m, 1, :, cols] = dot(g_in[m], soft.astype(BF), 1, 1).astype(BF)
            dq[...] += dot(qkv_in[m, HEAD : 2 * HEAD, cols], raw)
            for i in range(block // width):
                send(m, j * (block // width) + i, 1)
                send(m, j * (block // width) + i, 2)
            if m == micro - 1:

                @pl.when((step + 1) * block * 2 == length)
                def _():
                    f_line.quarter(3)
                    f_line.right(3, 0)

        dq_low[m] = dq[...].astype(BF)

        @pl.loop(1, 16)
        def _(d, m=m):
            to_owner(m, ring_peer(p, d), 0).start()

        if m == 0:
            halves.halve(2)
            halves.halve(1)
        here = lanes(p.ctx)
        to = slice(m * width, (m + 1) * width)
        grad_qkv[rows_of(0, p.ctx), to] = dq_low[m, :, here]
        grad_qkv[rows_of(1, p.ctx), to] = dkv_low[m, 0, :, here]
        grad_qkv[rows_of(2, p.ctx), to] = dkv_low[m, 1, :, here]

    f_line.cross(2)
    f_line.cross(1)
    layer_cross.wait()
    layer_out[...] = (out_part[...] + out_came[...].astype(F32)).astype(BF)
    f_line.quarter(0)
    f_line.left(0, 3)
    f_line.right(3, 1)
    f_line.left(0, 2)

    for m in range(micro):

        @pl.loop(1, 16)
        def _(d, m=m):
            c = ring_peer(p, d)
            for part in range(3):
                push(
                    dq_low.at[m, :, 0:width],
                    grad_qkv.at[rows_of(part, c), m * width : (m + 1) * width],
                    back_s.at[m, 0, part], back_r.at[m, c, part], {"ctx": c},
                ).wait_recv()

    low_half = HEAD // 2

    @pl.loop(0, 2 * model // HEAD)
    def _(h):
        upper = pl.ds(pl.multiple_of(h * HEAD, HEAD), low_half)
        lower = pl.ds(pl.multiple_of(h * HEAD + low_half, low_half), low_half)
        first, second = grad_qkv[upper, :].astype(F32), grad_qkv[lower, :].astype(F32)
        grad_qkv[upper, :] = (first * cosine[...] + second * sine[...]).astype(BF)
        grad_qkv[lower, :] = (second * cosine[...] - first * sine[...]).astype(BF)


    group = 4 * depth

    def q_to_twin(w, z, y):
        return push(
            term.at[w, p.index(z, y, 1 - p.core)], q_twin.at[w, z, y], q_ts.at[w, z, y], q_tr.at[w, z, y], p.twin
        )

    def q_to_pair(z, y):
        return push(
            term.at[1 - p.wt, p.index(z, y, p.core)], q_pair.at[z, y], q_ps.at[z, y], q_pr.at[z, y], p.pair
        )

    def with_twin(w, z, y):
        q_to_twin(w, z, y).wait_recv()
        here = p.index(z, y, p.core)
        term[w, here] = (term[w, here].astype(F32) + q_twin[w, z, y].astype(F32)).astype(BF)

    def product(w, z):
        start_row = pl.multiple_of(w * (model // 2) + z * group, group)
        rows = dot(norm_t[pl.ds(start_row, group), :], grad_qkv[...], 1, 1).astype(BF)
        for i in range(4):
            term[w, 4 * z + i] = rows[i * depth : (i + 1) * depth]
        for y in range(2):
            q_to_twin(w, z, y).start()

    def by_order(step):
        odd = lax.rem(step, 2)
        return (1 - odd) * (DEPTH - 1 - lax.div(step, 2)) + odd * lax.div(step, 2)

    @pl.loop(0, DEPTH)
    def _(step):
        product(1 - p.wt, by_order(step))

    f_line.right(3, 2)
    f_line.left(0, 1)

    @pl.loop(0, 2 * DEPTH)
    def _(step):
        z, y = by_order(lax.div(step, 2)), lax.rem(step, 2)
        with_twin(1 - p.wt, z, y)
        q_to_pair(z, y).start()

    @pl.loop(0, DEPTH)
    def _(step):
        product(p.wt, by_order(step))


    @pl.loop(0, chunks)
    def _(k):
        w_chunk(k).wait()
        grad_norm_t[pl.ds(pl.multiple_of(k * chunk, chunk), chunk), :] = dot(w_hold[lax.rem(k, 2)], grad_qkv[...])
        pl.when(k + 2 < chunks)(lambda: w_chunk(k + 2).start())

    grad_norm = grad_norm_t[...].T
    c_rows = grad_norm * (g_one[...] * scale_one[...])
    input_grad[...] = (
        grad_mid[...]
        + (
            c_rows
            - jnp.mean(c_rows, axis=-1, keepdims=True)
            - hat[...] * jnp.mean(c_rows * hat[...], axis=-1, keepdims=True)
        )
        * rs_one[...]
    ).astype(BF)
    eh = grad_norm * hat[...]
    grad_scale_one = (eh * g_one[...]).astype(BF)
    gain_one = jnp.sum(eh * scale_one[...], axis=0, keepdims=True)

    levels = LEVELS
    marks = lax.broadcasted_iota(jnp.int32, (levels, levels_row.shape[1]), 0)
    onehot_t = (marks == levels_row[...]).astype(F32).astype(BF)
    fill = jnp.zeros((small.shape[1] - levels - 1, 128), BF)
    for side, shifts, gain in ((0, grad_scale_one, gain_one), (1, grad_scale_two[...], gain_two[...])):
        level = dot(onehot_t, shifts).astype(BF)
        for k in range(8):
            cols = slice(k * 128, (k + 1) * 128)
            small[8 * side + k, 0:levels, :] = level[:, cols]
            small[8 * side + k, levels:, :] = jnp.concatenate([gain[:, cols].astype(BF), fill])

    def small_to(d):
        peer = ring_peer(p, d)
        return push(small.at[peer], small_in.at[p.ctx], small_s.at[d], small_r.at[d], {"ctx": peer})


    @pl.loop(1, 16)
    def _(d):
        small_to(d).start()

    small_in[p.ctx] = small[p.ctx]

    @pl.loop(0, 2 * DEPTH)
    def _(step):
        with_twin(p.wt, by_order(lax.div(step, 2)), lax.rem(step, 2))


    out_cross = push(out_sum.at[1 - p.wt], out_pair, cross_s.at[0], cross_r.at[0], p.pair)
    up_cross = push(up_sum.at[1 - p.wt], up_all.at[p.wt, p.ctx], cross_s.at[1], cross_r.at[1], p.pair)
    up_came = push(up_sum.at[p.wt], up_all.at[1 - p.wt, p.ctx], cross_s.at[1], cross_r.at[1], p.pair)
    sources = {0: up_sum.at[p.wt], 2: down_sum.at[0:half], 3: down_sum.at[half:], 4: out_own,
               5: qkv_sum.at[0:split], 6: qkv_sum.at[split:]}

    def f_end(z):
        @pl.when(p.z == z)
        def _():
            f_line.end(z, [up_sum, down_sum, out_sum])
            out_cross.start()
            up_cross.start()

    def q_cross(z):
        for y in (1 - p.y, p.y):
            q_to_pair(z, y).wait_recv()
            here = p.index(z, y, p.core)
            term[p.wt, here] = (term[p.wt, here].astype(F32) + q_pair[z, y].astype(F32)).astype(BF)
        q_line.cross(z)

    f_line.quarter(2)
    f_line.right(2, 0)
    q_cross(3)
    f_line.right(2, 1)
    f_line.quarter(1)
    f_line.left(1, 3)
    f_line.right(1, 0)
    f_line.left(2, 3)
    q_cross(0)
    q_line.quarter(3)
    q_line.right(3, 0)
    f_line.left(1, 2)
    q_cross(2)
    q_line.quarter(0)
    q_line.left(0, 3)
    q_line.right(3, 1)
    q_line.left(0, 2)
    q_cross(1)
    q_line.right(3, 2)
    q_line.left(0, 1)
    q_line.quarter(2)
    q_line.right(2, 0)
    q_line.quarter(1)
    q_line.left(1, 3)
    q_line.right(1, 0)
    q_line.left(2, 3)
    for z in range(DEPTH):
        f_end(z)

    @pl.loop(1, 16)
    def _(d):
        small_to(d).wait_recv()

    small_pair[0] = jnp.sum(small_in[...].astype(F32), axis=0).astype(BF)
    small_cross = push(small_pair.at[0], small_pair.at[1], small_x.at[0], small_x.at[1], p.pair)
    small_cross.start()
    q_line.right(2, 1)
    q_line.left(1, 2)

    for t in (3, 2, 0):
        g.own(t, sources[t])
    out_cross.wait_recv()
    out_own[...] = (out_sum[p.wt].astype(F32) + out_pair[...].astype(F32)).astype(BF)
    g.own(4, sources[4])
    up_came.wait_recv()
    g.own(1)
    for z in range(DEPTH):
        pl.when(p.z == z)(lambda z=z: q_line.end(z, [qkv_sum]))
    for t in late:
        g.own(t, sources[t])

    small_cross.wait()
    small_all[p.ctx] = (small_pair[0].astype(F32) + small_pair[1].astype(F32)).astype(BF)

    def small_spread(d):
        peer = ring_peer(p, d)
        return push(small_all.at[p.ctx], small_all.at[p.ctx], spread_s.at[d], spread_r.at[d], {"ctx": peer})


    @pl.loop(1, 16)
    def _(d):
        small_spread(d).start()

    copies = [pltpu.make_async_copy(sources[t], g.items[t](p.ctx), local_s.at[t]) for t in sources]
    for copy in copies:
        copy.start()
    every = fixed + late
    for t in every:
        g.along(t, 1)
    for t in every:
        g.along(t, 2)
    for t in every:
        if t not in g.wide:
            g.crossed_at(t, 0)
    for t in every:
        g.along(t, 3)
    for d in (1, 2, 3):
        for t in every:
            g.crossed_at(t, d)

    for copy in copies:
        copy.wait()
    for t in range(len(g.items)):
        g.finish(t)
    halves.finish()
    f_line.finish()
    q_line.finish()
    out_cross.wait_send()
    up_cross.wait_send()

    @pl.loop(1, 16)
    def _(d):
        small_to(d).wait_send()
        small_spread(d).wait()

    for z in range(DEPTH):
        for y in range(2):
            q_to_pair(z, y).wait_send()
            for w in range(2):
                q_to_twin(w, z, y).wait_send()
    for m in range(micro):

        @pl.loop(1, 16)
        def _(d, m=m):
            to_head(m, d).wait_send()
            for part in range(3):
                to_owner(m, ring_peer(p, d), part).wait_send()


def back_pass(grad_t, qkv_in, full, lse, up, down, out, w_qkv, rest, block):
    dma = pltpu.SemaphoreType.DMA
    vmem = pl.BlockSpec(memory_space=pltpu.VMEM)
    anywhere = pl.BlockSpec(memory_space=pltpu.HBM)
    micro, _, length = qkv_in.shape
    model, rows = grad_t.shape
    pieces = [up.shape[:1] + up.shape[2:], down.shape[1:], out.shape[:1] + out.shape[2:]]
    piece = (model // 32, 3 * model)
    small = (16, 80, 128)
    return pl.pallas_call(
        functools.partial(back_kernel, block),
        out_shape=[
            jax.ShapeDtypeStruct((rows, model), BF),
            jax.ShapeDtypeStruct((rows, model), BF),
            jax.ShapeDtypeStruct((2, 16) + up.shape[2:], BF),
            jax.ShapeDtypeStruct(down.shape, BF),
            jax.ShapeDtypeStruct(out.shape[1:], BF),
            jax.ShapeDtypeStruct((16,) + piece, BF),
            jax.ShapeDtypeStruct(small, BF),
        ],
        in_specs=[vmem] * 4 + [anywhere] * 4 + [vmem] * len(rest),
        out_specs=[vmem] * 2 + [anywhere] * 4 + [vmem],
        scratch_shapes=[
            pltpu.VMEM((length, HEAD), BF),
            pltpu.VMEM((length, HEAD), BF),
            pltpu.VMEM((micro, HEAD, length), BF),
            pltpu.VMEM((HEAD, length), F32),
            pltpu.VMEM((micro, HEAD, length), BF),
            pltpu.VMEM((micro, 2, HEAD, length), BF),
            pltpu.VMEM((1, length), F32),
            pltpu.VMEM((3 * model, rows), BF),
            pltpu.VMEM((2, 128, 3 * model), BF),
            pltpu.VMEM((model, rows), F32),
            pltpu.VMEM((2, 16) + piece, BF),
            pltpu.VMEM((2, DEPTH, 2) + piece, BF),
            pltpu.VMEM((DEPTH, 2) + piece, BF),
            pltpu.VMEM(pieces[0], BF),
            pltpu.VMEM(pieces[1], BF),
            pltpu.VMEM(pieces[2], BF),
            pltpu.VMEM(pieces[2][1:], BF),
            pltpu.VMEM(pieces[2][1:], BF),
            pltpu.VMEM(piece, BF),
            pltpu.VMEM(small, BF),
            pltpu.VMEM(small, BF),
            pltpu.VMEM((2,) + small[1:], BF),
            pltpu.VMEM((rows, model), BF),
            pltpu.VMEM((model, rows), BF),
            pltpu.VMEM((rows, model), F32),
            pltpu.VMEM((rows, 1), F32),
            dma((micro,)),
            dma((micro, 16)),
            dma((micro, 16)),
            dma((micro, 16, 3)),
            dma((micro, 16, 3)),
            dma((2,)),
            dma((2, DEPTH, 2)),
            dma((2, DEPTH, 2)),
            dma((DEPTH, 2)),
            dma((DEPTH, 2)),
            dma((3,)),
            dma((3,)),
            dma((7,)),
            dma((16,)),
            dma((16,)),
            dma((2,)),
            dma((16,)),
            dma((16,)),
        ]
        + Halves.scratch(pieces)
        + Line.scratch(pieces)
        + Line.scratch([piece])
        + Gather.semaphores(7),
        compiler_params=pltpu.CompilerParams(
            collective_id=4, has_side_effects=True, vmem_limit_bytes=63 << 20
        ),
        name="back_pass",
    )(grad_t, qkv_in, full, lse, up, down, out, w_qkv, *rest)


def spread(source, pieces, first, target):
    width = source.shape[-1]
    for c in range(pieces):
        target[:, c * width : (c + 1) * width] = source[c, 0, first : first + HEAD, :]


def attend_kernel(pieces, block, qkv_ref, low_ref, full_ref, lse_ref, q_t, k_t, v_t, keys):
    length = q_t.shape[1]
    width = length // pieces
    spread(qkv_ref, pieces, 0, q_t)
    spread(qkv_ref, pieces, HEAD, k_t)
    spread(qkv_ref, pieces, 2 * HEAD, v_t)
    keys[...] = k_t[...].T
    for j in range(length // block):
        cols = slice(j * block, (j + 1) * block)
        scores = dot(keys[...], q_t[:, cols]) * (SCALE * LOG2E)
        top = jnp.max(scores, axis=0, keepdims=True)
        exps = jnp.exp2(scores - top)
        total = jnp.sum(exps, axis=0, keepdims=True)
        out = dot(v_t[...], exps.astype(BF)) / total
        full_ref[0, :, cols] = out
        lse_ref[0, :, cols] = top + jnp.log2(total)
        for c in range(block // width):
            low_ref[j * (block // width) + c, 0] = out[:, c * width : (c + 1) * width].astype(BF)


def attend(qkv, block):
    pieces, pairs, _, width = qkv.shape
    length = pieces * width
    return pl.pallas_call(
        functools.partial(attend_kernel, pieces, block),
        grid=(pairs,),
        in_specs=[pl.BlockSpec((pieces, 1, 3 * HEAD, width), lambda p: (0, p, 0, 0))],
        out_specs=[
            pl.BlockSpec((pieces, 1, HEAD, width), lambda p: (0, p, 0, 0)),
            pl.BlockSpec((1, HEAD, length), lambda p: (p, 0, 0)),
            pl.BlockSpec((1, 1, length), lambda p: (p, 0, 0)),
        ],
        out_shape=[
            jax.ShapeDtypeStruct((pieces, pairs, HEAD, width), BF),
            jax.ShapeDtypeStruct((pairs, HEAD, length), F32),
            jax.ShapeDtypeStruct((pairs, 1, length), F32),
        ],
        scratch_shapes=[pltpu.VMEM((HEAD, length), BF)] * 3 + [pltpu.VMEM((length, HEAD), BF)],
        compiler_params=pltpu.CompilerParams(vmem_limit_bytes=48 << 20),
        name="attend",
    )(qkv)


def attend_back_kernel(
    pieces, block, qkv_ref, grad_ref, full_ref, lse_ref, out_ref,
    q_t, k_t, v_t, g_t, keys, values, dq_t, dk, dv,
):
    length = q_t.shape[1]
    width = length // pieces
    spread(qkv_ref, pieces, 0, q_t)
    spread(qkv_ref, pieces, HEAD, k_t)
    spread(qkv_ref, pieces, 2 * HEAD, v_t)
    spread(grad_ref, pieces, 0, g_t)
    keys[...] = k_t[...].T
    values[...] = v_t[...].T
    for j in range(length // block):
        cols = slice(j * block, (j + 1) * block)
        query = q_t[:, cols]
        grad = g_t[:, cols]
        delta = jnp.sum(grad.astype(F32) * full_ref[0, :, cols], axis=0, keepdims=True)
        scores = dot(keys[...], query) * (SCALE * LOG2E)
        soft = jnp.exp2(scores - lse_ref[0, :, cols])
        term_v = dot(soft.astype(BF), grad, 1, 1)
        grad_soft = dot(values[...], grad)
        raw = (soft * (grad_soft - delta) * SCALE).astype(BF)
        term_k = dot(raw, query, 1, 1)
        dq_t[:, cols] = dot(k_t[...], raw)
        if j == 0:
            dv[...] = term_v
            dk[...] = term_k
        else:
            dv[...] += term_v
            dk[...] += term_k
    dk_t = dk[...].T.astype(BF)
    dv_t = dv[...].T.astype(BF)
    for c in range(pieces):
        piece = slice(c * width, (c + 1) * width)
        out_ref[c, 0, 0:HEAD, :] = dq_t[:, piece].astype(BF)
        out_ref[c, 0, HEAD : 2 * HEAD, :] = dk_t[:, piece]
        out_ref[c, 0, 2 * HEAD :, :] = dv_t[:, piece]


def attend_back(qkv, grad, full, lse, block):
    pieces, pairs, _, width = qkv.shape
    length = pieces * width
    return pl.pallas_call(
        functools.partial(attend_back_kernel, pieces, block),
        grid=(pairs,),
        in_specs=[
            pl.BlockSpec((pieces, 1, 3 * HEAD, width), lambda p: (0, p, 0, 0)),
            pl.BlockSpec((pieces, 1, HEAD, width), lambda p: (0, p, 0, 0)),
            pl.BlockSpec((1, HEAD, length), lambda p: (p, 0, 0)),
            pl.BlockSpec((1, 1, length), lambda p: (p, 0, 0)),
        ],
        out_specs=pl.BlockSpec((pieces, 1, 3 * HEAD, width), lambda p: (0, p, 0, 0)),
        out_shape=jax.ShapeDtypeStruct(qkv.shape, BF),
        scratch_shapes=[pltpu.VMEM((HEAD, length), BF)] * 4
        + [pltpu.VMEM((length, HEAD), BF)] * 2
        + [pltpu.VMEM((HEAD, length), F32)]
        + [pltpu.VMEM((length, HEAD), F32)] * 2,
        compiler_params=pltpu.CompilerParams(vmem_limit_bytes=56 << 20),
        name="attend_back",
    )(qkv, grad, full, lse)


def normed(rows):
    centered = rows - jnp.mean(rows, axis=-1, keepdims=True)
    scale = lax.rsqrt(jnp.mean(centered * centered, axis=-1, keepdims=True) + EPSILON)
    return centered * scale, scale


def norm_back(grad, hat, scale, weight):
    c = grad * weight
    return (
        c - jnp.mean(c, axis=-1, keepdims=True) - hat * jnp.mean(c * hat, axis=-1, keepdims=True)
    ) * scale


def turn(first, second, cosine, sine):
    return first * cosine - second * sine, second * cosine + first * sine


def shards(
    tokens, positions, buckets, qkv_w, out_w, up_w, down_w, time_w, noise_table,
    gain_one, gain_two, cotangent,
):
    n, ring = lax.axis_size("wt"), lax.axis_size("ctx")
    me = lax.axis_index("wt")
    micro, _, width, model = tokens.shape
    rows = micro * width
    pairs = HEADS * micro // ring
    block = 256
    planar = n == 2 and ring == 16

    x = tokens.reshape(rows, model).astype(F32)
    cot_low = cotangent.reshape(rows, model)
    places = positions.reshape(rows)
    levels = buckets.reshape(rows)

    def whole_rows(weight):
        return lax.all_gather(weight, "wt", axis=0, tiled=True)

    frequency = jnp.exp(
        jnp.arange(HEAD // 2, dtype=F32) * (-math.log(10000.0) * 2.0 / HEAD)
    )
    angles = frequency[:, None] * places.astype(F32)[None, :]
    cosine, sine = jnp.cos(angles), jnp.sin(angles)
    stacked = jnp.stack([gain_one, gain_two])
    if planar:
        w_qkv, w_time, table, gains, qkv_t, scale_one, scale_two = start(
            qkv_w, time_w, noise_table, stacked, tokens.reshape(rows, model), levels[:, None], cosine, sine
        )
        g_one, g_two = gains[0].astype(F32), gains[1].astype(F32)
    else:
        w_qkv = whole_rows(qkv_w)
        w_out = whole_rows(out_w)
        w_time = whole_rows(time_w)
        table = whole_rows(noise_table)
        gains = lax.all_gather(stacked, "wt", axis=1, tiled=True)
        w_up = lax.all_to_all(up_w, "wt", 1, 0, tiled=True)
        g_one, g_two = gains[0].astype(F32), gains[1].astype(F32)

        onehot = levels[:, None] == jnp.arange(table.shape[0], dtype=jnp.int32)[None, :]
        embed = dot(onehot.astype(BF), table).astype(BF)
        shifts = dot(embed, w_time)
        scale_one = 1.0 + shifts[:, :model]
        scale_two = 1.0 + shifts[:, model:]

        hat_one, rs_one = normed(x)
        weight_one = g_one * scale_one
        norm_one = (hat_one * weight_one).astype(BF)

        qkv_t = dot(w_qkv, norm_one, 0, 1).reshape(3, HEADS, 2, HEAD // 2, rows)
        turned = turn(qkv_t[:2, :, 0], qkv_t[:2, :, 1], cosine, sine)
        queries_keys = jnp.stack(turned, axis=2)
        qkv_low = jnp.concatenate([queries_keys.astype(BF), qkv_t[2:].astype(BF)])

    def to_heads(columns):
        parts = columns.shape[0]
        split = columns.reshape(parts, HEADS, HEAD, micro, width)
        split = jnp.transpose(split, (1, 3, 0, 2, 4))
        split = split.reshape(ring, pairs, parts * HEAD, width)
        return lax.all_to_all(split, "ctx", 0, 0, tiled=True)

    def to_tokens(pieces):
        parts = pieces.shape[2] // HEAD
        back = lax.all_to_all(pieces, "ctx", 0, 0, tiled=True)
        back = back.reshape(HEADS, micro, parts, HEAD, width)
        return jnp.transpose(back, (2, 0, 3, 1, 4)).reshape(parts, HEADS * HEAD, rows)

    if planar:
        qkv_heads, attended, full, lse, w_up, w_out, cot = heads(
            qkv_t, up_w, out_w, cot_low, micro, block
        )
    else:
        qkv_heads = to_heads(qkv_low.reshape(3, HEADS, HEAD, rows))
        low, full, lse = attend(qkv_heads, block)
        attended = to_tokens(low)[0]
        cot = gather_slots(cot_low).reshape(n * rows, model)

    if not planar:
        middle = x + dot(attended, w_out, 0, 0)
        hat_two, rs_two = normed(middle)
        weight_two = g_two * scale_two
        norm_two_own = (hat_two * weight_two).astype(BF)

        norm_two = gather_slots(norm_two_own).reshape(n * rows, model)
        pre = dot(norm_two, w_up)
        phi_cdf = 0.5 * (1.0 + lax.erf(pre * (2.0**-0.5)))
        hidden = (pre * phi_cdf).astype(BF)
        out_parts = dot(hidden, down_w).reshape(n, rows, model)

        grad_hidden = dot(cot, down_w, 1, 1)
        density = jnp.exp(-0.5 * pre * pre) * (1.0 / math.sqrt(2.0 * math.pi))
        grad_pre = (grad_hidden * (phi_cdf + pre * density)).astype(BF)
        grad_norm_two = sum_slots(dot(grad_pre, w_up, 1, 1).reshape(n, rows, model))
        down_term = dot(hidden, cot, 0, 0).astype(BF)
        up_term = dot(norm_two, grad_pre, 0, 0).astype(BF)
        grad_mid = cot_low.astype(F32) + norm_back(grad_norm_two, hat_two, rs_two, weight_two)
        grad_branch = grad_mid.astype(BF)
        eh_two = grad_norm_two * hat_two
        grad_scale_two = eh_two * g_two
        gain_two_term = jnp.sum(eh_two * scale_two, axis=0)
        out_term = dot(attended, grad_branch, 1, 0).astype(BF)
        grad_attn = dot(w_out, grad_branch, 1, 1).astype(BF)

    if planar:

        def pieces_of(array, *lead):
            return array.reshape(lead + (-1, array.shape[-1]))

        (
            out_part, out_other, grad_attn, grad_mid, grad_scale_two, gain_two_term, up_term, down_term, out_term,
        ) = mid_pass(attended, tokens.reshape(rows, model), scale_two, g_two[None], w_out, w_up, down_w, cot)
        rest = (
            cosine, sine, tokens.reshape(rows, model), levels[None], g_one[None], scale_one, grad_mid,
            grad_scale_two, gain_two_term, out_part, out_other,
        )
        input_grad, layer_out, up_all, down_all, out_all, qkv_all, small_all = back_pass(
            grad_attn, qkv_heads, full, lse, pieces_of(up_term, n, ring), pieces_of(down_term, ring),
            pieces_of(out_term, n, ring), w_qkv, rest, block,
        )
        time_here = time_w.shape[0]
        table_rows = lax.dynamic_slice_in_dim(table, me * time_here, time_here, 1)
        (
            up_grad, down_grad, out_grad, qkv_grad, time_grad, table_grad, gain_one_grad, gain_two_grad,
            input_grad, layer_out,
        ) = widen(up_all, down_all, out_all, qkv_all, small_all, table_rows, w_time, input_grad, layer_out)
        gain_one_grad, gain_two_grad = gain_one_grad[0], gain_two_grad[0]
    else:
        layer_out = middle + sum_slots(out_parts)
        up_share = lax.psum_scatter(
            up_term.reshape(n, model // n, -1), "ctx", scatter_dimension=1, tiled=True
        )
        down_share = lax.psum_scatter(down_term, "ctx", scatter_dimension=0, tiled=True)
        out_share = lax.psum_scatter(
            out_term.reshape(n, model // n, model), "ctx", scatter_dimension=1, tiled=True
        )
        grad_heads = to_heads(grad_attn.reshape(1, HEADS, HEAD, rows))
        back = to_tokens(attend_back(qkv_heads, grad_heads, full, lse, block))
        back = back.reshape(3, HEADS, 2, HEAD // 2, rows)
        unturned = turn(back[:2, :, 0].astype(F32), back[:2, :, 1].astype(F32), cosine, -sine)
        grad_qkv = jnp.concatenate([jnp.stack(unturned, axis=2).astype(BF), back[2:]])
        grad_qkv = grad_qkv.reshape(3 * model, rows)
        qkv_term = dot(norm_one, grad_qkv, 0, 1).astype(BF)
        grad_norm_one = dot(grad_qkv, w_qkv, 0, 1)

        input_grad = grad_mid + norm_back(grad_norm_one, hat_one, rs_one, weight_one)
        eh_one = grad_norm_one * hat_one
        grad_scale_one = eh_one * g_one
        gain_one_term = jnp.sum(eh_one * scale_one, axis=0)

        grad_shifts = jnp.concatenate([grad_scale_one, grad_scale_two], axis=1).astype(BF)
        level_term = dot(onehot.astype(BF), grad_shifts, 0, 0)
        gain_terms = jnp.concatenate([gain_one_term, gain_two_term])
        small = lax.psum(jnp.concatenate([level_term, gain_terms[None]]), ("ctx", "wt"))
        share = lax.psum_scatter(
            qkv_term.reshape(n, model // n, -1), "ctx", scatter_dimension=1, tiled=True
        )

        def spread_rows(share):
            return lax.all_gather(share, "ctx", axis=0, tiled=True).astype(F32)

        up_share = lax.all_to_all(up_share, "wt", 0, 0, tiled=True)
        up_grad = lax.all_gather(up_share, "ctx", axis=1, tiled=True).astype(F32)
        up_grad = jnp.transpose(up_grad, (1, 0, 2)).reshape(model // n, -1)
        down_grad = spread_rows(down_share)
        out_grad = spread_rows(sum_owned(out_share))
        qkv_grad = spread_rows(sum_owned(share))

        by_level = small[: table.shape[0]]
        gain_sums = small[table.shape[0]]
        levels_here, time_here = noise_table.shape[0], time_w.shape[0]
        high = lax.Precision.HIGHEST
        time_rows = lax.dynamic_slice_in_dim(table, me * time_here, time_here, 1).astype(F32)
        time_grad = lax.dot_general(
            time_rows, by_level, (((0,), (0,)), ((), ())), precision=high, preferred_element_type=F32
        )
        level_rows = lax.dynamic_slice_in_dim(by_level, me * levels_here, levels_here, 0)
        table_grad = lax.dot_general(
            level_rows, w_time.astype(F32), (((1,), (1,)), ((), ())), precision=high,
            preferred_element_type=F32,
        )

        gain_here = gain_one.shape[0]
        gain_one_grad = lax.dynamic_slice_in_dim(gain_sums, me * gain_here, gain_here, 0)
        gain_two_grad = lax.dynamic_slice_in_dim(gain_sums, model + me * gain_here, gain_here, 0)

    return (
        layer_out.astype(BF).reshape(tokens.shape),
        input_grad.astype(BF).reshape(tokens.shape),
        qkv_grad,
        out_grad,
        up_grad,
        down_grad,
        time_grad,
        table_grad,
        gain_one_grad,
        gain_two_grad,
    )


def sum_owned(share):
    n, me = lax.axis_size("wt"), lax.axis_index("wt")
    slots = jnp.stack(
        [lax.dynamic_index_in_dim(share, lax.rem(me + k, n), 0, keepdims=False) for k in range(n)]
    )
    return sum_slots(slots.astype(F32)).astype(BF)


def solution(mesh):
    rows = P(None, "wt", "ctx", None)
    marks = P(None, "wt", "ctx")
    weight = P("wt", None)
    gain = P("wt")
    return jax.shard_map(
        shards,
        mesh=mesh,
        in_specs=(rows, marks, marks) + (weight,) * 6 + (gain, gain, rows),
        out_specs=(rows, rows) + (weight,) * 6 + (gain, gain),
        check_vma=False,
    )
```

```python
import functools
import math

import jax
import jax.numpy as jnp
from jax import lax
from jax.experimental import pallas as pl
from jax.experimental.pallas import tpu as pltpu
from jax.sharding import PartitionSpec as P

HEADS = 16
HEAD = 64
LEVELS = 64
EPSILON = 1e-05
SCALE = 0.125
LOG2E = math.log2(math.e)
BF = jnp.bfloat16
F32 = jnp.float32


def dot(a, b, ca=1, cb=0):
    return lax.dot_general(a, b, (((ca,), (cb,)), ((), ())), preferred_element_type=F32)


def swap_ring(value, places):
    n = lax.axis_size("wt")
    return lax.ppermute(value, "wt", [((i + places) % n, i) for i in range(n)])


def gather_slots(own):
    n = lax.axis_size("wt")
    return jnp.stack([own] + [swap_ring(own, k) for k in range(1, n)])


def sum_slots(partial):
    n = lax.axis_size("wt")
    total = partial[0]
    for k in range(1, n):
        total = total + swap_ring(partial[k].astype(BF), n - k).astype(F32)
    return total


MESH = pl.DeviceIdType.MESH
DEPTH = 4


class Place:
    def __init__(self):
        self.ctx = lax.axis_index("ctx")
        self.wt = lax.axis_index("wt")
        self.z = lax.div(self.ctx, 4)
        self.y = lax.rem(lax.div(self.ctx, 2), 2)
        self.core = lax.rem(self.ctx, 2)
        self.right = {"ctx": self.index(lax.min(self.z + 1, DEPTH - 1), self.y, self.core)}
        self.left = {"ctx": self.index(lax.max(self.z - 1, 0), self.y, self.core)}
        self.across = {"ctx": self.index(self.z, 1 - self.y, self.core)}
        self.twin = {"ctx": self.index(self.z, self.y, 1 - self.core)}
        self.pair = {"wt": 1 - self.wt}

    @staticmethod
    def index(z, y, core):
        return (z * 2 + y) * 2 + core

    def greet(self, everyone=False, pair=True):
        barrier = pltpu.get_barrier_semaphore()

        def signal(device):
            pl.semaphore_signal(barrier, inc=1, device_id=device, device_id_type=MESH)

        if everyone:

            @pl.loop(1, 16)
            def _(d):
                signal({"ctx": lax.rem(self.ctx + d, 16)})

            count = 15
        else:
            signal(self.across)
            signal(self.twin)
            pl.when(self.z > 0)(lambda: signal(self.left))
            pl.when(self.z < DEPTH - 1)(lambda: signal(self.right))
            inner = jnp.logical_and(self.z > 0, self.z < DEPTH - 1).astype(jnp.int32)
            count = 3 + inner
        if pair:
            signal(self.pair)
            count = count + 1
        pl.semaphore_wait(barrier, count)


def push(source, target, send, receive, device):
    return pltpu.make_async_remote_copy(
        src_ref=source, dst_ref=target, send_sem=send, recv_sem=receive,
        device_id=device, device_id_type=MESH,
    )


class Gather:
    def __init__(self, place, items, sems, wide=()):
        self.p, self.items, self.wide = place, items, wide
        (self.sl, self.sr, self.sy, self.sc, self.rz, self.ry, self.rc) = sems

    @staticmethod
    def semaphores(count):
        dma = pltpu.SemaphoreType.DMA
        line, square = dma((count, DEPTH)), dma((count, DEPTH, 2))
        return [square, square, line, square, square, line, square]

    def piece(self, t, z, y, core):
        return self.items[t](self.p.index(z, y, core))

    def copy(self, t, z, y, source, send, receive, device):
        here = self.piece(t, z, y, self.p.core)
        return push(here if source is None else source, here, send, receive, device)

    def rightward(self, t, z, source=None, far=0):
        y = 1 - self.p.y if far else self.p.y
        return self.copy(t, z, y, source, self.sr.at[t, z, far], self.rz.at[t, z, far], self.p.right)

    def leftward(self, t, z, source=None, far=0):
        y = 1 - self.p.y if far else self.p.y
        return self.copy(t, z, y, source, self.sl.at[t, z, far], self.rz.at[t, z, far], self.p.left)

    def crossing(self, t, z, source=None):
        return self.copy(t, z, self.p.y, source, self.sy.at[t, z], self.ry.at[t, z], self.p.across)

    def twinning(self, t, z, y, source=None):
        return self.copy(t, z, y, source, self.sc.at[t, z, y], self.rc.at[t, z, y], self.p.twin)

    def own(self, t, source=None):
        p = self.p
        pl.when(p.z < DEPTH - 1)(lambda: self.rightward(t, p.z, source).start())
        pl.when(p.z > 0)(lambda: self.leftward(t, p.z, source).start())
        self.crossing(t, p.z, source).start()
        self.twinning(t, p.z, p.y, source).start()

    def arrived(self, t, z, y, core, semaphore):
        piece = self.piece(t, z, y, core)
        push(piece, piece, semaphore, semaphore, self.p.twin).wait_recv()

    def arrive(self, t, z, far=0):
        p = self.p
        y = 1 - p.y if far else p.y
        self.arrived(t, z, y, p.core, self.rz.at[t, z, far])
        pl.when(jnp.logical_and(p.z > z, p.z < DEPTH - 1))(lambda: self.rightward(t, z, far=far).start())
        pl.when(jnp.logical_and(p.z < z, p.z > 0))(lambda: self.leftward(t, z, far=far).start())
        if t not in self.wide:
            self.crossing(t, z).start()
        self.twinning(t, z, y).start()

    def along(self, t, d):
        p = self.p
        for far in (0, 1) if t in self.wide else (0,):
            pl.when(p.z - d >= 0)(lambda far=far: self.arrive(t, p.z - d, far))
            pl.when(p.z + d < DEPTH)(lambda far=far: self.arrive(t, p.z + d, far))

    def crossed(self, t, z):
        self.arrived(t, z, 1 - self.p.y, self.p.core, self.ry.at[t, z])
        self.twinning(t, z, 1 - self.p.y).start()

    def crossed_at(self, t, d):
        p = self.p
        if t in self.wide:
            if d == 0:
                self.arrived(t, p.z, 1 - p.y, p.core, self.ry.at[t, p.z])
                pl.when(p.z < DEPTH - 1)(lambda: self.rightward(t, p.z, far=1).start())
                pl.when(p.z > 0)(lambda: self.leftward(t, p.z, far=1).start())
                self.twinning(t, p.z, 1 - p.y).start()
        elif d == 0:
            self.crossed(t, p.z)
        else:
            pl.when(p.z - d >= 0)(lambda: self.crossed(t, p.z - d))
            pl.when(p.z + d < DEPTH)(lambda: self.crossed(t, p.z + d))

    def finish(self, t):
        p = self.p
        wide = t in self.wide
        if wide:
            self.crossing(t, p.z).wait_send()
        for z in range(DEPTH):
            if not wide:
                self.crossing(t, z).wait_send()
            for y in range(2):
                self.twinning(t, z, y).wait_send()
                self.arrived(t, z, y, 1 - p.core, self.rc.at[t, z, y])
            for far in (0, 1) if wide else (0,):
                pl.when(jnp.logical_and(p.z >= z, p.z < DEPTH - 1))(
                    lambda z=z, far=far: self.rightward(t, z, far=far).wait_send()
                )
                pl.when(jnp.logical_and(p.z <= z, p.z > 0))(
                    lambda z=z, far=far: self.leftward(t, z, far=far).wait_send()
                )


class Line:
    def __init__(self, place, count, mine, refs):
        self.p, self.mine, self.terms = place, mine, range(count)
        self.from_across, self.slots = refs[:count], refs[count : 2 * count]
        self.ys, self.yr, self.rs, self.rr, self.vs, self.vr = refs[2 * count :]

    @staticmethod
    def scratch(shapes):
        line = pltpu.SemaphoreType.DMA((len(shapes), DEPTH))
        return (
            [pltpu.VMEM((DEPTH,) + shape, BF) for shape in shapes]
            + [pltpu.VMEM((DEPTH + 1,) + shape, BF) for shape in shapes]
            + [line] * 6
        )

    def across(self, t, z):
        return push(
            self.mine(t, z, 1 - self.p.y), self.from_across[t].at[z], self.ys.at[t, z], self.yr.at[t, z], self.p.across
        )

    def rightward(self, t, j, first):
        target = self.slots[t].at[j + 1]
        return push(self.from_across[t].at[j] if first else target, target, self.rs.at[t, j], self.rr.at[t, j], self.p.right)

    def leftward(self, t, j, first):
        target = self.slots[t].at[j]
        return push(self.from_across[t].at[j] if first else target, target, self.vs.at[t, j], self.vr.at[t, j], self.p.left)

    def cross(self, z):
        for t in self.terms:
            self.across(t, z).start()

    def quarter(self, z):
        for t in self.terms:
            self.across(t, z).wait_recv()
            both = self.mine(t, z, self.p.y)[...].astype(F32) + self.from_across[t][z].astype(F32)
            self.from_across[t][z] = both.astype(BF)

    def with_left(self, t, j):
        self.rightward(t, j, False).wait_recv()
        return self.from_across[t][j].astype(F32) + self.slots[t][j + 1].astype(F32)

    def with_right(self, t, j):
        self.leftward(t, j, False).wait_recv()
        return self.from_across[t][j].astype(F32) + self.slots[t][j].astype(F32)

    def right(self, j, z):
        @pl.when(self.p.z == z)
        def _():
            for t in self.terms:
                if z > 0:
                    self.slots[t][j + 1] = self.with_left(t, j).astype(BF)
                self.rightward(t, j, z == 0).start()

    def left(self, j, z):
        @pl.when(self.p.z == z)
        def _():
            for t in self.terms:
                if z < DEPTH - 1:
                    self.slots[t][j] = self.with_right(t, j).astype(BF)
                self.leftward(t, j, z == DEPTH - 1).start()

    def end(self, z, results):
        for t in self.terms:
            if z == 0:
                total = self.with_right(t, z)
            else:
                total = self.with_left(t, z)
                if z < DEPTH - 1:
                    self.leftward(t, z, False).wait_recv()
                    total = total + self.slots[t][z].astype(F32)
            results[t][...] = total.astype(BF)

    def finish(self):
        p = self.p
        for t in self.terms:
            for z in range(DEPTH):
                self.across(t, z).wait_send()
                pl.when(p.z < z)(lambda t=t, z=z: self.rightward(t, z, False).wait_send())
                pl.when(p.z > z)(lambda t=t, z=z: self.leftward(t, z, False).wait_send())


class Halves:
    def __init__(self, place, sources, refs):
        count = len(sources)
        self.p, self.sources, self.terms = place, sources, range(count)
        self.kept, self.from_twin = refs[:count], refs[count : 2 * count]
        self.ls, self.ts, self.tr = refs[2 * count :]

    @staticmethod
    def scratch(shapes):
        square = pltpu.SemaphoreType.DMA((len(shapes), DEPTH, 2))
        return [pltpu.VMEM((DEPTH, 2) + shape, BF) for shape in shapes] * 2 + [square] * 3

    def mine(self, t, z, y):
        return self.kept[t].at[z, y]

    def load(self, t, z, y):
        source = self.sources[t](self.p.index(z, y, self.p.core))
        return pltpu.make_async_copy(source, self.kept[t].at[z, y], self.ls.at[t, z, y])

    def twin(self, t, z, y):
        source = self.sources[t](self.p.index(z, y, 1 - self.p.core))
        return push(source, self.from_twin[t].at[z, y], self.ts.at[t, z, y], self.tr.at[t, z, y], self.p.twin)

    def begin(self, z):
        for y in (1 - self.p.y, self.p.y):
            for t in self.terms:
                self.load(t, z, y).start()
                self.twin(t, z, y).start()

    def halve(self, z):
        for y in (1 - self.p.y, self.p.y):
            for t in self.terms:
                self.load(t, z, y).wait()
                self.twin(t, z, y).wait_recv()
                both = self.kept[t][z, y].astype(F32) + self.from_twin[t][z, y].astype(F32)
                self.kept[t][z, y] = both.astype(BF)

    def finish(self):
        for t in self.terms:
            for z in range(DEPTH):
                for y in range(2):
                    self.twin(t, z, y).wait_send()


def widen_kernel(
    up_ref, down_ref, out_ref, qkv_ref, small_ref, rows_ref, time_ref, grad_ref, layer_ref,
    up_to, down_to, out_to, qkv_to, time_to, table_to, gain_one_to, gain_two_to, grad_to, layer_to,
):
    grad_to[...] = grad_ref[...]
    layer_to[...] = layer_ref[...]
    columns = up_ref.shape[-1]
    levels, here = rows_ref.shape[0], table_to.shape[0]
    me, step = lax.axis_index("wt"), pl.program_id(0)
    mine = pl.ds(pl.multiple_of(me * here, here), here)
    table = None
    gains = []
    for i in range(up_ref.shape[1]):
        rows = slice(i * up_ref.shape[2], (i + 1) * up_ref.shape[2])
        up_to[rows, :columns] = up_ref[0, i].astype(F32)
        up_to[rows, columns:] = up_ref[1, i].astype(F32)
        for source, target in ((down_ref, down_to), (out_ref, out_to), (qkv_ref, qkv_to)):
            depth = source.shape[1]
            target[i * depth : (i + 1) * depth, :] = source[i].astype(F32)
        cols = slice(i * 128, (i + 1) * 128)
        time_to[:, cols] = dot(rows_ref[...], small_ref[i, 0:levels, :], 0, 0)
        gains.append(small_ref[i, levels : levels + 1, :].astype(F32))
        part = dot(small_ref[i, mine, :], time_ref[:, cols], 1, 1)
        table = part if table is None else table + part
    gain = jnp.concatenate(gains, axis=1)
    wide = gain.shape[1]
    count = gain_one_to.shape[1] // wide
    place = pl.ds(pl.multiple_of(lax.rem(step, count) * wide, wide), wide)

    @pl.when(lax.div(step, count) == me)
    def _():
        gain_one_to[:, place] = gain

    @pl.when(lax.div(step, count) == me + 2)
    def _():
        gain_two_to[:, place] = gain

    first = step == 0

    @pl.when(first)
    def _():
        table_to[...] = table

    @pl.when(jnp.logical_not(first))
    def _():
        table_to[...] += table


def widen(up, down, out, qkv, small, table_rows, w_time, grad, layer, step=2):
    _, ring, up_rows, up_columns = up.shape
    wide = small.shape[2]

    def piece(a):
        return pl.BlockSpec((step,) + a.shape[1:], lambda i: (i, 0, 0))

    def row_block(a):
        return pl.BlockSpec((step * a.shape[1], a.shape[2]), lambda i: (i, 0))

    def whole(a):
        return jax.ShapeDtypeStruct((ring * a.shape[1], a.shape[2]), F32)

    def columns(rows):
        return pl.BlockSpec((rows, step * wide), lambda i: (0, i))

    def share(a):
        return pl.BlockSpec((a.shape[0] * step // ring, a.shape[1]), lambda i: (i, 0))

    time_rows, depth = table_rows.shape[1], w_time.shape[0]
    gain = pl.BlockSpec((1, ring * wide // 4), lambda i: (0, 0))
    return pl.pallas_call(
        widen_kernel,
        grid=(ring // step,),
        in_specs=[
            pl.BlockSpec((2, step, up_rows, up_columns), lambda i: (0, i, 0, 0)),
            piece(down), piece(out), piece(qkv), piece(small),
            pl.BlockSpec(table_rows.shape, lambda i: (0, 0)), columns(depth), share(grad), share(layer),
        ],
        out_specs=[
            pl.BlockSpec((step * up_rows, 2 * up_columns), lambda i: (i, 0)),
            row_block(down), row_block(out), row_block(qkv),
            columns(time_rows), pl.BlockSpec((table_rows.shape[0] // 2, depth), lambda i: (0, 0)),
            gain, gain, share(grad), share(layer),
        ],
        out_shape=[
            jax.ShapeDtypeStruct((ring * up_rows, 2 * up_columns), F32),
            whole(down), whole(out), whole(qkv),
            jax.ShapeDtypeStruct((time_rows, ring * wide), F32),
            jax.ShapeDtypeStruct((table_rows.shape[0] // 2, depth), F32),
            jax.ShapeDtypeStruct((1, ring * wide // 4), F32),
            jax.ShapeDtypeStruct((1, ring * wide // 4), F32),
            jax.ShapeDtypeStruct(grad.shape, BF),
            jax.ShapeDtypeStruct(layer.shape, BF),
        ],
        compiler_params=pltpu.CompilerParams(vmem_limit_bytes=62 << 20),
        name="widen",
    )(up, down, out, qkv, small, table_rows, w_time, grad, layer)


def ring_peer(p, d):
    return lax.rem(p.ctx + d, 16)


def front_kernel(
    block, qkv_own, time_own, table_own, gain_own, tokens, levels, cosine, sine, up_w, out_w, cot,
    qkv_all, time_all, table_all, gain_all, scale_one, scale_two,
    qkv_keep, att, full_keep, lse_ref, up_all, out_all, cot_all,
    hold_qkv, hold_time, far_qkv, far_time, normal, embed, rows_one, qkv_t,
    qkv_in, full_ref, keys, low, hold_up, hold_out, hold_cot,
    block_in, block_out, time_s, first_s, first_r,
    keep_s, own_s, in_s, in_r, back_s, back_r, hold_in, hold_to, cross_s, cross_r, twin_s, twin_r, *gather_sems,
):
    p = Place()
    micro, _, length = qkv_in.shape
    width = length // 16
    model = att.shape[0]
    other = 1 - p.wt
    half = hold_qkv.shape[1]
    lane = 128
    blocks = hold_qkv.shape[2] // lane
    depth = far_qkv.shape[2]
    deep = far_time.shape[1]

    def natural(group, i):
        start_column = (i // DEPTH) * model + (i % DEPTH) * 2 * lane + group * lane
        return slice(start_column, start_column + lane)

    def held(i):
        return slice(i * lane, (i + 1) * lane)

    load = [[
        pltpu.make_async_copy(qkv_own.at[:, natural(k, i)], hold_qkv.at[k, :, held(i)], block_in.at[k, i])
        for i in range(blocks)] for k in range(2)]
    times = pltpu.make_async_copy(time_own, hold_time, time_s.at[0])
    for copy in load[0] + load[1]:
        copy.start()
    times.start()

    half_up, half_out = up_w.shape[0] // 2, out_w.shape[0] // 2
    columns = up_all.shape[2]
    mine = pl.ds(pl.multiple_of(p.wt * columns, columns), columns)
    theirs = pl.ds(pl.multiple_of(other * columns, columns), columns)
    holds = [
        pltpu.make_async_copy(up_w, hold_up, hold_in.at[0]),
        pltpu.make_async_copy(out_w, hold_out, hold_in.at[1]),
        pltpu.make_async_copy(cot, hold_cot, hold_in.at[2]),
    ]
    for copy in holds:
        copy.start()
    p.greet(everyone=True)
    g = Gather(
        p, [lambda c: far_time.at[c], lambda c: far_qkv.at[0, c], lambda c: far_qkv.at[1, c]], gather_sems
    )
    here = pl.ds(pl.multiple_of(depth * p.ctx, depth), depth)
    sent = [
        push(time_own.at[pl.ds(deep * p.ctx, deep)], far_time.at[p.ctx], first_s.at[0], first_r.at[0], p.pair),
        push(hold_qkv.at[0, here], far_qkv.at[0, p.ctx], first_s.at[1], first_r.at[1], p.pair),
        push(hold_qkv.at[1, here], far_qkv.at[1, p.ctx], first_s.at[2], first_r.at[2], p.pair),
        push(table_own, table_all.at[p.wt], first_s.at[3], first_r.at[3], p.pair),
        push(gain_own, gain_all.at[p.wt], first_s.at[4], first_r.at[4], p.pair),
    ]
    rows_up = pl.ds(pl.multiple_of(p.core * half_up, half_up), half_up)
    rows_out = pl.ds(pl.multiple_of(p.core * half_out, half_out), half_out)
    crossing = [
        push(hold_out.at[rows_out], out_all.at[p.wt, rows_out], cross_s.at[0], cross_r.at[0], p.pair),
        push(hold_up.at[rows_up, theirs], up_all.at[p.wt, rows_up], cross_s.at[1], cross_r.at[1], p.pair),
        push(hold_cot, cot_all.at[1], cross_s.at[2], cross_r.at[2], p.pair),
    ]
    twins = [
        push(out_all.at[other, rows_out], out_all.at[other, rows_out], twin_s.at[0], twin_r.at[0], p.twin),
        push(up_all.at[other, rows_up], up_all.at[other, rows_up], twin_s.at[1], twin_r.at[1], p.twin),
    ]
    for copy in sent[3:] + sent[:1]:
        copy.start()
    for k in range(2):
        for copy in load[k]:
            copy.wait()
        sent[1 + k].start()
    for copy in holds:
        copy.wait()
    for copy in crossing:
        copy.start()
    table_all[p.wt] = table_own[...]
    gain_all[p.wt] = gain_own[...]
    normal[...] = normed(tokens[...].astype(F32))[0]
    for t in range(2):
        sent[t].wait_recv()
        g.own(t)
    times.wait()
    out = [pltpu.make_async_copy(hold_time, time_all.at[p.wt], time_s.at[1])]
    for k in range(2):
        for i in range(blocks):
            out.append(pltpu.make_async_copy(
                hold_qkv.at[k, :, held(i)], qkv_all.at[p.wt, :, natural(k, i)], block_out.at[0, k, i]))
    for copy in out:
        copy.start()
    for copy in sent[3:]:
        copy.wait_recv()
    kinds = 2 * table_own.shape[0]
    onehot = (lax.broadcasted_iota(jnp.int32, (tokens.shape[0], kinds), 1) == levels[...]).astype(F32).astype(BF)
    embed[...] = dot(onehot, jnp.concatenate([table_all[0], table_all[1]])).astype(BF)
    for t in range(2):
        g.along(t, 1)
    for t in range(2):
        g.along(t, 2)
    sent[2].wait_recv()
    g.own(2)
    for t in range(2):
        g.crossed_at(t, 0)
    for t in range(2):
        g.along(t, 3)
    g.along(2, 1)
    for d in (1, 2, 3):
        g.crossed_at(0, d)
    g.finish(0)
    far_to = qkv_all.at[other].reshape(16, depth, 3 * model)
    out.append(pltpu.make_async_copy(far_time, time_all.at[other].reshape(far_time.shape), time_s.at[2]))
    out[-1].start()

    def part_of(w, size):
        return pl.ds(pl.multiple_of(w * size, size), size)

    thick = hold_time.shape[0]
    far_rows = jnp.concatenate([far_time[k] for k in range(16)])
    shifts = dot(embed[:, part_of(p.wt, thick)], hold_time[...]) + dot(embed[:, part_of(other, thick)], far_rows)
    scale_one[...] = 1.0 + shifts[:, :model]
    scale_two[...] = 1.0 + shifts[:, model:]
    gain_one = jnp.concatenate([gain_all[0, 0:1], gain_all[1, 0:1]], axis=1).astype(F32)
    rows_one[...] = (normal[...] * (gain_one * scale_one[...])).astype(BF)
    quarter = HEAD // 2
    wide = 2 * lane

    def project(group):
        near, far = rows_one[:, part_of(p.wt, half)], rows_one[:, part_of(other, half)]

        @pl.loop(0, blocks // 2)
        def _(k):
            cols = pl.ds(pl.multiple_of(k * wide, wide), wide)
            part = dot(near, hold_qkv[group, :, cols])
            part = (part + dot(far, far_qkv[group, :, :, cols].reshape(half, wide))).T
            base = lax.div(k, 2) * model + lax.rem(k, 2) * 2 * wide + group * lane

            @pl.when(k < blocks // 3)
            def _():
                for h in range(4):
                    first = part[h * HEAD : h * HEAD + quarter]
                    second = part[h * HEAD + quarter : (h + 1) * HEAD]
                    row = base + (h // 2) * wide + (h % 2) * HEAD
                    up, down = pl.multiple_of(row, HEAD), pl.multiple_of(row + quarter, quarter)
                    qkv_t[pl.ds(up, quarter), :] = (first * cosine[...] - second * sine[...]).astype(BF)
                    qkv_t[pl.ds(down, quarter), :] = (second * cosine[...] + first * sine[...]).astype(BF)

            @pl.when(k >= blocks // 3)
            def _():
                for h in range(2):
                    row = pl.multiple_of(base + h * wide, lane)
                    qkv_t[pl.ds(row, lane), :] = part[h * lane : (h + 1) * lane].astype(BF)

    def piece(part, c):
        return pl.ds(pl.multiple_of(part * model + c * HEAD, HEAD), HEAD)

    def lanes(c):
        return pl.ds(pl.multiple_of(c * width, width), width)

    def to_head(m, d, part):
        c = ring_peer(p, d)
        return push(
            qkv_t.at[piece(part, c), m * width : (m + 1) * width],
            qkv_in.at[m, part * HEAD : (part + 1) * HEAD, lanes(p.ctx)],
            in_s.at[m, d, part], in_r.at[m, d, part], {"ctx": c},
        )

    stay = [
        pltpu.make_async_copy(
            qkv_t.at[piece(part, p.ctx), m * width : (m + 1) * width],
            qkv_in.at[m, part * HEAD : (part + 1) * HEAD, lanes(p.ctx)],
            own_s.at[m, part],
        )
        for m in range(micro) for part in range(3)
    ]

    def to_group(group):
        @pl.when(p.y == group)
        def _():
            for copy in stay:
                copy.start()

        for m in range(micro):

            @pl.loop(0, 8)
            def _(e, m=m):
                i = lax.rem(e + p.ctx, 8)
                c = p.index(lax.div(i, 2), group, lax.rem(i, 2))

                @pl.when(c != p.ctx)
                def _():
                    for part in range(3):
                        to_head(m, lax.rem(c - p.ctx + 16, 16), part).start()

    def store_far(group):
        for i in range(blocks):
            out.append(pltpu.make_async_copy(
                far_qkv.at[group, :, :, held(i)], far_to.at[:, :, natural(group, i)], block_out.at[1, group, i]))
            out[-1].start()

    g.along(2, 2)
    for d in (1, 2, 3):
        g.crossed_at(1, d)
    g.finish(1)
    g.along(2, 3)
    project(0)
    to_group(0)
    store_far(0)
    for d in range(DEPTH):
        g.crossed_at(2, d)
    g.finish(2)
    project(1)
    to_group(1)
    store_far(1)
    placing = [
        pltpu.make_async_copy(hold_up.at[:, mine], up_all.at[p.wt], hold_to.at[0]),
        pltpu.make_async_copy(hold_out, out_all.at[p.wt], hold_to.at[1]),
        pltpu.make_async_copy(hold_cot, cot_all.at[0], hold_to.at[2]),
    ]
    for copy in placing:
        copy.start()

    def to_owner(m, c):
        return push(
            low.at[m, :, lanes(c)],
            att.at[pl.ds(pl.multiple_of(p.ctx * HEAD, HEAD), HEAD), m * width : (m + 1) * width],
            back_s.at[m, c], back_r.at[m, p.ctx], {"ctx": c},
        )

    keep_qkv = [pltpu.make_async_copy(qkv_in.at[m], qkv_keep.at[m], keep_s.at[0, m]) for m in range(micro)]
    keep_full = [pltpu.make_async_copy(full_ref.at[m], full_keep.at[m], keep_s.at[1, m]) for m in range(micro)]
    for m in range(micro):
        for part in range(3):
            stay[3 * m + part].wait()

        @pl.loop(1, 16)
        def _(d, m=m):
            for part in range(3):
                to_head(m, d, part).wait_recv()

        keep_qkv[m].start()
        keys[...] = qkv_in[m, HEAD : 2 * HEAD, :].T
        @pl.loop(0, length // block)
        def _(step, m=m):
            j = lax.rem(step + lax.div(p.ctx * width, block), length // block)
            cols = pl.ds(pl.multiple_of(j * block, block), block)
            scores = dot(keys[...], qkv_in[m, 0:HEAD, cols]) * (SCALE * LOG2E)
            top = jnp.max(scores, axis=0, keepdims=True)
            exps = jnp.exp2(scores - top)
            total = jnp.sum(exps, axis=0, keepdims=True)
            out = dot(qkv_in[m, 2 * HEAD :, :], exps.astype(BF)) / total
            full_ref[m, :, cols] = out
            lse_ref[m, :, cols] = top + jnp.log2(total)
            low[m, :, cols] = out.astype(BF)
            for i in range(block // width):
                c = j * (block // width) + i
                pl.when(p.ctx != c)(lambda c=c: to_owner(m, c).start())

        keep_full[m].start()
        att[pl.ds(pl.multiple_of(p.ctx * HEAD, HEAD), HEAD), m * width : (m + 1) * width] = low[
            m, :, pl.ds(pl.multiple_of(p.ctx * width, width), width)
        ]
        if m == 0:
            for t in range(2):
                crossing[t].wait_recv()
                twins[t].start()

    for m in range(micro):

        @pl.loop(1, 16)
        def _(d, m=m):
            c = ring_peer(p, d)
            push(
                low.at[m, :, 0:width],
                att.at[pl.ds(pl.multiple_of(c * HEAD, HEAD), HEAD), m * width : (m + 1) * width],
                back_s.at[m, 0], back_r.at[m, c], {"ctx": c},
            ).wait_recv()
            for part in range(3):
                to_head(m, d, part).wait_send()
            to_owner(m, c).wait_send()

    crossing[2].wait_recv()
    for copy in crossing:
        copy.wait_send()
    for copy in twins + placing + keep_qkv + keep_full + out:
        copy.wait()
    for copy in sent:
        copy.wait_send()


def front(qkv_w, time_w, table, gains, tokens, levels, cosine, sine, up_w, out_w, cot, micro, block):
    dma = pltpu.SemaphoreType.DMA
    vmem = pl.BlockSpec(memory_space=pltpu.VMEM)
    anywhere = pl.BlockSpec(memory_space=pltpu.HBM)
    shape = jax.ShapeDtypeStruct
    rows, model = tokens.shape
    length = rows // micro * 16
    columns = up_w.shape[1] // 2
    width = qkv_w.shape[1] // 2
    blocks = width // 128
    far_time = (16, time_w.shape[0] // 16, time_w.shape[1])
    outs = pl.pallas_call(
        functools.partial(front_kernel, block),
        out_shape=[
            shape((2,) + qkv_w.shape, BF),
            shape((2,) + time_w.shape, BF),
            shape((2,) + table.shape, BF),
            shape((2,) + gains.shape, BF),
            shape((rows, model), F32),
            shape((rows, model), F32),
            shape((micro, 3 * HEAD, length), BF),
            shape((model, rows), BF),
            shape((micro, HEAD, length), F32),
            shape((micro, 1, length), F32),
            shape((2, up_w.shape[0], columns), BF),
            shape((2,) + out_w.shape, BF),
            shape((2,) + cot.shape, BF),
        ],
        in_specs=[anywhere, anywhere] + [vmem] * 6 + [anywhere] * 3,
        out_specs=[anywhere, anywhere, vmem, vmem, vmem, vmem, anywhere, vmem, anywhere, vmem] + [anywhere] * 3,
        scratch_shapes=[
            pltpu.VMEM((2, qkv_w.shape[0], width), BF),
            pltpu.VMEM(time_w.shape, BF),
            pltpu.VMEM((2, 16, qkv_w.shape[0] // 16, width), BF),
            pltpu.VMEM(far_time, BF),
            pltpu.VMEM((rows, model), F32),
            pltpu.VMEM((rows, table.shape[1]), BF),
            pltpu.VMEM((rows, model), BF),
            pltpu.VMEM((qkv_w.shape[1], rows), BF),
            pltpu.VMEM((micro, 3 * HEAD, length), BF),
            pltpu.VMEM((micro, HEAD, length), F32),
            pltpu.VMEM((length, HEAD), BF),
            pltpu.VMEM((micro, HEAD, length), BF),
            pltpu.VMEM(up_w.shape, BF),
            pltpu.VMEM(out_w.shape, BF),
            pltpu.VMEM(cot.shape, BF),
            dma((2, blocks)),
            dma((2, 2, blocks)),
            dma((3,)),
            dma((5,)),
            dma((5,)),
            dma((2, micro)),
            dma((micro, 3)),
            dma((micro, 16, 3)),
            dma((micro, 16, 3)),
            dma((micro, 16)),
            dma((micro, 16)),
            dma((3,)),
            dma((3,)),
            dma((3,)),
            dma((3,)),
            dma((2,)),
            dma((2,)),
        ] + Gather.semaphores(3),
        compiler_params=pltpu.CompilerParams(
            collective_id=1, has_side_effects=True, vmem_limit_bytes=50 << 20
        ),
        name="front",
    )(qkv_w, time_w, table, gains, tokens, levels, cosine, sine, up_w, out_w, cot)
    qkv_all, time_all, table_all, gain_all, scale_one, scale_two, *attention, up_all, out_all, cot_all = outs
    return (
        qkv_all.reshape(-1, qkv_w.shape[1]),
        time_all.reshape(-1, time_w.shape[1]),
        table_all.reshape(-1, table.shape[1]),
        jnp.transpose(gain_all, (1, 0, 2)).reshape(gains.shape[0], -1),
        scale_one, scale_two, *attention,
        up_all.reshape(-1, columns), out_all.reshape(-1, model), cot_all.reshape(-1, model),
    )


def mid_kernel(
    att, tokens, scale_two, g_two, w_out, w_up, w_down, cot,
    out_part, out_other, grad_t, grad_mid, grad_scale, gain_two, up_term, down_term, out_term,
    middle, hat, scales, rows_two, hidden, grad_pre, far, far_grad, near_grad,
    go_s, go_r, back_s, back_r,
):
    p = Place()
    rows, model = tokens.shape
    half = rows // 2
    barrier = pltpu.get_barrier_semaphore()
    pl.semaphore_signal(barrier, inc=1, device_id=p.pair, device_id_type=MESH)

    def to_pair(m):
        part = pl.ds(pl.multiple_of(m * half, half), half)
        there = pl.ds(pl.multiple_of(rows + m * half, half), half)
        return push(rows_two.at[part], rows_two.at[there], go_s.at[m], go_r.at[m], p.pair)

    def to_owner(m):
        part = pl.ds(pl.multiple_of(m * half, half), half)
        return push(far.at[part], far_grad.at[part], back_s.at[m], back_r.at[m], p.pair)

    weight = g_two[...] * scale_two[...]
    for m in range(2):
        part = slice(m * half, (m + 1) * half)
        middle[part] = tokens[part].astype(F32) + dot(att[:, part], w_out[...], 0, 0)
        normal, scale = normed(middle[part])
        hat[part] = normal
        scales[part] = scale
        rows_two[part] = (normal * weight[part]).astype(BF)
        if m == 0:
            pl.semaphore_wait(barrier, 1)
        to_pair(m).start()

    wide = 512

    def chunk(k):
        return pl.ds(pl.multiple_of(k * wide, wide), wide)

    def feed(part):
        @pl.loop(0, w_up.shape[1] // wide)
        def _(k):
            cols = chunk(k)
            pre = dot(rows_two[part], w_up[:, cols])
            cdf = 0.5 * (1.0 + lax.erf(pre * (2.0**-0.5)))
            hidden[part, cols] = (pre * cdf).astype(BF)
            density = jnp.exp(-0.5 * pre * pre) * (1.0 / math.sqrt(2.0 * math.pi))
            grad_pre[part, cols] = (dot(cot[part], w_down[cols, :], 1, 1) * (cdf + pre * density)).astype(BF)

    feed(slice(0, rows))

    @pl.loop(0, 2)
    def _(m):
        to_pair(m).wait_recv()
        there = pl.ds(pl.multiple_of(rows + m * half, half), half)
        feed(there)
        far[pl.ds(pl.multiple_of(m * half, half), half)] = dot(grad_pre[there], w_up[...], 1, 1).astype(BF)
        to_owner(m).start()

    @pl.loop(0, model // wide)
    def _(k):
        cols = chunk(k)
        near_grad[:, cols] = dot(grad_pre[0:rows], w_up[cols, :], 1, 1)

    @pl.loop(0, up_term.shape[1] // wide)
    def _(k):
        cols = chunk(k)
        up_term[:, cols] = dot(rows_two[...], grad_pre[:, cols], 0, 0).astype(BF)
        down_term[cols, :] = dot(hidden[:, cols], cot[...], 0, 0).astype(BF)

    @pl.loop(0, model // wide)
    def _(k):
        cols = chunk(k)
        both = dot(hidden[...], w_down[:, cols])
        out_part[:, cols] = middle[:, cols] + both[:rows]
        out_other[:, cols] = both[rows:].astype(BF)


    for m in range(2):
        to_owner(m).wait_recv()
    grad = near_grad[...] + far_grad[...].astype(F32)
    mid = cot[0:rows].astype(F32) + norm_back(grad, hat[...], scales[...], weight)
    grad_mid[...] = mid
    low = mid.astype(BF)
    grad_t[...] = dot(w_out[...], low, 1, 1).astype(BF)
    eh = grad * hat[...]
    grad_scale[...] = (eh * g_two[...]).astype(BF)
    gain_two[...] = jnp.sum(eh * scale_two[...], axis=0, keepdims=True)
    out_term[...] = dot(att[...], low).astype(BF)
    for m in range(2):
        to_pair(m).wait_send()
        to_owner(m).wait_send()


def mid_pass(att, tokens, scale_two, g_two, w_out, w_up, w_down, cot):
    dma = pltpu.SemaphoreType.DMA
    vmem = pl.BlockSpec(memory_space=pltpu.VMEM)
    rows, model = tokens.shape
    hidden = w_up.shape[1]
    shape = jax.ShapeDtypeStruct
    return pl.pallas_call(
        mid_kernel,
        out_shape=[
            shape((rows, model), F32), shape((rows, model), BF), shape((model, rows), BF),
            shape((rows, model), F32), shape((rows, model), BF), shape((1, model), F32),
            shape((model, hidden), BF), shape((hidden, model), BF), shape((model, model), BF),
        ],
        in_specs=[vmem] * 8,
        out_specs=[vmem] * 9,
        scratch_shapes=[
            pltpu.VMEM((rows, model), F32),
            pltpu.VMEM((rows, model), F32),
            pltpu.VMEM((rows, 1), F32),
            pltpu.VMEM((2 * rows, model), BF),
            pltpu.VMEM((2 * rows, hidden), BF),
            pltpu.VMEM((2 * rows, hidden), BF),
            pltpu.VMEM((rows, model), BF),
            pltpu.VMEM((rows, model), BF),
            pltpu.VMEM((rows, model), F32),
            dma((2,)), dma((2,)), dma((2,)), dma((2,)),
        ],
        compiler_params=pltpu.CompilerParams(
            collective_id=5, has_side_effects=True, vmem_limit_bytes=60 << 20
        ),
        name="mid_pass",
    )(att, tokens, scale_two, g_two, w_out, w_up, w_down, cot)


ORDER = (3, 0, 2, 1)


def back_kernel(
    block, grad_t, qkv_in, full_ref, lse_ref, up_term, down_term, out_term, w_qkv,
    cosine, sine, tokens, levels_row, g_one, scale_one, grad_mid, grad_scale_two, gain_two,
    out_part, out_other, input_grad, layer_out, up_all, down_all, out_all, qkv_all, small_all,
    keys, values, g_in, dq, dq_low, dkv_low, delta, grad_qkv, w_hold, grad_norm_t,
    term, q_twin, q_pair, up_sum, down_sum, out_sum, out_pair, out_own, qkv_sum, small, small_in, small_pair, out_came, norm_t, hat, rs_one,
    own_s, in_s, in_r, back_s, back_r, w_s, q_ts, q_tr, q_ps, q_pr, cross_s, cross_r, local_s,
    small_s, small_r, small_x, spread_s, spread_r, *more,
):
    p = Place()
    micro, _, length = qkv_in.shape
    width = length // 16
    model = grad_t.shape[0]
    count = 3
    cut = 2 * count + 3
    halves = Halves(
        p, [lambda c: up_term.at[:, c], lambda c: down_term.at[c], lambda c: out_term.at[:, c]], more[:cut]
    )
    more = more[cut:]
    cut = 2 * count + 6
    f_line = Line(p, count, halves.mine, more[:cut])
    more = more[cut:]
    q_line = Line(p, 1, lambda t, z, y: term.at[p.wt, p.index(z, y, p.core)], more[:8])
    half = down_term.shape[1] // 2
    depth = term.shape[2]
    split = depth // 2
    g = Gather(
        p,
        [
            lambda c: up_all.at[p.wt, c],
            lambda c: up_all.at[1 - p.wt, c],
            lambda c: down_all.at[c, 0:half],
            lambda c: down_all.at[c, half:],
            lambda c: out_all.at[c],
            lambda c: qkv_all.at[c, 0:split],
            lambda c: qkv_all.at[c, split:],
        ],
        more[8:],
        wide=(),
    )
    fixed, late = (3, 2, 0, 4, 1), (5, 6)
    p.greet(everyone=True)

    def rows_of(part, c):
        return pl.ds(pl.multiple_of(part * model + c * HEAD, HEAD), HEAD)

    def lanes(c):
        return pl.ds(pl.multiple_of(c * width, width), width)

    def to_head(m, d):
        c = ring_peer(p, d)
        return push(
            grad_t.at[rows_of(0, c), m * width : (m + 1) * width],
            g_in.at[m, :, lanes(p.ctx)], in_s.at[m, d], in_r.at[m, d], {"ctx": c},
        )

    stay = [
        pltpu.make_async_copy(
            grad_t.at[rows_of(0, p.ctx), m * width : (m + 1) * width],
            g_in.at[m, :, lanes(p.ctx)], own_s.at[m],
        )
        for m in range(micro)
    ]
    layer_cross = push(out_other, out_came, cross_s.at[2], cross_r.at[2], p.pair)
    layer_cross.start()
    for m in range(micro):
        stay[m].start()

        @pl.loop(1, 16)
        def _(d, m=m):
            to_head(m, d).start()

        halves.begin(ORDER[m])
    for z in ORDER[micro:]:
        halves.begin(z)
    chunk = w_hold.shape[1]
    chunks = model // chunk

    normal, rs_one[...] = normed(tokens[...].astype(F32))
    hat[...] = normal
    norm_t[...] = (normal * (g_one[...] * scale_one[...])).T.astype(BF)

    def w_chunk(k):
        slot = lax.rem(k, 2)
        return pltpu.make_async_copy(
            w_qkv.at[pl.ds(pl.multiple_of(k * chunk, chunk), chunk)], w_hold.at[slot], w_s.at[slot]
        )

    w_chunk(jnp.int32(0)).start()
    w_chunk(jnp.int32(1)).start()
    for z in (3, 0):
        halves.halve(z)
        f_line.cross(z)

    def to_owner(m, c, part):
        source = dq_low.at[m] if part == 0 else dkv_low.at[m, part - 1]
        return push(
            source.at[:, lanes(c)],
            grad_qkv.at[rows_of(part, p.ctx), m * width : (m + 1) * width],
            back_s.at[m, c, part], back_r.at[m, p.ctx, part], {"ctx": c},
        )

    def send(m, c, part):
        pl.when(p.ctx != c)(lambda: to_owner(m, c, part).start())

    for m in range(micro):
        keys[...] = qkv_in[m, HEAD : 2 * HEAD, :].T
        values[...] = qkv_in[m, 2 * HEAD :, :].T
        stay[m].wait()

        @pl.loop(1, 16)
        def _(d, m=m):
            to_head(m, d).wait_recv()

        delta[...] = jnp.sum(g_in[m].astype(F32) * full_ref[m], axis=0, keepdims=True)
        dq[...] = jnp.zeros_like(dq)

        @pl.loop(0, length // block)
        def _(step, m=m):
            j = lax.rem(step + lax.div(p.ctx * width, block), length // block)
            cols = pl.ds(pl.multiple_of(j * block, block), block)
            scores = dot(keys[cols, :], qkv_in[m, 0:HEAD, :]) * (SCALE * LOG2E)
            soft = jnp.exp2(scores - lse_ref[m])
            grad_soft = dot(values[cols, :], g_in[m])
            raw = (soft * (grad_soft - delta[...]) * SCALE).astype(BF)
            dkv_low[m, 0, :, cols] = dot(qkv_in[m, 0:HEAD, :], raw, 1, 1).astype(BF)
            dkv_low[m, 1, :, cols] = dot(g_in[m], soft.astype(BF), 1, 1).astype(BF)
            dq[...] += dot(qkv_in[m, HEAD : 2 * HEAD, cols], raw)
            for i in range(block // width):
                send(m, j * (block // width) + i, 1)
                send(m, j * (block // width) + i, 2)
            if m == micro - 1:

                @pl.when((step + 1) * block * 2 == length)
                def _():
                    f_line.quarter(3)
                    f_line.right(3, 0)

        dq_low[m] = dq[...].astype(BF)

        @pl.loop(1, 16)
        def _(d, m=m):
            to_owner(m, ring_peer(p, d), 0).start()

        if m == 0:
            halves.halve(2)
            halves.halve(1)
        here = lanes(p.ctx)
        to = slice(m * width, (m + 1) * width)
        grad_qkv[rows_of(0, p.ctx), to] = dq_low[m, :, here]
        grad_qkv[rows_of(1, p.ctx), to] = dkv_low[m, 0, :, here]
        grad_qkv[rows_of(2, p.ctx), to] = dkv_low[m, 1, :, here]

    f_line.cross(2)
    f_line.cross(1)
    layer_cross.wait()
    layer_out[...] = (out_part[...] + out_came[...].astype(F32)).astype(BF)
    f_line.quarter(0)
    f_line.left(0, 3)
    f_line.right(3, 1)
    f_line.left(0, 2)

    for m in range(micro):

        @pl.loop(1, 16)
        def _(d, m=m):
            c = ring_peer(p, d)
            for part in range(3):
                push(
                    dq_low.at[m, :, 0:width],
                    grad_qkv.at[rows_of(part, c), m * width : (m + 1) * width],
                    back_s.at[m, 0, part], back_r.at[m, c, part], {"ctx": c},
                ).wait_recv()

    low_half = HEAD // 2

    @pl.loop(0, 2 * model // HEAD)
    def _(h):
        upper = pl.ds(pl.multiple_of(h * HEAD, HEAD), low_half)
        lower = pl.ds(pl.multiple_of(h * HEAD + low_half, low_half), low_half)
        first, second = grad_qkv[upper, :].astype(F32), grad_qkv[lower, :].astype(F32)
        grad_qkv[upper, :] = (first * cosine[...] + second * sine[...]).astype(BF)
        grad_qkv[lower, :] = (second * cosine[...] - first * sine[...]).astype(BF)


    group = 4 * depth

    def q_to_twin(w, z, y):
        return push(
            term.at[w, p.index(z, y, 1 - p.core)], q_twin.at[w, z, y], q_ts.at[w, z, y], q_tr.at[w, z, y], p.twin
        )

    def q_to_pair(z, y):
        return push(
            term.at[1 - p.wt, p.index(z, y, p.core)], q_pair.at[z, y], q_ps.at[z, y], q_pr.at[z, y], p.pair
        )

    def with_twin(w, z, y):
        q_to_twin(w, z, y).wait_recv()
        here = p.index(z, y, p.core)
        term[w, here] = (term[w, here].astype(F32) + q_twin[w, z, y].astype(F32)).astype(BF)

    def product(w, z):
        start_row = pl.multiple_of(w * (model // 2) + z * group, group)
        rows = dot(norm_t[pl.ds(start_row, group), :], grad_qkv[...], 1, 1).astype(BF)
        for i in range(4):
            term[w, 4 * z + i] = rows[i * depth : (i + 1) * depth]
        for y in range(2):
            q_to_twin(w, z, y).start()

    def by_order(step):
        odd = lax.rem(step, 2)
        return (1 - odd) * (DEPTH - 1 - lax.div(step, 2)) + odd * lax.div(step, 2)

    @pl.loop(0, DEPTH)
    def _(step):
        product(1 - p.wt, by_order(step))

    f_line.right(3, 2)
    f_line.left(0, 1)

    @pl.loop(0, 2 * DEPTH)
    def _(step):
        z, y = by_order(lax.div(step, 2)), lax.rem(step, 2)
        with_twin(1 - p.wt, z, y)
        q_to_pair(z, y).start()

    @pl.loop(0, DEPTH)
    def _(step):
        product(p.wt, by_order(step))


    @pl.loop(0, chunks)
    def _(k):
        w_chunk(k).wait()
        grad_norm_t[pl.ds(pl.multiple_of(k * chunk, chunk), chunk), :] = dot(w_hold[lax.rem(k, 2)], grad_qkv[...])
        pl.when(k + 2 < chunks)(lambda: w_chunk(k + 2).start())

    grad_norm = grad_norm_t[...].T
    c_rows = grad_norm * (g_one[...] * scale_one[...])
    input_grad[...] = (
        grad_mid[...]
        + (
            c_rows
            - jnp.mean(c_rows, axis=-1, keepdims=True)
            - hat[...] * jnp.mean(c_rows * hat[...], axis=-1, keepdims=True)
        )
        * rs_one[...]
    ).astype(BF)
    eh = grad_norm * hat[...]
    grad_scale_one = (eh * g_one[...]).astype(BF)
    gain_one = jnp.sum(eh * scale_one[...], axis=0, keepdims=True)

    levels = LEVELS
    marks = lax.broadcasted_iota(jnp.int32, (levels, levels_row.shape[1]), 0)
    onehot_t = (marks == levels_row[...]).astype(F32).astype(BF)
    fill = jnp.zeros((small.shape[1] - levels - 1, 128), BF)
    for side, shifts, gain in ((0, grad_scale_one, gain_one), (1, grad_scale_two[...], gain_two[...])):
        level = dot(onehot_t, shifts).astype(BF)
        for k in range(8):
            cols = slice(k * 128, (k + 1) * 128)
            small[8 * side + k, 0:levels, :] = level[:, cols]
            small[8 * side + k, levels:, :] = jnp.concatenate([gain[:, cols].astype(BF), fill])

    def small_to(d):
        peer = ring_peer(p, d)
        return push(small.at[peer], small_in.at[p.ctx], small_s.at[d], small_r.at[d], {"ctx": peer})


    @pl.loop(1, 16)
    def _(d):
        small_to(d).start()

    small_in[p.ctx] = small[p.ctx]

    @pl.loop(0, 2 * DEPTH)
    def _(step):
        with_twin(p.wt, by_order(lax.div(step, 2)), lax.rem(step, 2))


    out_cross = push(out_sum.at[1 - p.wt], out_pair, cross_s.at[0], cross_r.at[0], p.pair)
    up_cross = push(up_sum.at[1 - p.wt], up_all.at[p.wt, p.ctx], cross_s.at[1], cross_r.at[1], p.pair)
    up_came = push(up_sum.at[p.wt], up_all.at[1 - p.wt, p.ctx], cross_s.at[1], cross_r.at[1], p.pair)
    sources = {0: up_sum.at[p.wt], 2: down_sum.at[0:half], 3: down_sum.at[half:], 4: out_own,
               5: qkv_sum.at[0:split], 6: qkv_sum.at[split:]}

    def f_end(z):
        @pl.when(p.z == z)
        def _():
            f_line.end(z, [up_sum, down_sum, out_sum])
            out_cross.start()
            up_cross.start()

    def q_cross(z):
        for y in (1 - p.y, p.y):
            q_to_pair(z, y).wait_recv()
            here = p.index(z, y, p.core)
            term[p.wt, here] = (term[p.wt, here].astype(F32) + q_pair[z, y].astype(F32)).astype(BF)
        q_line.cross(z)

    f_line.quarter(2)
    f_line.right(2, 0)
    q_cross(3)
    f_line.right(2, 1)
    f_line.quarter(1)
    f_line.left(1, 3)
    f_line.right(1, 0)
    f_line.left(2, 3)
    q_cross(0)
    q_line.quarter(3)
    q_line.right(3, 0)
    f_line.left(1, 2)
    q_cross(2)
    q_line.quarter(0)
    q_line.left(0, 3)
    q_line.right(3, 1)
    q_line.left(0, 2)
    q_cross(1)
    q_line.right(3, 2)
    q_line.left(0, 1)
    q_line.quarter(2)
    q_line.right(2, 0)
    q_line.quarter(1)
    q_line.left(1, 3)
    q_line.right(1, 0)
    q_line.left(2, 3)
    for z in range(DEPTH):
        f_end(z)

    @pl.loop(1, 16)
    def _(d):
        small_to(d).wait_recv()

    small_pair[0] = jnp.sum(small_in[...].astype(F32), axis=0).astype(BF)
    small_cross = push(small_pair.at[0], small_pair.at[1], small_x.at[0], small_x.at[1], p.pair)
    small_cross.start()
    q_line.right(2, 1)
    q_line.left(1, 2)

    for t in (3, 2, 0):
        g.own(t, sources[t])
    out_cross.wait_recv()
    out_own[...] = (out_sum[p.wt].astype(F32) + out_pair[...].astype(F32)).astype(BF)
    g.own(4, sources[4])
    up_came.wait_recv()
    g.own(1)
    for z in range(DEPTH):
        pl.when(p.z == z)(lambda z=z: q_line.end(z, [qkv_sum]))
    for t in late:
        g.own(t, sources[t])

    small_cross.wait()
    small_all[p.ctx] = (small_pair[0].astype(F32) + small_pair[1].astype(F32)).astype(BF)

    def small_spread(d):
        peer = ring_peer(p, d)
        return push(small_all.at[p.ctx], small_all.at[p.ctx], spread_s.at[d], spread_r.at[d], {"ctx": peer})


    @pl.loop(1, 16)
    def _(d):
        small_spread(d).start()

    copies = [pltpu.make_async_copy(sources[t], g.items[t](p.ctx), local_s.at[t]) for t in sources]
    for copy in copies:
        copy.start()
    every = fixed + late
    for t in every:
        g.along(t, 1)
    for t in every:
        g.along(t, 2)
    for t in every:
        if t not in g.wide:
            g.crossed_at(t, 0)
    for t in every:
        g.along(t, 3)
    for d in (1, 2, 3):
        for t in every:
            g.crossed_at(t, d)

    for copy in copies:
        copy.wait()
    for t in range(len(g.items)):
        g.finish(t)
    halves.finish()
    f_line.finish()
    q_line.finish()
    out_cross.wait_send()
    up_cross.wait_send()

    @pl.loop(1, 16)
    def _(d):
        small_to(d).wait_send()
        small_spread(d).wait()

    for z in range(DEPTH):
        for y in range(2):
            q_to_pair(z, y).wait_send()
            for w in range(2):
                q_to_twin(w, z, y).wait_send()
    for m in range(micro):

        @pl.loop(1, 16)
        def _(d, m=m):
            to_head(m, d).wait_send()
            for part in range(3):
                to_owner(m, ring_peer(p, d), part).wait_send()


def back_pass(grad_t, qkv_in, full, lse, up, down, out, w_qkv, rest, block):
    dma = pltpu.SemaphoreType.DMA
    vmem = pl.BlockSpec(memory_space=pltpu.VMEM)
    anywhere = pl.BlockSpec(memory_space=pltpu.HBM)
    micro, _, length = qkv_in.shape
    model, rows = grad_t.shape
    pieces = [up.shape[:1] + up.shape[2:], down.shape[1:], out.shape[:1] + out.shape[2:]]
    piece = (model // 32, 3 * model)
    small = (16, 80, 128)
    return pl.pallas_call(
        functools.partial(back_kernel, block),
        out_shape=[
            jax.ShapeDtypeStruct((rows, model), BF),
            jax.ShapeDtypeStruct((rows, model), BF),
            jax.ShapeDtypeStruct((2, 16) + up.shape[2:], BF),
            jax.ShapeDtypeStruct(down.shape, BF),
            jax.ShapeDtypeStruct(out.shape[1:], BF),
            jax.ShapeDtypeStruct((16,) + piece, BF),
            jax.ShapeDtypeStruct(small, BF),
        ],
        in_specs=[vmem] * 4 + [anywhere] * 4 + [vmem] * len(rest),
        out_specs=[vmem] * 2 + [anywhere] * 4 + [vmem],
        scratch_shapes=[
            pltpu.VMEM((length, HEAD), BF),
            pltpu.VMEM((length, HEAD), BF),
            pltpu.VMEM((micro, HEAD, length), BF),
            pltpu.VMEM((HEAD, length), F32),
            pltpu.VMEM((micro, HEAD, length), BF),
            pltpu.VMEM((micro, 2, HEAD, length), BF),
            pltpu.VMEM((1, length), F32),
            pltpu.VMEM((3 * model, rows), BF),
            pltpu.VMEM((2, 128, 3 * model), BF),
            pltpu.VMEM((model, rows), F32),
            pltpu.VMEM((2, 16) + piece, BF),
            pltpu.VMEM((2, DEPTH, 2) + piece, BF),
            pltpu.VMEM((DEPTH, 2) + piece, BF),
            pltpu.VMEM(pieces[0], BF),
            pltpu.VMEM(pieces[1], BF),
            pltpu.VMEM(pieces[2], BF),
            pltpu.VMEM(pieces[2][1:], BF),
            pltpu.VMEM(pieces[2][1:], BF),
            pltpu.VMEM(piece, BF),
            pltpu.VMEM(small, BF),
            pltpu.VMEM(small, BF),
            pltpu.VMEM((2,) + small[1:], BF),
            pltpu.VMEM((rows, model), BF),
            pltpu.VMEM((model, rows), BF),
            pltpu.VMEM((rows, model), F32),
            pltpu.VMEM((rows, 1), F32),
            dma((micro,)),
            dma((micro, 16)),
            dma((micro, 16)),
            dma((micro, 16, 3)),
            dma((micro, 16, 3)),
            dma((2,)),
            dma((2, DEPTH, 2)),
            dma((2, DEPTH, 2)),
            dma((DEPTH, 2)),
            dma((DEPTH, 2)),
            dma((3,)),
            dma((3,)),
            dma((7,)),
            dma((16,)),
            dma((16,)),
            dma((2,)),
            dma((16,)),
            dma((16,)),
        ]
        + Halves.scratch(pieces)
        + Line.scratch(pieces)
        + Line.scratch([piece])
        + Gather.semaphores(7),
        compiler_params=pltpu.CompilerParams(
            collective_id=4, has_side_effects=True, vmem_limit_bytes=63 << 20
        ),
        name="back_pass",
    )(grad_t, qkv_in, full, lse, up, down, out, w_qkv, *rest)


def spread(source, pieces, first, target):
    width = source.shape[-1]
    for c in range(pieces):
        target[:, c * width : (c + 1) * width] = source[c, 0, first : first + HEAD, :]


def attend_kernel(pieces, block, qkv_ref, low_ref, full_ref, lse_ref, q_t, k_t, v_t, keys):
    length = q_t.shape[1]
    width = length // pieces
    spread(qkv_ref, pieces, 0, q_t)
    spread(qkv_ref, pieces, HEAD, k_t)
    spread(qkv_ref, pieces, 2 * HEAD, v_t)
    keys[...] = k_t[...].T
    for j in range(length // block):
        cols = slice(j * block, (j + 1) * block)
        scores = dot(keys[...], q_t[:, cols]) * (SCALE * LOG2E)
        top = jnp.max(scores, axis=0, keepdims=True)
        exps = jnp.exp2(scores - top)
        total = jnp.sum(exps, axis=0, keepdims=True)
        out = dot(v_t[...], exps.astype(BF)) / total
        full_ref[0, :, cols] = out
        lse_ref[0, :, cols] = top + jnp.log2(total)
        for c in range(block // width):
            low_ref[j * (block // width) + c, 0] = out[:, c * width : (c + 1) * width].astype(BF)


def attend(qkv, block):
    pieces, pairs, _, width = qkv.shape
    length = pieces * width
    return pl.pallas_call(
        functools.partial(attend_kernel, pieces, block),
        grid=(pairs,),
        in_specs=[pl.BlockSpec((pieces, 1, 3 * HEAD, width), lambda p: (0, p, 0, 0))],
        out_specs=[
            pl.BlockSpec((pieces, 1, HEAD, width), lambda p: (0, p, 0, 0)),
            pl.BlockSpec((1, HEAD, length), lambda p: (p, 0, 0)),
            pl.BlockSpec((1, 1, length), lambda p: (p, 0, 0)),
        ],
        out_shape=[
            jax.ShapeDtypeStruct((pieces, pairs, HEAD, width), BF),
            jax.ShapeDtypeStruct((pairs, HEAD, length), F32),
            jax.ShapeDtypeStruct((pairs, 1, length), F32),
        ],
        scratch_shapes=[pltpu.VMEM((HEAD, length), BF)] * 3 + [pltpu.VMEM((length, HEAD), BF)],
        compiler_params=pltpu.CompilerParams(vmem_limit_bytes=48 << 20),
        name="attend",
    )(qkv)


def attend_back_kernel(
    pieces, block, qkv_ref, grad_ref, full_ref, lse_ref, out_ref,
    q_t, k_t, v_t, g_t, keys, values, dq_t, dk, dv,
):
    length = q_t.shape[1]
    width = length // pieces
    spread(qkv_ref, pieces, 0, q_t)
    spread(qkv_ref, pieces, HEAD, k_t)
    spread(qkv_ref, pieces, 2 * HEAD, v_t)
    spread(grad_ref, pieces, 0, g_t)
    keys[...] = k_t[...].T
    values[...] = v_t[...].T
    for j in range(length // block):
        cols = slice(j * block, (j + 1) * block)
        query = q_t[:, cols]
        grad = g_t[:, cols]
        delta = jnp.sum(grad.astype(F32) * full_ref[0, :, cols], axis=0, keepdims=True)
        scores = dot(keys[...], query) * (SCALE * LOG2E)
        soft = jnp.exp2(scores - lse_ref[0, :, cols])
        term_v = dot(soft.astype(BF), grad, 1, 1)
        grad_soft = dot(values[...], grad)
        raw = (soft * (grad_soft - delta) * SCALE).astype(BF)
        term_k = dot(raw, query, 1, 1)
        dq_t[:, cols] = dot(k_t[...], raw)
        if j == 0:
            dv[...] = term_v
            dk[...] = term_k
        else:
            dv[...] += term_v
            dk[...] += term_k
    dk_t = dk[...].T.astype(BF)
    dv_t = dv[...].T.astype(BF)
    for c in range(pieces):
        piece = slice(c * width, (c + 1) * width)
        out_ref[c, 0, 0:HEAD, :] = dq_t[:, piece].astype(BF)
        out_ref[c, 0, HEAD : 2 * HEAD, :] = dk_t[:, piece]
        out_ref[c, 0, 2 * HEAD :, :] = dv_t[:, piece]


def attend_back(qkv, grad, full, lse, block):
    pieces, pairs, _, width = qkv.shape
    length = pieces * width
    return pl.pallas_call(
        functools.partial(attend_back_kernel, pieces, block),
        grid=(pairs,),
        in_specs=[
            pl.BlockSpec((pieces, 1, 3 * HEAD, width), lambda p: (0, p, 0, 0)),
            pl.BlockSpec((pieces, 1, HEAD, width), lambda p: (0, p, 0, 0)),
            pl.BlockSpec((1, HEAD, length), lambda p: (p, 0, 0)),
            pl.BlockSpec((1, 1, length), lambda p: (p, 0, 0)),
        ],
        out_specs=pl.BlockSpec((pieces, 1, 3 * HEAD, width), lambda p: (0, p, 0, 0)),
        out_shape=jax.ShapeDtypeStruct(qkv.shape, BF),
        scratch_shapes=[pltpu.VMEM((HEAD, length), BF)] * 4
        + [pltpu.VMEM((length, HEAD), BF)] * 2
        + [pltpu.VMEM((HEAD, length), F32)]
        + [pltpu.VMEM((length, HEAD), F32)] * 2,
        compiler_params=pltpu.CompilerParams(vmem_limit_bytes=56 << 20),
        name="attend_back",
    )(qkv, grad, full, lse)


def normed(rows):
    centered = rows - jnp.mean(rows, axis=-1, keepdims=True)
    scale = lax.rsqrt(jnp.mean(centered * centered, axis=-1, keepdims=True) + EPSILON)
    return centered * scale, scale


def norm_back(grad, hat, scale, weight):
    c = grad * weight
    return (
        c - jnp.mean(c, axis=-1, keepdims=True) - hat * jnp.mean(c * hat, axis=-1, keepdims=True)
    ) * scale


def turn(first, second, cosine, sine):
    return first * cosine - second * sine, second * cosine + first * sine


def shards(
    tokens, positions, buckets, qkv_w, out_w, up_w, down_w, time_w, noise_table,
    gain_one, gain_two, cotangent,
):
    n, ring = lax.axis_size("wt"), lax.axis_size("ctx")
    me = lax.axis_index("wt")
    micro, _, width, model = tokens.shape
    rows = micro * width
    pairs = HEADS * micro // ring
    block = 256
    planar = n == 2 and ring == 16

    x = tokens.reshape(rows, model).astype(F32)
    cot_low = cotangent.reshape(rows, model)
    places = positions.reshape(rows)
    levels = buckets.reshape(rows)

    def whole_rows(weight):
        return lax.all_gather(weight, "wt", axis=0, tiled=True)

    frequency = jnp.exp(
        jnp.arange(HEAD // 2, dtype=F32) * (-math.log(10000.0) * 2.0 / HEAD)
    )
    angles = frequency[:, None] * places.astype(F32)[None, :]
    cosine, sine = jnp.cos(angles), jnp.sin(angles)
    stacked = jnp.stack([gain_one, gain_two])
    if planar:
        (
            w_qkv, w_time, table, gains, scale_one, scale_two, qkv_heads, attended, full, lse, w_up, w_out, cot,
        ) = front(
            qkv_w, time_w, noise_table, stacked, tokens.reshape(rows, model), levels[:, None], cosine, sine,
            up_w, out_w, cot_low, micro, block,
        )
        g_one, g_two = gains[0].astype(F32), gains[1].astype(F32)
    else:
        w_qkv = whole_rows(qkv_w)
        w_out = whole_rows(out_w)
        w_time = whole_rows(time_w)
        table = whole_rows(noise_table)
        gains = lax.all_gather(stacked, "wt", axis=1, tiled=True)
        w_up = lax.all_to_all(up_w, "wt", 1, 0, tiled=True)
        g_one, g_two = gains[0].astype(F32), gains[1].astype(F32)

        onehot = levels[:, None] == jnp.arange(table.shape[0], dtype=jnp.int32)[None, :]
        embed = dot(onehot.astype(BF), table).astype(BF)
        shifts = dot(embed, w_time)
        scale_one = 1.0 + shifts[:, :model]
        scale_two = 1.0 + shifts[:, model:]

        hat_one, rs_one = normed(x)
        weight_one = g_one * scale_one
        norm_one = (hat_one * weight_one).astype(BF)

        qkv_t = dot(w_qkv, norm_one, 0, 1).reshape(3, HEADS, 2, HEAD // 2, rows)
        turned = turn(qkv_t[:2, :, 0], qkv_t[:2, :, 1], cosine, sine)
        queries_keys = jnp.stack(turned, axis=2)
        qkv_low = jnp.concatenate([queries_keys.astype(BF), qkv_t[2:].astype(BF)])

    def to_heads(columns):
        parts = columns.shape[0]
        split = columns.reshape(parts, HEADS, HEAD, micro, width)
        split = jnp.transpose(split, (1, 3, 0, 2, 4))
        split = split.reshape(ring, pairs, parts * HEAD, width)
        return lax.all_to_all(split, "ctx", 0, 0, tiled=True)

    def to_tokens(pieces):
        parts = pieces.shape[2] // HEAD
        back = lax.all_to_all(pieces, "ctx", 0, 0, tiled=True)
        back = back.reshape(HEADS, micro, parts, HEAD, width)
        return jnp.transpose(back, (2, 0, 3, 1, 4)).reshape(parts, HEADS * HEAD, rows)

    if not planar:
        qkv_heads = to_heads(qkv_low.reshape(3, HEADS, HEAD, rows))
        low, full, lse = attend(qkv_heads, block)
        attended = to_tokens(low)[0]
        cot = gather_slots(cot_low).reshape(n * rows, model)

    if not planar:
        middle = x + dot(attended, w_out, 0, 0)
        hat_two, rs_two = normed(middle)
        weight_two = g_two * scale_two
        norm_two_own = (hat_two * weight_two).astype(BF)

        norm_two = gather_slots(norm_two_own).reshape(n * rows, model)
        pre = dot(norm_two, w_up)
        phi_cdf = 0.5 * (1.0 + lax.erf(pre * (2.0**-0.5)))
        hidden = (pre * phi_cdf).astype(BF)
        out_parts = dot(hidden, down_w).reshape(n, rows, model)

        grad_hidden = dot(cot, down_w, 1, 1)
        density = jnp.exp(-0.5 * pre * pre) * (1.0 / math.sqrt(2.0 * math.pi))
        grad_pre = (grad_hidden * (phi_cdf + pre * density)).astype(BF)
        grad_norm_two = sum_slots(dot(grad_pre, w_up, 1, 1).reshape(n, rows, model))
        down_term = dot(hidden, cot, 0, 0).astype(BF)
        up_term = dot(norm_two, grad_pre, 0, 0).astype(BF)
        grad_mid = cot_low.astype(F32) + norm_back(grad_norm_two, hat_two, rs_two, weight_two)
        grad_branch = grad_mid.astype(BF)
        eh_two = grad_norm_two * hat_two
        grad_scale_two = eh_two * g_two
        gain_two_term = jnp.sum(eh_two * scale_two, axis=0)
        out_term = dot(attended, grad_branch, 1, 0).astype(BF)
        grad_attn = dot(w_out, grad_branch, 1, 1).astype(BF)

    if planar:

        def pieces_of(array, *lead):
            return array.reshape(lead + (-1, array.shape[-1]))

        (
            out_part, out_other, grad_attn, grad_mid, grad_scale_two, gain_two_term, up_term, down_term, out_term,
        ) = mid_pass(attended, tokens.reshape(rows, model), scale_two, g_two[None], w_out, w_up, down_w, cot)
        rest = (
            cosine, sine, tokens.reshape(rows, model), levels[None], g_one[None], scale_one, grad_mid,
            grad_scale_two, gain_two_term, out_part, out_other,
        )
        input_grad, layer_out, up_all, down_all, out_all, qkv_all, small_all = back_pass(
            grad_attn, qkv_heads, full, lse, pieces_of(up_term, n, ring), pieces_of(down_term, ring),
            pieces_of(out_term, n, ring), w_qkv, rest, block,
        )
        time_here = time_w.shape[0]
        table_rows = lax.dynamic_slice_in_dim(table, me * time_here, time_here, 1)
        (
            up_grad, down_grad, out_grad, qkv_grad, time_grad, table_grad, gain_one_grad, gain_two_grad,
            input_grad, layer_out,
        ) = widen(up_all, down_all, out_all, qkv_all, small_all, table_rows, w_time, input_grad, layer_out)
        gain_one_grad, gain_two_grad = gain_one_grad[0], gain_two_grad[0]
    else:
        layer_out = middle + sum_slots(out_parts)
        up_share = lax.psum_scatter(
            up_term.reshape(n, model // n, -1), "ctx", scatter_dimension=1, tiled=True
        )
        down_share = lax.psum_scatter(down_term, "ctx", scatter_dimension=0, tiled=True)
        out_share = lax.psum_scatter(
            out_term.reshape(n, model // n, model), "ctx", scatter_dimension=1, tiled=True
        )
        grad_heads = to_heads(grad_attn.reshape(1, HEADS, HEAD, rows))
        back = to_tokens(attend_back(qkv_heads, grad_heads, full, lse, block))
        back = back.reshape(3, HEADS, 2, HEAD // 2, rows)
        unturned = turn(back[:2, :, 0].astype(F32), back[:2, :, 1].astype(F32), cosine, -sine)
        grad_qkv = jnp.concatenate([jnp.stack(unturned, axis=2).astype(BF), back[2:]])
        grad_qkv = grad_qkv.reshape(3 * model, rows)
        qkv_term = dot(norm_one, grad_qkv, 0, 1).astype(BF)
        grad_norm_one = dot(grad_qkv, w_qkv, 0, 1)

        input_grad = grad_mid + norm_back(grad_norm_one, hat_one, rs_one, weight_one)
        eh_one = grad_norm_one * hat_one
        grad_scale_one = eh_one * g_one
        gain_one_term = jnp.sum(eh_one * scale_one, axis=0)

        grad_shifts = jnp.concatenate([grad_scale_one, grad_scale_two], axis=1).astype(BF)
        level_term = dot(onehot.astype(BF), grad_shifts, 0, 0)
        gain_terms = jnp.concatenate([gain_one_term, gain_two_term])
        small = lax.psum(jnp.concatenate([level_term, gain_terms[None]]), ("ctx", "wt"))
        share = lax.psum_scatter(
            qkv_term.reshape(n, model // n, -1), "ctx", scatter_dimension=1, tiled=True
        )

        def spread_rows(share):
            return lax.all_gather(share, "ctx", axis=0, tiled=True).astype(F32)

        up_share = lax.all_to_all(up_share, "wt", 0, 0, tiled=True)
        up_grad = lax.all_gather(up_share, "ctx", axis=1, tiled=True).astype(F32)
        up_grad = jnp.transpose(up_grad, (1, 0, 2)).reshape(model // n, -1)
        down_grad = spread_rows(down_share)
        out_grad = spread_rows(sum_owned(out_share))
        qkv_grad = spread_rows(sum_owned(share))

        by_level = small[: table.shape[0]]
        gain_sums = small[table.shape[0]]
        levels_here, time_here = noise_table.shape[0], time_w.shape[0]
        high = lax.Precision.HIGHEST
        time_rows = lax.dynamic_slice_in_dim(table, me * time_here, time_here, 1).astype(F32)
        time_grad = lax.dot_general(
            time_rows, by_level, (((0,), (0,)), ((), ())), precision=high, preferred_element_type=F32
        )
        level_rows = lax.dynamic_slice_in_dim(by_level, me * levels_here, levels_here, 0)
        table_grad = lax.dot_general(
            level_rows, w_time.astype(F32), (((1,), (1,)), ((), ())), precision=high,
            preferred_element_type=F32,
        )

        gain_here = gain_one.shape[0]
        gain_one_grad = lax.dynamic_slice_in_dim(gain_sums, me * gain_here, gain_here, 0)
        gain_two_grad = lax.dynamic_slice_in_dim(gain_sums, model + me * gain_here, gain_here, 0)

    return (
        layer_out.astype(BF).reshape(tokens.shape),
        input_grad.astype(BF).reshape(tokens.shape),
        qkv_grad,
        out_grad,
        up_grad,
        down_grad,
        time_grad,
        table_grad,
        gain_one_grad,
        gain_two_grad,
    )


def sum_owned(share):
    n, me = lax.axis_size("wt"), lax.axis_index("wt")
    slots = jnp.stack(
        [lax.dynamic_index_in_dim(share, lax.rem(me + k, n), 0, keepdims=False) for k in range(n)]
    )
    return sum_slots(slots.astype(F32)).astype(BF)


def solution(mesh):
    rows = P(None, "wt", "ctx", None)
    marks = P(None, "wt", "ctx")
    weight = P("wt", None)
    gain = P("wt")
    return jax.shard_map(
        shards,
        mesh=mesh,
        in_specs=(rows, marks, marks) + (weight,) * 6 + (gain, gain, rows),
        out_specs=(rows, rows) + (weight,) * 6 + (gain, gain),
        check_vma=False,
    )
```

```python
import functools
import math

import jax
import jax.numpy as jnp
from jax import lax
from jax.experimental import pallas as pl
from jax.experimental.pallas import tpu as pltpu
from jax.sharding import PartitionSpec as P

HEADS = 16
HEAD = 64
LEVELS = 64
EPSILON = 1e-05
SCALE = 0.125
LOG2E = math.log2(math.e)
BF = jnp.bfloat16
F32 = jnp.float32


def dot(a, b, ca=1, cb=0):
    return lax.dot_general(a, b, (((ca,), (cb,)), ((), ())), preferred_element_type=F32)


def swap_ring(value, places):
    n = lax.axis_size("wt")
    return lax.ppermute(value, "wt", [((i + places) % n, i) for i in range(n)])


def gather_slots(own):
    n = lax.axis_size("wt")
    return jnp.stack([own] + [swap_ring(own, k) for k in range(1, n)])


def sum_slots(partial):
    n = lax.axis_size("wt")
    total = partial[0]
    for k in range(1, n):
        total = total + swap_ring(partial[k].astype(BF), n - k).astype(F32)
    return total


MESH = pl.DeviceIdType.MESH
DEPTH = 4


class Place:
    def __init__(self):
        self.ctx = lax.axis_index("ctx")
        self.wt = lax.axis_index("wt")
        self.z = lax.div(self.ctx, 4)
        self.y = lax.rem(lax.div(self.ctx, 2), 2)
        self.core = lax.rem(self.ctx, 2)
        self.right = {"ctx": self.index(lax.min(self.z + 1, DEPTH - 1), self.y, self.core)}
        self.left = {"ctx": self.index(lax.max(self.z - 1, 0), self.y, self.core)}
        self.across = {"ctx": self.index(self.z, 1 - self.y, self.core)}
        self.twin = {"ctx": self.index(self.z, self.y, 1 - self.core)}
        self.pair = {"wt": 1 - self.wt}

    @staticmethod
    def index(z, y, core):
        return (z * 2 + y) * 2 + core

    def greet(self, everyone=False, pair=True):
        barrier = pltpu.get_barrier_semaphore()

        def signal(device):
            pl.semaphore_signal(barrier, inc=1, device_id=device, device_id_type=MESH)

        if everyone:

            @pl.loop(1, 16)
            def _(d):
                signal({"ctx": lax.rem(self.ctx + d, 16)})

            count = 15
        else:
            signal(self.across)
            signal(self.twin)
            pl.when(self.z > 0)(lambda: signal(self.left))
            pl.when(self.z < DEPTH - 1)(lambda: signal(self.right))
            inner = jnp.logical_and(self.z > 0, self.z < DEPTH - 1).astype(jnp.int32)
            count = 3 + inner
        if pair:
            signal(self.pair)
            count = count + 1
        pl.semaphore_wait(barrier, count)


def push(source, target, send, receive, device):
    return pltpu.make_async_remote_copy(
        src_ref=source, dst_ref=target, send_sem=send, recv_sem=receive,
        device_id=device, device_id_type=MESH,
    )


class Gather:
    def __init__(self, place, items, sems, wide=()):
        self.p, self.items, self.wide = place, items, wide
        (self.sl, self.sr, self.sy, self.sc, self.rz, self.ry, self.rc) = sems

    @staticmethod
    def semaphores(count):
        dma = pltpu.SemaphoreType.DMA
        line, square = dma((count, DEPTH)), dma((count, DEPTH, 2))
        return [square, square, line, square, square, line, square]

    def piece(self, t, z, y, core):
        return self.items[t](self.p.index(z, y, core))

    def copy(self, t, z, y, source, send, receive, device):
        here = self.piece(t, z, y, self.p.core)
        return push(here if source is None else source, here, send, receive, device)

    def rightward(self, t, z, source=None, far=0):
        y = 1 - self.p.y if far else self.p.y
        return self.copy(t, z, y, source, self.sr.at[t, z, far], self.rz.at[t, z, far], self.p.right)

    def leftward(self, t, z, source=None, far=0):
        y = 1 - self.p.y if far else self.p.y
        return self.copy(t, z, y, source, self.sl.at[t, z, far], self.rz.at[t, z, far], self.p.left)

    def crossing(self, t, z, source=None):
        return self.copy(t, z, self.p.y, source, self.sy.at[t, z], self.ry.at[t, z], self.p.across)

    def twinning(self, t, z, y, source=None):
        return self.copy(t, z, y, source, self.sc.at[t, z, y], self.rc.at[t, z, y], self.p.twin)

    def own(self, t, source=None):
        p = self.p
        pl.when(p.z < DEPTH - 1)(lambda: self.rightward(t, p.z, source).start())
        pl.when(p.z > 0)(lambda: self.leftward(t, p.z, source).start())
        self.crossing(t, p.z, source).start()
        self.twinning(t, p.z, p.y, source).start()

    def arrived(self, t, z, y, core, semaphore):
        piece = self.piece(t, z, y, core)
        push(piece, piece, semaphore, semaphore, self.p.twin).wait_recv()

    def arrive(self, t, z, far=0):
        p = self.p
        y = 1 - p.y if far else p.y
        self.arrived(t, z, y, p.core, self.rz.at[t, z, far])
        pl.when(jnp.logical_and(p.z > z, p.z < DEPTH - 1))(lambda: self.rightward(t, z, far=far).start())
        pl.when(jnp.logical_and(p.z < z, p.z > 0))(lambda: self.leftward(t, z, far=far).start())
        if t not in self.wide:
            self.crossing(t, z).start()
        self.twinning(t, z, y).start()

    def along(self, t, d):
        p = self.p
        for far in (0, 1) if t in self.wide else (0,):
            pl.when(p.z - d >= 0)(lambda far=far: self.arrive(t, p.z - d, far))
            pl.when(p.z + d < DEPTH)(lambda far=far: self.arrive(t, p.z + d, far))

    def crossed(self, t, z):
        self.arrived(t, z, 1 - self.p.y, self.p.core, self.ry.at[t, z])
        self.twinning(t, z, 1 - self.p.y).start()

    def crossed_at(self, t, d):
        p = self.p
        if t in self.wide:
            if d == 0:
                self.arrived(t, p.z, 1 - p.y, p.core, self.ry.at[t, p.z])
                pl.when(p.z < DEPTH - 1)(lambda: self.rightward(t, p.z, far=1).start())
                pl.when(p.z > 0)(lambda: self.leftward(t, p.z, far=1).start())
                self.twinning(t, p.z, 1 - p.y).start()
        elif d == 0:
            self.crossed(t, p.z)
        else:
            pl.when(p.z - d >= 0)(lambda: self.crossed(t, p.z - d))
            pl.when(p.z + d < DEPTH)(lambda: self.crossed(t, p.z + d))

    def finish(self, t):
        p = self.p
        wide = t in self.wide
        if wide:
            self.crossing(t, p.z).wait_send()
        for z in range(DEPTH):
            if not wide:
                self.crossing(t, z).wait_send()
            for y in range(2):
                self.twinning(t, z, y).wait_send()
                self.arrived(t, z, y, 1 - p.core, self.rc.at[t, z, y])
            for far in (0, 1) if wide else (0,):
                pl.when(jnp.logical_and(p.z >= z, p.z < DEPTH - 1))(
                    lambda z=z, far=far: self.rightward(t, z, far=far).wait_send()
                )
                pl.when(jnp.logical_and(p.z <= z, p.z > 0))(
                    lambda z=z, far=far: self.leftward(t, z, far=far).wait_send()
                )


class Line:
    def __init__(self, place, count, mine, refs):
        self.p, self.mine, self.terms = place, mine, range(count)
        self.from_across, self.slots = refs[:count], refs[count : 2 * count]
        self.ys, self.yr, self.rs, self.rr, self.vs, self.vr = refs[2 * count :]

    @staticmethod
    def scratch(shapes):
        line = pltpu.SemaphoreType.DMA((len(shapes), DEPTH))
        return (
            [pltpu.VMEM((DEPTH,) + shape, BF) for shape in shapes]
            + [pltpu.VMEM((DEPTH + 1,) + shape, BF) for shape in shapes]
            + [line] * 6
        )

    def across(self, t, z):
        return push(
            self.mine(t, z, 1 - self.p.y), self.from_across[t].at[z], self.ys.at[t, z], self.yr.at[t, z], self.p.across
        )

    def rightward(self, t, j, first):
        target = self.slots[t].at[j + 1]
        return push(self.from_across[t].at[j] if first else target, target, self.rs.at[t, j], self.rr.at[t, j], self.p.right)

    def leftward(self, t, j, first):
        target = self.slots[t].at[j]
        return push(self.from_across[t].at[j] if first else target, target, self.vs.at[t, j], self.vr.at[t, j], self.p.left)

    def cross(self, z):
        for t in self.terms:
            self.across(t, z).start()

    def quarter(self, z):
        for t in self.terms:
            self.across(t, z).wait_recv()
            both = self.mine(t, z, self.p.y)[...].astype(F32) + self.from_across[t][z].astype(F32)
            self.from_across[t][z] = both.astype(BF)

    def with_left(self, t, j):
        self.rightward(t, j, False).wait_recv()
        return self.from_across[t][j].astype(F32) + self.slots[t][j + 1].astype(F32)

    def with_right(self, t, j):
        self.leftward(t, j, False).wait_recv()
        return self.from_across[t][j].astype(F32) + self.slots[t][j].astype(F32)

    def right(self, j, z):
        @pl.when(self.p.z == z)
        def _():
            for t in self.terms:
                if z > 0:
                    self.slots[t][j + 1] = self.with_left(t, j).astype(BF)
                self.rightward(t, j, z == 0).start()

    def left(self, j, z):
        @pl.when(self.p.z == z)
        def _():
            for t in self.terms:
                if z < DEPTH - 1:
                    self.slots[t][j] = self.with_right(t, j).astype(BF)
                self.leftward(t, j, z == DEPTH - 1).start()

    def end(self, z, results):
        for t in self.terms:
            if z == 0:
                total = self.with_right(t, z)
            else:
                total = self.with_left(t, z)
                if z < DEPTH - 1:
                    self.leftward(t, z, False).wait_recv()
                    total = total + self.slots[t][z].astype(F32)
            results[t][...] = total.astype(BF)

    def finish(self):
        p = self.p
        for t in self.terms:
            for z in range(DEPTH):
                self.across(t, z).wait_send()
                pl.when(p.z < z)(lambda t=t, z=z: self.rightward(t, z, False).wait_send())
                pl.when(p.z > z)(lambda t=t, z=z: self.leftward(t, z, False).wait_send())


class Halves:
    def __init__(self, place, sources, refs):
        count = len(sources)
        self.p, self.sources, self.terms = place, sources, range(count)
        self.kept, self.from_twin = refs[:count], refs[count : 2 * count]
        self.ls, self.ts, self.tr = refs[2 * count :]

    @staticmethod
    def scratch(shapes):
        square = pltpu.SemaphoreType.DMA((len(shapes), DEPTH, 2))
        return [pltpu.VMEM((DEPTH, 2) + shape, BF) for shape in shapes] * 2 + [square] * 3

    def mine(self, t, z, y):
        return self.kept[t].at[z, y]

    def load(self, t, z, y):
        source = self.sources[t](self.p.index(z, y, self.p.core))
        return pltpu.make_async_copy(source, self.kept[t].at[z, y], self.ls.at[t, z, y])

    def twin(self, t, z, y):
        source = self.sources[t](self.p.index(z, y, 1 - self.p.core))
        return push(source, self.from_twin[t].at[z, y], self.ts.at[t, z, y], self.tr.at[t, z, y], self.p.twin)

    def begin(self, z):
        for y in (1 - self.p.y, self.p.y):
            for t in self.terms:
                self.load(t, z, y).start()
                self.twin(t, z, y).start()

    def halve(self, z):
        for y in (1 - self.p.y, self.p.y):
            for t in self.terms:
                self.load(t, z, y).wait()
                self.twin(t, z, y).wait_recv()
                both = self.kept[t][z, y].astype(F32) + self.from_twin[t][z, y].astype(F32)
                self.kept[t][z, y] = both.astype(BF)

    def finish(self):
        for t in self.terms:
            for z in range(DEPTH):
                for y in range(2):
                    self.twin(t, z, y).wait_send()


def widen_kernel(
    up_ref, down_ref, out_ref, qkv_ref, small_ref, rows_ref, time_ref, grad_ref, layer_ref,
    up_to, down_to, out_to, qkv_to, time_to, table_to, gain_one_to, gain_two_to, grad_to, layer_to,
):
    grad_to[...] = grad_ref[...]
    layer_to[...] = layer_ref[...]
    columns = up_ref.shape[-1]
    levels, here = rows_ref.shape[0], table_to.shape[0]
    me, step = lax.axis_index("wt"), pl.program_id(0)
    mine = pl.ds(pl.multiple_of(me * here, here), here)
    table = None
    gains = []
    for i in range(up_ref.shape[1]):
        rows = slice(i * up_ref.shape[2], (i + 1) * up_ref.shape[2])
        up_to[rows, :columns] = up_ref[0, i].astype(F32)
        up_to[rows, columns:] = up_ref[1, i].astype(F32)
        for source, target in ((down_ref, down_to), (out_ref, out_to), (qkv_ref, qkv_to)):
            depth = source.shape[1]
            target[i * depth : (i + 1) * depth, :] = source[i].astype(F32)
        cols = slice(i * 128, (i + 1) * 128)
        time_to[:, cols] = dot(rows_ref[...], small_ref[i, 0:levels, :], 0, 0)
        gains.append(small_ref[i, levels : levels + 1, :].astype(F32))
        part = dot(small_ref[i, mine, :], time_ref[:, cols], 1, 1)
        table = part if table is None else table + part
    gain = jnp.concatenate(gains, axis=1)
    wide = gain.shape[1]
    count = gain_one_to.shape[1] // wide
    place = pl.ds(pl.multiple_of(lax.rem(step, count) * wide, wide), wide)

    @pl.when(lax.div(step, count) == me)
    def _():
        gain_one_to[:, place] = gain

    @pl.when(lax.div(step, count) == me + 2)
    def _():
        gain_two_to[:, place] = gain

    first = step == 0

    @pl.when(first)
    def _():
        table_to[...] = table

    @pl.when(jnp.logical_not(first))
    def _():
        table_to[...] += table


def widen(up, down, out, qkv, small, table_rows, w_time, grad, layer, step=2):
    _, ring, up_rows, up_columns = up.shape
    wide = small.shape[2]

    def piece(a):
        return pl.BlockSpec((step,) + a.shape[1:], lambda i: (i, 0, 0))

    def row_block(a):
        return pl.BlockSpec((step * a.shape[1], a.shape[2]), lambda i: (i, 0))

    def whole(a):
        return jax.ShapeDtypeStruct((ring * a.shape[1], a.shape[2]), F32)

    def columns(rows):
        return pl.BlockSpec((rows, step * wide), lambda i: (0, i))

    def share(a):
        return pl.BlockSpec((a.shape[0] * step // ring, a.shape[1]), lambda i: (i, 0))

    time_rows, depth = table_rows.shape[1], w_time.shape[0]
    gain = pl.BlockSpec((1, ring * wide // 4), lambda i: (0, 0))
    return pl.pallas_call(
        widen_kernel,
        grid=(ring // step,),
        in_specs=[
            pl.BlockSpec((2, step, up_rows, up_columns), lambda i: (0, i, 0, 0)),
            piece(down), piece(out), piece(qkv), piece(small),
            pl.BlockSpec(table_rows.shape, lambda i: (0, 0)), columns(depth), share(grad), share(layer),
        ],
        out_specs=[
            pl.BlockSpec((step * up_rows, 2 * up_columns), lambda i: (i, 0)),
            row_block(down), row_block(out), row_block(qkv),
            columns(time_rows), pl.BlockSpec((table_rows.shape[0] // 2, depth), lambda i: (0, 0)),
            gain, gain, share(grad), share(layer),
        ],
        out_shape=[
            jax.ShapeDtypeStruct((ring * up_rows, 2 * up_columns), F32),
            whole(down), whole(out), whole(qkv),
            jax.ShapeDtypeStruct((time_rows, ring * wide), F32),
            jax.ShapeDtypeStruct((table_rows.shape[0] // 2, depth), F32),
            jax.ShapeDtypeStruct((1, ring * wide // 4), F32),
            jax.ShapeDtypeStruct((1, ring * wide // 4), F32),
            jax.ShapeDtypeStruct(grad.shape, BF),
            jax.ShapeDtypeStruct(layer.shape, BF),
        ],
        compiler_params=pltpu.CompilerParams(vmem_limit_bytes=62 << 20),
        name="widen",
    )(up, down, out, qkv, small, table_rows, w_time, grad, layer)


def ring_peer(p, d):
    return lax.rem(p.ctx + d, 16)


def front_kernel(
    block, qkv_own, time_own, table_own, gain_own, tokens, levels, cosine, sine, up_w, out_w, cot,
    qkv_all, time_all, table_rows, g_one, g_two, scale_one, scale_two,
    qkv_keep, att, full_keep, lse_ref, up_all, out_all, cot_all,
    table_all, gain_all, hold_qkv, hold_time, far_qkv, far_time, normal, embed, rows_one, qkv_t,
    qkv_in, full_ref, keys, low, hold_up, hold_out, hold_cot,
    block_in, block_out, time_s, first_s, first_r,
    keep_s, own_s, in_s, in_r, back_s, back_r, hold_in, hold_to, cross_s, cross_r, twin_s, twin_r, *gather_sems,
):
    p = Place()
    micro, _, length = qkv_in.shape
    width = length // 16
    model = att.shape[0]
    other = 1 - p.wt
    half = hold_qkv.shape[1]
    lane = 128
    blocks = hold_qkv.shape[2] // lane
    depth = far_qkv.shape[2]
    deep = far_time.shape[1]

    def natural(group, i):
        start_column = (i // DEPTH) * model + (i % DEPTH) * 2 * lane + group * lane
        return slice(start_column, start_column + lane)

    def held(i):
        return slice(i * lane, (i + 1) * lane)

    load = [[
        pltpu.make_async_copy(qkv_own.at[:, natural(k, i)], hold_qkv.at[k, :, held(i)], block_in.at[k, i])
        for i in range(blocks)] for k in range(2)]
    times = pltpu.make_async_copy(time_own, hold_time, time_s.at[0])
    for copy in load[0] + load[1]:
        copy.start()
    times.start()

    half_up, half_out = up_w.shape[0] // 2, out_w.shape[0] // 2
    columns = up_all.shape[2]
    mine = pl.ds(pl.multiple_of(p.wt * columns, columns), columns)
    theirs = pl.ds(pl.multiple_of(other * columns, columns), columns)
    holds = [
        pltpu.make_async_copy(up_w, hold_up, hold_in.at[0]),
        pltpu.make_async_copy(out_w, hold_out, hold_in.at[1]),
        pltpu.make_async_copy(cot, hold_cot, hold_in.at[2]),
    ]
    for copy in holds:
        copy.start()
    p.greet(everyone=True)
    g = Gather(
        p, [lambda c: far_time.at[c], lambda c: far_qkv.at[0, c], lambda c: far_qkv.at[1, c]], gather_sems
    )
    here = pl.ds(pl.multiple_of(depth * p.ctx, depth), depth)
    sent = [
        push(time_own.at[pl.ds(deep * p.ctx, deep)], far_time.at[p.ctx], first_s.at[0], first_r.at[0], p.pair),
        push(hold_qkv.at[0, here], far_qkv.at[0, p.ctx], first_s.at[1], first_r.at[1], p.pair),
        push(hold_qkv.at[1, here], far_qkv.at[1, p.ctx], first_s.at[2], first_r.at[2], p.pair),
        push(table_own, table_all.at[p.wt], first_s.at[3], first_r.at[3], p.pair),
        push(gain_own, gain_all.at[p.wt], first_s.at[4], first_r.at[4], p.pair),
    ]
    rows_up = pl.ds(pl.multiple_of(p.core * half_up, half_up), half_up)
    rows_out = pl.ds(pl.multiple_of(p.core * half_out, half_out), half_out)
    crossing = [
        push(hold_out.at[rows_out], out_all.at[p.wt, rows_out], cross_s.at[0], cross_r.at[0], p.pair),
        push(hold_up.at[rows_up, theirs], up_all.at[p.wt, rows_up], cross_s.at[1], cross_r.at[1], p.pair),
        push(hold_cot, cot_all.at[1], cross_s.at[2], cross_r.at[2], p.pair),
    ]
    twins = [
        push(out_all.at[other, rows_out], out_all.at[other, rows_out], twin_s.at[0], twin_r.at[0], p.twin),
        push(up_all.at[other, rows_up], up_all.at[other, rows_up], twin_s.at[1], twin_r.at[1], p.twin),
    ]
    for copy in sent[3:] + sent[:1]:
        copy.start()
    for k in range(2):
        for copy in load[k]:
            copy.wait()
        sent[1 + k].start()
    for copy in holds:
        copy.wait()
    for copy in crossing:
        copy.start()
    table_all[p.wt] = table_own[...]
    gain_all[p.wt] = gain_own[...]
    normal[...] = normed(tokens[...].astype(F32))[0]
    for t in range(2):
        sent[t].wait_recv()
        g.own(t)
    times.wait()
    out = [pltpu.make_async_copy(hold_time, time_all.at[p.wt], time_s.at[1])]
    for k in range(2):
        for i in range(blocks):
            out.append(pltpu.make_async_copy(
                hold_qkv.at[k, :, held(i)], qkv_all.at[p.wt, :, natural(k, i)], block_out.at[0, k, i]))
    for copy in out:
        copy.start()
    for copy in sent[3:]:
        copy.wait_recv()
    kinds = 2 * table_own.shape[0]
    onehot = (lax.broadcasted_iota(jnp.int32, (kinds, tokens.shape[0]), 0) == levels[...]).astype(F32).astype(BF)
    embed[...] = dot(onehot, jnp.concatenate([table_all[0], table_all[1]]), 0, 0).astype(BF)
    thick = hold_time.shape[0]
    table_columns = pl.ds(pl.multiple_of(p.wt * thick, thick), thick)
    table_rows[...] = jnp.concatenate([table_all[k, :, table_columns] for k in range(2)])
    g_one[...] = jnp.concatenate([gain_all[0, 0:1], gain_all[1, 0:1]], axis=1).astype(F32)
    g_two[...] = jnp.concatenate([gain_all[0, 1:2], gain_all[1, 1:2]], axis=1).astype(F32)
    for t in range(2):
        g.along(t, 1)
    for t in range(2):
        g.along(t, 2)
    sent[2].wait_recv()
    g.own(2)
    for t in range(2):
        g.crossed_at(t, 0)
    for t in range(2):
        g.along(t, 3)
    g.along(2, 1)
    for d in (1, 2, 3):
        g.crossed_at(0, d)
    g.finish(0)
    far_to = qkv_all.at[other].reshape(16, depth, 3 * model)
    out.append(pltpu.make_async_copy(far_time, time_all.at[other].reshape(far_time.shape), time_s.at[2]))
    out[-1].start()

    def part_of(w, size):
        return pl.ds(pl.multiple_of(w * size, size), size)

    far_rows = jnp.concatenate([far_time[k] for k in range(16)])
    shifts = dot(embed[:, part_of(p.wt, thick)], hold_time[...]) + dot(embed[:, part_of(other, thick)], far_rows)
    scale_one[...] = 1.0 + shifts[:, :model]
    scale_two[...] = 1.0 + shifts[:, model:]
    rows_one[...] = (normal[...] * (g_one[...] * scale_one[...])).astype(BF)
    quarter = HEAD // 2
    wide = 2 * lane

    def project(group):
        near, far = rows_one[:, part_of(p.wt, half)], rows_one[:, part_of(other, half)]

        @pl.loop(0, blocks // 2)
        def _(k):
            cols = pl.ds(pl.multiple_of(k * wide, wide), wide)
            part = dot(near, hold_qkv[group, :, cols])
            part = (part + dot(far, far_qkv[group, :, :, cols].reshape(half, wide))).T
            base = lax.div(k, 2) * model + lax.rem(k, 2) * 2 * wide + group * lane

            @pl.when(k < blocks // 3)
            def _():
                for h in range(4):
                    first = part[h * HEAD : h * HEAD + quarter]
                    second = part[h * HEAD + quarter : (h + 1) * HEAD]
                    row = base + (h // 2) * wide + (h % 2) * HEAD
                    up, down = pl.multiple_of(row, HEAD), pl.multiple_of(row + quarter, quarter)
                    qkv_t[pl.ds(up, quarter), :] = (first * cosine[...] - second * sine[...]).astype(BF)
                    qkv_t[pl.ds(down, quarter), :] = (second * cosine[...] + first * sine[...]).astype(BF)

            @pl.when(k >= blocks // 3)
            def _():
                for h in range(2):
                    row = pl.multiple_of(base + h * wide, lane)
                    qkv_t[pl.ds(row, lane), :] = part[h * lane : (h + 1) * lane].astype(BF)

    def piece(part, c):
        return pl.ds(pl.multiple_of(part * model + c * HEAD, HEAD), HEAD)

    def lanes(c):
        return pl.ds(pl.multiple_of(c * width, width), width)

    def to_head(m, d, part):
        c = ring_peer(p, d)
        return push(
            qkv_t.at[piece(part, c), m * width : (m + 1) * width],
            qkv_in.at[m, part * HEAD : (part + 1) * HEAD, lanes(p.ctx)],
            in_s.at[m, d, part], in_r.at[m, d, part], {"ctx": c},
        )

    stay = [
        pltpu.make_async_copy(
            qkv_t.at[piece(part, p.ctx), m * width : (m + 1) * width],
            qkv_in.at[m, part * HEAD : (part + 1) * HEAD, lanes(p.ctx)],
            own_s.at[m, part],
        )
        for m in range(micro) for part in range(3)
    ]

    def to_group(group):
        @pl.when(p.y == group)
        def _():
            for copy in stay:
                copy.start()

        for m in range(micro):

            @pl.loop(0, 8)
            def _(e, m=m):
                i = lax.rem(e + p.ctx, 8)
                c = p.index(lax.div(i, 2), group, lax.rem(i, 2))

                @pl.when(c != p.ctx)
                def _():
                    for part in range(3):
                        to_head(m, lax.rem(c - p.ctx + 16, 16), part).start()

    def store_far(group):
        for i in range(blocks):
            out.append(pltpu.make_async_copy(
                far_qkv.at[group, :, :, held(i)], far_to.at[:, :, natural(group, i)], block_out.at[1, group, i]))
            out[-1].start()

    g.along(2, 2)
    for d in (1, 2, 3):
        g.crossed_at(1, d)
    g.finish(1)
    g.along(2, 3)
    project(0)
    to_group(0)
    store_far(0)
    for d in range(DEPTH):
        g.crossed_at(2, d)
    g.finish(2)
    project(1)
    to_group(1)
    store_far(1)
    placing = [
        pltpu.make_async_copy(hold_up.at[:, mine], up_all.at[p.wt], hold_to.at[0]),
        pltpu.make_async_copy(hold_out, out_all.at[p.wt], hold_to.at[1]),
        pltpu.make_async_copy(hold_cot, cot_all.at[0], hold_to.at[2]),
    ]
    for copy in placing:
        copy.start()

    def to_owner(m, c):
        return push(
            low.at[m, :, lanes(c)],
            att.at[pl.ds(pl.multiple_of(p.ctx * HEAD, HEAD), HEAD), m * width : (m + 1) * width],
            back_s.at[m, c], back_r.at[m, p.ctx], {"ctx": c},
        )

    keep_qkv = [pltpu.make_async_copy(qkv_in.at[m], qkv_keep.at[m], keep_s.at[0, m]) for m in range(micro)]
    keep_full = [pltpu.make_async_copy(full_ref.at[m], full_keep.at[m], keep_s.at[1, m]) for m in range(micro)]
    for m in range(micro):
        for part in range(3):
            stay[3 * m + part].wait()

        @pl.loop(1, 16)
        def _(d, m=m):
            for part in range(3):
                to_head(m, d, part).wait_recv()

        keep_qkv[m].start()
        keys[...] = qkv_in[m, HEAD : 2 * HEAD, :].T
        @pl.loop(0, length // block)
        def _(step, m=m):
            j = lax.rem(step + lax.div(p.ctx * width, block), length // block)
            cols = pl.ds(pl.multiple_of(j * block, block), block)
            scores = dot(keys[...], qkv_in[m, 0:HEAD, cols]) * (SCALE * LOG2E)
            top = jnp.max(scores, axis=0, keepdims=True)
            exps = jnp.exp2(scores - top)
            total = jnp.sum(exps, axis=0, keepdims=True)
            out = dot(qkv_in[m, 2 * HEAD :, :], exps.astype(BF)) / total
            full_ref[m, :, cols] = out
            lse_ref[m, :, cols] = top + jnp.log2(total)
            low[m, :, cols] = out.astype(BF)
            for i in range(block // width):
                c = j * (block // width) + i
                pl.when(p.ctx != c)(lambda c=c: to_owner(m, c).start())

        keep_full[m].start()
        att[pl.ds(pl.multiple_of(p.ctx * HEAD, HEAD), HEAD), m * width : (m + 1) * width] = low[
            m, :, pl.ds(pl.multiple_of(p.ctx * width, width), width)
        ]
        if m == 0:
            for t in range(2):
                crossing[t].wait_recv()
                twins[t].start()

    for m in range(micro):

        @pl.loop(1, 16)
        def _(d, m=m):
            c = ring_peer(p, d)
            push(
                low.at[m, :, 0:width],
                att.at[pl.ds(pl.multiple_of(c * HEAD, HEAD), HEAD), m * width : (m + 1) * width],
                back_s.at[m, 0], back_r.at[m, c], {"ctx": c},
            ).wait_recv()
            for part in range(3):
                to_head(m, d, part).wait_send()
            to_owner(m, c).wait_send()

    crossing[2].wait_recv()
    for copy in crossing:
        copy.wait_send()
    for copy in twins + placing + keep_qkv + keep_full + out:
        copy.wait()
    for copy in sent:
        copy.wait_send()


def front(qkv_w, time_w, table, gains, tokens, levels, cosine, sine, up_w, out_w, cot, micro, block):
    dma = pltpu.SemaphoreType.DMA
    vmem = pl.BlockSpec(memory_space=pltpu.VMEM)
    anywhere = pl.BlockSpec(memory_space=pltpu.HBM)
    shape = jax.ShapeDtypeStruct
    rows, model = tokens.shape
    length = rows // micro * 16
    columns = up_w.shape[1] // 2
    width = qkv_w.shape[1] // 2
    blocks = width // 128
    far_time = (16, time_w.shape[0] // 16, time_w.shape[1])
    outs = pl.pallas_call(
        functools.partial(front_kernel, block),
        out_shape=[
            shape((2,) + qkv_w.shape, BF),
            shape((2,) + time_w.shape, BF),
            shape((2 * table.shape[0], time_w.shape[0]), BF),
            shape((1, model), F32),
            shape((1, model), F32),
            shape((rows, model), F32),
            shape((rows, model), F32),
            shape((micro, 3 * HEAD, length), BF),
            shape((model, rows), BF),
            shape((micro, HEAD, length), F32),
            shape((micro, 1, length), F32),
            shape((2, up_w.shape[0], columns), BF),
            shape((2,) + out_w.shape, BF),
            shape((2,) + cot.shape, BF),
        ],
        in_specs=[anywhere, anywhere] + [vmem] * 6 + [anywhere] * 3,
        out_specs=[anywhere, anywhere] + [vmem] * 5 + [anywhere, vmem, anywhere, vmem] + [anywhere] * 3,
        scratch_shapes=[
            pltpu.VMEM((2,) + table.shape, BF),
            pltpu.VMEM((2,) + gains.shape, BF),
            pltpu.VMEM((2, qkv_w.shape[0], width), BF),
            pltpu.VMEM(time_w.shape, BF),
            pltpu.VMEM((2, 16, qkv_w.shape[0] // 16, width), BF),
            pltpu.VMEM(far_time, BF),
            pltpu.VMEM((rows, model), F32),
            pltpu.VMEM((rows, table.shape[1]), BF),
            pltpu.VMEM((rows, model), BF),
            pltpu.VMEM((qkv_w.shape[1], rows), BF),
            pltpu.VMEM((micro, 3 * HEAD, length), BF),
            pltpu.VMEM((micro, HEAD, length), F32),
            pltpu.VMEM((length, HEAD), BF),
            pltpu.VMEM((micro, HEAD, length), BF),
            pltpu.VMEM(up_w.shape, BF),
            pltpu.VMEM(out_w.shape, BF),
            pltpu.VMEM(cot.shape, BF),
            dma((2, blocks)),
            dma((2, 2, blocks)),
            dma((3,)),
            dma((5,)),
            dma((5,)),
            dma((2, micro)),
            dma((micro, 3)),
            dma((micro, 16, 3)),
            dma((micro, 16, 3)),
            dma((micro, 16)),
            dma((micro, 16)),
            dma((3,)),
            dma((3,)),
            dma((3,)),
            dma((3,)),
            dma((2,)),
            dma((2,)),
        ] + Gather.semaphores(3),
        compiler_params=pltpu.CompilerParams(
            collective_id=1, has_side_effects=True, vmem_limit_bytes=62 << 20
        ),
        name="front",
    )(qkv_w, time_w, table, gains, tokens, levels, cosine, sine, up_w, out_w, cot)
    qkv_all, time_all, table_rows, g_one, g_two, scale_one, scale_two, *attention, up_all, out_all, cot_all = outs
    return (
        qkv_all.reshape(-1, qkv_w.shape[1]),
        time_all.reshape(-1, time_w.shape[1]),
        table_rows, g_one, g_two, scale_one, scale_two, *attention,
        up_all.reshape(-1, columns), out_all.reshape(-1, model), cot_all.reshape(-1, model),
    )


def mid_kernel(
    att, tokens, scale_two, g_two, w_out, w_up, w_down, cot,
    out_part, out_other, grad_t, grad_mid, grad_scale, gain_two, up_term, down_term, out_term,
    middle, hat, scales, rows_two, hidden, grad_pre, far, far_grad, near_grad,
    go_s, go_r, back_s, back_r,
):
    p = Place()
    rows, model = tokens.shape
    half = rows // 2
    barrier = pltpu.get_barrier_semaphore()
    pl.semaphore_signal(barrier, inc=1, device_id=p.pair, device_id_type=MESH)

    def to_pair(m):
        part = pl.ds(pl.multiple_of(m * half, half), half)
        there = pl.ds(pl.multiple_of(rows + m * half, half), half)
        return push(rows_two.at[part], rows_two.at[there], go_s.at[m], go_r.at[m], p.pair)

    def to_owner(m):
        part = pl.ds(pl.multiple_of(m * half, half), half)
        return push(far.at[part], far_grad.at[part], back_s.at[m], back_r.at[m], p.pair)

    weight = g_two[...] * scale_two[...]
    for m in range(2):
        part = slice(m * half, (m + 1) * half)
        middle[part] = tokens[part].astype(F32) + dot(att[:, part], w_out[...], 0, 0)
        normal, scale = normed(middle[part])
        hat[part] = normal
        scales[part] = scale
        rows_two[part] = (normal * weight[part]).astype(BF)
        if m == 0:
            pl.semaphore_wait(barrier, 1)
        to_pair(m).start()

    wide = 512

    def chunk(k):
        return pl.ds(pl.multiple_of(k * wide, wide), wide)

    def feed(part):
        @pl.loop(0, w_up.shape[1] // wide)
        def _(k):
            cols = chunk(k)
            pre = dot(rows_two[part], w_up[:, cols])
            cdf = 0.5 * (1.0 + lax.erf(pre * (2.0**-0.5)))
            hidden[part, cols] = (pre * cdf).astype(BF)
            density = jnp.exp(-0.5 * pre * pre) * (1.0 / math.sqrt(2.0 * math.pi))
            grad_pre[part, cols] = (dot(cot[part], w_down[cols, :], 1, 1) * (cdf + pre * density)).astype(BF)

    feed(slice(0, rows))

    @pl.loop(0, 2)
    def _(m):
        to_pair(m).wait_recv()
        there = pl.ds(pl.multiple_of(rows + m * half, half), half)
        feed(there)
        far[pl.ds(pl.multiple_of(m * half, half), half)] = dot(grad_pre[there], w_up[...], 1, 1).astype(BF)
        to_owner(m).start()

    @pl.loop(0, model // wide)
    def _(k):
        cols = chunk(k)
        near_grad[:, cols] = dot(grad_pre[0:rows], w_up[cols, :], 1, 1)

    @pl.loop(0, up_term.shape[1] // wide)
    def _(k):
        cols = chunk(k)
        up_term[:, cols] = dot(rows_two[...], grad_pre[:, cols], 0, 0).astype(BF)
        down_term[cols, :] = dot(hidden[:, cols], cot[...], 0, 0).astype(BF)

    @pl.loop(0, model // wide)
    def _(k):
        cols = chunk(k)
        both = dot(hidden[...], w_down[:, cols])
        out_part[:, cols] = middle[:, cols] + both[:rows]
        out_other[:, cols] = both[rows:].astype(BF)


    for m in range(2):
        to_owner(m).wait_recv()
    grad = near_grad[...] + far_grad[...].astype(F32)
    mid = cot[0:rows].astype(F32) + norm_back(grad, hat[...], scales[...], weight)
    grad_mid[...] = mid
    low = mid.astype(BF)
    grad_t[...] = dot(w_out[...], low, 1, 1).astype(BF)
    eh = grad * hat[...]
    grad_scale[...] = (eh * g_two[...]).astype(BF)
    gain_two[...] = jnp.sum(eh * scale_two[...], axis=0, keepdims=True)
    out_term[...] = dot(att[...], low).astype(BF)
    for m in range(2):
        to_pair(m).wait_send()
        to_owner(m).wait_send()


def mid_pass(att, tokens, scale_two, g_two, w_out, w_up, w_down, cot):
    dma = pltpu.SemaphoreType.DMA
    vmem = pl.BlockSpec(memory_space=pltpu.VMEM)
    rows, model = tokens.shape
    hidden = w_up.shape[1]
    shape = jax.ShapeDtypeStruct
    return pl.pallas_call(
        mid_kernel,
        out_shape=[
            shape((rows, model), F32), shape((rows, model), BF), shape((model, rows), BF),
            shape((rows, model), F32), shape((rows, model), BF), shape((1, model), F32),
            shape((model, hidden), BF), shape((hidden, model), BF), shape((model, model), BF),
        ],
        in_specs=[vmem] * 8,
        out_specs=[vmem] * 9,
        scratch_shapes=[
            pltpu.VMEM((rows, model), F32),
            pltpu.VMEM((rows, model), F32),
            pltpu.VMEM((rows, 1), F32),
            pltpu.VMEM((2 * rows, model), BF),
            pltpu.VMEM((2 * rows, hidden), BF),
            pltpu.VMEM((2 * rows, hidden), BF),
            pltpu.VMEM((rows, model), BF),
            pltpu.VMEM((rows, model), BF),
            pltpu.VMEM((rows, model), F32),
            dma((2,)), dma((2,)), dma((2,)), dma((2,)),
        ],
        compiler_params=pltpu.CompilerParams(
            collective_id=5, has_side_effects=True, vmem_limit_bytes=60 << 20
        ),
        name="mid_pass",
    )(att, tokens, scale_two, g_two, w_out, w_up, w_down, cot)


ORDER = (3, 0, 2, 1)


def back_kernel(
    block, grad_t, qkv_in, full_ref, lse_ref, up_term, down_term, out_term, w_qkv,
    cosine, sine, tokens, levels_row, g_one, scale_one, grad_mid, grad_scale_two, gain_two,
    out_part, out_other, input_grad, layer_out, up_all, down_all, out_all, qkv_all, small_all,
    keys, values, g_in, dq, dq_low, dkv_low, delta, grad_qkv, w_hold, grad_norm_t,
    term, q_twin, q_pair, up_sum, down_sum, out_sum, out_pair, out_own, qkv_sum, small, small_in, small_pair, out_came, norm_t, hat, rs_one,
    own_s, in_s, in_r, back_s, back_r, w_s, q_ts, q_tr, q_ps, q_pr, cross_s, cross_r, local_s,
    small_s, small_r, small_x, spread_s, spread_r, *more,
):
    p = Place()
    micro, _, length = qkv_in.shape
    width = length // 16
    model = grad_t.shape[0]
    count = 3
    cut = 2 * count + 3
    halves = Halves(
        p, [lambda c: up_term.at[:, c], lambda c: down_term.at[c], lambda c: out_term.at[:, c]], more[:cut]
    )
    more = more[cut:]
    cut = 2 * count + 6
    f_line = Line(p, count, halves.mine, more[:cut])
    more = more[cut:]
    q_line = Line(p, 1, lambda t, z, y: term.at[p.wt, p.index(z, y, p.core)], more[:8])
    half = down_term.shape[1] // 2
    depth = term.shape[2]
    split = depth // 2
    g = Gather(
        p,
        [
            lambda c: up_all.at[p.wt, c],
            lambda c: up_all.at[1 - p.wt, c],
            lambda c: down_all.at[c, 0:half],
            lambda c: down_all.at[c, half:],
            lambda c: out_all.at[c],
            lambda c: qkv_all.at[c, 0:split],
            lambda c: qkv_all.at[c, split:],
        ],
        more[8:],
        wide=(),
    )
    fixed, late = (3, 2, 0, 4, 1), (5, 6)
    p.greet(everyone=True)

    def rows_of(part, c):
        return pl.ds(pl.multiple_of(part * model + c * HEAD, HEAD), HEAD)

    def lanes(c):
        return pl.ds(pl.multiple_of(c * width, width), width)

    def to_head(m, d):
        c = ring_peer(p, d)
        return push(
            grad_t.at[rows_of(0, c), m * width : (m + 1) * width],
            g_in.at[m, :, lanes(p.ctx)], in_s.at[m, d], in_r.at[m, d], {"ctx": c},
        )

    stay = [
        pltpu.make_async_copy(
            grad_t.at[rows_of(0, p.ctx), m * width : (m + 1) * width],
            g_in.at[m, :, lanes(p.ctx)], own_s.at[m],
        )
        for m in range(micro)
    ]
    layer_cross = push(out_other, out_came, cross_s.at[2], cross_r.at[2], p.pair)
    layer_cross.start()
    for m in range(micro):
        stay[m].start()

        @pl.loop(1, 16)
        def _(d, m=m):
            to_head(m, d).start()

        halves.begin(ORDER[m])
    for z in ORDER[micro:]:
        halves.begin(z)
    chunk = w_hold.shape[1]
    chunks = model // chunk

    normal, rs_one[...] = normed(tokens[...].astype(F32))
    hat[...] = normal
    norm_t[...] = (normal * (g_one[...] * scale_one[...])).T.astype(BF)

    def w_chunk(k):
        slot = lax.rem(k, 2)
        return pltpu.make_async_copy(
            w_qkv.at[pl.ds(pl.multiple_of(k * chunk, chunk), chunk)], w_hold.at[slot], w_s.at[slot]
        )

    w_chunk(jnp.int32(0)).start()
    w_chunk(jnp.int32(1)).start()
    for z in (3, 0):
        halves.halve(z)
        f_line.cross(z)

    def to_owner(m, c, part):
        source = dq_low.at[m] if part == 0 else dkv_low.at[m, part - 1]
        return push(
            source.at[:, lanes(c)],
            grad_qkv.at[rows_of(part, p.ctx), m * width : (m + 1) * width],
            back_s.at[m, c, part], back_r.at[m, p.ctx, part], {"ctx": c},
        )

    def send(m, c, part):
        pl.when(p.ctx != c)(lambda: to_owner(m, c, part).start())

    for m in range(micro):
        keys[...] = qkv_in[m, HEAD : 2 * HEAD, :].T
        values[...] = qkv_in[m, 2 * HEAD :, :].T
        stay[m].wait()

        @pl.loop(1, 16)
        def _(d, m=m):
            to_head(m, d).wait_recv()

        delta[...] = jnp.sum(g_in[m].astype(F32) * full_ref[m], axis=0, keepdims=True)
        dq[...] = jnp.zeros_like(dq)

        @pl.loop(0, length // block)
        def _(step, m=m):
            j = lax.rem(step + lax.div(p.ctx * width, block), length // block)
            cols = pl.ds(pl.multiple_of(j * block, block), block)
            scores = dot(keys[cols, :], qkv_in[m, 0:HEAD, :]) * (SCALE * LOG2E)
            soft = jnp.exp2(scores - lse_ref[m])
            grad_soft = dot(values[cols, :], g_in[m])
            raw = (soft * (grad_soft - delta[...]) * SCALE).astype(BF)
            dkv_low[m, 0, :, cols] = dot(qkv_in[m, 0:HEAD, :], raw, 1, 1).astype(BF)
            dkv_low[m, 1, :, cols] = dot(g_in[m], soft.astype(BF), 1, 1).astype(BF)
            dq[...] += dot(qkv_in[m, HEAD : 2 * HEAD, cols], raw)
            for i in range(block // width):
                send(m, j * (block // width) + i, 1)
                send(m, j * (block // width) + i, 2)
            if m == micro - 1:

                @pl.when((step + 1) * block * 2 == length)
                def _():
                    f_line.quarter(3)
                    f_line.right(3, 0)

        dq_low[m] = dq[...].astype(BF)

        @pl.loop(1, 16)
        def _(d, m=m):
            to_owner(m, ring_peer(p, d), 0).start()

        if m == 0:
            halves.halve(2)
            halves.halve(1)
        here = lanes(p.ctx)
        to = slice(m * width, (m + 1) * width)
        grad_qkv[rows_of(0, p.ctx), to] = dq_low[m, :, here]
        grad_qkv[rows_of(1, p.ctx), to] = dkv_low[m, 0, :, here]
        grad_qkv[rows_of(2, p.ctx), to] = dkv_low[m, 1, :, here]

    f_line.cross(2)
    f_line.cross(1)
    layer_cross.wait()
    layer_out[...] = (out_part[...] + out_came[...].astype(F32)).astype(BF)
    f_line.quarter(0)
    f_line.left(0, 3)
    f_line.right(3, 1)
    f_line.left(0, 2)

    for m in range(micro):

        @pl.loop(1, 16)
        def _(d, m=m):
            c = ring_peer(p, d)
            for part in range(3):
                push(
                    dq_low.at[m, :, 0:width],
                    grad_qkv.at[rows_of(part, c), m * width : (m + 1) * width],
                    back_s.at[m, 0, part], back_r.at[m, c, part], {"ctx": c},
                ).wait_recv()

    low_half = HEAD // 2

    @pl.loop(0, 2 * model // HEAD)
    def _(h):
        upper = pl.ds(pl.multiple_of(h * HEAD, HEAD), low_half)
        lower = pl.ds(pl.multiple_of(h * HEAD + low_half, low_half), low_half)
        first, second = grad_qkv[upper, :].astype(F32), grad_qkv[lower, :].astype(F32)
        grad_qkv[upper, :] = (first * cosine[...] + second * sine[...]).astype(BF)
        grad_qkv[lower, :] = (second * cosine[...] - first * sine[...]).astype(BF)


    group = 4 * depth

    def q_to_twin(w, z, y):
        return push(
            term.at[w, p.index(z, y, 1 - p.core)], q_twin.at[w, z, y], q_ts.at[w, z, y], q_tr.at[w, z, y], p.twin
        )

    def q_to_pair(z, y):
        return push(
            term.at[1 - p.wt, p.index(z, y, p.core)], q_pair.at[z, y], q_ps.at[z, y], q_pr.at[z, y], p.pair
        )

    def with_twin(w, z, y):
        q_to_twin(w, z, y).wait_recv()
        here = p.index(z, y, p.core)
        term[w, here] = (term[w, here].astype(F32) + q_twin[w, z, y].astype(F32)).astype(BF)

    def product(w, z):
        start_row = pl.multiple_of(w * (model // 2) + z * group, group)
        rows = dot(norm_t[pl.ds(start_row, group), :], grad_qkv[...], 1, 1).astype(BF)
        for i in range(4):
            term[w, 4 * z + i] = rows[i * depth : (i + 1) * depth]
        for y in range(2):
            q_to_twin(w, z, y).start()

    def by_order(step):
        odd = lax.rem(step, 2)
        return (1 - odd) * (DEPTH - 1 - lax.div(step, 2)) + odd * lax.div(step, 2)

    @pl.loop(0, DEPTH)
    def _(step):
        product(1 - p.wt, by_order(step))

    f_line.right(3, 2)
    f_line.left(0, 1)

    @pl.loop(0, 2 * DEPTH)
    def _(step):
        z, y = by_order(lax.div(step, 2)), lax.rem(step, 2)
        with_twin(1 - p.wt, z, y)
        q_to_pair(z, y).start()

    @pl.loop(0, DEPTH)
    def _(step):
        product(p.wt, by_order(step))


    @pl.loop(0, chunks)
    def _(k):
        w_chunk(k).wait()
        grad_norm_t[pl.ds(pl.multiple_of(k * chunk, chunk), chunk), :] = dot(w_hold[lax.rem(k, 2)], grad_qkv[...])
        pl.when(k + 2 < chunks)(lambda: w_chunk(k + 2).start())

    grad_norm = grad_norm_t[...].T
    c_rows = grad_norm * (g_one[...] * scale_one[...])
    input_grad[...] = (
        grad_mid[...]
        + (
            c_rows
            - jnp.mean(c_rows, axis=-1, keepdims=True)
            - hat[...] * jnp.mean(c_rows * hat[...], axis=-1, keepdims=True)
        )
        * rs_one[...]
    ).astype(BF)
    eh = grad_norm * hat[...]
    grad_scale_one = (eh * g_one[...]).astype(BF)
    gain_one = jnp.sum(eh * scale_one[...], axis=0, keepdims=True)

    levels = LEVELS
    marks = lax.broadcasted_iota(jnp.int32, (levels, levels_row.shape[1]), 0)
    onehot_t = (marks == levels_row[...]).astype(F32).astype(BF)
    fill = jnp.zeros((small.shape[1] - levels - 1, 128), BF)
    for side, shifts, gain in ((0, grad_scale_one, gain_one), (1, grad_scale_two[...], gain_two[...])):
        level = dot(onehot_t, shifts).astype(BF)
        for k in range(8):
            cols = slice(k * 128, (k + 1) * 128)
            small[8 * side + k, 0:levels, :] = level[:, cols]
            small[8 * side + k, levels:, :] = jnp.concatenate([gain[:, cols].astype(BF), fill])

    def small_to(d):
        peer = ring_peer(p, d)
        return push(small.at[peer], small_in.at[p.ctx], small_s.at[d], small_r.at[d], {"ctx": peer})


    @pl.loop(1, 16)
    def _(d):
        small_to(d).start()

    small_in[p.ctx] = small[p.ctx]

    @pl.loop(0, 2 * DEPTH)
    def _(step):
        with_twin(p.wt, by_order(lax.div(step, 2)), lax.rem(step, 2))


    out_cross = push(out_sum.at[1 - p.wt], out_pair, cross_s.at[0], cross_r.at[0], p.pair)
    up_cross = push(up_sum.at[1 - p.wt], up_all.at[p.wt, p.ctx], cross_s.at[1], cross_r.at[1], p.pair)
    up_came = push(up_sum.at[p.wt], up_all.at[1 - p.wt, p.ctx], cross_s.at[1], cross_r.at[1], p.pair)
    sources = {0: up_sum.at[p.wt], 2: down_sum.at[0:half], 3: down_sum.at[half:], 4: out_own,
               5: qkv_sum.at[0:split], 6: qkv_sum.at[split:]}

    def f_end(z):
        @pl.when(p.z == z)
        def _():
            f_line.end(z, [up_sum, down_sum, out_sum])
            out_cross.start()
            up_cross.start()

    def q_cross(z):
        for y in (1 - p.y, p.y):
            q_to_pair(z, y).wait_recv()
            here = p.index(z, y, p.core)
            term[p.wt, here] = (term[p.wt, here].astype(F32) + q_pair[z, y].astype(F32)).astype(BF)
        q_line.cross(z)

    f_line.quarter(2)
    f_line.right(2, 0)
    q_cross(3)
    f_line.right(2, 1)
    f_line.quarter(1)
    f_line.left(1, 3)
    f_line.right(1, 0)
    f_line.left(2, 3)
    q_cross(0)
    q_line.quarter(3)
    q_line.right(3, 0)
    f_line.left(1, 2)
    q_cross(2)
    q_line.quarter(0)
    q_line.left(0, 3)
    q_line.right(3, 1)
    q_line.left(0, 2)
    q_cross(1)
    q_line.right(3, 2)
    q_line.left(0, 1)
    q_line.quarter(2)
    q_line.right(2, 0)
    q_line.quarter(1)
    q_line.left(1, 3)
    q_line.right(1, 0)
    q_line.left(2, 3)
    for z in range(DEPTH):
        f_end(z)

    @pl.loop(1, 16)
    def _(d):
        small_to(d).wait_recv()

    small_pair[0] = jnp.sum(small_in[...].astype(F32), axis=0).astype(BF)
    small_cross = push(small_pair.at[0], small_pair.at[1], small_x.at[0], small_x.at[1], p.pair)
    small_cross.start()
    q_line.right(2, 1)
    q_line.left(1, 2)

    for t in (3, 2, 0):
        g.own(t, sources[t])
    out_cross.wait_recv()
    out_own[...] = (out_sum[p.wt].astype(F32) + out_pair[...].astype(F32)).astype(BF)
    g.own(4, sources[4])
    up_came.wait_recv()
    g.own(1)
    for z in range(DEPTH):
        pl.when(p.z == z)(lambda z=z: q_line.end(z, [qkv_sum]))
    for t in late:
        g.own(t, sources[t])

    small_cross.wait()
    small_all[p.ctx] = (small_pair[0].astype(F32) + small_pair[1].astype(F32)).astype(BF)

    def small_spread(d):
        peer = ring_peer(p, d)
        return push(small_all.at[p.ctx], small_all.at[p.ctx], spread_s.at[d], spread_r.at[d], {"ctx": peer})


    @pl.loop(1, 16)
    def _(d):
        small_spread(d).start()

    copies = [pltpu.make_async_copy(sources[t], g.items[t](p.ctx), local_s.at[t]) for t in sources]
    for copy in copies:
        copy.start()
    every = fixed + late
    for t in every:
        g.along(t, 1)
    for t in every:
        g.along(t, 2)
    for t in every:
        if t not in g.wide:
            g.crossed_at(t, 0)
    for t in every:
        g.along(t, 3)
    for d in (1, 2, 3):
        for t in every:
            g.crossed_at(t, d)

    for copy in copies:
        copy.wait()
    for t in range(len(g.items)):
        g.finish(t)
    halves.finish()
    f_line.finish()
    q_line.finish()
    out_cross.wait_send()
    up_cross.wait_send()

    @pl.loop(1, 16)
    def _(d):
        small_to(d).wait_send()
        small_spread(d).wait()

    for z in range(DEPTH):
        for y in range(2):
            q_to_pair(z, y).wait_send()
            for w in range(2):
                q_to_twin(w, z, y).wait_send()
    for m in range(micro):

        @pl.loop(1, 16)
        def _(d, m=m):
            to_head(m, d).wait_send()
            for part in range(3):
                to_owner(m, ring_peer(p, d), part).wait_send()


def back_pass(grad_t, qkv_in, full, lse, up, down, out, w_qkv, rest, block):
    dma = pltpu.SemaphoreType.DMA
    vmem = pl.BlockSpec(memory_space=pltpu.VMEM)
    anywhere = pl.BlockSpec(memory_space=pltpu.HBM)
    micro, _, length = qkv_in.shape
    model, rows = grad_t.shape
    pieces = [up.shape[:1] + up.shape[2:], down.shape[1:], out.shape[:1] + out.shape[2:]]
    piece = (model // 32, 3 * model)
    small = (16, 80, 128)
    return pl.pallas_call(
        functools.partial(back_kernel, block),
        out_shape=[
            jax.ShapeDtypeStruct((rows, model), BF),
            jax.ShapeDtypeStruct((rows, model), BF),
            jax.ShapeDtypeStruct((2, 16) + up.shape[2:], BF),
            jax.ShapeDtypeStruct(down.shape, BF),
            jax.ShapeDtypeStruct(out.shape[1:], BF),
            jax.ShapeDtypeStruct((16,) + piece, BF),
            jax.ShapeDtypeStruct(small, BF),
        ],
        in_specs=[vmem] * 4 + [anywhere] * 4 + [vmem] * len(rest),
        out_specs=[vmem] * 2 + [anywhere] * 4 + [vmem],
        scratch_shapes=[
            pltpu.VMEM((length, HEAD), BF),
            pltpu.VMEM((length, HEAD), BF),
            pltpu.VMEM((micro, HEAD, length), BF),
            pltpu.VMEM((HEAD, length), F32),
            pltpu.VMEM((micro, HEAD, length), BF),
            pltpu.VMEM((micro, 2, HEAD, length), BF),
            pltpu.VMEM((1, length), F32),
            pltpu.VMEM((3 * model, rows), BF),
            pltpu.VMEM((2, 128, 3 * model), BF),
            pltpu.VMEM((model, rows), F32),
            pltpu.VMEM((2, 16) + piece, BF),
            pltpu.VMEM((2, DEPTH, 2) + piece, BF),
            pltpu.VMEM((DEPTH, 2) + piece, BF),
            pltpu.VMEM(pieces[0], BF),
            pltpu.VMEM(pieces[1], BF),
            pltpu.VMEM(pieces[2], BF),
            pltpu.VMEM(pieces[2][1:], BF),
            pltpu.VMEM(pieces[2][1:], BF),
            pltpu.VMEM(piece, BF),
            pltpu.VMEM(small, BF),
            pltpu.VMEM(small, BF),
            pltpu.VMEM((2,) + small[1:], BF),
            pltpu.VMEM((rows, model), BF),
            pltpu.VMEM((model, rows), BF),
            pltpu.VMEM((rows, model), F32),
            pltpu.VMEM((rows, 1), F32),
            dma((micro,)),
            dma((micro, 16)),
            dma((micro, 16)),
            dma((micro, 16, 3)),
            dma((micro, 16, 3)),
            dma((2,)),
            dma((2, DEPTH, 2)),
            dma((2, DEPTH, 2)),
            dma((DEPTH, 2)),
            dma((DEPTH, 2)),
            dma((3,)),
            dma((3,)),
            dma((7,)),
            dma((16,)),
            dma((16,)),
            dma((2,)),
            dma((16,)),
            dma((16,)),
        ]
        + Halves.scratch(pieces)
        + Line.scratch(pieces)
        + Line.scratch([piece])
        + Gather.semaphores(7),
        compiler_params=pltpu.CompilerParams(
            collective_id=4, has_side_effects=True, vmem_limit_bytes=63 << 20
        ),
        name="back_pass",
    )(grad_t, qkv_in, full, lse, up, down, out, w_qkv, *rest)


def spread(source, pieces, first, target):
    width = source.shape[-1]
    for c in range(pieces):
        target[:, c * width : (c + 1) * width] = source[c, 0, first : first + HEAD, :]


def attend_kernel(pieces, block, qkv_ref, low_ref, full_ref, lse_ref, q_t, k_t, v_t, keys):
    length = q_t.shape[1]
    width = length // pieces
    spread(qkv_ref, pieces, 0, q_t)
    spread(qkv_ref, pieces, HEAD, k_t)
    spread(qkv_ref, pieces, 2 * HEAD, v_t)
    keys[...] = k_t[...].T
    for j in range(length // block):
        cols = slice(j * block, (j + 1) * block)
        scores = dot(keys[...], q_t[:, cols]) * (SCALE * LOG2E)
        top = jnp.max(scores, axis=0, keepdims=True)
        exps = jnp.exp2(scores - top)
        total = jnp.sum(exps, axis=0, keepdims=True)
        out = dot(v_t[...], exps.astype(BF)) / total
        full_ref[0, :, cols] = out
        lse_ref[0, :, cols] = top + jnp.log2(total)
        for c in range(block // width):
            low_ref[j * (block // width) + c, 0] = out[:, c * width : (c + 1) * width].astype(BF)


def attend(qkv, block):
    pieces, pairs, _, width = qkv.shape
    length = pieces * width
    return pl.pallas_call(
        functools.partial(attend_kernel, pieces, block),
        grid=(pairs,),
        in_specs=[pl.BlockSpec((pieces, 1, 3 * HEAD, width), lambda p: (0, p, 0, 0))],
        out_specs=[
            pl.BlockSpec((pieces, 1, HEAD, width), lambda p: (0, p, 0, 0)),
            pl.BlockSpec((1, HEAD, length), lambda p: (p, 0, 0)),
            pl.BlockSpec((1, 1, length), lambda p: (p, 0, 0)),
        ],
        out_shape=[
            jax.ShapeDtypeStruct((pieces, pairs, HEAD, width), BF),
            jax.ShapeDtypeStruct((pairs, HEAD, length), F32),
            jax.ShapeDtypeStruct((pairs, 1, length), F32),
        ],
        scratch_shapes=[pltpu.VMEM((HEAD, length), BF)] * 3 + [pltpu.VMEM((length, HEAD), BF)],
        compiler_params=pltpu.CompilerParams(vmem_limit_bytes=48 << 20),
        name="attend",
    )(qkv)


def attend_back_kernel(
    pieces, block, qkv_ref, grad_ref, full_ref, lse_ref, out_ref,
    q_t, k_t, v_t, g_t, keys, values, dq_t, dk, dv,
):
    length = q_t.shape[1]
    width = length // pieces
    spread(qkv_ref, pieces, 0, q_t)
    spread(qkv_ref, pieces, HEAD, k_t)
    spread(qkv_ref, pieces, 2 * HEAD, v_t)
    spread(grad_ref, pieces, 0, g_t)
    keys[...] = k_t[...].T
    values[...] = v_t[...].T
    for j in range(length // block):
        cols = slice(j * block, (j + 1) * block)
        query = q_t[:, cols]
        grad = g_t[:, cols]
        delta = jnp.sum(grad.astype(F32) * full_ref[0, :, cols], axis=0, keepdims=True)
        scores = dot(keys[...], query) * (SCALE * LOG2E)
        soft = jnp.exp2(scores - lse_ref[0, :, cols])
        term_v = dot(soft.astype(BF), grad, 1, 1)
        grad_soft = dot(values[...], grad)
        raw = (soft * (grad_soft - delta) * SCALE).astype(BF)
        term_k = dot(raw, query, 1, 1)
        dq_t[:, cols] = dot(k_t[...], raw)
        if j == 0:
            dv[...] = term_v
            dk[...] = term_k
        else:
            dv[...] += term_v
            dk[...] += term_k
    dk_t = dk[...].T.astype(BF)
    dv_t = dv[...].T.astype(BF)
    for c in range(pieces):
        piece = slice(c * width, (c + 1) * width)
        out_ref[c, 0, 0:HEAD, :] = dq_t[:, piece].astype(BF)
        out_ref[c, 0, HEAD : 2 * HEAD, :] = dk_t[:, piece]
        out_ref[c, 0, 2 * HEAD :, :] = dv_t[:, piece]


def attend_back(qkv, grad, full, lse, block):
    pieces, pairs, _, width = qkv.shape
    length = pieces * width
    return pl.pallas_call(
        functools.partial(attend_back_kernel, pieces, block),
        grid=(pairs,),
        in_specs=[
            pl.BlockSpec((pieces, 1, 3 * HEAD, width), lambda p: (0, p, 0, 0)),
            pl.BlockSpec((pieces, 1, HEAD, width), lambda p: (0, p, 0, 0)),
            pl.BlockSpec((1, HEAD, length), lambda p: (p, 0, 0)),
            pl.BlockSpec((1, 1, length), lambda p: (p, 0, 0)),
        ],
        out_specs=pl.BlockSpec((pieces, 1, 3 * HEAD, width), lambda p: (0, p, 0, 0)),
        out_shape=jax.ShapeDtypeStruct(qkv.shape, BF),
        scratch_shapes=[pltpu.VMEM((HEAD, length), BF)] * 4
        + [pltpu.VMEM((length, HEAD), BF)] * 2
        + [pltpu.VMEM((HEAD, length), F32)]
        + [pltpu.VMEM((length, HEAD), F32)] * 2,
        compiler_params=pltpu.CompilerParams(vmem_limit_bytes=56 << 20),
        name="attend_back",
    )(qkv, grad, full, lse)


def normed(rows):
    centered = rows - jnp.mean(rows, axis=-1, keepdims=True)
    scale = lax.rsqrt(jnp.mean(centered * centered, axis=-1, keepdims=True) + EPSILON)
    return centered * scale, scale


def norm_back(grad, hat, scale, weight):
    c = grad * weight
    return (
        c - jnp.mean(c, axis=-1, keepdims=True) - hat * jnp.mean(c * hat, axis=-1, keepdims=True)
    ) * scale


def turn(first, second, cosine, sine):
    return first * cosine - second * sine, second * cosine + first * sine


def shards(
    tokens, positions, buckets, qkv_w, out_w, up_w, down_w, time_w, noise_table,
    gain_one, gain_two, cotangent,
):
    n, ring = lax.axis_size("wt"), lax.axis_size("ctx")
    me = lax.axis_index("wt")
    micro, _, width, model = tokens.shape
    rows = micro * width
    pairs = HEADS * micro // ring
    block = 256
    planar = n == 2 and ring == 16

    x = tokens.reshape(rows, model).astype(F32)
    cot_low = cotangent.reshape(rows, model)
    places = positions.reshape(rows)
    levels = buckets.reshape(rows)

    def whole_rows(weight):
        return lax.all_gather(weight, "wt", axis=0, tiled=True)

    frequency = jnp.exp(
        jnp.arange(HEAD // 2, dtype=F32) * (-math.log(10000.0) * 2.0 / HEAD)
    )
    angles = frequency[:, None] * places.astype(F32)[None, :]
    cosine, sine = jnp.cos(angles), jnp.sin(angles)
    stacked = jnp.stack([gain_one, gain_two])
    if planar:
        (
            w_qkv, w_time, table_rows, g_one, g_two, scale_one, scale_two, qkv_heads, attended, full, lse, w_up, w_out, cot,
        ) = front(
            qkv_w, time_w, noise_table, stacked, tokens.reshape(rows, model), levels[None], cosine, sine,
            up_w, out_w, cot_low, micro, block,
        )
    else:
        w_qkv = whole_rows(qkv_w)
        w_out = whole_rows(out_w)
        w_time = whole_rows(time_w)
        table = whole_rows(noise_table)
        gains = lax.all_gather(stacked, "wt", axis=1, tiled=True)
        w_up = lax.all_to_all(up_w, "wt", 1, 0, tiled=True)
        g_one, g_two = gains[0].astype(F32), gains[1].astype(F32)

        onehot = levels[:, None] == jnp.arange(table.shape[0], dtype=jnp.int32)[None, :]
        embed = dot(onehot.astype(BF), table).astype(BF)
        shifts = dot(embed, w_time)
        scale_one = 1.0 + shifts[:, :model]
        scale_two = 1.0 + shifts[:, model:]

        hat_one, rs_one = normed(x)
        weight_one = g_one * scale_one
        norm_one = (hat_one * weight_one).astype(BF)

        qkv_t = dot(w_qkv, norm_one, 0, 1).reshape(3, HEADS, 2, HEAD // 2, rows)
        turned = turn(qkv_t[:2, :, 0], qkv_t[:2, :, 1], cosine, sine)
        queries_keys = jnp.stack(turned, axis=2)
        qkv_low = jnp.concatenate([queries_keys.astype(BF), qkv_t[2:].astype(BF)])

    def to_heads(columns):
        parts = columns.shape[0]
        split = columns.reshape(parts, HEADS, HEAD, micro, width)
        split = jnp.transpose(split, (1, 3, 0, 2, 4))
        split = split.reshape(ring, pairs, parts * HEAD, width)
        return lax.all_to_all(split, "ctx", 0, 0, tiled=True)

    def to_tokens(pieces):
        parts = pieces.shape[2] // HEAD
        back = lax.all_to_all(pieces, "ctx", 0, 0, tiled=True)
        back = back.reshape(HEADS, micro, parts, HEAD, width)
        return jnp.transpose(back, (2, 0, 3, 1, 4)).reshape(parts, HEADS * HEAD, rows)

    if not planar:
        qkv_heads = to_heads(qkv_low.reshape(3, HEADS, HEAD, rows))
        low, full, lse = attend(qkv_heads, block)
        attended = to_tokens(low)[0]
        cot = gather_slots(cot_low).reshape(n * rows, model)

    if not planar:
        middle = x + dot(attended, w_out, 0, 0)
        hat_two, rs_two = normed(middle)
        weight_two = g_two * scale_two
        norm_two_own = (hat_two * weight_two).astype(BF)

        norm_two = gather_slots(norm_two_own).reshape(n * rows, model)
        pre = dot(norm_two, w_up)
        phi_cdf = 0.5 * (1.0 + lax.erf(pre * (2.0**-0.5)))
        hidden = (pre * phi_cdf).astype(BF)
        out_parts = dot(hidden, down_w).reshape(n, rows, model)

        grad_hidden = dot(cot, down_w, 1, 1)
        density = jnp.exp(-0.5 * pre * pre) * (1.0 / math.sqrt(2.0 * math.pi))
        grad_pre = (grad_hidden * (phi_cdf + pre * density)).astype(BF)
        grad_norm_two = sum_slots(dot(grad_pre, w_up, 1, 1).reshape(n, rows, model))
        down_term = dot(hidden, cot, 0, 0).astype(BF)
        up_term = dot(norm_two, grad_pre, 0, 0).astype(BF)
        grad_mid = cot_low.astype(F32) + norm_back(grad_norm_two, hat_two, rs_two, weight_two)
        grad_branch = grad_mid.astype(BF)
        eh_two = grad_norm_two * hat_two
        grad_scale_two = eh_two * g_two
        gain_two_term = jnp.sum(eh_two * scale_two, axis=0)
        out_term = dot(attended, grad_branch, 1, 0).astype(BF)
        grad_attn = dot(w_out, grad_branch, 1, 1).astype(BF)

    if planar:

        def pieces_of(array, *lead):
            return array.reshape(lead + (-1, array.shape[-1]))

        (
            out_part, out_other, grad_attn, grad_mid, grad_scale_two, gain_two_term, up_term, down_term, out_term,
        ) = mid_pass(attended, tokens.reshape(rows, model), scale_two, g_two, w_out, w_up, down_w, cot)
        rest = (
            cosine, sine, tokens.reshape(rows, model), levels[None], g_one, scale_one, grad_mid,
            grad_scale_two, gain_two_term, out_part, out_other,
        )
        input_grad, layer_out, up_all, down_all, out_all, qkv_all, small_all = back_pass(
            grad_attn, qkv_heads, full, lse, pieces_of(up_term, n, ring), pieces_of(down_term, ring),
            pieces_of(out_term, n, ring), w_qkv, rest, block,
        )
        (
            up_grad, down_grad, out_grad, qkv_grad, time_grad, table_grad, gain_one_grad, gain_two_grad,
            input_grad, layer_out,
        ) = widen(up_all, down_all, out_all, qkv_all, small_all, table_rows, w_time, input_grad, layer_out)
        gain_one_grad, gain_two_grad = gain_one_grad[0], gain_two_grad[0]
    else:
        layer_out = middle + sum_slots(out_parts)
        up_share = lax.psum_scatter(
            up_term.reshape(n, model // n, -1), "ctx", scatter_dimension=1, tiled=True
        )
        down_share = lax.psum_scatter(down_term, "ctx", scatter_dimension=0, tiled=True)
        out_share = lax.psum_scatter(
            out_term.reshape(n, model // n, model), "ctx", scatter_dimension=1, tiled=True
        )
        grad_heads = to_heads(grad_attn.reshape(1, HEADS, HEAD, rows))
        back = to_tokens(attend_back(qkv_heads, grad_heads, full, lse, block))
        back = back.reshape(3, HEADS, 2, HEAD // 2, rows)
        unturned = turn(back[:2, :, 0].astype(F32), back[:2, :, 1].astype(F32), cosine, -sine)
        grad_qkv = jnp.concatenate([jnp.stack(unturned, axis=2).astype(BF), back[2:]])
        grad_qkv = grad_qkv.reshape(3 * model, rows)
        qkv_term = dot(norm_one, grad_qkv, 0, 1).astype(BF)
        grad_norm_one = dot(grad_qkv, w_qkv, 0, 1)

        input_grad = grad_mid + norm_back(grad_norm_one, hat_one, rs_one, weight_one)
        eh_one = grad_norm_one * hat_one
        grad_scale_one = eh_one * g_one
        gain_one_term = jnp.sum(eh_one * scale_one, axis=0)

        grad_shifts = jnp.concatenate([grad_scale_one, grad_scale_two], axis=1).astype(BF)
        level_term = dot(onehot.astype(BF), grad_shifts, 0, 0)
        gain_terms = jnp.concatenate([gain_one_term, gain_two_term])
        small = lax.psum(jnp.concatenate([level_term, gain_terms[None]]), ("ctx", "wt"))
        share = lax.psum_scatter(
            qkv_term.reshape(n, model // n, -1), "ctx", scatter_dimension=1, tiled=True
        )

        def spread_rows(share):
            return lax.all_gather(share, "ctx", axis=0, tiled=True).astype(F32)

        up_share = lax.all_to_all(up_share, "wt", 0, 0, tiled=True)
        up_grad = lax.all_gather(up_share, "ctx", axis=1, tiled=True).astype(F32)
        up_grad = jnp.transpose(up_grad, (1, 0, 2)).reshape(model // n, -1)
        down_grad = spread_rows(down_share)
        out_grad = spread_rows(sum_owned(out_share))
        qkv_grad = spread_rows(sum_owned(share))

        by_level = small[: table.shape[0]]
        gain_sums = small[table.shape[0]]
        levels_here, time_here = noise_table.shape[0], time_w.shape[0]
        high = lax.Precision.HIGHEST
        time_rows = lax.dynamic_slice_in_dim(table, me * time_here, time_here, 1).astype(F32)
        time_grad = lax.dot_general(
            time_rows, by_level, (((0,), (0,)), ((), ())), precision=high, preferred_element_type=F32
        )
        level_rows = lax.dynamic_slice_in_dim(by_level, me * levels_here, levels_here, 0)
        table_grad = lax.dot_general(
            level_rows, w_time.astype(F32), (((1,), (1,)), ((), ())), precision=high,
            preferred_element_type=F32,
        )

        gain_here = gain_one.shape[0]
        gain_one_grad = lax.dynamic_slice_in_dim(gain_sums, me * gain_here, gain_here, 0)
        gain_two_grad = lax.dynamic_slice_in_dim(gain_sums, model + me * gain_here, gain_here, 0)

    return (
        layer_out.astype(BF).reshape(tokens.shape),
        input_grad.astype(BF).reshape(tokens.shape),
        qkv_grad,
        out_grad,
        up_grad,
        down_grad,
        time_grad,
        table_grad,
        gain_one_grad,
        gain_two_grad,
    )


def sum_owned(share):
    n, me = lax.axis_size("wt"), lax.axis_index("wt")
    slots = jnp.stack(
        [lax.dynamic_index_in_dim(share, lax.rem(me + k, n), 0, keepdims=False) for k in range(n)]
    )
    return sum_slots(slots.astype(F32)).astype(BF)


def solution(mesh):
    rows = P(None, "wt", "ctx", None)
    marks = P(None, "wt", "ctx")
    weight = P("wt", None)
    gain = P("wt")
    return jax.shard_map(
        shards,
        mesh=mesh,
        in_specs=(rows, marks, marks) + (weight,) * 6 + (gain, gain, rows),
        out_specs=(rows, rows) + (weight,) * 6 + (gain, gain),
        check_vma=False,
    )
```

```python
import functools
import math

import jax
import jax.numpy as jnp
from jax import lax
from jax.experimental import pallas as pl
from jax.experimental.pallas import tpu as pltpu
from jax.sharding import PartitionSpec as P

HEADS = 16
HEAD = 64
LEVELS = 64
EPSILON = 1e-05
SCALE = 0.125
LOG2E = math.log2(math.e)
BF = jnp.bfloat16
F32 = jnp.float32


def dot(a, b, ca=1, cb=0):
    return lax.dot_general(a, b, (((ca,), (cb,)), ((), ())), preferred_element_type=F32)


def swap_ring(value, places):
    n = lax.axis_size("wt")
    return lax.ppermute(value, "wt", [((i + places) % n, i) for i in range(n)])


def gather_slots(own):
    n = lax.axis_size("wt")
    return jnp.stack([own] + [swap_ring(own, k) for k in range(1, n)])


def sum_slots(partial):
    n = lax.axis_size("wt")
    total = partial[0]
    for k in range(1, n):
        total = total + swap_ring(partial[k].astype(BF), n - k).astype(F32)
    return total


MESH = pl.DeviceIdType.MESH
DEPTH = 4


class Place:
    def __init__(self):
        self.ctx = lax.axis_index("ctx")
        self.wt = lax.axis_index("wt")
        self.z = lax.div(self.ctx, 4)
        self.y = lax.rem(lax.div(self.ctx, 2), 2)
        self.core = lax.rem(self.ctx, 2)
        self.right = {"ctx": self.index(lax.min(self.z + 1, DEPTH - 1), self.y, self.core)}
        self.left = {"ctx": self.index(lax.max(self.z - 1, 0), self.y, self.core)}
        self.across = {"ctx": self.index(self.z, 1 - self.y, self.core)}
        self.twin = {"ctx": self.index(self.z, self.y, 1 - self.core)}
        self.pair = {"wt": 1 - self.wt}

    @staticmethod
    def index(z, y, core):
        return (z * 2 + y) * 2 + core

    def greet(self, everyone=False, pair=True):
        barrier = pltpu.get_barrier_semaphore()

        def signal(device):
            pl.semaphore_signal(barrier, inc=1, device_id=device, device_id_type=MESH)

        if everyone:

            @pl.loop(1, 16)
            def _(d):
                signal({"ctx": lax.rem(self.ctx + d, 16)})

            count = 15
        else:
            signal(self.across)
            signal(self.twin)
            pl.when(self.z > 0)(lambda: signal(self.left))
            pl.when(self.z < DEPTH - 1)(lambda: signal(self.right))
            inner = jnp.logical_and(self.z > 0, self.z < DEPTH - 1).astype(jnp.int32)
            count = 3 + inner
        if pair:
            signal(self.pair)
            count = count + 1
        pl.semaphore_wait(barrier, count)


def push(source, target, send, receive, device):
    return pltpu.make_async_remote_copy(
        src_ref=source, dst_ref=target, send_sem=send, recv_sem=receive,
        device_id=device, device_id_type=MESH,
    )


class Gather:
    def __init__(self, place, items, sems, wide=()):
        self.p, self.items, self.wide = place, items, wide
        (self.sl, self.sr, self.sy, self.sc, self.rz, self.ry, self.rc) = sems

    @staticmethod
    def semaphores(count):
        dma = pltpu.SemaphoreType.DMA
        line, square = dma((count, DEPTH)), dma((count, DEPTH, 2))
        return [square, square, line, square, square, line, square]

    def piece(self, t, z, y, core):
        return self.items[t](self.p.index(z, y, core))

    def copy(self, t, z, y, source, send, receive, device):
        here = self.piece(t, z, y, self.p.core)
        return push(here if source is None else source, here, send, receive, device)

    def rightward(self, t, z, source=None, far=0):
        y = 1 - self.p.y if far else self.p.y
        return self.copy(t, z, y, source, self.sr.at[t, z, far], self.rz.at[t, z, far], self.p.right)

    def leftward(self, t, z, source=None, far=0):
        y = 1 - self.p.y if far else self.p.y
        return self.copy(t, z, y, source, self.sl.at[t, z, far], self.rz.at[t, z, far], self.p.left)

    def crossing(self, t, z, source=None):
        return self.copy(t, z, self.p.y, source, self.sy.at[t, z], self.ry.at[t, z], self.p.across)

    def twinning(self, t, z, y, source=None):
        return self.copy(t, z, y, source, self.sc.at[t, z, y], self.rc.at[t, z, y], self.p.twin)

    def own(self, t, source=None):
        p = self.p
        pl.when(p.z < DEPTH - 1)(lambda: self.rightward(t, p.z, source).start())
        pl.when(p.z > 0)(lambda: self.leftward(t, p.z, source).start())
        self.crossing(t, p.z, source).start()
        self.twinning(t, p.z, p.y, source).start()

    def arrived(self, t, z, y, core, semaphore):
        piece = self.piece(t, z, y, core)
        push(piece, piece, semaphore, semaphore, self.p.twin).wait_recv()

    def arrive(self, t, z, far=0):
        p = self.p
        y = 1 - p.y if far else p.y
        self.arrived(t, z, y, p.core, self.rz.at[t, z, far])
        pl.when(jnp.logical_and(p.z > z, p.z < DEPTH - 1))(lambda: self.rightward(t, z, far=far).start())
        pl.when(jnp.logical_and(p.z < z, p.z > 0))(lambda: self.leftward(t, z, far=far).start())
        if t not in self.wide:
            self.crossing(t, z).start()
        self.twinning(t, z, y).start()

    def along(self, t, d):
        p = self.p
        for far in (0, 1) if t in self.wide else (0,):
            pl.when(p.z - d >= 0)(lambda far=far: self.arrive(t, p.z - d, far))
            pl.when(p.z + d < DEPTH)(lambda far=far: self.arrive(t, p.z + d, far))

    def crossed(self, t, z):
        self.arrived(t, z, 1 - self.p.y, self.p.core, self.ry.at[t, z])
        self.twinning(t, z, 1 - self.p.y).start()

    def crossed_at(self, t, d):
        p = self.p
        if t in self.wide:
            if d == 0:
                self.arrived(t, p.z, 1 - p.y, p.core, self.ry.at[t, p.z])
                pl.when(p.z < DEPTH - 1)(lambda: self.rightward(t, p.z, far=1).start())
                pl.when(p.z > 0)(lambda: self.leftward(t, p.z, far=1).start())
                self.twinning(t, p.z, 1 - p.y).start()
        elif d == 0:
            self.crossed(t, p.z)
        else:
            pl.when(p.z - d >= 0)(lambda: self.crossed(t, p.z - d))
            pl.when(p.z + d < DEPTH)(lambda: self.crossed(t, p.z + d))

    def finish(self, t):
        p = self.p
        wide = t in self.wide
        if wide:
            self.crossing(t, p.z).wait_send()
        for z in range(DEPTH):
            if not wide:
                self.crossing(t, z).wait_send()
            for y in range(2):
                self.twinning(t, z, y).wait_send()
                self.arrived(t, z, y, 1 - p.core, self.rc.at[t, z, y])
            for far in (0, 1) if wide else (0,):
                pl.when(jnp.logical_and(p.z >= z, p.z < DEPTH - 1))(
                    lambda z=z, far=far: self.rightward(t, z, far=far).wait_send()
                )
                pl.when(jnp.logical_and(p.z <= z, p.z > 0))(
                    lambda z=z, far=far: self.leftward(t, z, far=far).wait_send()
                )


class Line:
    def __init__(self, place, count, mine, refs):
        self.p, self.mine, self.terms = place, mine, range(count)
        self.from_across, self.slots = refs[:count], refs[count : 2 * count]
        self.ys, self.yr, self.rs, self.rr, self.vs, self.vr = refs[2 * count :]

    @staticmethod
    def scratch(shapes):
        line = pltpu.SemaphoreType.DMA((len(shapes), DEPTH))
        return (
            [pltpu.VMEM((DEPTH,) + shape, BF) for shape in shapes]
            + [pltpu.VMEM((DEPTH + 1,) + shape, BF) for shape in shapes]
            + [line] * 6
        )

    def across(self, t, z):
        return push(
            self.mine(t, z, 1 - self.p.y), self.from_across[t].at[z], self.ys.at[t, z], self.yr.at[t, z], self.p.across
        )

    def rightward(self, t, j, first):
        target = self.slots[t].at[j + 1]
        return push(self.from_across[t].at[j] if first else target, target, self.rs.at[t, j], self.rr.at[t, j], self.p.right)

    def leftward(self, t, j, first):
        target = self.slots[t].at[j]
        return push(self.from_across[t].at[j] if first else target, target, self.vs.at[t, j], self.vr.at[t, j], self.p.left)

    def cross(self, z):
        for t in self.terms:
            self.across(t, z).start()

    def quarter(self, z):
        for t in self.terms:
            self.across(t, z).wait_recv()
            both = self.mine(t, z, self.p.y)[...].astype(F32) + self.from_across[t][z].astype(F32)
            self.from_across[t][z] = both.astype(BF)

    def with_left(self, t, j):
        self.rightward(t, j, False).wait_recv()
        return self.from_across[t][j].astype(F32) + self.slots[t][j + 1].astype(F32)

    def with_right(self, t, j):
        self.leftward(t, j, False).wait_recv()
        return self.from_across[t][j].astype(F32) + self.slots[t][j].astype(F32)

    def right(self, j, z):
        @pl.when(self.p.z == z)
        def _():
            for t in self.terms:
                if z > 0:
                    self.slots[t][j + 1] = self.with_left(t, j).astype(BF)
                self.rightward(t, j, z == 0).start()

    def left(self, j, z):
        @pl.when(self.p.z == z)
        def _():
            for t in self.terms:
                if z < DEPTH - 1:
                    self.slots[t][j] = self.with_right(t, j).astype(BF)
                self.leftward(t, j, z == DEPTH - 1).start()

    def end(self, z, results):
        for t in self.terms:
            if z == 0:
                total = self.with_right(t, z)
            else:
                total = self.with_left(t, z)
                if z < DEPTH - 1:
                    self.leftward(t, z, False).wait_recv()
                    total = total + self.slots[t][z].astype(F32)
            results[t][...] = total.astype(BF)

    def finish(self):
        p = self.p
        for t in self.terms:
            for z in range(DEPTH):
                self.across(t, z).wait_send()
                pl.when(p.z < z)(lambda t=t, z=z: self.rightward(t, z, False).wait_send())
                pl.when(p.z > z)(lambda t=t, z=z: self.leftward(t, z, False).wait_send())


class Halves:
    def __init__(self, place, sources, refs):
        count = len(sources)
        self.p, self.sources, self.terms = place, sources, range(count)
        self.kept, self.from_twin = refs[:count], refs[count : 2 * count]
        self.ls, self.ts, self.tr = refs[2 * count :]

    @staticmethod
    def scratch(shapes):
        square = pltpu.SemaphoreType.DMA((len(shapes), DEPTH, 2))
        return [pltpu.VMEM((DEPTH, 2) + shape, BF) for shape in shapes] * 2 + [square] * 3

    def mine(self, t, z, y):
        return self.kept[t].at[z, y]

    def load(self, t, z, y):
        source = self.sources[t](self.p.index(z, y, self.p.core))
        return pltpu.make_async_copy(source, self.kept[t].at[z, y], self.ls.at[t, z, y])

    def twin(self, t, z, y):
        source = self.sources[t](self.p.index(z, y, 1 - self.p.core))
        return push(source, self.from_twin[t].at[z, y], self.ts.at[t, z, y], self.tr.at[t, z, y], self.p.twin)

    def begin(self, z):
        for y in (1 - self.p.y, self.p.y):
            for t in self.terms:
                self.load(t, z, y).start()
                self.twin(t, z, y).start()

    def halve(self, z):
        for y in (1 - self.p.y, self.p.y):
            for t in self.terms:
                self.load(t, z, y).wait()
                self.twin(t, z, y).wait_recv()
                both = self.kept[t][z, y].astype(F32) + self.from_twin[t][z, y].astype(F32)
                self.kept[t][z, y] = both.astype(BF)

    def finish(self):
        for t in self.terms:
            for z in range(DEPTH):
                for y in range(2):
                    self.twin(t, z, y).wait_send()


def widen_kernel(
    up_ref, down_ref, out_ref, qkv_ref, small_ref, rows_ref, time_ref, grad_ref, layer_ref,
    up_to, down_to, out_to, qkv_to, time_to, table_to, gain_one_to, gain_two_to, grad_to, layer_to,
):
    grad_to[...] = grad_ref[...]
    layer_to[...] = layer_ref[...]
    columns = up_ref.shape[-1]
    levels, here = rows_ref.shape[0], table_to.shape[0]
    me, step = lax.axis_index("wt"), pl.program_id(0)
    mine = pl.ds(pl.multiple_of(me * here, here), here)
    table = None
    gains = []
    for i in range(up_ref.shape[1]):
        rows = slice(i * up_ref.shape[2], (i + 1) * up_ref.shape[2])
        up_to[rows, :columns] = up_ref[0, i].astype(F32)
        up_to[rows, columns:] = up_ref[1, i].astype(F32)
        for source, target in ((down_ref, down_to), (out_ref, out_to), (qkv_ref, qkv_to)):
            depth = source.shape[1]
            target[i * depth : (i + 1) * depth, :] = source[i].astype(F32)
        cols = slice(i * 128, (i + 1) * 128)
        time_to[:, cols] = dot(rows_ref[...], small_ref[i, 0:levels, :], 0, 0)
        gains.append(small_ref[i, levels : levels + 1, :].astype(F32))
        part = dot(small_ref[i, mine, :], time_ref[:, cols], 1, 1)
        table = part if table is None else table + part
    gain = jnp.concatenate(gains, axis=1)
    wide = gain.shape[1]
    count = gain_one_to.shape[1] // wide
    place = pl.ds(pl.multiple_of(lax.rem(step, count) * wide, wide), wide)

    @pl.when(lax.div(step, count) == me)
    def _():
        gain_one_to[:, place] = gain

    @pl.when(lax.div(step, count) == me + 2)
    def _():
        gain_two_to[:, place] = gain

    first = step == 0

    @pl.when(first)
    def _():
        table_to[...] = table

    @pl.when(jnp.logical_not(first))
    def _():
        table_to[...] += table


def widen(up, down, out, qkv, small, table_rows, w_time, grad, layer, step=2):
    _, ring, up_rows, up_columns = up.shape
    wide = small.shape[2]

    def piece(a):
        return pl.BlockSpec((step,) + a.shape[1:], lambda i: (i, 0, 0))

    def row_block(a):
        return pl.BlockSpec((step * a.shape[1], a.shape[2]), lambda i: (i, 0))

    def whole(a):
        return jax.ShapeDtypeStruct((ring * a.shape[1], a.shape[2]), F32)

    def columns(rows):
        return pl.BlockSpec((rows, step * wide), lambda i: (0, i))

    def share(a):
        return pl.BlockSpec((a.shape[0] * step // ring, a.shape[1]), lambda i: (i, 0))

    time_rows, depth = table_rows.shape[1], w_time.shape[0]
    gain = pl.BlockSpec((1, ring * wide // 4), lambda i: (0, 0))
    return pl.pallas_call(
        widen_kernel,
        grid=(ring // step,),
        in_specs=[
            pl.BlockSpec((2, step, up_rows, up_columns), lambda i: (0, i, 0, 0)),
            piece(down), piece(out), piece(qkv), piece(small),
            pl.BlockSpec(table_rows.shape, lambda i: (0, 0)), columns(depth), share(grad), share(layer),
        ],
        out_specs=[
            pl.BlockSpec((step * up_rows, 2 * up_columns), lambda i: (i, 0)),
            row_block(down), row_block(out), row_block(qkv),
            columns(time_rows), pl.BlockSpec((table_rows.shape[0] // 2, depth), lambda i: (0, 0)),
            gain, gain, share(grad), share(layer),
        ],
        out_shape=[
            jax.ShapeDtypeStruct((ring * up_rows, 2 * up_columns), F32),
            whole(down), whole(out), whole(qkv),
            jax.ShapeDtypeStruct((time_rows, ring * wide), F32),
            jax.ShapeDtypeStruct((table_rows.shape[0] // 2, depth), F32),
            jax.ShapeDtypeStruct((1, ring * wide // 4), F32),
            jax.ShapeDtypeStruct((1, ring * wide // 4), F32),
            jax.ShapeDtypeStruct(grad.shape, BF),
            jax.ShapeDtypeStruct(layer.shape, BF),
        ],
        compiler_params=pltpu.CompilerParams(vmem_limit_bytes=62 << 20),
        name="widen",
    )(up, down, out, qkv, small, table_rows, w_time, grad, layer)


def ring_peer(p, d):
    return lax.rem(p.ctx + d, 16)


def front_kernel(
    block, qkv_own, time_own, table_own, gain_own, tokens, levels, cosine, sine, up_w, out_w, cot,
    qkv_all, time_all, table_rows, g_one, g_two, scale_one, scale_two,
    qkv_keep, att, full_keep, lse_ref, up_all, out_all, cot_all,
    table_all, gain_all, hold_qkv, hold_time, far_qkv, far_time, normal, embed, rows_one, qkv_t,
    qkv_in, full_ref, keys, low, hold_up, hold_out, hold_cot,
    block_in, block_out, time_s, first_s, first_r,
    keep_s, own_s, in_s, in_r, back_s, back_r, hold_in, hold_to, cross_s, cross_r, twin_s, twin_r, *gather_sems,
):
    p = Place()
    micro, _, length = qkv_in.shape
    width = length // 16
    model = att.shape[0]
    other = 1 - p.wt
    half = hold_qkv.shape[1]
    lane = 128
    blocks = hold_qkv.shape[2] // lane
    depth = far_qkv.shape[2]
    deep = far_time.shape[1]

    def natural(group, i):
        start_column = (i // DEPTH) * model + (i % DEPTH) * 2 * lane + group * lane
        return slice(start_column, start_column + lane)

    def held(i):
        return slice(i * lane, (i + 1) * lane)

    load = [[
        pltpu.make_async_copy(qkv_own.at[:, natural(k, i)], hold_qkv.at[k, :, held(i)], block_in.at[k, i])
        for i in range(blocks)] for k in range(2)]
    times = pltpu.make_async_copy(time_own, hold_time, time_s.at[0])
    for copy in load[0] + load[1]:
        copy.start()
    times.start()

    half_up, half_out = up_w.shape[0] // 2, out_w.shape[0] // 2
    columns = up_all.shape[2]
    mine = pl.ds(pl.multiple_of(p.wt * columns, columns), columns)
    theirs = pl.ds(pl.multiple_of(other * columns, columns), columns)
    holds = [
        pltpu.make_async_copy(up_w, hold_up, hold_in.at[0]),
        pltpu.make_async_copy(out_w, hold_out, hold_in.at[1]),
        pltpu.make_async_copy(cot, hold_cot, hold_in.at[2]),
    ]
    for copy in holds:
        copy.start()
    p.greet(everyone=True)
    g = Gather(
        p, [lambda c: far_time.at[c], lambda c: far_qkv.at[0, c], lambda c: far_qkv.at[1, c]], gather_sems
    )
    here = pl.ds(pl.multiple_of(depth * p.ctx, depth), depth)
    sent = [
        push(time_own.at[pl.ds(deep * p.ctx, deep)], far_time.at[p.ctx], first_s.at[0], first_r.at[0], p.pair),
        push(hold_qkv.at[0, here], far_qkv.at[0, p.ctx], first_s.at[1], first_r.at[1], p.pair),
        push(hold_qkv.at[1, here], far_qkv.at[1, p.ctx], first_s.at[2], first_r.at[2], p.pair),
        push(table_own, table_all.at[p.wt], first_s.at[3], first_r.at[3], p.pair),
        push(gain_own, gain_all.at[p.wt], first_s.at[4], first_r.at[4], p.pair),
    ]
    rows_up = pl.ds(pl.multiple_of(p.core * half_up, half_up), half_up)
    rows_out = pl.ds(pl.multiple_of(p.core * half_out, half_out), half_out)
    crossing = [
        push(hold_out.at[rows_out], out_all.at[p.wt, rows_out], cross_s.at[0], cross_r.at[0], p.pair),
        push(hold_up.at[rows_up, theirs], up_all.at[p.wt, rows_up], cross_s.at[1], cross_r.at[1], p.pair),
        push(hold_cot, cot_all.at[1], cross_s.at[2], cross_r.at[2], p.pair),
    ]
    twins = [
        push(out_all.at[other, rows_out], out_all.at[other, rows_out], twin_s.at[0], twin_r.at[0], p.twin),
        push(up_all.at[other, rows_up], up_all.at[other, rows_up], twin_s.at[1], twin_r.at[1], p.twin),
    ]
    for copy in sent[3:] + sent[:1]:
        copy.start()
    for k in range(2):
        for copy in load[k]:
            copy.wait()
        sent[1 + k].start()
    for copy in holds:
        copy.wait()
    for copy in crossing:
        copy.start()
    table_all[p.wt] = table_own[...]
    gain_all[p.wt] = gain_own[...]
    normal[...] = normed(tokens[...].astype(F32))[0]
    for t in range(2):
        sent[t].wait_recv()
        g.own(t)
    times.wait()
    out = [pltpu.make_async_copy(hold_time, time_all.at[p.wt], time_s.at[1])]
    for k in range(2):
        for i in range(blocks):
            out.append(pltpu.make_async_copy(
                hold_qkv.at[k, :, held(i)], qkv_all.at[p.wt, :, natural(k, i)], block_out.at[0, k, i]))
    for copy in out:
        copy.start()
    for copy in sent[3:]:
        copy.wait_recv()
    kinds = 2 * table_own.shape[0]
    onehot = (lax.broadcasted_iota(jnp.int32, (kinds, tokens.shape[0]), 0) == levels[...]).astype(F32).astype(BF)
    embed[...] = dot(onehot, jnp.concatenate([table_all[0], table_all[1]]), 0, 0).astype(BF)
    thick = hold_time.shape[0]
    table_columns = pl.ds(pl.multiple_of(p.wt * thick, thick), thick)
    table_rows[...] = jnp.concatenate([table_all[k, :, table_columns] for k in range(2)])
    g_one[...] = jnp.concatenate([gain_all[0, 0:1], gain_all[1, 0:1]], axis=1).astype(F32)
    g_two[...] = jnp.concatenate([gain_all[0, 1:2], gain_all[1, 1:2]], axis=1).astype(F32)
    for t in range(2):
        g.along(t, 1)
    for t in range(2):
        g.along(t, 2)
    sent[2].wait_recv()
    g.own(2)
    for t in range(2):
        g.crossed_at(t, 0)
    for t in range(2):
        g.along(t, 3)
    g.along(2, 1)
    for d in (1, 2, 3):
        g.crossed_at(0, d)
    g.finish(0)
    far_to = qkv_all.at[other].reshape(16, depth, 3 * model)
    out.append(pltpu.make_async_copy(far_time, time_all.at[other].reshape(far_time.shape), time_s.at[2]))
    out[-1].start()

    def part_of(w, size):
        return pl.ds(pl.multiple_of(w * size, size), size)

    far_rows = jnp.concatenate([far_time[k] for k in range(16)])
    shifts = dot(embed[:, part_of(p.wt, thick)], hold_time[...]) + dot(embed[:, part_of(other, thick)], far_rows)
    scale_one[...] = 1.0 + shifts[:, :model]
    scale_two[...] = 1.0 + shifts[:, model:]
    rows_one[...] = (normal[...] * (g_one[...] * scale_one[...])).astype(BF)
    quarter = HEAD // 2
    wide = 2 * lane

    def project(group):
        near, far = rows_one[:, part_of(p.wt, half)], rows_one[:, part_of(other, half)]

        @pl.loop(0, blocks // 2)
        def _(k):
            cols = pl.ds(pl.multiple_of(k * wide, wide), wide)
            part = dot(near, hold_qkv[group, :, cols])
            part = (part + dot(far, far_qkv[group, :, :, cols].reshape(half, wide))).T
            base = lax.div(k, 2) * model + lax.rem(k, 2) * 2 * wide + group * lane

            @pl.when(k < blocks // 3)
            def _():
                for h in range(4):
                    first = part[h * HEAD : h * HEAD + quarter]
                    second = part[h * HEAD + quarter : (h + 1) * HEAD]
                    row = base + (h // 2) * wide + (h % 2) * HEAD
                    up, down = pl.multiple_of(row, HEAD), pl.multiple_of(row + quarter, quarter)
                    qkv_t[pl.ds(up, quarter), :] = (first * cosine[...] - second * sine[...]).astype(BF)
                    qkv_t[pl.ds(down, quarter), :] = (second * cosine[...] + first * sine[...]).astype(BF)

            @pl.when(k >= blocks // 3)
            def _():
                for h in range(2):
                    row = pl.multiple_of(base + h * wide, lane)
                    qkv_t[pl.ds(row, lane), :] = part[h * lane : (h + 1) * lane].astype(BF)

    def piece(part, c):
        return pl.ds(pl.multiple_of(part * model + c * HEAD, HEAD), HEAD)

    def lanes(c):
        return pl.ds(pl.multiple_of(c * width, width), width)

    def to_head(m, d, part):
        c = ring_peer(p, d)
        return push(
            qkv_t.at[piece(part, c), m * width : (m + 1) * width],
            qkv_in.at[m, part * HEAD : (part + 1) * HEAD, lanes(p.ctx)],
            in_s.at[m, d, part], in_r.at[m, d, part], {"ctx": c},
        )

    stay = [
        pltpu.make_async_copy(
            qkv_t.at[piece(part, p.ctx), m * width : (m + 1) * width],
            qkv_in.at[m, part * HEAD : (part + 1) * HEAD, lanes(p.ctx)],
            own_s.at[m, part],
        )
        for m in range(micro) for part in range(3)
    ]

    def to_group(group):
        @pl.when(p.y == group)
        def _():
            for copy in stay:
                copy.start()

        for m in range(micro):

            @pl.loop(0, 8)
            def _(e, m=m):
                i = lax.rem(e + p.ctx, 8)
                c = p.index(lax.div(i, 2), group, lax.rem(i, 2))

                @pl.when(c != p.ctx)
                def _():
                    for part in range(3):
                        to_head(m, lax.rem(c - p.ctx + 16, 16), part).start()

    def store_far(group):
        for i in range(blocks):
            out.append(pltpu.make_async_copy(
                far_qkv.at[group, :, :, held(i)], far_to.at[:, :, natural(group, i)], block_out.at[1, group, i]))
            out[-1].start()

    g.along(2, 2)
    for d in (1, 2, 3):
        g.crossed_at(1, d)
    g.finish(1)
    g.along(2, 3)
    project(0)
    to_group(0)
    store_far(0)
    for d in range(DEPTH):
        g.crossed_at(2, d)
    g.finish(2)
    project(1)
    to_group(1)
    store_far(1)
    placing = [
        pltpu.make_async_copy(hold_up.at[:, mine], up_all.at[p.wt], hold_to.at[0]),
        pltpu.make_async_copy(hold_out, out_all.at[p.wt], hold_to.at[1]),
        pltpu.make_async_copy(hold_cot, cot_all.at[0], hold_to.at[2]),
    ]
    for copy in placing:
        copy.start()

    def to_owner(m, c):
        return push(
            low.at[m, :, lanes(c)],
            att.at[pl.ds(pl.multiple_of(p.ctx * HEAD, HEAD), HEAD), m * width : (m + 1) * width],
            back_s.at[m, c], back_r.at[m, p.ctx], {"ctx": c},
        )

    keep_qkv = [pltpu.make_async_copy(qkv_in.at[m], qkv_keep.at[m], keep_s.at[0, m]) for m in range(micro)]
    keep_full = [pltpu.make_async_copy(full_ref.at[m], full_keep.at[m], keep_s.at[1, m]) for m in range(micro)]
    for m in range(micro):
        for part in range(3):
            stay[3 * m + part].wait()

        @pl.loop(1, 16)
        def _(d, m=m):
            for part in range(3):
                to_head(m, d, part).wait_recv()

        keep_qkv[m].start()
        keys[...] = qkv_in[m, HEAD : 2 * HEAD, :].T
        @pl.loop(0, length // block)
        def _(step, m=m):
            j = lax.rem(step + lax.div(p.ctx * width, block), length // block)
            cols = pl.ds(pl.multiple_of(j * block, block), block)
            scores = dot(keys[...], qkv_in[m, 0:HEAD, cols]) * (SCALE * LOG2E)
            top = jnp.max(scores, axis=0, keepdims=True)
            exps = jnp.exp2(scores - top)
            total = jnp.sum(exps, axis=0, keepdims=True)
            out = dot(qkv_in[m, 2 * HEAD :, :], exps.astype(BF)) / total
            full_ref[m, :, cols] = out
            lse_ref[m, :, cols] = top + jnp.log2(total)
            low[m, :, cols] = out.astype(BF)
            for i in range(block // width):
                c = j * (block // width) + i
                pl.when(p.ctx != c)(lambda c=c: to_owner(m, c).start())

        keep_full[m].start()
        att[pl.ds(pl.multiple_of(p.ctx * HEAD, HEAD), HEAD), m * width : (m + 1) * width] = low[
            m, :, pl.ds(pl.multiple_of(p.ctx * width, width), width)
        ]
        if m == 0:
            for t in range(2):
                crossing[t].wait_recv()
                twins[t].start()

    for m in range(micro):

        @pl.loop(1, 16)
        def _(d, m=m):
            c = ring_peer(p, d)
            push(
                low.at[m, :, 0:width],
                att.at[pl.ds(pl.multiple_of(c * HEAD, HEAD), HEAD), m * width : (m + 1) * width],
                back_s.at[m, 0], back_r.at[m, c], {"ctx": c},
            ).wait_recv()
            for part in range(3):
                to_head(m, d, part).wait_send()
            to_owner(m, c).wait_send()

    crossing[2].wait_recv()
    for copy in crossing:
        copy.wait_send()
    for copy in twins + placing + keep_qkv + keep_full + out:
        copy.wait()
    for copy in sent:
        copy.wait_send()


def front(qkv_w, time_w, table, gains, tokens, levels, cosine, sine, up_w, out_w, cot, micro, block):
    dma = pltpu.SemaphoreType.DMA
    vmem = pl.BlockSpec(memory_space=pltpu.VMEM)
    anywhere = pl.BlockSpec(memory_space=pltpu.HBM)
    shape = jax.ShapeDtypeStruct
    rows, model = tokens.shape
    length = rows // micro * 16
    columns = up_w.shape[1] // 2
    width = qkv_w.shape[1] // 2
    blocks = width // 128
    far_time = (16, time_w.shape[0] // 16, time_w.shape[1])
    outs = pl.pallas_call(
        functools.partial(front_kernel, block),
        out_shape=[
            shape((2,) + qkv_w.shape, BF),
            shape((2,) + time_w.shape, BF),
            shape((2 * table.shape[0], time_w.shape[0]), BF),
            shape((1, model), F32),
            shape((1, model), F32),
            shape((rows, model), F32),
            shape((rows, model), F32),
            shape((micro, 3 * HEAD, length), BF),
            shape((model, rows), BF),
            shape((micro, HEAD, length), F32),
            shape((micro, 1, length), F32),
            shape((2, up_w.shape[0], columns), BF),
            shape((2,) + out_w.shape, BF),
            shape((2,) + cot.shape, BF),
        ],
        in_specs=[anywhere, anywhere] + [vmem] * 6 + [anywhere] * 3,
        out_specs=[anywhere, anywhere] + [vmem] * 5 + [anywhere, vmem, anywhere, vmem] + [anywhere] * 3,
        scratch_shapes=[
            pltpu.VMEM((2,) + table.shape, BF),
            pltpu.VMEM((2,) + gains.shape, BF),
            pltpu.VMEM((2, qkv_w.shape[0], width), BF),
            pltpu.VMEM(time_w.shape, BF),
            pltpu.VMEM((2, 16, qkv_w.shape[0] // 16, width), BF),
            pltpu.VMEM(far_time, BF),
            pltpu.VMEM((rows, model), F32),
            pltpu.VMEM((rows, table.shape[1]), BF),
            pltpu.VMEM((rows, model), BF),
            pltpu.VMEM((qkv_w.shape[1], rows), BF),
            pltpu.VMEM((micro, 3 * HEAD, length), BF),
            pltpu.VMEM((micro, HEAD, length), F32),
            pltpu.VMEM((length, HEAD), BF),
            pltpu.VMEM((micro, HEAD, length), BF),
            pltpu.VMEM(up_w.shape, BF),
            pltpu.VMEM(out_w.shape, BF),
            pltpu.VMEM(cot.shape, BF),
            dma((2, blocks)),
            dma((2, 2, blocks)),
            dma((3,)),
            dma((5,)),
            dma((5,)),
            dma((2, micro)),
            dma((micro, 3)),
            dma((micro, 16, 3)),
            dma((micro, 16, 3)),
            dma((micro, 16)),
            dma((micro, 16)),
            dma((3,)),
            dma((3,)),
            dma((3,)),
            dma((3,)),
            dma((2,)),
            dma((2,)),
        ] + Gather.semaphores(3),
        compiler_params=pltpu.CompilerParams(
            collective_id=1, has_side_effects=True, vmem_limit_bytes=62 << 20
        ),
        name="front",
    )(qkv_w, time_w, table, gains, tokens, levels, cosine, sine, up_w, out_w, cot)
    qkv_all, time_all, table_rows, g_one, g_two, scale_one, scale_two, *attention, up_all, out_all, cot_all = outs
    return (
        qkv_all.reshape(-1, qkv_w.shape[1]),
        time_all.reshape(-1, time_w.shape[1]),
        table_rows, g_one, g_two, scale_one, scale_two, *attention,
        up_all.reshape(-1, columns), out_all.reshape(-1, model), cot_all.reshape(-1, model),
    )


def mid_kernel(
    att, tokens, scale_two, g_two, w_out, w_up_at, w_down_at, cot_at,
    out_part, out_other, grad_t, grad_mid, grad_scale, gain_two, up_to, down_to, out_term,
    middle, hat, scales, rows_two, hidden, grad_pre, far, far_grad, near_grad,
    w_up, w_down, cot, up_term, down_term,
    go_s, go_r, back_s, back_r, load_s, store_s,
):
    p = Place()
    rows, model = tokens.shape
    half = rows // 2
    loads = [
        pltpu.make_async_copy(source, target, load_s.at[i])
        for i, (source, target) in enumerate(((w_up_at, w_up), (cot_at, cot), (w_down_at, w_down)))
    ]
    for copy in loads:
        copy.start()
    barrier = pltpu.get_barrier_semaphore()
    pl.semaphore_signal(barrier, inc=1, device_id=p.pair, device_id_type=MESH)

    def to_pair(m):
        part = pl.ds(pl.multiple_of(m * half, half), half)
        there = pl.ds(pl.multiple_of(rows + m * half, half), half)
        return push(rows_two.at[part], rows_two.at[there], go_s.at[m], go_r.at[m], p.pair)

    def to_owner(m):
        part = pl.ds(pl.multiple_of(m * half, half), half)
        return push(far.at[part], far_grad.at[part], back_s.at[m], back_r.at[m], p.pair)

    weight = g_two[...] * scale_two[...]
    for m in range(2):
        part = slice(m * half, (m + 1) * half)
        middle[part] = tokens[part].astype(F32) + dot(att[:, part], w_out[...], 0, 0)
        normal, scale = normed(middle[part])
        hat[part] = normal
        scales[part] = scale
        rows_two[part] = (normal * weight[part]).astype(BF)
        if m == 0:
            pl.semaphore_wait(barrier, 1)
        to_pair(m).start()

    wide = 512

    def chunk(k):
        return pl.ds(pl.multiple_of(k * wide, wide), wide)

    def feed(part):
        @pl.loop(0, w_up.shape[1] // wide)
        def _(k):
            cols = chunk(k)
            pre = dot(rows_two[part], w_up[:, cols])
            cdf = 0.5 * (1.0 + lax.erf(pre * (2.0**-0.5)))
            hidden[part, cols] = (pre * cdf).astype(BF)
            density = jnp.exp(-0.5 * pre * pre) * (1.0 / math.sqrt(2.0 * math.pi))
            grad_pre[part, cols] = (dot(cot[part], w_down[cols, :], 1, 1) * (cdf + pre * density)).astype(BF)

    for copy in loads:
        copy.wait()
    feed(slice(0, rows))

    @pl.loop(0, 2)
    def _(m):
        to_pair(m).wait_recv()
        there = pl.ds(pl.multiple_of(rows + m * half, half), half)
        feed(there)
        far[pl.ds(pl.multiple_of(m * half, half), half)] = dot(grad_pre[there], w_up[...], 1, 1).astype(BF)
        to_owner(m).start()

    @pl.loop(0, model // wide)
    def _(k):
        cols = chunk(k)
        near_grad[:, cols] = dot(grad_pre[0:rows], w_up[cols, :], 1, 1)

    def stores(k):
        cols = chunk(k)
        return (
            pltpu.make_async_copy(up_term.at[:, cols], up_to.at[:, cols], store_s.at[0, k]),
            pltpu.make_async_copy(down_term.at[cols, :], down_to.at[cols, :], store_s.at[1, k]),
        )

    @pl.loop(0, up_term.shape[1] // wide)
    def _(k):
        cols = chunk(k)
        up_term[:, cols] = dot(rows_two[...], grad_pre[:, cols], 0, 0).astype(BF)
        down_term[cols, :] = dot(hidden[:, cols], cot[...], 0, 0).astype(BF)
        for copy in stores(k):
            copy.start()

    @pl.loop(0, model // wide)
    def _(k):
        cols = chunk(k)
        both = dot(hidden[...], w_down[:, cols])
        out_part[:, cols] = middle[:, cols] + both[:rows]
        out_other[:, cols] = both[rows:].astype(BF)


    for m in range(2):
        to_owner(m).wait_recv()
    grad = near_grad[...] + far_grad[...].astype(F32)
    mid = cot[0:rows].astype(F32) + norm_back(grad, hat[...], scales[...], weight)
    grad_mid[...] = mid
    low = mid.astype(BF)
    grad_t[...] = dot(w_out[...], low, 1, 1).astype(BF)
    eh = grad * hat[...]
    grad_scale[...] = (eh * g_two[...]).astype(BF)
    gain_two[...] = jnp.sum(eh * scale_two[...], axis=0, keepdims=True)
    out_term[...] = dot(att[...], low).astype(BF)
    for k in range(up_term.shape[1] // wide):
        for copy in stores(k):
            copy.wait()
    for m in range(2):
        to_pair(m).wait_send()
        to_owner(m).wait_send()


def mid_pass(att, tokens, scale_two, g_two, w_out, w_up, w_down, cot):
    dma = pltpu.SemaphoreType.DMA
    vmem = pl.BlockSpec(memory_space=pltpu.VMEM)
    anywhere = pl.BlockSpec(memory_space=pltpu.HBM)
    rows, model = tokens.shape
    hidden = w_up.shape[1]
    shape = jax.ShapeDtypeStruct
    return pl.pallas_call(
        mid_kernel,
        out_shape=[
            shape((rows, model), F32), shape((rows, model), BF), shape((model, rows), BF),
            shape((rows, model), F32), shape((rows, model), BF), shape((1, model), F32),
            shape((model, hidden), BF), shape((hidden, model), BF), shape((model, model), BF),
        ],
        in_specs=[vmem] * 5 + [anywhere] * 3,
        out_specs=[vmem] * 6 + [anywhere] * 2 + [vmem],
        scratch_shapes=[
            pltpu.VMEM((rows, model), F32),
            pltpu.VMEM((rows, model), F32),
            pltpu.VMEM((rows, 1), F32),
            pltpu.VMEM((2 * rows, model), BF),
            pltpu.VMEM((2 * rows, hidden), BF),
            pltpu.VMEM((2 * rows, hidden), BF),
            pltpu.VMEM((rows, model), BF),
            pltpu.VMEM((rows, model), BF),
            pltpu.VMEM((rows, model), F32),
            pltpu.VMEM(w_up.shape, BF),
            pltpu.VMEM(w_down.shape, BF),
            pltpu.VMEM(cot.shape, BF),
            pltpu.VMEM((model, hidden), BF),
            pltpu.VMEM((hidden, model), BF),
            dma((2,)), dma((2,)), dma((2,)), dma((2,)), dma((3,)), dma((2, hidden // 512)),
        ],
        compiler_params=pltpu.CompilerParams(
            collective_id=5, has_side_effects=True, vmem_limit_bytes=60 << 20
        ),
        name="mid_pass",
    )(att, tokens, scale_two, g_two, w_out, w_up, w_down, cot)


ORDER = (3, 0, 2, 1)


def back_kernel(
    block, grad_t, qkv_in, full_ref, lse_ref, up_term, down_term, out_term, w_qkv,
    cosine, sine, tokens, levels_row, g_one, scale_one, grad_mid, grad_scale_two, gain_two,
    out_part, out_other, input_grad, layer_out, up_all, down_all, out_all, qkv_all, small_all,
    keys, values, g_in, dq, dq_low, dkv_low, delta, grad_qkv, w_hold, grad_norm_t,
    term, q_twin, q_pair, up_sum, down_sum, out_sum, out_pair, out_own, qkv_sum, small, small_in, small_pair, out_came, norm_t, hat, rs_one,
    own_s, in_s, in_r, back_s, back_r, w_s, q_ts, q_tr, q_ps, q_pr, cross_s, cross_r, local_s,
    small_s, small_r, small_x, spread_s, spread_r, *more,
):
    p = Place()
    micro, _, length = qkv_in.shape
    width = length // 16
    model = grad_t.shape[0]
    count = 3
    cut = 2 * count + 3
    halves = Halves(
        p, [lambda c: up_term.at[:, c], lambda c: down_term.at[c], lambda c: out_term.at[:, c]], more[:cut]
    )
    more = more[cut:]
    cut = 2 * count + 6
    f_line = Line(p, count, halves.mine, more[:cut])
    more = more[cut:]
    q_line = Line(p, 1, lambda t, z, y: term.at[p.wt, p.index(z, y, p.core)], more[:8])
    half = down_term.shape[1] // 2
    depth = term.shape[2]
    split = depth // 2
    g = Gather(
        p,
        [
            lambda c: up_all.at[p.wt, c],
            lambda c: up_all.at[1 - p.wt, c],
            lambda c: down_all.at[c, 0:half],
            lambda c: down_all.at[c, half:],
            lambda c: out_all.at[c],
            lambda c: qkv_all.at[c, 0:split],
            lambda c: qkv_all.at[c, split:],
        ],
        more[8:],
        wide=(),
    )
    fixed, late = (3, 2, 0, 4, 1), (5, 6)
    p.greet(everyone=True)

    def rows_of(part, c):
        return pl.ds(pl.multiple_of(part * model + c * HEAD, HEAD), HEAD)

    def lanes(c):
        return pl.ds(pl.multiple_of(c * width, width), width)

    def to_head(m, d):
        c = ring_peer(p, d)
        return push(
            grad_t.at[rows_of(0, c), m * width : (m + 1) * width],
            g_in.at[m, :, lanes(p.ctx)], in_s.at[m, d], in_r.at[m, d], {"ctx": c},
        )

    stay = [
        pltpu.make_async_copy(
            grad_t.at[rows_of(0, p.ctx), m * width : (m + 1) * width],
            g_in.at[m, :, lanes(p.ctx)], own_s.at[m],
        )
        for m in range(micro)
    ]
    layer_cross = push(out_other, out_came, cross_s.at[2], cross_r.at[2], p.pair)
    layer_cross.start()
    for m in range(micro):
        stay[m].start()

        @pl.loop(1, 16)
        def _(d, m=m):
            to_head(m, d).start()

        halves.begin(ORDER[m])
    for z in ORDER[micro:]:
        halves.begin(z)
    chunk = w_hold.shape[1]
    chunks = model // chunk

    normal, rs_one[...] = normed(tokens[...].astype(F32))
    hat[...] = normal
    norm_t[...] = (normal * (g_one[...] * scale_one[...])).T.astype(BF)

    def w_chunk(k):
        slot = lax.rem(k, 2)
        return pltpu.make_async_copy(
            w_qkv.at[pl.ds(pl.multiple_of(k * chunk, chunk), chunk)], w_hold.at[slot], w_s.at[slot]
        )

    w_chunk(jnp.int32(0)).start()
    w_chunk(jnp.int32(1)).start()
    for z in (3, 0):
        halves.halve(z)
        f_line.cross(z)

    def to_owner(m, c, part):
        source = dq_low.at[m] if part == 0 else dkv_low.at[m, part - 1]
        return push(
            source.at[:, lanes(c)],
            grad_qkv.at[rows_of(part, p.ctx), m * width : (m + 1) * width],
            back_s.at[m, c, part], back_r.at[m, p.ctx, part], {"ctx": c},
        )

    def send(m, c, part):
        pl.when(p.ctx != c)(lambda: to_owner(m, c, part).start())

    for m in range(micro):
        keys[...] = qkv_in[m, HEAD : 2 * HEAD, :].T
        values[...] = qkv_in[m, 2 * HEAD :, :].T
        stay[m].wait()

        @pl.loop(1, 16)
        def _(d, m=m):
            to_head(m, d).wait_recv()

        delta[...] = jnp.sum(g_in[m].astype(F32) * full_ref[m], axis=0, keepdims=True)
        dq[...] = jnp.zeros_like(dq)

        @pl.loop(0, length // block)
        def _(step, m=m):
            j = lax.rem(step + lax.div(p.ctx * width, block), length // block)
            cols = pl.ds(pl.multiple_of(j * block, block), block)
            scores = dot(keys[cols, :], qkv_in[m, 0:HEAD, :]) * (SCALE * LOG2E)
            soft = jnp.exp2(scores - lse_ref[m])
            grad_soft = dot(values[cols, :], g_in[m])
            raw = (soft * (grad_soft - delta[...]) * SCALE).astype(BF)
            dkv_low[m, 0, :, cols] = dot(qkv_in[m, 0:HEAD, :], raw, 1, 1).astype(BF)
            dkv_low[m, 1, :, cols] = dot(g_in[m], soft.astype(BF), 1, 1).astype(BF)
            dq[...] += dot(qkv_in[m, HEAD : 2 * HEAD, cols], raw)
            for i in range(block // width):
                send(m, j * (block // width) + i, 1)
                send(m, j * (block // width) + i, 2)
            if m == micro - 1:

                @pl.when((step + 1) * block * 2 == length)
                def _():
                    f_line.quarter(3)
                    f_line.right(3, 0)

        dq_low[m] = dq[...].astype(BF)

        @pl.loop(1, 16)
        def _(d, m=m):
            to_owner(m, ring_peer(p, d), 0).start()

        if m == 0:
            halves.halve(2)
            halves.halve(1)
        here = lanes(p.ctx)
        to = slice(m * width, (m + 1) * width)
        grad_qkv[rows_of(0, p.ctx), to] = dq_low[m, :, here]
        grad_qkv[rows_of(1, p.ctx), to] = dkv_low[m, 0, :, here]
        grad_qkv[rows_of(2, p.ctx), to] = dkv_low[m, 1, :, here]

    f_line.cross(2)
    f_line.cross(1)
    layer_cross.wait()
    layer_out[...] = (out_part[...] + out_came[...].astype(F32)).astype(BF)
    f_line.quarter(0)
    f_line.left(0, 3)
    f_line.right(3, 1)
    f_line.left(0, 2)

    for m in range(micro):

        @pl.loop(1, 16)
        def _(d, m=m):
            c = ring_peer(p, d)
            for part in range(3):
                push(
                    dq_low.at[m, :, 0:width],
                    grad_qkv.at[rows_of(part, c), m * width : (m + 1) * width],
                    back_s.at[m, 0, part], back_r.at[m, c, part], {"ctx": c},
                ).wait_recv()

    low_half = HEAD // 2

    @pl.loop(0, 2 * model // HEAD)
    def _(h):
        upper = pl.ds(pl.multiple_of(h * HEAD, HEAD), low_half)
        lower = pl.ds(pl.multiple_of(h * HEAD + low_half, low_half), low_half)
        first, second = grad_qkv[upper, :].astype(F32), grad_qkv[lower, :].astype(F32)
        grad_qkv[upper, :] = (first * cosine[...] + second * sine[...]).astype(BF)
        grad_qkv[lower, :] = (second * cosine[...] - first * sine[...]).astype(BF)


    group = 4 * depth

    def q_to_twin(w, z, y):
        return push(
            term.at[w, p.index(z, y, 1 - p.core)], q_twin.at[w, z, y], q_ts.at[w, z, y], q_tr.at[w, z, y], p.twin
        )

    def q_to_pair(z, y):
        return push(
            term.at[1 - p.wt, p.index(z, y, p.core)], q_pair.at[z, y], q_ps.at[z, y], q_pr.at[z, y], p.pair
        )

    def with_twin(w, z, y):
        q_to_twin(w, z, y).wait_recv()
        here = p.index(z, y, p.core)
        term[w, here] = (term[w, here].astype(F32) + q_twin[w, z, y].astype(F32)).astype(BF)

    def product(w, z):
        start_row = pl.multiple_of(w * (model // 2) + z * group, group)
        rows = dot(norm_t[pl.ds(start_row, group), :], grad_qkv[...], 1, 1).astype(BF)
        for i in range(4):
            term[w, 4 * z + i] = rows[i * depth : (i + 1) * depth]
        for y in range(2):
            q_to_twin(w, z, y).start()

    def by_order(step):
        odd = lax.rem(step, 2)
        return (1 - odd) * (DEPTH - 1 - lax.div(step, 2)) + odd * lax.div(step, 2)

    @pl.loop(0, DEPTH)
    def _(step):
        product(1 - p.wt, by_order(step))

    f_line.right(3, 2)
    f_line.left(0, 1)

    @pl.loop(0, 2 * DEPTH)
    def _(step):
        z, y = by_order(lax.div(step, 2)), lax.rem(step, 2)
        with_twin(1 - p.wt, z, y)
        q_to_pair(z, y).start()

    @pl.loop(0, DEPTH)
    def _(step):
        product(p.wt, by_order(step))


    @pl.loop(0, chunks)
    def _(k):
        w_chunk(k).wait()
        grad_norm_t[pl.ds(pl.multiple_of(k * chunk, chunk), chunk), :] = dot(w_hold[lax.rem(k, 2)], grad_qkv[...])
        pl.when(k + 2 < chunks)(lambda: w_chunk(k + 2).start())

    grad_norm = grad_norm_t[...].T
    c_rows = grad_norm * (g_one[...] * scale_one[...])
    input_grad[...] = (
        grad_mid[...]
        + (
            c_rows
            - jnp.mean(c_rows, axis=-1, keepdims=True)
            - hat[...] * jnp.mean(c_rows * hat[...], axis=-1, keepdims=True)
        )
        * rs_one[...]
    ).astype(BF)
    eh = grad_norm * hat[...]
    grad_scale_one = (eh * g_one[...]).astype(BF)
    gain_one = jnp.sum(eh * scale_one[...], axis=0, keepdims=True)

    levels = LEVELS
    marks = lax.broadcasted_iota(jnp.int32, (levels, levels_row.shape[1]), 0)
    onehot_t = (marks == levels_row[...]).astype(F32).astype(BF)
    fill = jnp.zeros((small.shape[1] - levels - 1, 128), BF)
    for side, shifts, gain in ((0, grad_scale_one, gain_one), (1, grad_scale_two[...], gain_two[...])):
        level = dot(onehot_t, shifts).astype(BF)
        for k in range(8):
            cols = slice(k * 128, (k + 1) * 128)
            small[8 * side + k, 0:levels, :] = level[:, cols]
            small[8 * side + k, levels:, :] = jnp.concatenate([gain[:, cols].astype(BF), fill])

    def small_to(d):
        peer = ring_peer(p, d)
        return push(small.at[peer], small_in.at[p.ctx], small_s.at[d], small_r.at[d], {"ctx": peer})


    @pl.loop(1, 16)
    def _(d):
        small_to(d).start()

    small_in[p.ctx] = small[p.ctx]

    @pl.loop(0, 2 * DEPTH)
    def _(step):
        with_twin(p.wt, by_order(lax.div(step, 2)), lax.rem(step, 2))


    out_cross = push(out_sum.at[1 - p.wt], out_pair, cross_s.at[0], cross_r.at[0], p.pair)
    up_cross = push(up_sum.at[1 - p.wt], up_all.at[p.wt, p.ctx], cross_s.at[1], cross_r.at[1], p.pair)
    up_came = push(up_sum.at[p.wt], up_all.at[1 - p.wt, p.ctx], cross_s.at[1], cross_r.at[1], p.pair)
    sources = {0: up_sum.at[p.wt], 2: down_sum.at[0:half], 3: down_sum.at[half:], 4: out_own,
               5: qkv_sum.at[0:split], 6: qkv_sum.at[split:]}

    def f_end(z):
        @pl.when(p.z == z)
        def _():
            f_line.end(z, [up_sum, down_sum, out_sum])
            out_cross.start()
            up_cross.start()

    def q_cross(z):
        for y in (1 - p.y, p.y):
            q_to_pair(z, y).wait_recv()
            here = p.index(z, y, p.core)
            term[p.wt, here] = (term[p.wt, here].astype(F32) + q_pair[z, y].astype(F32)).astype(BF)
        q_line.cross(z)

    f_line.quarter(2)
    f_line.right(2, 0)
    q_cross(3)
    f_line.right(2, 1)
    f_line.quarter(1)
    f_line.left(1, 3)
    f_line.right(1, 0)
    f_line.left(2, 3)
    q_cross(0)
    q_line.quarter(3)
    q_line.right(3, 0)
    f_line.left(1, 2)
    q_cross(2)
    q_line.quarter(0)
    q_line.left(0, 3)
    q_line.right(3, 1)
    q_line.left(0, 2)
    q_cross(1)
    q_line.right(3, 2)
    q_line.left(0, 1)
    q_line.quarter(2)
    q_line.right(2, 0)
    q_line.quarter(1)
    q_line.left(1, 3)
    q_line.right(1, 0)
    q_line.left(2, 3)
    for z in range(DEPTH):
        f_end(z)

    @pl.loop(1, 16)
    def _(d):
        small_to(d).wait_recv()

    small_pair[0] = jnp.sum(small_in[...].astype(F32), axis=0).astype(BF)
    small_cross = push(small_pair.at[0], small_pair.at[1], small_x.at[0], small_x.at[1], p.pair)
    small_cross.start()
    q_line.right(2, 1)
    q_line.left(1, 2)

    for t in (3, 2, 0):
        g.own(t, sources[t])
    out_cross.wait_recv()
    out_own[...] = (out_sum[p.wt].astype(F32) + out_pair[...].astype(F32)).astype(BF)
    g.own(4, sources[4])
    up_came.wait_recv()
    g.own(1)
    for z in range(DEPTH):
        pl.when(p.z == z)(lambda z=z: q_line.end(z, [qkv_sum]))
    for t in late:
        g.own(t, sources[t])

    small_cross.wait()
    small_all[p.ctx] = (small_pair[0].astype(F32) + small_pair[1].astype(F32)).astype(BF)

    def small_spread(d):
        peer = ring_peer(p, d)
        return push(small_all.at[p.ctx], small_all.at[p.ctx], spread_s.at[d], spread_r.at[d], {"ctx": peer})


    @pl.loop(1, 16)
    def _(d):
        small_spread(d).start()

    copies = [pltpu.make_async_copy(sources[t], g.items[t](p.ctx), local_s.at[t]) for t in sources]
    for copy in copies:
        copy.start()
    every = fixed + late
    for t in every:
        g.along(t, 1)
    for t in every:
        g.along(t, 2)
    for t in every:
        if t not in g.wide:
            g.crossed_at(t, 0)
    for t in every:
        g.along(t, 3)
    for d in (1, 2, 3):
        for t in every:
            g.crossed_at(t, d)

    for copy in copies:
        copy.wait()
    for t in range(len(g.items)):
        g.finish(t)
    halves.finish()
    f_line.finish()
    q_line.finish()
    out_cross.wait_send()
    up_cross.wait_send()

    @pl.loop(1, 16)
    def _(d):
        small_to(d).wait_send()
        small_spread(d).wait()

    for z in range(DEPTH):
        for y in range(2):
            q_to_pair(z, y).wait_send()
            for w in range(2):
                q_to_twin(w, z, y).wait_send()
    for m in range(micro):

        @pl.loop(1, 16)
        def _(d, m=m):
            to_head(m, d).wait_send()
            for part in range(3):
                to_owner(m, ring_peer(p, d), part).wait_send()


def back_pass(grad_t, qkv_in, full, lse, up, down, out, w_qkv, rest, block):
    dma = pltpu.SemaphoreType.DMA
    vmem = pl.BlockSpec(memory_space=pltpu.VMEM)
    anywhere = pl.BlockSpec(memory_space=pltpu.HBM)
    micro, _, length = qkv_in.shape
    model, rows = grad_t.shape
    pieces = [up.shape[:1] + up.shape[2:], down.shape[1:], out.shape[:1] + out.shape[2:]]
    piece = (model // 32, 3 * model)
    small = (16, 80, 128)
    return pl.pallas_call(
        functools.partial(back_kernel, block),
        out_shape=[
            jax.ShapeDtypeStruct((rows, model), BF),
            jax.ShapeDtypeStruct((rows, model), BF),
            jax.ShapeDtypeStruct((2, 16) + up.shape[2:], BF),
            jax.ShapeDtypeStruct(down.shape, BF),
            jax.ShapeDtypeStruct(out.shape[1:], BF),
            jax.ShapeDtypeStruct((16,) + piece, BF),
            jax.ShapeDtypeStruct(small, BF),
        ],
        in_specs=[vmem] * 4 + [anywhere] * 4 + [vmem] * len(rest),
        out_specs=[vmem] * 2 + [anywhere] * 4 + [vmem],
        scratch_shapes=[
            pltpu.VMEM((length, HEAD), BF),
            pltpu.VMEM((length, HEAD), BF),
            pltpu.VMEM((micro, HEAD, length), BF),
            pltpu.VMEM((HEAD, length), F32),
            pltpu.VMEM((micro, HEAD, length), BF),
            pltpu.VMEM((micro, 2, HEAD, length), BF),
            pltpu.VMEM((1, length), F32),
            pltpu.VMEM((3 * model, rows), BF),
            pltpu.VMEM((2, 128, 3 * model), BF),
            pltpu.VMEM((model, rows), F32),
            pltpu.VMEM((2, 16) + piece, BF),
            pltpu.VMEM((2, DEPTH, 2) + piece, BF),
            pltpu.VMEM((DEPTH, 2) + piece, BF),
            pltpu.VMEM(pieces[0], BF),
            pltpu.VMEM(pieces[1], BF),
            pltpu.VMEM(pieces[2], BF),
            pltpu.VMEM(pieces[2][1:], BF),
            pltpu.VMEM(pieces[2][1:], BF),
            pltpu.VMEM(piece, BF),
            pltpu.VMEM(small, BF),
            pltpu.VMEM(small, BF),
            pltpu.VMEM((2,) + small[1:], BF),
            pltpu.VMEM((rows, model), BF),
            pltpu.VMEM((model, rows), BF),
            pltpu.VMEM((rows, model), F32),
            pltpu.VMEM((rows, 1), F32),
            dma((micro,)),
            dma((micro, 16)),
            dma((micro, 16)),
            dma((micro, 16, 3)),
            dma((micro, 16, 3)),
            dma((2,)),
            dma((2, DEPTH, 2)),
            dma((2, DEPTH, 2)),
            dma((DEPTH, 2)),
            dma((DEPTH, 2)),
            dma((3,)),
            dma((3,)),
            dma((7,)),
            dma((16,)),
            dma((16,)),
            dma((2,)),
            dma((16,)),
            dma((16,)),
        ]
        + Halves.scratch(pieces)
        + Line.scratch(pieces)
        + Line.scratch([piece])
        + Gather.semaphores(7),
        compiler_params=pltpu.CompilerParams(
            collective_id=4, has_side_effects=True, vmem_limit_bytes=63 << 20
        ),
        name="back_pass",
    )(grad_t, qkv_in, full, lse, up, down, out, w_qkv, *rest)


def spread(source, pieces, first, target):
    width = source.shape[-1]
    for c in range(pieces):
        target[:, c * width : (c + 1) * width] = source[c, 0, first : first + HEAD, :]


def attend_kernel(pieces, block, qkv_ref, low_ref, full_ref, lse_ref, q_t, k_t, v_t, keys):
    length = q_t.shape[1]
    width = length // pieces
    spread(qkv_ref, pieces, 0, q_t)
    spread(qkv_ref, pieces, HEAD, k_t)
    spread(qkv_ref, pieces, 2 * HEAD, v_t)
    keys[...] = k_t[...].T
    for j in range(length // block):
        cols = slice(j * block, (j + 1) * block)
        scores = dot(keys[...], q_t[:, cols]) * (SCALE * LOG2E)
        top = jnp.max(scores, axis=0, keepdims=True)
        exps = jnp.exp2(scores - top)
        total = jnp.sum(exps, axis=0, keepdims=True)
        out = dot(v_t[...], exps.astype(BF)) / total
        full_ref[0, :, cols] = out
        lse_ref[0, :, cols] = top + jnp.log2(total)
        for c in range(block // width):
            low_ref[j * (block // width) + c, 0] = out[:, c * width : (c + 1) * width].astype(BF)


def attend(qkv, block):
    pieces, pairs, _, width = qkv.shape
    length = pieces * width
    return pl.pallas_call(
        functools.partial(attend_kernel, pieces, block),
        grid=(pairs,),
        in_specs=[pl.BlockSpec((pieces, 1, 3 * HEAD, width), lambda p: (0, p, 0, 0))],
        out_specs=[
            pl.BlockSpec((pieces, 1, HEAD, width), lambda p: (0, p, 0, 0)),
            pl.BlockSpec((1, HEAD, length), lambda p: (p, 0, 0)),
            pl.BlockSpec((1, 1, length), lambda p: (p, 0, 0)),
        ],
        out_shape=[
            jax.ShapeDtypeStruct((pieces, pairs, HEAD, width), BF),
            jax.ShapeDtypeStruct((pairs, HEAD, length), F32),
            jax.ShapeDtypeStruct((pairs, 1, length), F32),
        ],
        scratch_shapes=[pltpu.VMEM((HEAD, length), BF)] * 3 + [pltpu.VMEM((length, HEAD), BF)],
        compiler_params=pltpu.CompilerParams(vmem_limit_bytes=48 << 20),
        name="attend",
    )(qkv)


def attend_back_kernel(
    pieces, block, qkv_ref, grad_ref, full_ref, lse_ref, out_ref,
    q_t, k_t, v_t, g_t, keys, values, dq_t, dk, dv,
):
    length = q_t.shape[1]
    width = length // pieces
    spread(qkv_ref, pieces, 0, q_t)
    spread(qkv_ref, pieces, HEAD, k_t)
    spread(qkv_ref, pieces, 2 * HEAD, v_t)
    spread(grad_ref, pieces, 0, g_t)
    keys[...] = k_t[...].T
    values[...] = v_t[...].T
    for j in range(length // block):
        cols = slice(j * block, (j + 1) * block)
        query = q_t[:, cols]
        grad = g_t[:, cols]
        delta = jnp.sum(grad.astype(F32) * full_ref[0, :, cols], axis=0, keepdims=True)
        scores = dot(keys[...], query) * (SCALE * LOG2E)
        soft = jnp.exp2(scores - lse_ref[0, :, cols])
        term_v = dot(soft.astype(BF), grad, 1, 1)
        grad_soft = dot(values[...], grad)
        raw = (soft * (grad_soft - delta) * SCALE).astype(BF)
        term_k = dot(raw, query, 1, 1)
        dq_t[:, cols] = dot(k_t[...], raw)
        if j == 0:
            dv[...] = term_v
            dk[...] = term_k
        else:
            dv[...] += term_v
            dk[...] += term_k
    dk_t = dk[...].T.astype(BF)
    dv_t = dv[...].T.astype(BF)
    for c in range(pieces):
        piece = slice(c * width, (c + 1) * width)
        out_ref[c, 0, 0:HEAD, :] = dq_t[:, piece].astype(BF)
        out_ref[c, 0, HEAD : 2 * HEAD, :] = dk_t[:, piece]
        out_ref[c, 0, 2 * HEAD :, :] = dv_t[:, piece]


def attend_back(qkv, grad, full, lse, block):
    pieces, pairs, _, width = qkv.shape
    length = pieces * width
    return pl.pallas_call(
        functools.partial(attend_back_kernel, pieces, block),
        grid=(pairs,),
        in_specs=[
            pl.BlockSpec((pieces, 1, 3 * HEAD, width), lambda p: (0, p, 0, 0)),
            pl.BlockSpec((pieces, 1, HEAD, width), lambda p: (0, p, 0, 0)),
            pl.BlockSpec((1, HEAD, length), lambda p: (p, 0, 0)),
            pl.BlockSpec((1, 1, length), lambda p: (p, 0, 0)),
        ],
        out_specs=pl.BlockSpec((pieces, 1, 3 * HEAD, width), lambda p: (0, p, 0, 0)),
        out_shape=jax.ShapeDtypeStruct(qkv.shape, BF),
        scratch_shapes=[pltpu.VMEM((HEAD, length), BF)] * 4
        + [pltpu.VMEM((length, HEAD), BF)] * 2
        + [pltpu.VMEM((HEAD, length), F32)]
        + [pltpu.VMEM((length, HEAD), F32)] * 2,
        compiler_params=pltpu.CompilerParams(vmem_limit_bytes=56 << 20),
        name="attend_back",
    )(qkv, grad, full, lse)


def normed(rows):
    centered = rows - jnp.mean(rows, axis=-1, keepdims=True)
    scale = lax.rsqrt(jnp.mean(centered * centered, axis=-1, keepdims=True) + EPSILON)
    return centered * scale, scale


def norm_back(grad, hat, scale, weight):
    c = grad * weight
    return (
        c - jnp.mean(c, axis=-1, keepdims=True) - hat * jnp.mean(c * hat, axis=-1, keepdims=True)
    ) * scale


def turn(first, second, cosine, sine):
    return first * cosine - second * sine, second * cosine + first * sine


def shards(
    tokens, positions, buckets, qkv_w, out_w, up_w, down_w, time_w, noise_table,
    gain_one, gain_two, cotangent,
):
    n, ring = lax.axis_size("wt"), lax.axis_size("ctx")
    me = lax.axis_index("wt")
    micro, _, width, model = tokens.shape
    rows = micro * width
    pairs = HEADS * micro // ring
    block = 256
    planar = n == 2 and ring == 16

    x = tokens.reshape(rows, model).astype(F32)
    cot_low = cotangent.reshape(rows, model)
    places = positions.reshape(rows)
    levels = buckets.reshape(rows)

    def whole_rows(weight):
        return lax.all_gather(weight, "wt", axis=0, tiled=True)

    frequency = jnp.exp(
        jnp.arange(HEAD // 2, dtype=F32) * (-math.log(10000.0) * 2.0 / HEAD)
    )
    angles = frequency[:, None] * places.astype(F32)[None, :]
    cosine, sine = jnp.cos(angles), jnp.sin(angles)
    stacked = jnp.stack([gain_one, gain_two])
    if planar:
        (
            w_qkv, w_time, table_rows, g_one, g_two, scale_one, scale_two, qkv_heads, attended, full, lse, w_up, w_out, cot,
        ) = front(
            qkv_w, time_w, noise_table, stacked, tokens.reshape(rows, model), levels[None], cosine, sine,
            up_w, out_w, cot_low, micro, block,
        )
    else:
        w_qkv = whole_rows(qkv_w)
        w_out = whole_rows(out_w)
        w_time = whole_rows(time_w)
        table = whole_rows(noise_table)
        gains = lax.all_gather(stacked, "wt", axis=1, tiled=True)
        w_up = lax.all_to_all(up_w, "wt", 1, 0, tiled=True)
        g_one, g_two = gains[0].astype(F32), gains[1].astype(F32)

        onehot = levels[:, None] == jnp.arange(table.shape[0], dtype=jnp.int32)[None, :]
        embed = dot(onehot.astype(BF), table).astype(BF)
        shifts = dot(embed, w_time)
        scale_one = 1.0 + shifts[:, :model]
        scale_two = 1.0 + shifts[:, model:]

        hat_one, rs_one = normed(x)
        weight_one = g_one * scale_one
        norm_one = (hat_one * weight_one).astype(BF)

        qkv_t = dot(w_qkv, norm_one, 0, 1).reshape(3, HEADS, 2, HEAD // 2, rows)
        turned = turn(qkv_t[:2, :, 0], qkv_t[:2, :, 1], cosine, sine)
        queries_keys = jnp.stack(turned, axis=2)
        qkv_low = jnp.concatenate([queries_keys.astype(BF), qkv_t[2:].astype(BF)])

    def to_heads(columns):
        parts = columns.shape[0]
        split = columns.reshape(parts, HEADS, HEAD, micro, width)
        split = jnp.transpose(split, (1, 3, 0, 2, 4))
        split = split.reshape(ring, pairs, parts * HEAD, width)
        return lax.all_to_all(split, "ctx", 0, 0, tiled=True)

    def to_tokens(pieces):
        parts = pieces.shape[2] // HEAD
        back = lax.all_to_all(pieces, "ctx", 0, 0, tiled=True)
        back = back.reshape(HEADS, micro, parts, HEAD, width)
        return jnp.transpose(back, (2, 0, 3, 1, 4)).reshape(parts, HEADS * HEAD, rows)

    if not planar:
        qkv_heads = to_heads(qkv_low.reshape(3, HEADS, HEAD, rows))
        low, full, lse = attend(qkv_heads, block)
        attended = to_tokens(low)[0]
        cot = gather_slots(cot_low).reshape(n * rows, model)

    if not planar:
        middle = x + dot(attended, w_out, 0, 0)
        hat_two, rs_two = normed(middle)
        weight_two = g_two * scale_two
        norm_two_own = (hat_two * weight_two).astype(BF)

        norm_two = gather_slots(norm_two_own).reshape(n * rows, model)
        pre = dot(norm_two, w_up)
        phi_cdf = 0.5 * (1.0 + lax.erf(pre * (2.0**-0.5)))
        hidden = (pre * phi_cdf).astype(BF)
        out_parts = dot(hidden, down_w).reshape(n, rows, model)

        grad_hidden = dot(cot, down_w, 1, 1)
        density = jnp.exp(-0.5 * pre * pre) * (1.0 / math.sqrt(2.0 * math.pi))
        grad_pre = (grad_hidden * (phi_cdf + pre * density)).astype(BF)
        grad_norm_two = sum_slots(dot(grad_pre, w_up, 1, 1).reshape(n, rows, model))
        down_term = dot(hidden, cot, 0, 0).astype(BF)
        up_term = dot(norm_two, grad_pre, 0, 0).astype(BF)
        grad_mid = cot_low.astype(F32) + norm_back(grad_norm_two, hat_two, rs_two, weight_two)
        grad_branch = grad_mid.astype(BF)
        eh_two = grad_norm_two * hat_two
        grad_scale_two = eh_two * g_two
        gain_two_term = jnp.sum(eh_two * scale_two, axis=0)
        out_term = dot(attended, grad_branch, 1, 0).astype(BF)
        grad_attn = dot(w_out, grad_branch, 1, 1).astype(BF)

    if planar:

        def pieces_of(array, *lead):
            return array.reshape(lead + (-1, array.shape[-1]))

        (
            out_part, out_other, grad_attn, grad_mid, grad_scale_two, gain_two_term, up_term, down_term, out_term,
        ) = mid_pass(attended, tokens.reshape(rows, model), scale_two, g_two, w_out, w_up, down_w, cot)
        rest = (
            cosine, sine, tokens.reshape(rows, model), levels[None], g_one, scale_one, grad_mid,
            grad_scale_two, gain_two_term, out_part, out_other,
        )
        input_grad, layer_out, up_all, down_all, out_all, qkv_all, small_all = back_pass(
            grad_attn, qkv_heads, full, lse, pieces_of(up_term, n, ring), pieces_of(down_term, ring),
            pieces_of(out_term, n, ring), w_qkv, rest, block,
        )
        (
            up_grad, down_grad, out_grad, qkv_grad, time_grad, table_grad, gain_one_grad, gain_two_grad,
            input_grad, layer_out,
        ) = widen(up_all, down_all, out_all, qkv_all, small_all, table_rows, w_time, input_grad, layer_out)
        gain_one_grad, gain_two_grad = gain_one_grad[0], gain_two_grad[0]
    else:
        layer_out = middle + sum_slots(out_parts)
        up_share = lax.psum_scatter(
            up_term.reshape(n, model // n, -1), "ctx", scatter_dimension=1, tiled=True
        )
        down_share = lax.psum_scatter(down_term, "ctx", scatter_dimension=0, tiled=True)
        out_share = lax.psum_scatter(
            out_term.reshape(n, model // n, model), "ctx", scatter_dimension=1, tiled=True
        )
        grad_heads = to_heads(grad_attn.reshape(1, HEADS, HEAD, rows))
        back = to_tokens(attend_back(qkv_heads, grad_heads, full, lse, block))
        back = back.reshape(3, HEADS, 2, HEAD // 2, rows)
        unturned = turn(back[:2, :, 0].astype(F32), back[:2, :, 1].astype(F32), cosine, -sine)
        grad_qkv = jnp.concatenate([jnp.stack(unturned, axis=2).astype(BF), back[2:]])
        grad_qkv = grad_qkv.reshape(3 * model, rows)
        qkv_term = dot(norm_one, grad_qkv, 0, 1).astype(BF)
        grad_norm_one = dot(grad_qkv, w_qkv, 0, 1)

        input_grad = grad_mid + norm_back(grad_norm_one, hat_one, rs_one, weight_one)
        eh_one = grad_norm_one * hat_one
        grad_scale_one = eh_one * g_one
        gain_one_term = jnp.sum(eh_one * scale_one, axis=0)

        grad_shifts = jnp.concatenate([grad_scale_one, grad_scale_two], axis=1).astype(BF)
        level_term = dot(onehot.astype(BF), grad_shifts, 0, 0)
        gain_terms = jnp.concatenate([gain_one_term, gain_two_term])
        small = lax.psum(jnp.concatenate([level_term, gain_terms[None]]), ("ctx", "wt"))
        share = lax.psum_scatter(
            qkv_term.reshape(n, model // n, -1), "ctx", scatter_dimension=1, tiled=True
        )

        def spread_rows(share):
            return lax.all_gather(share, "ctx", axis=0, tiled=True).astype(F32)

        up_share = lax.all_to_all(up_share, "wt", 0, 0, tiled=True)
        up_grad = lax.all_gather(up_share, "ctx", axis=1, tiled=True).astype(F32)
        up_grad = jnp.transpose(up_grad, (1, 0, 2)).reshape(model // n, -1)
        down_grad = spread_rows(down_share)
        out_grad = spread_rows(sum_owned(out_share))
        qkv_grad = spread_rows(sum_owned(share))

        by_level = small[: table.shape[0]]
        gain_sums = small[table.shape[0]]
        levels_here, time_here = noise_table.shape[0], time_w.shape[0]
        high = lax.Precision.HIGHEST
        time_rows = lax.dynamic_slice_in_dim(table, me * time_here, time_here, 1).astype(F32)
        time_grad = lax.dot_general(
            time_rows, by_level, (((0,), (0,)), ((), ())), precision=high, preferred_element_type=F32
        )
        level_rows = lax.dynamic_slice_in_dim(by_level, me * levels_here, levels_here, 0)
        table_grad = lax.dot_general(
            level_rows, w_time.astype(F32), (((1,), (1,)), ((), ())), precision=high,
            preferred_element_type=F32,
        )

        gain_here = gain_one.shape[0]
        gain_one_grad = lax.dynamic_slice_in_dim(gain_sums, me * gain_here, gain_here, 0)
        gain_two_grad = lax.dynamic_slice_in_dim(gain_sums, model + me * gain_here, gain_here, 0)

    return (
        layer_out.astype(BF).reshape(tokens.shape),
        input_grad.astype(BF).reshape(tokens.shape),
        qkv_grad,
        out_grad,
        up_grad,
        down_grad,
        time_grad,
        table_grad,
        gain_one_grad,
        gain_two_grad,
    )


def sum_owned(share):
    n, me = lax.axis_size("wt"), lax.axis_index("wt")
    slots = jnp.stack(
        [lax.dynamic_index_in_dim(share, lax.rem(me + k, n), 0, keepdims=False) for k in range(n)]
    )
    return sum_slots(slots.astype(F32)).astype(BF)


def solution(mesh):
    rows = P(None, "wt", "ctx", None)
    marks = P(None, "wt", "ctx")
    weight = P("wt", None)
    gain = P("wt")
    return jax.shard_map(
        shards,
        mesh=mesh,
        in_specs=(rows, marks, marks) + (weight,) * 6 + (gain, gain, rows),
        out_specs=(rows, rows) + (weight,) * 6 + (gain, gain),
        check_vma=False,
    )
```
